32 devices in a mesh: wide: 8 (over y, x, core), narrow: 4 (over z).
Axes of the slice: x: 2, y: 2, z: 4, core: 2. Of those that a mesh axis runs over, the one named last changes fastest.
Arguments:
- tokens: bfloat16 [10240, 2048], P(('wide', 'narrow')), may hold values from -6 to 6
- cotangent: bfloat16 [10240, 2048], P(('wide', 'narrow')), may hold values from -6 to 6
- lengths: int32 [32], P(('wide', 'narrow')), may hold values from 40 to 320, as said below
- positions: int32 [10240], P(('wide', 'narrow')), may hold values from 0 to 319, as said below
- norm_attn: bfloat16 [2048], P(('wide', 'narrow')), may hold values from 0.25 to 1.75
- w_query: bfloat16 [2048, 2048], P(('wide', 'narrow')), may hold values from -0.1875 to 0.1875
- w_key: bfloat16 [2048, 256], P(('wide', 'narrow')), may hold values from -0.1875 to 0.1875
- w_value: bfloat16 [2048, 256], P(('wide', 'narrow')), may hold values from -0.125 to 0.125
- w_output: bfloat16 [2048, 2048], P(('wide', 'narrow')), may hold values from -0.5 to 0.5
- norm_mlp: bfloat16 [2048], P(('wide', 'narrow')), may hold values from 0.25 to 1.75
- w_gate: bfloat16 [2048, 5632], P(('wide', 'narrow')), may hold values from -0.125 to 0.125
- w_up: bfloat16 [2048, 5632], P(('wide', 'narrow')), may hold values from -0.125 to 0.125
- w_down: bfloat16 [2048, 5632], P(('wide', 'narrow')), may hold values from -0.109375 to 0.109375
Outputs:
- output: bfloat16 [10240, 2048], P(('wide', 'narrow'))
- grad_tokens: float32 [10240, 2048], P(('wide', 'narrow'))
- grad_norm_attn: float32 [2048], P(('wide', 'narrow'))
- grad_w_query: float32 [2048, 2048], P(('wide', 'narrow'))
- grad_w_key: float32 [2048, 256], P(('wide', 'narrow'))
- grad_w_value: float32 [2048, 256], P(('wide', 'narrow'))
- grad_w_output: float32 [2048, 2048], P(('wide', 'narrow'))
- grad_norm_mlp: float32 [2048], P(('wide', 'narrow'))
- grad_w_gate: float32 [2048, 5632], P(('wide', 'narrow'))
- grad_w_up: float32 [2048, 5632], P(('wide', 'narrow'))
- grad_w_down: float32 [2048, 5632], P(('wide', 'narrow'))
The draws below stay inside these ranges and needn't reach their ends.
Inputs may be any that keep to these rules, and one draw needn't show every extreme that they name: `lengths`: one sequence of every draw uses all 320 slots. Within a sequence positions rise by one from slot to slot and restart at 0 where a packed document starts; every sequence starts at position 0, and the first sequence holds a single document.
All inputs are finite; a program needn't handle non-finite values.
Results may differ from the reference program's by a relative error of at most 0.014.
The reference program's roundings to bfloat16 on the way count: a program that leaves them out, or rounds other values in their place, can miss the bound.
Values may be sent and summed in bfloat16 or wider, within the bound.
A program may use at most 384 MiB of HBM per device.

```python
import math
import jax
import jax.numpy as jnp
from jax import lax

D = 2048
QUERY_HEADS = 32
KEY_VALUE_HEADS = 4
HEAD_SIZE = 64
FF = 5632
SLOTS = 320
QD = 2048
KD = 256
SEQS = 32
TOKENS = 10240


def draw_lengths(key, part):
    drawn_lengths = jax.random.randint(key, (SEQS,), SLOTS // 8, SLOTS + 1, dtype=jnp.int32)
    chosen = jax.random.randint(jax.random.fold_in(key, 7), (), 0, SEQS, dtype=jnp.int32)
    return jnp.where(jnp.arange(SEQS, dtype=jnp.int32) == chosen, SLOTS, drawn_lengths).astype(jnp.int32)


def draw_positions(key, part):
    doc_marks = jax.random.randint(key, (SEQS, SLOTS), 0, 48, dtype=jnp.int32) == 0
    doc_marks = jnp.logical_and(doc_marks, jnp.arange(SEQS, dtype=jnp.int32)[:, None] > 0)
    slot_index = jnp.broadcast_to(jnp.arange(SLOTS, dtype=jnp.int32)[None, :], (SEQS, SLOTS))
    starts = lax.cummax(jnp.where(doc_marks, slot_index, 0), axis=1)
    return (slot_index - starts).reshape(SEQS * SLOTS).astype(jnp.int32)


def raised(values, stream_key, source, target, parts, factor):
    def block_of(dim):
        return (jnp.arange(values.shape[dim]) // (values.shape[dim] // parts)).reshape((-1,) + (1,) * (values.ndim - 1 - dim))

    first = jax.random.permutation(stream_key, parts)[block_of(target)]
    far = (block_of(target) + parts // 2) % parts
    return jnp.where((block_of(source) == first) | (block_of(source) == far), factor * values, values)


def steps_of(rng, extent, pieces, least, high):
    loudness, own = 1.0, jax.random.fold_in(rng, 6)
    for position, shards_of in pieces:
        draws = jnp.exp(jax.random.uniform(jax.random.fold_in(own, position), (shards_of,), jnp.float32, least / len(pieces), high / len(pieces)))
        loudness = loudness * jnp.repeat(draws, extent[position] // shards_of).reshape([-1 if axis == position else 1 for axis in range(len(extent))])
    return loudness


def gaussian(own_key, dims, width, bound, split=(), kind=jnp.bfloat16):
    loudness = steps_of(own_key, dims, split, -0.22, 0.18) if split else 1.0
    drawn = jax.random.normal(own_key, dims, jnp.float32) * width * loudness
    return jnp.minimum(jnp.maximum(drawn, -bound), bound).astype(kind)


def heavy_noise(own_key, dims, scale, limit, pieces, heavy, held_as=jnp.bfloat16):
    values = scale * jax.random.normal(own_key, dims, jnp.float32)
    if pieces:
        values = values * steps_of(own_key, dims, pieces, -0.22, 0.18)
    return jnp.clip(raised(values, jax.random.fold_in(own_key, 3), *heavy), -limit, limit).astype(held_as)


def setup_inputs(seed: int = 0) -> dict:
    splits = jax.random.split(jax.random.key(seed), 14)
    return {
        "tokens": heavy_noise(splits[0], (TOKENS, D), 1.0, 6.0, ((0, 32),), (0, 1, 32, 2.75)),
        "cotangent": heavy_noise(splits[1], (TOKENS, D), 1.0, 6.0, ((0, 32),), (0, 1, 32, 2.75)),
        "lengths": draw_lengths(jax.random.fold_in(splits[13], 71), 0),
        "positions": draw_positions(jax.random.fold_in(splits[13], 71), 0),
        "norm_attn": jnp.clip(1.0 + 0.15 * jax.random.normal(splits[4], (D,), jnp.float32), 0.25, 1.75).astype(jnp.bfloat16),
        "w_query": gaussian(splits[5], (D, QD), (D // 2) ** -0.5, 0.1875, ((0, 32),)),
        "w_key": gaussian(splits[6], (D, KD), (D // 2) ** -0.5, 0.1875, ((0, 32),)),
        "w_value": gaussian(splits[7], (D, KD), D ** -0.5, 0.125, ((0, 32),)),
        "w_output": gaussian(splits[8], (D, QD), (QD // 16) ** -0.5, 0.5, ((0, 32),)),
        "norm_mlp": jnp.clip(1.0 + 0.15 * jax.random.normal(splits[9], (D,), jnp.float32), 0.25, 1.75).astype(jnp.bfloat16),
        "w_gate": gaussian(splits[10], (D, FF), D ** -0.5, 0.125, ((0, 32),)),
        "w_up": gaussian(splits[11], (D, FF), D ** -0.5, 0.125, ((0, 32),)),
        "w_down": gaussian(splits[12], (D, FF), (FF // 2) ** -0.5, 0.109375, ((0, 32),)),
    }


@jax.custom_vjp
def reduced_precision(v):
    return lax.optimization_barrier(v.astype(jnp.bfloat16)).astype(jnp.float32)

@jax.custom_vjp
def low_back(v):
    return v

def low_keep(v):
    return (reduced_precision(v), None)

def low_pass(kept, grad):
    return (grad,)

def back_keep(v):
    return (v, None)

def back_low(kept, grad):
    return (reduced_precision(grad),)
reduced_precision.defvjp(low_keep, low_pass)
low_back.defvjp(back_keep, back_low)
norm_eps = 1e-05
rope_base = 10000.0
masked_score = -1e+30
highest = lax.Precision.HIGHEST

def rope_tables(positions):
    half_dim = HEAD_SIZE // 2
    inv_freq = jnp.exp(-math.log(rope_base) * jnp.arange(half_dim, dtype=jnp.float32) * 2.0 / HEAD_SIZE)
    angles = positions.astype(jnp.float32)[..., None] * inv_freq
    cosine = jnp.cos(angles)
    sine_part = jnp.sin(angles)
    return (jnp.concatenate([cosine, cosine], -1), jnp.concatenate([sine_part, sine_part], -1))

def apply_rotary(values, cosine_table, sine_table):
    half_dim = values.shape[-1] // 2
    turned = jnp.concatenate([-values[..., half_dim:], values[..., :half_dim]], -1)
    return values * cosine_table[..., None, :] + turned * sine_table[..., None, :]

def normalize(values):
    return values * lax.rsqrt(lax.optimization_barrier(jnp.mean(values * values, axis=-1, keepdims=True)) + norm_eps)

def layer(token_rows, gain_attn, w_query, w_key, w_value, w_output, gain_mlp, w_gate, w_up, w_down, cosine_table, sine_table, valid_rows):
    batch_total = token_rows.shape[0]
    row_total_count = token_rows.shape[1]
    heads_per_group = QUERY_HEADS // KEY_VALUE_HEADS
    scaled_attn = reduced_precision(normalize(token_rows) * gain_attn)
    query_pre = low_back(jnp.einsum('btd,de->bte', scaled_attn, w_query, precision=highest))
    key_unrotated = low_back(jnp.einsum('btd,de->bte', scaled_attn, w_key, precision=highest))
    value_reduced = reduced_precision(low_back(jnp.einsum('btd,de->bte', scaled_attn, w_value, precision=highest)))
    query_rotated = reduced_precision(apply_rotary(query_pre.reshape(batch_total, row_total_count, QUERY_HEADS, HEAD_SIZE), cosine_table, sine_table))
    key_rotated = reduced_precision(apply_rotary(key_unrotated.reshape(batch_total, row_total_count, KEY_VALUE_HEADS, HEAD_SIZE), cosine_table, sine_table))
    value_head_rows = value_reduced.reshape(batch_total, row_total_count, KEY_VALUE_HEADS, HEAD_SIZE)
    query_rotated = query_rotated.reshape(batch_total, row_total_count, KEY_VALUE_HEADS, heads_per_group, HEAD_SIZE)
    raw_scores = low_back(jnp.einsum('bqhrd,bkhd->bhrqk', query_rotated, key_rotated, precision=highest))
    causal = jnp.arange(row_total_count)[:, None] >= jnp.arange(row_total_count)[None, :]
    scores = jnp.where(causal, raw_scores * HEAD_SIZE ** (-0.5), masked_score)
    row_peak = lax.optimization_barrier(jnp.max(scores, axis=-1, keepdims=True))
    exp_scores = jnp.exp(scores - row_peak)
    probs = exp_scores / lax.optimization_barrier(jnp.sum(exp_scores, axis=-1, keepdims=True))
    context = jnp.einsum('bhrqk,bkhd->bqhrd', reduced_precision(probs), value_head_rows, precision=highest)
    context = reduced_precision(low_back(context.reshape(batch_total, row_total_count, QUERY_HEADS * HEAD_SIZE)))
    attn_out = low_back(jnp.einsum('btc,dc->btd', context, w_output, precision=highest))
    hidden = token_rows + attn_out
    scaled_mlp = reduced_precision(normalize(hidden) * gain_mlp)
    gate_proj = low_back(jnp.einsum('btd,df->btf', scaled_mlp, w_gate, precision=highest))
    up_proj = low_back(jnp.einsum('btd,df->btf', scaled_mlp, w_up, precision=highest))
    mixed_low = reduced_precision(gate_proj * jax.nn.sigmoid(gate_proj) * up_proj)
    mlp_out = low_back(jnp.einsum('btf,df->btd', mixed_low, w_down, precision=highest))
    return valid_rows * (hidden + mlp_out)

def reference(tokens, cotangent, lengths, positions, norm_attn, w_query, w_key, w_value, w_output, norm_mlp, w_gate, w_up, w_down):
    upper_group = max(1, min(SEQS, 4096 // SLOTS))
    group_size = max([candidate for candidate in range(1, upper_group + 1) if SEQS % candidate == 0])
    step_count = SEQS // group_size
    params = tuple((weight.astype(jnp.float32) for weight in (norm_attn, w_query, w_key, w_value, w_output, norm_mlp, w_gate, w_up, w_down)))
    token_blocks = tokens.astype(jnp.float32).reshape(step_count, group_size, SLOTS, D)
    cot_blocks = cotangent.astype(jnp.float32).reshape(step_count, group_size, SLOTS, D)
    length_blocks = lengths.reshape(step_count, group_size)
    position_blocks = positions.reshape(step_count, group_size, SLOTS)

    def one_step(totals, blocks):
        token_block, cot_block, length_block, position_block = blocks
        cosine_table, sine_table = rope_tables(position_block)
        valid_rows = (jnp.arange(SLOTS)[None, :] < length_block[:, None]).astype(jnp.float32)[..., None]

        def forward(token_rows, *weights):
            return layer(token_rows, *weights, cosine_table, sine_table, valid_rows)
        result, pullback = jax.vjp(forward, token_block, *params)
        grad_list = pullback(cot_block)
        totals = tuple((running + addend for running, addend in zip(totals, grad_list[1:])))
        return (totals, (result.astype(jnp.bfloat16), grad_list[0]))
    zero_sums = tuple((jnp.zeros(weight.shape, jnp.float32) for weight in params))
    totals, (outputs, input_grads) = lax.scan(one_step, zero_sums, (token_blocks, cot_blocks, length_blocks, position_blocks))
    return (outputs.reshape(TOKENS, D), input_grads.reshape(TOKENS, D), totals[0], totals[1], totals[2], totals[3], totals[4], totals[5], totals[6], totals[7], totals[8])
```

```python
import functools
import math

import jax
import jax.numpy as jnp
from jax import lax
from jax.experimental import pallas as pl
from jax.experimental.pallas import tpu as pltpu
from jax.sharding import PartitionSpec as P

QUERY_HEADS = 32
KEY_VALUE_HEADS = 4
HEAD_SIZE = 64


norm_eps = 1e-05
rope_base = 10000.0
masked_score = -1e30
contract_last = (((1,), (1,)), ((), ()))
contract_first = (((0,), (0,)), ((), ()))


def rope_tables(positions):
    half_dim = HEAD_SIZE // 2
    inv_freq = jnp.exp(
        -math.log(rope_base) * jnp.arange(half_dim, dtype=jnp.float32) * 2.0 / HEAD_SIZE
    )
    angles = positions.astype(jnp.float32)[..., None] * inv_freq
    cosine = jnp.cos(angles)
    sine_part = jnp.sin(angles)
    return (jnp.concatenate([cosine, cosine], -1), jnp.concatenate([sine_part, sine_part], -1))


def apply_rotary(values, cosine_table, sine_table):
    half_dim = values.shape[-1] // 2
    turned = jnp.concatenate([-values[..., half_dim:], values[..., :half_dim]], -1)
    return values * cosine_table[..., None, :] + turned * sine_table[..., None, :]


def invert_rotary(grad_rows, cosine_table, sine_table):
    half_dim = grad_rows.shape[-1] // 2
    with_cos = grad_rows * cosine_table[..., None, :]
    with_sin = grad_rows * sine_table[..., None, :]
    return with_cos + jnp.concatenate([with_sin[..., half_dim:], -with_sin[..., :half_dim]], -1)


def normalize(values):
    return values * lax.rsqrt(jnp.mean(values * values, axis=-1, keepdims=True) + norm_eps)


def norm_back(grad_hat, normed, values):
    row_scale = lax.rsqrt(jnp.mean(values * values, axis=-1, keepdims=True) + norm_eps)
    return row_scale * (grad_hat - normed * jnp.mean(grad_hat * normed, axis=-1, keepdims=True))


def attention_inputs(normed, norm_attn, w_query, w_key, w_value):
    gain_piece = lax.all_gather(norm_attn, ("wide", "narrow"), axis=0, tiled=True)
    query_rows = lax.all_gather(w_query, ("wide", "narrow"), axis=0, tiled=True)
    key_rows = lax.all_gather(w_key, ("wide", "narrow"), axis=0, tiled=True)
    value_rows = lax.all_gather(w_value, ("wide", "narrow"), axis=0, tiled=True)
    gain_float = gain_piece.astype(jnp.float32)
    columns = (normed * gain_float).astype(jnp.bfloat16)
    query_sum = jnp.dot(columns, query_rows, preferred_element_type=jnp.float32)
    key_sum = jnp.dot(columns, key_rows, preferred_element_type=jnp.float32)
    value_sum = jnp.dot(columns, value_rows, preferred_element_type=jnp.float32)
    return (gain_float, columns, query_sum, key_sum, value_sum)


def mlp_inputs(normed, norm_mlp, w_gate, w_up):
    gain_piece = lax.all_gather(norm_mlp, ("wide", "narrow"), axis=0, tiled=True)
    gate_rows = lax.all_gather(w_gate, ("wide", "narrow"), axis=0, tiled=True)
    up_rows = lax.all_gather(w_up, ("wide", "narrow"), axis=0, tiled=True)
    gain_float = gain_piece.astype(jnp.float32)
    columns = (normed * gain_float).astype(jnp.bfloat16)
    gate_sum = jnp.dot(columns, gate_rows, preferred_element_type=jnp.float32)
    up_sum = jnp.dot(columns, up_rows, preferred_element_type=jnp.float32)
    return (gain_float, columns, gate_sum, up_sum)


def head_slices(query_rotated, key_rotated, value_reduced, shared_key_head):
    row_total_count = query_rotated.shape[0]
    heads_per_group = QUERY_HEADS // KEY_VALUE_HEADS
    query_head = query_rotated[
        :,
        shared_key_head
        * heads_per_group
        * HEAD_SIZE : (shared_key_head + 1)
        * heads_per_group
        * HEAD_SIZE,
    ].reshape(row_total_count, heads_per_group, HEAD_SIZE)
    key_head = key_rotated[:, shared_key_head * HEAD_SIZE : (shared_key_head + 1) * HEAD_SIZE]
    value_head = value_reduced[:, shared_key_head * HEAD_SIZE : (shared_key_head + 1) * HEAD_SIZE]
    return (query_head, key_head, value_head)


def head_scores(query_head, key_head):
    row_total_count = query_head.shape[0]
    causal = jnp.arange(row_total_count)[:, None] >= jnp.arange(row_total_count)[None, :]
    raw_scores = jnp.einsum("qrd,kd->rqk", query_head, key_head, preferred_element_type=jnp.float32)
    return jnp.where(causal, raw_scores * HEAD_SIZE ** (-0.5), masked_score)


def attend(query_rotated, key_rotated, value_reduced):
    row_total_count = query_rotated.shape[0]
    heads_per_group = QUERY_HEADS // KEY_VALUE_HEADS
    contexts = []
    log_totals = []
    for shared_key_head in range(KEY_VALUE_HEADS):
        query_head, key_head, value_head = head_slices(
            query_rotated, key_rotated, value_reduced, shared_key_head
        )
        scores = head_scores(query_head, key_head)
        row_peak = jnp.max(scores, axis=-1, keepdims=True)
        exp_scores = jnp.exp(scores - row_peak)
        row_total = jnp.sum(exp_scores, axis=-1, keepdims=True)
        probs = exp_scores / row_total
        context_head = jnp.einsum(
            "rqk,kd->qrd",
            probs.astype(jnp.bfloat16),
            value_head,
            preferred_element_type=jnp.float32,
        )
        contexts.append(context_head.reshape(row_total_count, heads_per_group * HEAD_SIZE))
        log_totals.append(row_peak + jnp.log(row_total))
    return (jnp.concatenate(contexts, 1).astype(jnp.bfloat16), log_totals)


def attend_back(query_rotated, key_rotated, value_reduced, log_totals, grad_context):
    row_total_count = query_rotated.shape[0]
    heads_per_group = QUERY_HEADS // KEY_VALUE_HEADS
    score_scale = HEAD_SIZE ** (-0.5)
    query_grads = []
    key_grads = []
    value_grads = []
    for shared_key_head in range(KEY_VALUE_HEADS):
        query_head, key_head, value_head = head_slices(
            query_rotated, key_rotated, value_reduced, shared_key_head
        )
        scores = head_scores(query_head, key_head)
        probs = jnp.exp(scores - log_totals[shared_key_head])
        probs_low = probs.astype(jnp.bfloat16)
        grad_head = grad_context[
            :,
            shared_key_head
            * heads_per_group
            * HEAD_SIZE : (shared_key_head + 1)
            * heads_per_group
            * HEAD_SIZE,
        ].reshape(row_total_count, heads_per_group, HEAD_SIZE)
        grad_probs = jnp.einsum(
            "qrd,kd->rqk", grad_head, value_head, preferred_element_type=jnp.float32
        )
        value_grads.append(
            jnp.einsum("rqk,qrd->kd", probs_low, grad_head, preferred_element_type=jnp.float32)
        )
        inner_sum = jnp.sum(grad_probs * probs, axis=-1, keepdims=True)
        grad_scores = (probs * (grad_probs - inner_sum) * score_scale).astype(jnp.bfloat16)
        query_grad = jnp.einsum(
            "rqk,kd->qrd", grad_scores, key_head, preferred_element_type=jnp.float32
        )
        query_grads.append(query_grad.reshape(row_total_count, heads_per_group * HEAD_SIZE))
        key_grads.append(
            jnp.einsum("rqk,qrd->kd", grad_scores, query_head, preferred_element_type=jnp.float32)
        )
    return (
        jnp.concatenate(query_grads, 1),
        jnp.concatenate(key_grads, 1),
        jnp.concatenate(value_grads, 1),
    )


def make_term(width_sides, other_sides):
    down_side, mlp_side, attn_side, qkv_side = width_sides
    mixed_rows, gate_rows, up_rows, context_rows, query_rows, key_rows, value_rows = other_sides

    def grad_term(first_row, row_span):
        pieces = [
            lax.dot_general(
                down_side, mixed_rows, contract_first, preferred_element_type=jnp.float32
            ),
            lax.dot_general(
                mlp_side, gate_rows, contract_first, preferred_element_type=jnp.float32
            ),
            lax.dot_general(mlp_side, up_rows, contract_first, preferred_element_type=jnp.float32),
            lax.dot_general(
                attn_side, context_rows, contract_first, preferred_element_type=jnp.float32
            ),
            lax.dot_general(
                qkv_side, query_rows, contract_first, preferred_element_type=jnp.float32
            ),
            lax.dot_general(qkv_side, key_rows, contract_first, preferred_element_type=jnp.float32),
            lax.dot_general(
                qkv_side, value_rows, contract_first, preferred_element_type=jnp.float32
            ),
        ]
        return jnp.concatenate(pieces, 1)

    return grad_term


def per_device(
    tokens,
    cotangent,
    lengths,
    positions,
    norm_attn,
    w_query,
    w_key,
    w_value,
    w_output,
    norm_mlp,
    w_gate,
    w_up,
    w_down,
):
    row_total_count = tokens.shape[0]
    shard_rows = w_query.shape[0]
    query_width = w_query.shape[1]
    key_width = w_key.shape[1]
    hidden_width = w_gate.shape[1]
    inputs = tokens.astype(jnp.float32)
    valid_rows = (jnp.arange(row_total_count) < lengths[0]).astype(jnp.float32)[:, None]
    cosine_table, sine_table = rope_tables(positions)
    normed_attn = normalize(inputs)
    gain_attn_full, scaled_attn, query_pre, key_unrotated, value_pre = attention_inputs(
        normed_attn, norm_attn, w_query, w_key, w_value
    )
    query_rotated = (
        apply_rotary(
            query_pre.reshape(row_total_count, QUERY_HEADS, HEAD_SIZE), cosine_table, sine_table
        )
        .reshape(row_total_count, query_width)
        .astype(jnp.bfloat16)
    )
    key_rotated = (
        apply_rotary(
            key_unrotated.reshape(row_total_count, KEY_VALUE_HEADS, HEAD_SIZE),
            cosine_table,
            sine_table,
        )
        .reshape(row_total_count, key_width)
        .astype(jnp.bfloat16)
    )
    value_reduced = value_pre.astype(jnp.bfloat16)
    context, log_totals = attend(query_rotated, key_rotated, value_reduced)
    attn_out = lax.dot_general(
        context,
        lax.all_gather(w_output, ("wide", "narrow"), axis=0, tiled=True),
        contract_last,
        preferred_element_type=jnp.float32,
    )
    hidden = inputs + attn_out
    normed_mlp = normalize(hidden)
    gain_mlp_full, scaled_mlp, gate_proj, up_proj = mlp_inputs(normed_mlp, norm_mlp, w_gate, w_up)
    mixed_low = (gate_proj * jax.nn.sigmoid(gate_proj) * up_proj).astype(jnp.bfloat16)
    mlp_out = lax.dot_general(
        mixed_low,
        lax.all_gather(w_down, ("wide", "narrow"), axis=0, tiled=True),
        contract_last,
        preferred_element_type=jnp.float32,
    )
    output = (valid_rows * (hidden + mlp_out)).astype(jnp.bfloat16)
    grad_y = cotangent.astype(jnp.float32) * valid_rows
    grad_y_low = grad_y.astype(jnp.bfloat16)
    grad_cols = grad_y_low
    grad_mixed = jnp.dot(
        grad_cols,
        lax.all_gather(w_down, ("wide", "narrow"), axis=0, tiled=True),
        preferred_element_type=jnp.float32,
    )
    again_values = mlp_inputs(normed_mlp, norm_mlp, w_gate, w_up)
    gate_proj = again_values[2]
    up_proj = again_values[3]
    sigmoid_gate = jax.nn.sigmoid(gate_proj)
    grad_gate = (
        grad_mixed * up_proj * (sigmoid_gate * (1.0 + gate_proj * (1.0 - sigmoid_gate)))
    ).astype(jnp.bfloat16)
    grad_up = (grad_mixed * (gate_proj * sigmoid_gate)).astype(jnp.bfloat16)
    gate_rows = lax.all_gather(w_gate, ("wide", "narrow"), axis=0, tiled=True)
    up_rows = lax.all_gather(w_up, ("wide", "narrow"), axis=0, tiled=True)
    columns = lax.dot_general(
        grad_gate, gate_rows, contract_last, preferred_element_type=jnp.float32
    )
    columns = columns + lax.dot_general(
        grad_up, up_rows, contract_last, preferred_element_type=jnp.float32
    )
    grad_xn2 = columns
    grad_gain_mlp = jnp.sum(grad_xn2 * normed_mlp, axis=0)
    grad_hidden = grad_y + norm_back(grad_xn2 * gain_mlp_full, normed_mlp, hidden)
    grad_attn_low = grad_hidden.astype(jnp.bfloat16)
    grad_cols = grad_attn_low
    grad_context = jnp.dot(
        grad_cols,
        lax.all_gather(w_output, ("wide", "narrow"), axis=0, tiled=True),
        preferred_element_type=jnp.float32,
    )
    grad_context = grad_context.astype(jnp.bfloat16)
    grad_query_rot, gradient_key_rotated, grad_value_sum = attend_back(
        query_rotated, key_rotated, value_reduced, log_totals, grad_context
    )
    grad_query = (
        invert_rotary(
            grad_query_rot.reshape(row_total_count, QUERY_HEADS, HEAD_SIZE),
            cosine_table,
            sine_table,
        )
        .reshape(row_total_count, query_width)
        .astype(jnp.bfloat16)
    )
    grad_key = (
        invert_rotary(
            gradient_key_rotated.reshape(row_total_count, KEY_VALUE_HEADS, HEAD_SIZE),
            cosine_table,
            sine_table,
        )
        .reshape(row_total_count, key_width)
        .astype(jnp.bfloat16)
    )
    grad_value = grad_value_sum.astype(jnp.bfloat16)
    query_rows = lax.all_gather(w_query, ("wide", "narrow"), axis=0, tiled=True)
    key_rows = lax.all_gather(w_key, ("wide", "narrow"), axis=0, tiled=True)
    value_rows = lax.all_gather(w_value, ("wide", "narrow"), axis=0, tiled=True)
    columns = lax.dot_general(
        grad_query, query_rows, contract_last, preferred_element_type=jnp.float32
    )
    columns = columns + lax.dot_general(
        grad_key, key_rows, contract_last, preferred_element_type=jnp.float32
    )
    columns = columns + lax.dot_general(
        grad_value, value_rows, contract_last, preferred_element_type=jnp.float32
    )
    local_term = make_term(
        (grad_y_low, scaled_mlp, grad_attn_low, scaled_attn),
        (mixed_low, grad_gate, grad_up, context, grad_query, grad_key, grad_value),
    )
    all_sums = lax.psum_scatter(
        local_term(jnp.int32(0), lax.axis_size(("wide", "narrow")) * shard_rows),
        ("wide", "narrow"),
        scatter_dimension=0,
        tiled=True,
    )
    edges = [0]
    for width in (
        hidden_width,
        hidden_width,
        hidden_width,
        query_width,
        query_width,
        key_width,
        key_width,
    ):
        edges.append(edges[-1] + width)
    grad_w_down = all_sums[:, edges[0] : edges[1]]
    grad_w_gate = all_sums[:, edges[1] : edges[2]]
    grad_w_up = all_sums[:, edges[2] : edges[3]]
    grad_w_output = all_sums[:, edges[3] : edges[4]]
    grad_w_query = all_sums[:, edges[4] : edges[5]]
    grad_w_key = all_sums[:, edges[5] : edges[6]]
    grad_w_value = all_sums[:, edges[6] : edges[7]]
    grad_gain_attn = jnp.sum(columns * normed_attn, axis=0)
    grad_tokens = grad_hidden + norm_back(columns * gain_attn_full, normed_attn, inputs)
    grad_norm_attn, grad_norm_mlp = (
        lax.psum_scatter(grad_gain_attn, ("wide", "narrow"), scatter_dimension=0, tiled=True),
        lax.psum_scatter(grad_gain_mlp, ("wide", "narrow"), scatter_dimension=0, tiled=True),
    )
    return (
        output,
        grad_tokens,
        grad_norm_attn,
        grad_w_query,
        grad_w_key,
        grad_w_value,
        grad_w_output,
        grad_norm_mlp,
        grad_w_gate,
        grad_w_up,
        grad_w_down,
    )


MESH = pl.DeviceIdType.MESH
ANY = pl.BlockSpec(memory_space=pl.ANY)

CHIPS, CORES = 4, 2

def place():
    w = lax.axis_index("wide"); n = lax.axis_index("narrow")
    return w // CORES, w % CORES, n

def remote(src, dst, send, recv, chip, core, z):
    return pltpu.make_async_remote_copy(src_ref=src, dst_ref=dst, send_sem=send, recv_sem=recv,
        device_id={"wide": chip * CORES + core, "narrow": z}, device_id_type=MESH)

def hello(partners):
    barrier = pltpu.get_barrier_semaphore()
    count = 0
    for cond, chip, core, z in partners:
        def sig(chip=chip, core=core, z=z):
            pl.semaphore_signal(barrier, inc=1, device_id={"wide": chip * CORES + core, "narrow": z}, device_id_type=MESH)
        if cond is None:
            sig(); count = count + 1
        else:
            pl.when(cond)(sig); count = count + jnp.where(cond, 1, 0)
    pl.semaphore_wait(barrier, count)

def gather_kernel(nz, wq, wk, wv, wo, gains, wg, wu, wd, gy, QKV, WO, GAIN, G0, G1, G2, GY,
                  loc, a2a_s, a2a_r, gy_s, gy_r, z_s, z_r, d_s, d_r, p_s, p_r, e_s, e_r):
    c, k, n = place()
    G = (G0, G1, G2); W = (wg, wu, wd)
    cols = G0.shape[-1]
    rows = wq.shape[0]
    other = 1 - k
    left, right = n > 0, n < nz - 1
    others = [(c + i) % CHIPS for i in range(1, CHIPS)]
    hello([(None, cc, k, n) for cc in others] + [(None, c, other, n), (left, c, k, n - 1), (right, c, k, n + 1)])
    kn = k * nz + n
    b = (c * CORES + k) * nz + n
    started = []
    def start(cond, desc):
        if cond is None: desc.start()
        else: pl.when(cond)(lambda: desc.start())
        started.append((cond, desc))
    def recv(cond, desc):
        if cond is None: desc.wait_recv()
        else: pl.when(cond)(lambda: desc.wait_recv())
    def blk(z): return pl.ds(pl.multiple_of(((c * CORES + k) * nz + z) * rows, rows), rows)
    mine = blk(n)
    q, kv = wq.shape[1], wk.shape[1]
    for i, cc in enumerate(others):
        for m in range(3):
            start(None, remote(W[m].at[:, pl.ds(pl.multiple_of(cc * cols, 128), cols)], G[m].at[c, kn], a2a_s.at[m, i], a2a_r.at[m, i], cc, k, n))
    own = [pltpu.make_async_copy(wq, QKV.at[mine, pl.ds(0, q)], loc.at[0]),
           pltpu.make_async_copy(wk, QKV.at[mine, pl.ds(q, kv)], loc.at[1]),
           pltpu.make_async_copy(wv, QKV.at[mine, pl.ds(q + kv, kv)], loc.at[2]),
           pltpu.make_async_copy(wo, WO.at[mine], loc.at[3]),
           pltpu.make_async_copy(gains, GAIN.at[mine], loc.at[4])]
    ownff = [pltpu.make_async_copy(W[m].at[:, pl.ds(pl.multiple_of(c * cols, 128), cols)], G[m].at[c, kn], loc.at[5 + m]) for m in range(3)]
    owngy = pltpu.make_async_copy(gy, GY.at[c], loc.at[8])
    for cp in own + ownff + [owngy]: cp.start()
    for cp in own: cp.wait()
    A = (QKV, WO, GAIN)
    def zsend(item, ref, dirn, s):
        cond = (right & (n - s >= 0)) if dirn == 0 else (left & (n + s <= nz - 1))
        z = n + 1 if dirn == 0 else n - 1
        return cond, remote(ref, ref, z_s.at[item, dirn, s], z_r.at[item, dirn, s], c, k, z)
    def zrecv(item, ref, dirn, s):
        cond = (n - s >= 0) if dirn == 0 else (n + s <= nz - 1)
        return cond, remote(ref, ref, z_s.at[item, dirn, s - 1], z_r.at[item, dirn, s - 1], c, k, n)
    def origin(dirn, s):
        o = n - s if dirn == 0 else n + s
        return jnp.clip(o, 0, nz - 1)
    for a in range(3):
        for dirn in range(2):
            start(*zsend(a, A[a].at[mine], dirn, 0))
    for i, cc in enumerate(others):
        start(None, remote(gy, GY.at[c], gy_s.at[i], gy_r.at[i], cc, k, n))
    for s in range(1, nz):
        for dirn in range(2):
            for a in range(3):
                ref = A[a].at[blk(origin(dirn, s))]
                recv(*zrecv(a, ref, dirn, s))
                if s < nz - 1: start(*zsend(a, ref, dirn, s))
    def part(cc, kk): return pl.ds(pl.multiple_of((cc * CORES + kk) * nz * rows, rows), nz * rows)
    for a in range(3):
        for i, cc in enumerate(others):
            start(None, remote(A[a].at[part(c, k)], A[a].at[part(c, k)], p_s.at[a, i], p_r.at[a, i], cc, k, n))
        start(None, remote(A[a].at[part(c, k)], A[a].at[part(c, k)], d_s.at[a, 0], d_r.at[a, 0], c, other, n))
    for m in range(3):
        ownff[m].wait()
        for i in range(CHIPS - 1):
            remote(G[m].at[c, kn], G[m].at[c, kn], a2a_s.at[m, i], a2a_r.at[m, i], c, k, n).wait_recv()
        ref = G[m].at[:, kn]
        for dirn in range(2): start(*zsend(3 + m, ref, dirn, 0))
        start(None, remote(ref, ref, e_s.at[m, 0, 0], e_r.at[m, 0, 0], c, other, n))
    for s in range(1, nz):
        for dirn in range(2):
            for m in range(3):
                ref = G[m].at[:, k * nz + origin(dirn, s)]
                cond, d = zrecv(3 + m, ref, dirn, s)
                recv(cond, d)
                if s < nz - 1: start(*zsend(3 + m, ref, dirn, s))
                start(cond, remote(ref, ref, e_s.at[m, dirn, s], e_r.at[m, dirn, s], c, other, n))
    for i in range(CHIPS - 1):
        cc = (c + CHIPS - 1 - i) % CHIPS
        for a in range(3):
            ref = A[a].at[part(cc, k)]
            remote(ref, ref, p_s.at[a, i], p_r.at[a, i], c, k, n).wait_recv()
            start(None, remote(ref, ref, d_s.at[a, 1 + i], d_r.at[a, 1 + i], c, other, n))
    owngy.wait()
    for i in range(CHIPS - 1):
        remote(gy, GY.at[c], gy_s.at[i], gy_r.at[i], c, k, n).wait_recv()
    for a in range(3):
        for i in range(CHIPS):
            remote(A[a].at[part(c, k)], A[a].at[part(c, k)], d_s.at[a, i], d_r.at[a, i], c, k, n).wait_recv()
    for m in range(3):
        ref = G[m].at[:, kn]
        remote(ref, ref, e_s.at[m, 0, 0], e_r.at[m, 0, 0], c, k, n).wait_recv()
        for s in range(1, nz):
            for dirn in range(2):
                cond = (n - s >= 0) if dirn == 0 else (n + s <= nz - 1)
                recv(cond, remote(ref, ref, e_s.at[m, dirn, s], e_r.at[m, dirn, s], c, k, n))
    for cond, desc in started:
        if cond is None: desc.wait_send()
        else: pl.when(cond)(lambda desc=desc: desc.wait_send())

def gather_all(nz, wq, wk, wv, wo, gains, wg, wu, wd, gy):
    D = wq.shape[0] * CHIPS * CORES * nz
    cols = wg.shape[1] // CHIPS
    bf = jnp.bfloat16
    ff = jax.ShapeDtypeStruct((CHIPS, CORES * nz, wg.shape[0], cols), bf)
    dma = pltpu.SemaphoreType.DMA
    return pl.pallas_call(
        functools.partial(gather_kernel, nz),
        out_shape=(jax.ShapeDtypeStruct((D, wq.shape[1] + 2 * wk.shape[1]), bf), jax.ShapeDtypeStruct((D, wo.shape[1]), bf),
                   jax.ShapeDtypeStruct((D, 128), bf), ff, ff, ff, jax.ShapeDtypeStruct((CHIPS,) + gy.shape, bf)),
        in_specs=[ANY] * 9, out_specs=(ANY,) * 7,
        scratch_shapes=[dma((9,)), dma((3, 3)), dma((3, 3)), dma((3,)), dma((3,)), dma((6, 2, nz)), dma((6, 2, nz)),
                        dma((3, 4)), dma((3, 4)), dma((3, 3)), dma((3, 3)), dma((3, 2, nz)), dma((3, 2, nz))],
        compiler_params=pltpu.CompilerParams(collective_id=0, has_side_effects=True),
        name="gather_all",
    )(wq, wk, wv, wo, gains, wg, wu, wd, gy)

def exchange_kernel(scatter, src, dst, loc, s_s, s_r):
    c, k, n = place()
    others = [(c + i) % CHIPS for i in range(1, CHIPS)]
    hello([(None, cc, k, n) for cc in others])
    cps = []
    for i, cc in enumerate(others):
        cp = remote(src.at[cc] if scatter else src, dst.at[c], s_s.at[i], s_r.at[i], cc, k, n)
        cp.start(); cps.append(cp)
    own = pltpu.make_async_copy(src.at[c] if scatter else src, dst.at[c], loc)
    own.start(); own.wait()
    for cp in cps: cp.wait()

def exchange(x, scatter, cid):
    dma = pltpu.SemaphoreType.DMA
    shape = x.shape if scatter else (CHIPS,) + x.shape
    return pl.pallas_call(
        functools.partial(exchange_kernel, scatter),
        out_shape=jax.ShapeDtypeStruct(shape, x.dtype), in_specs=[ANY], out_specs=ANY,
        scratch_shapes=[dma, dma((3,)), dma((3,))],
        compiler_params=pltpu.CompilerParams(collective_id=cid, has_side_effects=True),
        name="exchange%d" % cid,
    )(x)


def core_kernel(srcs, *refs):
    src, dst = refs[:srcs], refs[srcs : 2 * srcs]
    s_s, s_r = refs[2 * srcs :]
    c, k, n = place()
    hello([(None, c, 1 - k, n)])
    cps = []
    for m in range(srcs):
        cp = remote(src[m].at[:, 1 - k], dst[m], s_s.at[m], s_r.at[m], c, 1 - k, n)
        cp.start(); cps.append(cp)
    for cp in cps: cp.wait()

def core_exchange(xs, cid):
    dma = pltpu.SemaphoreType.DMA
    m = len(xs)
    return pl.pallas_call(
        functools.partial(core_kernel, m),
        out_shape=tuple(jax.ShapeDtypeStruct((x.shape[0],) + x.shape[2:], x.dtype) for x in xs),
        in_specs=[ANY] * m, out_specs=(ANY,) * m,
        scratch_shapes=[dma((m,)), dma((m,))],
        compiler_params=pltpu.CompilerParams(collective_id=cid, has_side_effects=True),
        name="core_exchange",
    )(*xs)


def fits(mesh):
    return mesh.shape["wide"] == CHIPS * CORES


def fast_device(
    nz,
    tokens,
    cotangent,
    lengths,
    positions,
    norm_attn,
    w_query,
    w_key,
    w_value,
    w_output,
    norm_mlp,
    w_gate,
    w_up,
    w_down,
):
    f32, bf16 = jnp.float32, jnp.bfloat16
    c, k, n = place()
    slots, width = tokens.shape
    rows = w_query.shape[0]
    query_width, key_width = w_query.shape[1], w_key.shape[1]
    cols = w_gate.shape[1] // CHIPS
    inputs = tokens.astype(f32)
    valid_rows = (jnp.arange(slots) < lengths[0]).astype(f32)[:, None]
    cosine_table, sine_table = rope_tables(positions)
    grad_y = cotangent.astype(f32) * valid_rows
    grad_y_low = grad_y.astype(bf16)
    gains = jnp.zeros((rows, 128), bf16).at[:, 0].set(norm_attn).at[:, 1].set(norm_mlp)
    w_qkv, w_out, gain_cols, ff_gate, ff_up, ff_down, gy_all = gather_all(
        nz, w_query, w_key, w_value, w_output, gains, w_gate, w_up, w_down, grad_y_low
    )
    ff_gate, ff_up, ff_down = (w.reshape(width, cols) for w in (ff_gate, ff_up, ff_down))
    gy_all = gy_all.reshape(CHIPS * slots, width)
    gain_attn = gain_cols[:, 0].astype(f32)
    gain_mlp = gain_cols[:, 1].astype(f32)

    normed_attn = normalize(inputs)
    scaled_attn = (normed_attn * gain_attn).astype(bf16)
    qkv = jnp.dot(scaled_attn, w_qkv, preferred_element_type=f32)
    query_rotated = (
        apply_rotary(qkv[:, :query_width].reshape(slots, QUERY_HEADS, HEAD_SIZE), cosine_table, sine_table)
        .reshape(slots, query_width)
        .astype(bf16)
    )
    key_rotated = (
        apply_rotary(
            qkv[:, query_width : query_width + key_width].reshape(slots, KEY_VALUE_HEADS, HEAD_SIZE),
            cosine_table,
            sine_table,
        )
        .reshape(slots, key_width)
        .astype(bf16)
    )
    value_reduced = qkv[:, query_width + key_width :].astype(bf16)
    context, log_totals = attend(query_rotated, key_rotated, value_reduced)
    hidden = inputs + lax.dot_general(context, w_out, contract_last, preferred_element_type=f32)
    normed_mlp = normalize(hidden)
    scaled_mlp = (normed_mlp * gain_mlp).astype(bf16)

    x_all = exchange(scaled_mlp, False, 1).reshape(CHIPS * slots, width)
    gate = jnp.dot(x_all, ff_gate, preferred_element_type=f32)
    up = jnp.dot(x_all, ff_up, preferred_element_type=f32)
    sigmoid_gate = jax.nn.sigmoid(gate)
    mixed = (gate * sigmoid_gate * up).astype(bf16)
    grad_mixed = jnp.dot(gy_all, ff_down, preferred_element_type=f32)
    grad_gate = (grad_mixed * up * (sigmoid_gate * (1.0 + gate * (1.0 - sigmoid_gate)))).astype(bf16)
    grad_up = (grad_mixed * (gate * sigmoid_gate)).astype(bf16)
    grad_x = lax.dot_general(grad_gate, ff_gate, contract_last, preferred_element_type=f32)
    grad_x = grad_x + lax.dot_general(grad_up, ff_up, contract_last, preferred_element_type=f32)
    grad_x_parts = exchange(grad_x.astype(bf16).reshape(CHIPS, slots, width), True, 2)
    mlp_part = lax.dot_general(mixed, ff_down, contract_last, preferred_element_type=f32)
    mlp_parts = exchange(mlp_part.astype(bf16).reshape(CHIPS, slots, width), True, 3)
    output = (valid_rows * (hidden + jnp.sum(mlp_parts.astype(f32), axis=0))).astype(bf16)

    grad_xn2 = jnp.sum(grad_x_parts.astype(f32), axis=0)
    grad_gain_mlp = jnp.sum(grad_xn2 * normed_mlp, axis=0)
    grad_hidden = grad_y + norm_back(grad_xn2 * gain_mlp, normed_mlp, hidden)
    grad_attn_low = grad_hidden.astype(bf16)
    grad_context = jnp.dot(grad_attn_low, w_out, preferred_element_type=f32).astype(bf16)
    grad_query_rot, grad_key_rot, grad_value_sum = attend_back(
        query_rotated, key_rotated, value_reduced, log_totals, grad_context
    )
    grad_query = (
        invert_rotary(grad_query_rot.reshape(slots, QUERY_HEADS, HEAD_SIZE), cosine_table, sine_table)
        .reshape(slots, query_width)
        .astype(bf16)
    )
    grad_key = (
        invert_rotary(grad_key_rot.reshape(slots, KEY_VALUE_HEADS, HEAD_SIZE), cosine_table, sine_table)
        .reshape(slots, key_width)
        .astype(bf16)
    )
    grad_qkv = jnp.concatenate([grad_query, grad_key, grad_value_sum.astype(bf16)], 1)
    grad_xn1 = lax.dot_general(grad_qkv, w_qkv, contract_last, preferred_element_type=f32)
    grad_gain_attn = jnp.sum(grad_xn1 * normed_attn, axis=0)
    grad_tokens = grad_hidden + norm_back(grad_xn1 * gain_attn, normed_attn, inputs)

    def over_rows(left, right):
        return lax.dot_general(left, right, contract_first, preferred_element_type=f32)

    ff_terms = [
        over_rows(a, b).astype(bf16).reshape(CHIPS, CORES, nz, rows, cols)
        for a, b in ((gy_all, mixed), (x_all, grad_gate), (x_all, grad_up))
    ]
    from_core = core_exchange(ff_terms, 4)
    ff_sums = jnp.stack(
        [lax.dynamic_index_in_dim(t, k, 1, False).astype(f32) + r.astype(f32) for t, r in zip(ff_terms, from_core)], 2
    ).astype(bf16)
    ff_sums = lax.psum_scatter(ff_sums, "narrow", scatter_dimension=1, tiled=True)
    ff_sums = exchange(ff_sums.reshape(CHIPS, 3 * rows, cols), True, 5).reshape(CHIPS, 3, rows, cols)
    grad_w_down, grad_w_gate, grad_w_up = (
        jnp.transpose(ff_sums[:, m], (1, 0, 2)).reshape(rows, CHIPS * cols).astype(f32) for m in range(3)
    )
    attn_terms = jnp.concatenate([over_rows(grad_attn_low, context), over_rows(scaled_attn, grad_qkv)], 1)
    attn_sums = lax.psum_scatter(attn_terms.astype(bf16), ("wide", "narrow"), scatter_dimension=0, tiled=True).astype(f32)
    grad_w_output = attn_sums[:, :query_width]
    grad_w_query = attn_sums[:, query_width : 2 * query_width]
    grad_w_key = attn_sums[:, 2 * query_width : 2 * query_width + key_width]
    grad_w_value = attn_sums[:, 2 * query_width + key_width :]
    grad_norm_attn, grad_norm_mlp = (
        lax.psum_scatter(g, ("wide", "narrow"), scatter_dimension=0, tiled=True) for g in (grad_gain_attn, grad_gain_mlp)
    )
    return (
        output,
        grad_tokens,
        grad_norm_attn,
        grad_w_query,
        grad_w_key,
        grad_w_value,
        grad_w_output,
        grad_norm_mlp,
        grad_w_gate,
        grad_w_up,
        grad_w_down,
    )


def solution(mesh):
    in_specs = (
        P(("wide", "narrow"), None),
        P(("wide", "narrow"), None),
        P(("wide", "narrow")),
        P(("wide", "narrow")),
        P(("wide", "narrow")),
        P(("wide", "narrow"), None),
        P(("wide", "narrow"), None),
        P(("wide", "narrow"), None),
        P(("wide", "narrow"), None),
        P(("wide", "narrow")),
        P(("wide", "narrow"), None),
        P(("wide", "narrow"), None),
        P(("wide", "narrow"), None),
    )
    out_specs = (
        P(("wide", "narrow"), None),
        P(("wide", "narrow"), None),
        P(("wide", "narrow")),
        P(("wide", "narrow"), None),
        P(("wide", "narrow"), None),
        P(("wide", "narrow"), None),
        P(("wide", "narrow"), None),
        P(("wide", "narrow")),
        P(("wide", "narrow"), None),
        P(("wide", "narrow"), None),
        P(("wide", "narrow"), None),
    )
    body = functools.partial(fast_device, mesh.shape["narrow"]) if fits(mesh) else per_device
    return jax.shard_map(
        body, mesh=mesh, in_specs=in_specs, out_specs=out_specs, check_vma=False
    )
```

```python
import functools
import math

import jax
import jax.numpy as jnp
from jax import lax
from jax.experimental import pallas as pl
from jax.experimental.pallas import tpu as pltpu
from jax.sharding import PartitionSpec as P

QUERY_HEADS = 32
KEY_VALUE_HEADS = 4
HEAD_SIZE = 64


norm_eps = 1e-05
rope_base = 10000.0
masked_score = -1e30
contract_last = (((1,), (1,)), ((), ()))
contract_first = (((0,), (0,)), ((), ()))


def rope_tables(positions):
    half_dim = HEAD_SIZE // 2
    inv_freq = jnp.exp(
        -math.log(rope_base) * jnp.arange(half_dim, dtype=jnp.float32) * 2.0 / HEAD_SIZE
    )
    angles = positions.astype(jnp.float32)[..., None] * inv_freq
    cosine = jnp.cos(angles)
    sine_part = jnp.sin(angles)
    return (jnp.concatenate([cosine, cosine], -1), jnp.concatenate([sine_part, sine_part], -1))


def apply_rotary(values, cosine_table, sine_table):
    half_dim = values.shape[-1] // 2
    turned = jnp.concatenate([-values[..., half_dim:], values[..., :half_dim]], -1)
    return values * cosine_table[..., None, :] + turned * sine_table[..., None, :]


def invert_rotary(grad_rows, cosine_table, sine_table):
    half_dim = grad_rows.shape[-1] // 2
    with_cos = grad_rows * cosine_table[..., None, :]
    with_sin = grad_rows * sine_table[..., None, :]
    return with_cos + jnp.concatenate([with_sin[..., half_dim:], -with_sin[..., :half_dim]], -1)


def normalize(values):
    return values * lax.rsqrt(jnp.mean(values * values, axis=-1, keepdims=True) + norm_eps)


def norm_back(grad_hat, normed, values):
    row_scale = lax.rsqrt(jnp.mean(values * values, axis=-1, keepdims=True) + norm_eps)
    return row_scale * (grad_hat - normed * jnp.mean(grad_hat * normed, axis=-1, keepdims=True))


def attention_inputs(normed, norm_attn, w_query, w_key, w_value):
    gain_piece = lax.all_gather(norm_attn, ("wide", "narrow"), axis=0, tiled=True)
    query_rows = lax.all_gather(w_query, ("wide", "narrow"), axis=0, tiled=True)
    key_rows = lax.all_gather(w_key, ("wide", "narrow"), axis=0, tiled=True)
    value_rows = lax.all_gather(w_value, ("wide", "narrow"), axis=0, tiled=True)
    gain_float = gain_piece.astype(jnp.float32)
    columns = (normed * gain_float).astype(jnp.bfloat16)
    query_sum = jnp.dot(columns, query_rows, preferred_element_type=jnp.float32)
    key_sum = jnp.dot(columns, key_rows, preferred_element_type=jnp.float32)
    value_sum = jnp.dot(columns, value_rows, preferred_element_type=jnp.float32)
    return (gain_float, columns, query_sum, key_sum, value_sum)


def mlp_inputs(normed, norm_mlp, w_gate, w_up):
    gain_piece = lax.all_gather(norm_mlp, ("wide", "narrow"), axis=0, tiled=True)
    gate_rows = lax.all_gather(w_gate, ("wide", "narrow"), axis=0, tiled=True)
    up_rows = lax.all_gather(w_up, ("wide", "narrow"), axis=0, tiled=True)
    gain_float = gain_piece.astype(jnp.float32)
    columns = (normed * gain_float).astype(jnp.bfloat16)
    gate_sum = jnp.dot(columns, gate_rows, preferred_element_type=jnp.float32)
    up_sum = jnp.dot(columns, up_rows, preferred_element_type=jnp.float32)
    return (gain_float, columns, gate_sum, up_sum)


def head_slices(query_rotated, key_rotated, value_reduced, shared_key_head):
    row_total_count = query_rotated.shape[0]
    heads_per_group = QUERY_HEADS // KEY_VALUE_HEADS
    query_head = query_rotated[
        :,
        shared_key_head
        * heads_per_group
        * HEAD_SIZE : (shared_key_head + 1)
        * heads_per_group
        * HEAD_SIZE,
    ].reshape(row_total_count, heads_per_group, HEAD_SIZE)
    key_head = key_rotated[:, shared_key_head * HEAD_SIZE : (shared_key_head + 1) * HEAD_SIZE]
    value_head = value_reduced[:, shared_key_head * HEAD_SIZE : (shared_key_head + 1) * HEAD_SIZE]
    return (query_head, key_head, value_head)


def head_scores(query_head, key_head):
    row_total_count = query_head.shape[0]
    causal = jnp.arange(row_total_count)[:, None] >= jnp.arange(row_total_count)[None, :]
    raw_scores = jnp.einsum("qrd,kd->rqk", query_head, key_head, preferred_element_type=jnp.float32)
    return jnp.where(causal, raw_scores * HEAD_SIZE ** (-0.5), masked_score)


def attend(query_rotated, key_rotated, value_reduced):
    row_total_count = query_rotated.shape[0]
    heads_per_group = QUERY_HEADS // KEY_VALUE_HEADS
    contexts = []
    log_totals = []
    for shared_key_head in range(KEY_VALUE_HEADS):
        query_head, key_head, value_head = head_slices(
            query_rotated, key_rotated, value_reduced, shared_key_head
        )
        scores = head_scores(query_head, key_head)
        row_peak = jnp.max(scores, axis=-1, keepdims=True)
        exp_scores = jnp.exp(scores - row_peak)
        row_total = jnp.sum(exp_scores, axis=-1, keepdims=True)
        probs = exp_scores / row_total
        context_head = jnp.einsum(
            "rqk,kd->qrd",
            probs.astype(jnp.bfloat16),
            value_head,
            preferred_element_type=jnp.float32,
        )
        contexts.append(context_head.reshape(row_total_count, heads_per_group * HEAD_SIZE))
        log_totals.append(row_peak + jnp.log(row_total))
    return (jnp.concatenate(contexts, 1).astype(jnp.bfloat16), log_totals)


def attend_back(query_rotated, key_rotated, value_reduced, log_totals, grad_context):
    row_total_count = query_rotated.shape[0]
    heads_per_group = QUERY_HEADS // KEY_VALUE_HEADS
    score_scale = HEAD_SIZE ** (-0.5)
    query_grads = []
    key_grads = []
    value_grads = []
    for shared_key_head in range(KEY_VALUE_HEADS):
        query_head, key_head, value_head = head_slices(
            query_rotated, key_rotated, value_reduced, shared_key_head
        )
        scores = head_scores(query_head, key_head)
        probs = jnp.exp(scores - log_totals[shared_key_head])
        probs_low = probs.astype(jnp.bfloat16)
        grad_head = grad_context[
            :,
            shared_key_head
            * heads_per_group
            * HEAD_SIZE : (shared_key_head + 1)
            * heads_per_group
            * HEAD_SIZE,
        ].reshape(row_total_count, heads_per_group, HEAD_SIZE)
        grad_probs = jnp.einsum(
            "qrd,kd->rqk", grad_head, value_head, preferred_element_type=jnp.float32
        )
        value_grads.append(
            jnp.einsum("rqk,qrd->kd", probs_low, grad_head, preferred_element_type=jnp.float32)
        )
        inner_sum = jnp.sum(grad_probs * probs, axis=-1, keepdims=True)
        grad_scores = (probs * (grad_probs - inner_sum) * score_scale).astype(jnp.bfloat16)
        query_grad = jnp.einsum(
            "rqk,kd->qrd", grad_scores, key_head, preferred_element_type=jnp.float32
        )
        query_grads.append(query_grad.reshape(row_total_count, heads_per_group * HEAD_SIZE))
        key_grads.append(
            jnp.einsum("rqk,qrd->kd", grad_scores, query_head, preferred_element_type=jnp.float32)
        )
    return (
        jnp.concatenate(query_grads, 1),
        jnp.concatenate(key_grads, 1),
        jnp.concatenate(value_grads, 1),
    )


def make_term(width_sides, other_sides):
    down_side, mlp_side, attn_side, qkv_side = width_sides
    mixed_rows, gate_rows, up_rows, context_rows, query_rows, key_rows, value_rows = other_sides

    def grad_term(first_row, row_span):
        pieces = [
            lax.dot_general(
                down_side, mixed_rows, contract_first, preferred_element_type=jnp.float32
            ),
            lax.dot_general(
                mlp_side, gate_rows, contract_first, preferred_element_type=jnp.float32
            ),
            lax.dot_general(mlp_side, up_rows, contract_first, preferred_element_type=jnp.float32),
            lax.dot_general(
                attn_side, context_rows, contract_first, preferred_element_type=jnp.float32
            ),
            lax.dot_general(
                qkv_side, query_rows, contract_first, preferred_element_type=jnp.float32
            ),
            lax.dot_general(qkv_side, key_rows, contract_first, preferred_element_type=jnp.float32),
            lax.dot_general(
                qkv_side, value_rows, contract_first, preferred_element_type=jnp.float32
            ),
        ]
        return jnp.concatenate(pieces, 1)

    return grad_term


def per_device(
    tokens,
    cotangent,
    lengths,
    positions,
    norm_attn,
    w_query,
    w_key,
    w_value,
    w_output,
    norm_mlp,
    w_gate,
    w_up,
    w_down,
):
    row_total_count = tokens.shape[0]
    shard_rows = w_query.shape[0]
    query_width = w_query.shape[1]
    key_width = w_key.shape[1]
    hidden_width = w_gate.shape[1]
    inputs = tokens.astype(jnp.float32)
    valid_rows = (jnp.arange(row_total_count) < lengths[0]).astype(jnp.float32)[:, None]
    cosine_table, sine_table = rope_tables(positions)
    normed_attn = normalize(inputs)
    gain_attn_full, scaled_attn, query_pre, key_unrotated, value_pre = attention_inputs(
        normed_attn, norm_attn, w_query, w_key, w_value
    )
    query_rotated = (
        apply_rotary(
            query_pre.reshape(row_total_count, QUERY_HEADS, HEAD_SIZE), cosine_table, sine_table
        )
        .reshape(row_total_count, query_width)
        .astype(jnp.bfloat16)
    )
    key_rotated = (
        apply_rotary(
            key_unrotated.reshape(row_total_count, KEY_VALUE_HEADS, HEAD_SIZE),
            cosine_table,
            sine_table,
        )
        .reshape(row_total_count, key_width)
        .astype(jnp.bfloat16)
    )
    value_reduced = value_pre.astype(jnp.bfloat16)
    context, log_totals = attend(query_rotated, key_rotated, value_reduced)
    attn_out = lax.dot_general(
        context,
        lax.all_gather(w_output, ("wide", "narrow"), axis=0, tiled=True),
        contract_last,
        preferred_element_type=jnp.float32,
    )
    hidden = inputs + attn_out
    normed_mlp = normalize(hidden)
    gain_mlp_full, scaled_mlp, gate_proj, up_proj = mlp_inputs(normed_mlp, norm_mlp, w_gate, w_up)
    mixed_low = (gate_proj * jax.nn.sigmoid(gate_proj) * up_proj).astype(jnp.bfloat16)
    mlp_out = lax.dot_general(
        mixed_low,
        lax.all_gather(w_down, ("wide", "narrow"), axis=0, tiled=True),
        contract_last,
        preferred_element_type=jnp.float32,
    )
    output = (valid_rows * (hidden + mlp_out)).astype(jnp.bfloat16)
    grad_y = cotangent.astype(jnp.float32) * valid_rows
    grad_y_low = grad_y.astype(jnp.bfloat16)
    grad_cols = grad_y_low
    grad_mixed = jnp.dot(
        grad_cols,
        lax.all_gather(w_down, ("wide", "narrow"), axis=0, tiled=True),
        preferred_element_type=jnp.float32,
    )
    again_values = mlp_inputs(normed_mlp, norm_mlp, w_gate, w_up)
    gate_proj = again_values[2]
    up_proj = again_values[3]
    sigmoid_gate = jax.nn.sigmoid(gate_proj)
    grad_gate = (
        grad_mixed * up_proj * (sigmoid_gate * (1.0 + gate_proj * (1.0 - sigmoid_gate)))
    ).astype(jnp.bfloat16)
    grad_up = (grad_mixed * (gate_proj * sigmoid_gate)).astype(jnp.bfloat16)
    gate_rows = lax.all_gather(w_gate, ("wide", "narrow"), axis=0, tiled=True)
    up_rows = lax.all_gather(w_up, ("wide", "narrow"), axis=0, tiled=True)
    columns = lax.dot_general(
        grad_gate, gate_rows, contract_last, preferred_element_type=jnp.float32
    )
    columns = columns + lax.dot_general(
        grad_up, up_rows, contract_last, preferred_element_type=jnp.float32
    )
    grad_xn2 = columns
    grad_gain_mlp = jnp.sum(grad_xn2 * normed_mlp, axis=0)
    grad_hidden = grad_y + norm_back(grad_xn2 * gain_mlp_full, normed_mlp, hidden)
    grad_attn_low = grad_hidden.astype(jnp.bfloat16)
    grad_cols = grad_attn_low
    grad_context = jnp.dot(
        grad_cols,
        lax.all_gather(w_output, ("wide", "narrow"), axis=0, tiled=True),
        preferred_element_type=jnp.float32,
    )
    grad_context = grad_context.astype(jnp.bfloat16)
    grad_query_rot, gradient_key_rotated, grad_value_sum = attend_back(
        query_rotated, key_rotated, value_reduced, log_totals, grad_context
    )
    grad_query = (
        invert_rotary(
            grad_query_rot.reshape(row_total_count, QUERY_HEADS, HEAD_SIZE),
            cosine_table,
            sine_table,
        )
        .reshape(row_total_count, query_width)
        .astype(jnp.bfloat16)
    )
    grad_key = (
        invert_rotary(
            gradient_key_rotated.reshape(row_total_count, KEY_VALUE_HEADS, HEAD_SIZE),
            cosine_table,
            sine_table,
        )
        .reshape(row_total_count, key_width)
        .astype(jnp.bfloat16)
    )
    grad_value = grad_value_sum.astype(jnp.bfloat16)
    query_rows = lax.all_gather(w_query, ("wide", "narrow"), axis=0, tiled=True)
    key_rows = lax.all_gather(w_key, ("wide", "narrow"), axis=0, tiled=True)
    value_rows = lax.all_gather(w_value, ("wide", "narrow"), axis=0, tiled=True)
    columns = lax.dot_general(
        grad_query, query_rows, contract_last, preferred_element_type=jnp.float32
    )
    columns = columns + lax.dot_general(
        grad_key, key_rows, contract_last, preferred_element_type=jnp.float32
    )
    columns = columns + lax.dot_general(
        grad_value, value_rows, contract_last, preferred_element_type=jnp.float32
    )
    local_term = make_term(
        (grad_y_low, scaled_mlp, grad_attn_low, scaled_attn),
        (mixed_low, grad_gate, grad_up, context, grad_query, grad_key, grad_value),
    )
    all_sums = lax.psum_scatter(
        local_term(jnp.int32(0), lax.axis_size(("wide", "narrow")) * shard_rows),
        ("wide", "narrow"),
        scatter_dimension=0,
        tiled=True,
    )
    edges = [0]
    for width in (
        hidden_width,
        hidden_width,
        hidden_width,
        query_width,
        query_width,
        key_width,
        key_width,
    ):
        edges.append(edges[-1] + width)
    grad_w_down = all_sums[:, edges[0] : edges[1]]
    grad_w_gate = all_sums[:, edges[1] : edges[2]]
    grad_w_up = all_sums[:, edges[2] : edges[3]]
    grad_w_output = all_sums[:, edges[3] : edges[4]]
    grad_w_query = all_sums[:, edges[4] : edges[5]]
    grad_w_key = all_sums[:, edges[5] : edges[6]]
    grad_w_value = all_sums[:, edges[6] : edges[7]]
    grad_gain_attn = jnp.sum(columns * normed_attn, axis=0)
    grad_tokens = grad_hidden + norm_back(columns * gain_attn_full, normed_attn, inputs)
    grad_norm_attn, grad_norm_mlp = (
        lax.psum_scatter(grad_gain_attn, ("wide", "narrow"), scatter_dimension=0, tiled=True),
        lax.psum_scatter(grad_gain_mlp, ("wide", "narrow"), scatter_dimension=0, tiled=True),
    )
    return (
        output,
        grad_tokens,
        grad_norm_attn,
        grad_w_query,
        grad_w_key,
        grad_w_value,
        grad_w_output,
        grad_norm_mlp,
        grad_w_gate,
        grad_w_up,
        grad_w_down,
    )


MESH = pl.DeviceIdType.MESH
ANY = pl.BlockSpec(memory_space=pl.ANY)

CHIPS, CORES = 4, 2

def place():
    w = lax.axis_index("wide"); n = lax.axis_index("narrow")
    return w // CORES, w % CORES, n

def chip_at(c, r):
    xb, yb, rx, ry = c % 2, c // 2, r % 2, r // 2
    return (yb + ry - 2 * yb * ry) * 2 + (xb + rx - 2 * xb * rx)


def remote(src, dst, send, recv, chip, core, z):
    return pltpu.make_async_remote_copy(src_ref=src, dst_ref=dst, send_sem=send, recv_sem=recv,
        device_id={"wide": chip * CORES + core, "narrow": z}, device_id_type=MESH)

def hello(partners):
    barrier = pltpu.get_barrier_semaphore()
    count = 0
    for cond, chip, core, z in partners:
        def sig(chip=chip, core=core, z=z):
            pl.semaphore_signal(barrier, inc=1, device_id={"wide": chip * CORES + core, "narrow": z}, device_id_type=MESH)
        if cond is None:
            sig(); count = count + 1
        else:
            pl.when(cond)(sig); count = count + jnp.where(cond, 1, 0)
    pl.semaphore_wait(barrier, count)

def gather_kernel(nz, wq, wk, wv, wo, gains, wgu, wd, gy, QKV, WO, GAIN, G0, G1, GY,
                  loc, a2a_s, a2a_r, gy_s, gy_r, z_s, z_r, d_s, d_r, p_s, p_r, e_s, e_r):
    c, k, n = place()
    G = (G0, G1); W = (wgu, wd)
    FF = len(G)
    rows = wq.shape[0]
    other = 1 - k
    left, right = n > 0, n < nz - 1
    others = [chip_at(c, r) for r in range(1, CHIPS)]
    hello([(None, cc, k, n) for cc in others] + [(None, c, other, n), (left, c, k, n - 1), (right, c, k, n + 1)])
    kn = k * nz + n
    b = (c * CORES + k) * nz + n
    started = []
    def start(cond, desc):
        if cond is None: desc.start()
        else: pl.when(cond)(lambda: desc.start())
        started.append((cond, desc))
    def recv(cond, desc):
        if cond is None: desc.wait_recv()
        else: pl.when(cond)(lambda: desc.wait_recv())
    def blk(z): return pl.ds(pl.multiple_of(((c * CORES + k) * nz + z) * rows, rows), rows)
    mine = blk(n)
    def mycols(m, cc):
        cols = G[m].shape[-1]
        return W[m].at[:, pl.ds(pl.multiple_of(cc * cols, 128), cols)]
    q, kv = wq.shape[1], wk.shape[1]
    for i, cc in enumerate(others):
        for m in range(FF):
            start(None, remote(mycols(m, cc), G[m].at[c, kn], a2a_s.at[m, i], a2a_r.at[m, i], cc, k, n))
    own = [pltpu.make_async_copy(wq, QKV.at[mine, pl.ds(0, q)], loc.at[0]),
           pltpu.make_async_copy(wk, QKV.at[mine, pl.ds(q, kv)], loc.at[1]),
           pltpu.make_async_copy(wv, QKV.at[mine, pl.ds(q + kv, kv)], loc.at[2]),
           pltpu.make_async_copy(wo, WO.at[mine], loc.at[3]),
           pltpu.make_async_copy(gains, GAIN.at[mine], loc.at[4])]
    ownff = [pltpu.make_async_copy(mycols(m, c), G[m].at[c, kn], loc.at[5 + m]) for m in range(FF)]
    owngy = pltpu.make_async_copy(gy, GY.at[0], loc.at[8])
    for cp in own + ownff + [owngy]: cp.start()
    for cp in own: cp.wait()
    A = (QKV, WO, GAIN)
    def zsend(item, ref, dirn, s):
        cond = (right & (n - s >= 0)) if dirn == 0 else (left & (n + s <= nz - 1))
        z = n + 1 if dirn == 0 else n - 1
        return cond, remote(ref, ref, z_s.at[item, dirn, s], z_r.at[item, dirn, s], c, k, z)
    def zrecv(item, ref, dirn, s):
        cond = (n - s >= 0) if dirn == 0 else (n + s <= nz - 1)
        return cond, remote(ref, ref, z_s.at[item, dirn, s - 1], z_r.at[item, dirn, s - 1], c, k, n)
    def origin(dirn, s):
        o = n - s if dirn == 0 else n + s
        return jnp.clip(o, 0, nz - 1)
    for a in range(3):
        for dirn in range(2):
            start(*zsend(a, A[a].at[mine], dirn, 0))
    for i, cc in enumerate(others):
        start(None, remote(gy, GY.at[1 + i], gy_s.at[i], gy_r.at[i], cc, k, n))
    for s in range(1, nz):
        for dirn in range(2):
            for a in range(3):
                ref = A[a].at[blk(origin(dirn, s))]
                recv(*zrecv(a, ref, dirn, s))
                if s < nz - 1: start(*zsend(a, ref, dirn, s))
    def part(cc, kk): return pl.ds(pl.multiple_of((cc * CORES + kk) * nz * rows, rows), nz * rows)
    for a in range(3):
        for i, cc in enumerate(others):
            start(None, remote(A[a].at[part(c, k)], A[a].at[part(c, k)], p_s.at[a, i], p_r.at[a, i], cc, k, n))
        start(None, remote(A[a].at[part(c, k)], A[a].at[part(c, k)], d_s.at[a, 0], d_r.at[a, 0], c, other, n))
    for m in range(FF):
        ownff[m].wait()
        for i in range(CHIPS - 1):
            remote(G[m].at[c, kn], G[m].at[c, kn], a2a_s.at[m, i], a2a_r.at[m, i], c, k, n).wait_recv()
        ref = G[m].at[:, kn]
        for dirn in range(2): start(*zsend(3 + m, ref, dirn, 0))
        start(None, remote(ref, ref, e_s.at[m, 0, 0], e_r.at[m, 0, 0], c, other, n))
    for s in range(1, nz):
        for dirn in range(2):
            for m in range(FF):
                ref = G[m].at[:, k * nz + origin(dirn, s)]
                cond, d = zrecv(3 + m, ref, dirn, s)
                recv(cond, d)
                if s < nz - 1: start(*zsend(3 + m, ref, dirn, s))
                start(cond, remote(ref, ref, e_s.at[m, dirn, s], e_r.at[m, dirn, s], c, other, n))
    for i in range(CHIPS - 1):
        cc = others[i]
        for a in range(3):
            ref = A[a].at[part(cc, k)]
            remote(ref, ref, p_s.at[a, i], p_r.at[a, i], c, k, n).wait_recv()
            start(None, remote(ref, ref, d_s.at[a, 1 + i], d_r.at[a, 1 + i], c, other, n))
    owngy.wait()
    for i in range(CHIPS - 1):
        remote(gy, GY.at[1 + i], gy_s.at[i], gy_r.at[i], c, k, n).wait_recv()
    for a in range(3):
        for i in range(CHIPS):
            remote(A[a].at[part(c, k)], A[a].at[part(c, k)], d_s.at[a, i], d_r.at[a, i], c, k, n).wait_recv()
    for m in range(FF):
        ref = G[m].at[:, kn]
        remote(ref, ref, e_s.at[m, 0, 0], e_r.at[m, 0, 0], c, k, n).wait_recv()
        for s in range(1, nz):
            for dirn in range(2):
                cond = (n - s >= 0) if dirn == 0 else (n + s <= nz - 1)
                recv(cond, remote(ref, ref, e_s.at[m, dirn, s], e_r.at[m, dirn, s], c, k, n))
    for cond, desc in started:
        if cond is None: desc.wait_send()
        else: pl.when(cond)(lambda desc=desc: desc.wait_send())

def gather_all(nz, wq, wk, wv, wo, gains, wgu, wd, gy):
    D = wq.shape[0] * CHIPS * CORES * nz
    bf = jnp.bfloat16
    def ff(w):
        return jax.ShapeDtypeStruct((CHIPS, CORES * nz, w.shape[0], w.shape[1] // CHIPS), bf)
    dma = pltpu.SemaphoreType.DMA
    return pl.pallas_call(
        functools.partial(gather_kernel, nz),
        out_shape=(jax.ShapeDtypeStruct((D, wq.shape[1] + 2 * wk.shape[1]), bf), jax.ShapeDtypeStruct((D, wo.shape[1]), bf),
                   jax.ShapeDtypeStruct((D, 128), bf), ff(wgu), ff(wd), jax.ShapeDtypeStruct((CHIPS,) + gy.shape, bf)),
        in_specs=[ANY] * 8, out_specs=(ANY,) * 6,
        scratch_shapes=[dma((9,)), dma((3, 3)), dma((3, 3)), dma((3,)), dma((3,)), dma((6, 2, nz)), dma((6, 2, nz)),
                        dma((3, 4)), dma((3, 4)), dma((3, 3)), dma((3, 3)), dma((3, 2, nz)), dma((3, 2, nz))],
        compiler_params=pltpu.CompilerParams(collective_id=0, has_side_effects=True),
        name="gather_all",
    )(wq, wk, wv, wo, gains, wgu, wd, gy)

def exchange_kernel(by_chip, src, dst, loc, s_s, s_r):
    c, k, n = place()
    hello([(None, chip_at(c, r), k, n) for r in (1, 2, 3)])
    cps = [pltpu.make_async_copy(src.at[c if by_chip else 0], dst.at[c if by_chip else 0], loc)]
    for r in (1, 2, 3):
        cc = chip_at(c, r)
        cps.append(remote(src.at[cc if by_chip else r], dst.at[c if by_chip else r], s_s.at[r - 1], s_r.at[r - 1], cc, k, n))
    for cp in cps: cp.start()
    for cp in cps: cp.wait()


def exchange(x, cid, by_chip=False):
    dma = pltpu.SemaphoreType.DMA
    return pl.pallas_call(
        functools.partial(exchange_kernel, by_chip),
        out_shape=jax.ShapeDtypeStruct(x.shape, x.dtype), in_specs=[ANY], out_specs=ANY,
        scratch_shapes=[dma, dma((3,)), dma((3,))],
        compiler_params=pltpu.CompilerParams(collective_id=cid, has_side_effects=True),
        name="exchange",
    )(x)


def plane_swap(x, cid):
    return exchange(x, cid, True)


def core_kernel(srcs, *refs):
    src, dst = refs[:srcs], refs[srcs : 2 * srcs]
    s_s, s_r = refs[2 * srcs :]
    c, k, n = place()
    hello([(None, c, 1 - k, n)])
    cps = []
    for m in range(srcs):
        cp = remote(src[m].at[:, 1 - k], dst[m], s_s.at[m], s_r.at[m], c, 1 - k, n)
        cp.start(); cps.append(cp)
    for cp in cps: cp.wait()

def core_exchange(xs, cid):
    dma = pltpu.SemaphoreType.DMA
    m = len(xs)
    return pl.pallas_call(
        functools.partial(core_kernel, m),
        out_shape=tuple(jax.ShapeDtypeStruct((x.shape[0],) + x.shape[2:], x.dtype) for x in xs),
        in_specs=[ANY] * m, out_specs=(ANY,) * m,
        scratch_shapes=[dma((m,)), dma((m,))],
        compiler_params=pltpu.CompilerParams(collective_id=cid, has_side_effects=True),
        name="core_exchange",
    )(*xs)


def mlp_kernel(x, gy, gu_hbm, gd_hbm, x_all, mix_all, ggu_all, gx_parts, mlp_parts,
               xs, gys, gu, gd, mix, ggu, gx, mo, load, ag_s, ag_r, rs_s, rs_r, own, out):
    c, k, n = place()
    slots, width = x.shape
    half = slots // 2
    cols = gd.shape[-1]
    hello([(None, chip_at(c, r), k, n) for r in (1, 2, 3)])
    loads = [pltpu.make_async_copy(x, xs.at[0], load.at[0])]
    sends = [remote(x, xs.at[r], ag_s.at[r], ag_r.at[r], chip_at(c, r), k, n) for r in (1, 2)]
    for cp in sends: cp.start()
    loads += [pltpu.make_async_copy(gu_hbm, gu, load.at[1]), pltpu.make_async_copy(gd_hbm, gd, load.at[2]),
              pltpu.make_async_copy(gy, gys, load.at[3])]
    for cp in loads: cp.start()
    relays = [remote(xs.at[1, pl.ds(0, half)], xs.at[3, pl.ds(0, half)], ag_s.at[0], ag_r.at[0], chip_at(c, 2), k, n),
              remote(xs.at[2, pl.ds(half, half)], xs.at[3, pl.ds(half, half)], ag_s.at[3], ag_r.at[3], chip_at(c, 1), k, n)]
    for cp in loads: cp.wait()

    def block(r, carry):
        @pl.when(r == 1)
        def _():
            for cp in sends: cp.wait_recv()
            for cp in relays: cp.start()
        @pl.when(r == 3)
        def _():
            for cp in relays: cp.wait_recv()
        def chunk(col, w):
            h = jnp.dot(xs[r], gu[:, pl.ds(2 * col, 2 * w)], preferred_element_type=jnp.float32)
            gm = jnp.dot(gys[r], gd[:, pl.ds(col, w)], preferred_element_type=jnp.float32)
            for q in range(w // 128):
                gate, up, g = h[:, 256 * q : 256 * q + 128], h[:, 256 * q + 128 : 256 * q + 256], gm[:, 128 * q : 128 * q + 128]
                sg = 1.0 / (1.0 + jnp.exp(-gate))
                act = gate * sg
                mix[r, :, pl.ds(col + 128 * q, 128)] = (act * up).astype(jnp.bfloat16)
                ggu[r, :, pl.ds(2 * col + 256 * q, 128)] = (g * up * (sg * (1.0 + gate * (1.0 - sg)))).astype(jnp.bfloat16)
                ggu[r, :, pl.ds(2 * col + 256 * q + 128, 128)] = (g * act).astype(jnp.bfloat16)
        def pair(j, carry):
            chunk(pl.multiple_of(j * 256, 256), 256)
            return carry
        lax.fori_loop(0, cols // 256, pair, 0)
        if cols % 256: chunk(cols - 128, 128)
        def back(i, carry):
            at = pl.ds(pl.multiple_of(i * 256, 256), 256)
            gx[r, :, at] = lax.dot_general(ggu[r], gu[at, :], contract_last, preferred_element_type=jnp.float32).astype(jnp.bfloat16)
            return carry
        lax.fori_loop(0, width // 256, back, 0)
        @pl.when(r == 0)
        def _(): pltpu.make_async_copy(gx.at[0], gx_parts.at[0], own).start()
        @pl.when(r > 0)
        def _(): remote(gx.at[r], gx_parts.at[r], rs_s.at[r], rs_r.at[r], chip_at(c, r), k, n).start()
        def down(i, carry):
            at = pl.ds(pl.multiple_of(i * 256, 256), 256)
            mo[r, :, at] = lax.dot_general(mix[r], gd[at, :], contract_last, preferred_element_type=jnp.float32).astype(jnp.bfloat16)
            return carry
        lax.fori_loop(0, width // 256, down, 0)
        for i, (a, b) in enumerate(((xs, x_all), (mix, mix_all), (ggu, ggu_all), (mo, mlp_parts))):
            pltpu.make_async_copy(a.at[r], b.at[r], out.at[i, r]).start()
        return carry
    lax.fori_loop(0, CHIPS, block, 0)
    for cp in sends + relays: cp.wait_send()
    pltpu.make_async_copy(gx.at[0], gx_parts.at[0], own).wait()
    for r in range(CHIPS):
        for i, (a, b) in enumerate(((xs, x_all), (mix, mix_all), (ggu, ggu_all), (mo, mlp_parts))):
            pltpu.make_async_copy(a.at[r], b.at[r], out.at[i, r]).wait()
    for r in (1, 2, 3):
        remote(gx.at[r], gx_parts.at[r], rs_s.at[r], rs_r.at[r], chip_at(c, r), k, n).wait()


def mlp_all(x, gy, gu, gd):
    slots, width = x.shape
    cols = gd.shape[1]
    bf, dma, vm = jnp.bfloat16, pltpu.SemaphoreType.DMA, pltpu.VMEM
    def blocks(w): return jax.ShapeDtypeStruct((CHIPS, slots, w), bf)
    flops = 2 * 6 * CHIPS * slots * width * cols
    return pl.pallas_call(
        mlp_kernel,
        out_shape=(blocks(width), blocks(cols), blocks(2 * cols), blocks(width), blocks(width)),
        in_specs=[ANY] * 4, out_specs=(ANY,) * 5,
        scratch_shapes=[vm((CHIPS, slots, width), bf), vm((CHIPS, slots, width), bf), vm((width, 2 * cols), bf), vm((width, cols), bf),
                        vm((CHIPS, slots, cols), bf), vm((CHIPS, slots, 2 * cols), bf), vm((CHIPS, slots, width), bf),
                        vm((CHIPS, slots, width), bf), dma((4,)), dma((4,)), dma((4,)), dma((4,)), dma((4,)), dma, dma((4, 4))],
        compiler_params=pltpu.CompilerParams(collective_id=1, has_side_effects=True, vmem_limit_bytes=62 << 20),
        cost_estimate=pl.CostEstimate(flops=flops, bytes_accessed=60 << 20, transcendentals=CHIPS * slots * cols),
        name="mlp_all",
    )(x, gy, gu, gd)


PAIR = 2 * HEAD_SIZE
REPEAT = QUERY_HEADS // KEY_VALUE_HEADS
PAIRS = REPEAT // 2


def lane_tables(positions):
    cosine, sine = rope_tables(positions)
    first = jnp.arange(HEAD_SIZE) < HEAD_SIZE // 2
    low, high = jnp.where(first, -sine, 0.0), jnp.where(first, 0.0, sine)
    return jnp.stack([jnp.concatenate([t, t], 1) for t in (cosine, low, high)])


def rotate(u, tables):
    half = HEAD_SIZE // 2
    return u * tables[0] + pltpu.roll(u, PAIR - half, 1) * tables[1] + pltpu.roll(u, half, 1) * tables[2]


def unrotate(g, tables):
    half = HEAD_SIZE // 2
    return g * tables[0] + pltpu.roll(g * tables[2], PAIR - half, 1) + pltpu.roll(g * tables[1], half, 1)


def row_blocks(slots):
    return [(at, min(128, slots - at), at + 128) for at in range(0, slots, 128)]


def causal(s, below, fill):
    clear = s.shape[1] - 128
    last = jnp.where(below, s[:, clear:], fill)
    return jnp.concatenate([s[:, :clear], last], 1) if clear else last


def attend_kernel(q_ref, k_ref, v_ref, tab_ref, qr_ref, k_out, v_out, lse_ref, ctx_ref, ks, vs):
    g = pl.program_id(0)
    f32, bf16 = jnp.float32, jnp.bfloat16
    slots = q_ref.shape[0]
    @pl.when(g == 0)
    def _():
        ks[...] = jnp.zeros_like(ks)
        vs[...] = jnp.zeros_like(vs)
    lane = lax.broadcasted_iota(jnp.int32, (slots, PAIR), 1)
    tables = (tab_ref[0], tab_ref[1], tab_ref[2])
    key, val = rotate(k_ref[...], tables), v_ref[...]
    odd = g % 2 == 1
    for x, own, stack, scale in ((key, k_out, ks, HEAD_SIZE ** -0.5), (val, v_out, vs, 1.0)):
        x = jnp.where(lane < HEAD_SIZE, jnp.where(odd, pltpu.roll(x, HEAD_SIZE, 1), x), 0.0).astype(bf16)
        own[0] = x
        x = x.astype(f32) * scale
        stack[0, 0:slots, :] = x.astype(bf16)
        stack[1, 0:slots, :] = pltpu.roll(x, HEAD_SIZE, 1).astype(bf16)
    for at, size, keys in row_blocks(slots):
        below = lax.broadcasted_iota(jnp.int32, (size, 128), 0) >= lax.broadcasted_iota(jnp.int32, (size, 128), 1)
        lse = jnp.zeros((size, PAIR), f32)
        here = lane[0:size]
        for p in range(PAIRS):
            span = slice(p * PAIR, (p + 1) * PAIR)
            rows = slice(at, at + size)
            q = rotate(q_ref[rows, span], tuple(t[rows] for t in tables)).astype(bf16)
            qr_ref[rows, span] = q
            ctx = jnp.zeros((size, PAIR), f32)
            for h in range(2):
                s = lax.dot_general(q, ks[h, 0:keys, :], contract_last, preferred_element_type=f32)
                s = causal(s, below, masked_score)
                peak = jnp.max(s, axis=-1, keepdims=True)
                e = jnp.exp(s - peak)
                total = jnp.sum(e, axis=-1, keepdims=True)
                lse = jnp.where(here == 2 * p + h, peak + jnp.log(total), lse)
                probs = (e * (1.0 / total)).astype(bf16)
                ctx = ctx + jnp.dot(probs, vs[h, 0:keys, :], preferred_element_type=f32)
            ctx_ref[rows, span] = ctx.astype(bf16)
        lse_ref[0, at : at + size, :] = lse


def attend_all(qkv, tables):
    slots = qkv.shape[0]
    wide = REPEAT * HEAD_SIZE
    first = QUERY_HEADS * HEAD_SIZE // PAIR
    bf16 = jnp.bfloat16
    keys = -(-slots // 128) * 128
    shape = jax.ShapeDtypeStruct
    per_head = pl.BlockSpec((1, slots, PAIR), lambda g: (g, 0, 0))
    wide_spec = pl.BlockSpec((slots, wide), lambda g: (0, g))
    return pl.pallas_call(
        attend_kernel,
        grid=(KEY_VALUE_HEADS,),
        out_shape=(shape((slots, QUERY_HEADS * HEAD_SIZE), bf16), shape((KEY_VALUE_HEADS, slots, PAIR), bf16),
                   shape((KEY_VALUE_HEADS, slots, PAIR), bf16), shape((KEY_VALUE_HEADS, slots, PAIR), jnp.float32),
                   shape((slots, QUERY_HEADS * HEAD_SIZE), bf16)),
        in_specs=[wide_spec, pl.BlockSpec((slots, PAIR), lambda g: (0, first + g // 2)),
                  pl.BlockSpec((slots, PAIR), lambda g: (0, first + KEY_VALUE_HEADS // 2 + g // 2)),
                  pl.BlockSpec((3, slots, PAIR), lambda g: (0, 0, 0))],
        out_specs=(wide_spec, per_head, per_head, per_head, wide_spec),
        scratch_shapes=[pltpu.VMEM((2, keys, PAIR), bf16), pltpu.VMEM((2, keys, PAIR), bf16)],
        compiler_params=pltpu.CompilerParams(vmem_limit_bytes=32 << 20),
        name="attend",
    )(qkv, qkv, qkv, tables)


def attend_back_kernel(q_ref, k_ref, v_ref, lse_ref, gc_ref, tab_ref, gq_ref, gk_ref, gv_ref, ks, kt, vt, ds, pr, qs, gs):
    g = pl.program_id(0)
    f32, bf16 = jnp.float32, jnp.bfloat16
    slots = q_ref.shape[0]
    scale = HEAD_SIZE ** -0.5
    @pl.when(g == 0)
    def _():
        for ref in (ks, kt, vt, ds, pr): ref[...] = jnp.zeros_like(ref)
    lane = lax.broadcasted_iota(jnp.int32, (slots, PAIR), 1)
    tables = (tab_ref[0], tab_ref[1], tab_ref[2])
    key, val = k_ref[0].astype(f32), v_ref[0].astype(f32)
    for stack, x in ((ks, key * scale), (kt, key), (vt, val)):
        stack[0, 0:slots, :] = x.astype(bf16)
        stack[1, 0:slots, :] = pltpu.roll(x, HEAD_SIZE, 1).astype(bf16)
    for at, size, keys in row_blocks(slots):
        rows = slice(at, at + size)
        below = lax.broadcasted_iota(jnp.int32, (size, 128), 0) >= lax.broadcasted_iota(jnp.int32, (size, 128), 1)
        lse = lse_ref[0, rows, :]
        for p in range(PAIRS):
            span = slice(p * PAIR, (p + 1) * PAIR)
            deep = slice(p * slots + at, p * slots + at + size)
            q, gc = q_ref[rows, span], gc_ref[rows, span]
            qs[deep, :] = q
            gs[deep, :] = gc
            gq = jnp.zeros((size, PAIR), f32)
            for h in range(2):
                s = lax.dot_general(q, ks[h, 0:keys, :], contract_last, preferred_element_type=f32)
                e = jnp.exp(s - lse[:, 2 * p + h : 2 * p + h + 1])
                probs = causal(e, below, 0.0)
                pr[h, deep, 0:keys] = probs.astype(bf16)
                gp = lax.dot_general(gc, vt[h, 0:keys, :], contract_last, preferred_element_type=f32)
                inner = jnp.sum(gp * probs, axis=-1, keepdims=True)
                grad = (probs * (gp - inner) * scale).astype(bf16)
                ds[h, deep, 0:keys] = grad
                gq = gq + jnp.dot(grad, kt[h, 0:keys, :], preferred_element_type=f32)
            gq_ref[rows, span] = unrotate(gq, tuple(t[rows] for t in tables)).astype(bf16)
    for src, right, out, turn in ((ds, qs, gk_ref, True), (pr, gs, gv_ref, False)):
        lo, hi = (
            lax.dot_general(src[h], right[...], contract_first, preferred_element_type=f32)[0:slots] for h in range(2)
        )
        x = jnp.where(lane < HEAD_SIZE, lo + pltpu.roll(hi, HEAD_SIZE, 1), 0.0)
        if turn: x = unrotate(x, tables)
        @pl.when(g % 2 == 0)
        def _(): out[...] = x
        @pl.when(g % 2 == 1)
        def _(): out[...] = jnp.where(lane < HEAD_SIZE, out[...], pltpu.roll(x, HEAD_SIZE, 1))


def attend_back_all(q, k, v, lse, grad_context, tables):
    slots = q.shape[0]
    wide = REPEAT * HEAD_SIZE
    bf16, f32, vm = jnp.bfloat16, jnp.float32, pltpu.VMEM
    keys = -(-slots // 128) * 128
    shape = jax.ShapeDtypeStruct
    per_head = pl.BlockSpec((1, slots, PAIR), lambda g: (g, 0, 0))
    wide_spec = pl.BlockSpec((slots, wide), lambda g: (0, g))
    two = pl.BlockSpec((slots, PAIR), lambda g: (0, g // 2))
    return pl.pallas_call(
        attend_back_kernel,
        grid=(KEY_VALUE_HEADS,),
        out_shape=(shape((slots, QUERY_HEADS * HEAD_SIZE), bf16), shape((slots, KEY_VALUE_HEADS * HEAD_SIZE), f32),
                   shape((slots, KEY_VALUE_HEADS * HEAD_SIZE), f32)),
        in_specs=[wide_spec, per_head, per_head, per_head, wide_spec, pl.BlockSpec((3, slots, PAIR), lambda g: (0, 0, 0))],
        out_specs=(wide_spec, two, two),
        scratch_shapes=[vm((2, keys, PAIR), bf16)] * 3 + [vm((2, PAIRS * slots, keys), bf16)] * 2 + [vm((PAIRS * slots, PAIR), bf16)] * 2,
        compiler_params=pltpu.CompilerParams(vmem_limit_bytes=40 << 20),
        name="attend_back",
    )(q, k, v, lse, grad_context, tables)


def fits(mesh):
    return mesh.shape["wide"] == CHIPS * CORES


def fast_device(
    nz,
    tokens,
    cotangent,
    lengths,
    positions,
    norm_attn,
    w_query,
    w_key,
    w_value,
    w_output,
    norm_mlp,
    w_gate,
    w_up,
    w_down,
):
    f32, bf16 = jnp.float32, jnp.bfloat16
    c, k, n = place()
    slots, width = tokens.shape
    rows = w_query.shape[0]
    query_width, key_width = w_query.shape[1], w_key.shape[1]
    cols = w_gate.shape[1] // CHIPS
    inputs = tokens.astype(f32)
    valid_rows = (jnp.arange(slots) < lengths[0]).astype(f32)[:, None]
    tables = lane_tables(positions)
    grad_y = cotangent.astype(f32) * valid_rows
    grad_y_low = grad_y.astype(bf16)
    gains = jnp.zeros((rows, 128), bf16).at[:, 0].set(norm_attn).at[:, 1].set(norm_mlp)
    chunks = (rows, w_gate.shape[1] // 128, 128)
    w_gate_up = jnp.stack([w_gate.reshape(chunks), w_up.reshape(chunks)], 2).reshape(rows, 2 * w_gate.shape[1])
    w_qkv, w_out, gain_cols, ff_gate_up, ff_down, gy_all = gather_all(
        nz, w_query, w_key, w_value, w_output, gains, w_gate_up, w_down, grad_y_low
    )
    ff_gate_up, ff_down = ff_gate_up.reshape(width, 2 * cols), ff_down.reshape(width, cols)
    gain_attn = gain_cols[:, 0].astype(f32)
    gain_mlp = gain_cols[:, 1].astype(f32)

    normed_attn = normalize(inputs)
    scaled_attn = (normed_attn * gain_attn).astype(bf16)
    qkv = jnp.dot(scaled_attn, w_qkv, preferred_element_type=f32)
    query_rotated, key_rotated, value_reduced, log_totals, context = attend_all(qkv, tables)
    hidden = inputs + lax.dot_general(context, w_out, contract_last, preferred_element_type=f32)
    normed_mlp = normalize(hidden)
    scaled_mlp = (normed_mlp * gain_mlp).astype(bf16)

    x_all, mixed, grad_gate_up, grad_x_parts, mlp_part = mlp_all(scaled_mlp, gy_all, ff_gate_up, ff_down)
    x_all, mixed, grad_gate_up, gy_all = (t.reshape(CHIPS * slots, -1) for t in (x_all, mixed, grad_gate_up, gy_all))
    mlp_parts = exchange(mlp_part, 3)
    output = (valid_rows * (hidden + jnp.sum(mlp_parts.astype(f32), axis=0))).astype(bf16)

    grad_xn2 = jnp.sum(grad_x_parts.astype(f32), axis=0)
    grad_gain_mlp = jnp.sum(grad_xn2 * normed_mlp, axis=0)
    grad_hidden = grad_y + norm_back(grad_xn2 * gain_mlp, normed_mlp, hidden)
    grad_attn_low = grad_hidden.astype(bf16)
    grad_context = jnp.dot(grad_attn_low, w_out, preferred_element_type=f32).astype(bf16)
    grad_query, grad_key, grad_value = attend_back_all(
        query_rotated, key_rotated, value_reduced, log_totals, grad_context, tables
    )
    grad_qkv = jnp.concatenate([grad_query, grad_key.astype(bf16), grad_value.astype(bf16)], 1)
    grad_xn1 = lax.dot_general(grad_qkv, w_qkv, contract_last, preferred_element_type=f32)
    grad_gain_attn = jnp.sum(grad_xn1 * normed_attn, axis=0)
    grad_tokens = grad_hidden + norm_back(grad_xn1 * gain_attn, normed_attn, inputs)

    def over_rows(left, right):
        return lax.dot_general(left, right, contract_first, preferred_element_type=f32)

    ff_terms = [
        over_rows(a, b).astype(bf16).reshape(CHIPS, CORES, nz, rows, -1) for a, b in ((gy_all, mixed), (x_all, grad_gate_up))
    ]
    from_core = core_exchange(ff_terms, 4)
    ff_sums = jnp.concatenate(
        [lax.dynamic_index_in_dim(t, k, 1, False).astype(f32) + r.astype(f32) for t, r in zip(ff_terms, from_core)], 3
    ).astype(bf16)
    ff_sums = lax.psum_scatter(jnp.swapaxes(ff_sums, 0, 1), "narrow", scatter_dimension=0, tiled=True)
    ff_sums = plane_swap(ff_sums.reshape(CHIPS, rows, 3 * cols), 5)
    grad_w_down = jnp.swapaxes(ff_sums[:, :, :cols], 0, 1).reshape(rows, CHIPS * cols).astype(f32)
    grad_gate_up = jnp.swapaxes(ff_sums[:, :, cols:], 0, 1).reshape(rows, CHIPS * cols // 128, 2, 128).astype(f32)
    grad_w_gate = grad_gate_up[:, :, 0].reshape(rows, CHIPS * cols)
    grad_w_up = grad_gate_up[:, :, 1].reshape(rows, CHIPS * cols)
    attn_terms = jnp.concatenate([over_rows(grad_attn_low, context), over_rows(scaled_attn, grad_qkv)], 1)
    attn_sums = lax.psum_scatter(attn_terms.astype(bf16), ("wide", "narrow"), scatter_dimension=0, tiled=True).astype(f32)
    grad_w_output = attn_sums[:, :query_width]
    grad_w_query = attn_sums[:, query_width : 2 * query_width]
    grad_w_key = attn_sums[:, 2 * query_width : 2 * query_width + key_width]
    grad_w_value = attn_sums[:, 2 * query_width + key_width :]
    grad_norm_attn, grad_norm_mlp = (
        lax.psum_scatter(g, ("wide", "narrow"), scatter_dimension=0, tiled=True) for g in (grad_gain_attn, grad_gain_mlp)
    )
    return (
        output,
        grad_tokens,
        grad_norm_attn,
        grad_w_query,
        grad_w_key,
        grad_w_value,
        grad_w_output,
        grad_norm_mlp,
        grad_w_gate,
        grad_w_up,
        grad_w_down,
    )


def solution(mesh):
    in_specs = (
        P(("wide", "narrow"), None),
        P(("wide", "narrow"), None),
        P(("wide", "narrow")),
        P(("wide", "narrow")),
        P(("wide", "narrow")),
        P(("wide", "narrow"), None),
        P(("wide", "narrow"), None),
        P(("wide", "narrow"), None),
        P(("wide", "narrow"), None),
        P(("wide", "narrow")),
        P(("wide", "narrow"), None),
        P(("wide", "narrow"), None),
        P(("wide", "narrow"), None),
    )
    out_specs = (
        P(("wide", "narrow"), None),
        P(("wide", "narrow"), None),
        P(("wide", "narrow")),
        P(("wide", "narrow"), None),
        P(("wide", "narrow"), None),
        P(("wide", "narrow"), None),
        P(("wide", "narrow"), None),
        P(("wide", "narrow")),
        P(("wide", "narrow"), None),
        P(("wide", "narrow"), None),
        P(("wide", "narrow"), None),
    )
    body = functools.partial(fast_device, mesh.shape["narrow"]) if fits(mesh) else per_device
    return jax.shard_map(
        body, mesh=mesh, in_specs=in_specs, out_specs=out_specs, check_vma=False
    )
```

```python
import functools
import math

import jax
import jax.numpy as jnp
from jax import lax
from jax.experimental import pallas as pl
from jax.experimental.pallas import tpu as pltpu
from jax.sharding import PartitionSpec as P

QUERY_HEADS = 32
KEY_VALUE_HEADS = 4
HEAD_SIZE = 64


norm_eps = 1e-05
rope_base = 10000.0
masked_score = -1e30
contract_last = (((1,), (1,)), ((), ()))
contract_first = (((0,), (0,)), ((), ()))


def rope_tables(positions):
    half_dim = HEAD_SIZE // 2
    inv_freq = jnp.exp(
        -math.log(rope_base) * jnp.arange(half_dim, dtype=jnp.float32) * 2.0 / HEAD_SIZE
    )
    angles = positions.astype(jnp.float32)[..., None] * inv_freq
    cosine = jnp.cos(angles)
    sine_part = jnp.sin(angles)
    return (jnp.concatenate([cosine, cosine], -1), jnp.concatenate([sine_part, sine_part], -1))


def apply_rotary(values, cosine_table, sine_table):
    half_dim = values.shape[-1] // 2
    turned = jnp.concatenate([-values[..., half_dim:], values[..., :half_dim]], -1)
    return values * cosine_table[..., None, :] + turned * sine_table[..., None, :]


def invert_rotary(grad_rows, cosine_table, sine_table):
    half_dim = grad_rows.shape[-1] // 2
    with_cos = grad_rows * cosine_table[..., None, :]
    with_sin = grad_rows * sine_table[..., None, :]
    return with_cos + jnp.concatenate([with_sin[..., half_dim:], -with_sin[..., :half_dim]], -1)


def normalize(values):
    return values * lax.rsqrt(jnp.mean(values * values, axis=-1, keepdims=True) + norm_eps)


def norm_back(grad_hat, normed, values):
    row_scale = lax.rsqrt(jnp.mean(values * values, axis=-1, keepdims=True) + norm_eps)
    return row_scale * (grad_hat - normed * jnp.mean(grad_hat * normed, axis=-1, keepdims=True))


def attention_inputs(normed, norm_attn, w_query, w_key, w_value):
    gain_piece = lax.all_gather(norm_attn, ("wide", "narrow"), axis=0, tiled=True)
    query_rows = lax.all_gather(w_query, ("wide", "narrow"), axis=0, tiled=True)
    key_rows = lax.all_gather(w_key, ("wide", "narrow"), axis=0, tiled=True)
    value_rows = lax.all_gather(w_value, ("wide", "narrow"), axis=0, tiled=True)
    gain_float = gain_piece.astype(jnp.float32)
    columns = (normed * gain_float).astype(jnp.bfloat16)
    query_sum = jnp.dot(columns, query_rows, preferred_element_type=jnp.float32)
    key_sum = jnp.dot(columns, key_rows, preferred_element_type=jnp.float32)
    value_sum = jnp.dot(columns, value_rows, preferred_element_type=jnp.float32)
    return (gain_float, columns, query_sum, key_sum, value_sum)


def mlp_inputs(normed, norm_mlp, w_gate, w_up):
    gain_piece = lax.all_gather(norm_mlp, ("wide", "narrow"), axis=0, tiled=True)
    gate_rows = lax.all_gather(w_gate, ("wide", "narrow"), axis=0, tiled=True)
    up_rows = lax.all_gather(w_up, ("wide", "narrow"), axis=0, tiled=True)
    gain_float = gain_piece.astype(jnp.float32)
    columns = (normed * gain_float).astype(jnp.bfloat16)
    gate_sum = jnp.dot(columns, gate_rows, preferred_element_type=jnp.float32)
    up_sum = jnp.dot(columns, up_rows, preferred_element_type=jnp.float32)
    return (gain_float, columns, gate_sum, up_sum)


def head_slices(query_rotated, key_rotated, value_reduced, shared_key_head):
    row_total_count = query_rotated.shape[0]
    heads_per_group = QUERY_HEADS // KEY_VALUE_HEADS
    query_head = query_rotated[
        :,
        shared_key_head
        * heads_per_group
        * HEAD_SIZE : (shared_key_head + 1)
        * heads_per_group
        * HEAD_SIZE,
    ].reshape(row_total_count, heads_per_group, HEAD_SIZE)
    key_head = key_rotated[:, shared_key_head * HEAD_SIZE : (shared_key_head + 1) * HEAD_SIZE]
    value_head = value_reduced[:, shared_key_head * HEAD_SIZE : (shared_key_head + 1) * HEAD_SIZE]
    return (query_head, key_head, value_head)


def head_scores(query_head, key_head):
    row_total_count = query_head.shape[0]
    causal = jnp.arange(row_total_count)[:, None] >= jnp.arange(row_total_count)[None, :]
    raw_scores = jnp.einsum("qrd,kd->rqk", query_head, key_head, preferred_element_type=jnp.float32)
    return jnp.where(causal, raw_scores * HEAD_SIZE ** (-0.5), masked_score)


def attend(query_rotated, key_rotated, value_reduced):
    row_total_count = query_rotated.shape[0]
    heads_per_group = QUERY_HEADS // KEY_VALUE_HEADS
    contexts = []
    log_totals = []
    for shared_key_head in range(KEY_VALUE_HEADS):
        query_head, key_head, value_head = head_slices(
            query_rotated, key_rotated, value_reduced, shared_key_head
        )
        scores = head_scores(query_head, key_head)
        row_peak = jnp.max(scores, axis=-1, keepdims=True)
        exp_scores = jnp.exp(scores - row_peak)
        row_total = jnp.sum(exp_scores, axis=-1, keepdims=True)
        probs = exp_scores / row_total
        context_head = jnp.einsum(
            "rqk,kd->qrd",
            probs.astype(jnp.bfloat16),
            value_head,
            preferred_element_type=jnp.float32,
        )
        contexts.append(context_head.reshape(row_total_count, heads_per_group * HEAD_SIZE))
        log_totals.append(row_peak + jnp.log(row_total))
    return (jnp.concatenate(contexts, 1).astype(jnp.bfloat16), log_totals)


def attend_back(query_rotated, key_rotated, value_reduced, log_totals, grad_context):
    row_total_count = query_rotated.shape[0]
    heads_per_group = QUERY_HEADS // KEY_VALUE_HEADS
    score_scale = HEAD_SIZE ** (-0.5)
    query_grads = []
    key_grads = []
    value_grads = []
    for shared_key_head in range(KEY_VALUE_HEADS):
        query_head, key_head, value_head = head_slices(
            query_rotated, key_rotated, value_reduced, shared_key_head
        )
        scores = head_scores(query_head, key_head)
        probs = jnp.exp(scores - log_totals[shared_key_head])
        probs_low = probs.astype(jnp.bfloat16)
        grad_head = grad_context[
            :,
            shared_key_head
            * heads_per_group
            * HEAD_SIZE : (shared_key_head + 1)
            * heads_per_group
            * HEAD_SIZE,
        ].reshape(row_total_count, heads_per_group, HEAD_SIZE)
        grad_probs = jnp.einsum(
            "qrd,kd->rqk", grad_head, value_head, preferred_element_type=jnp.float32
        )
        value_grads.append(
            jnp.einsum("rqk,qrd->kd", probs_low, grad_head, preferred_element_type=jnp.float32)
        )
        inner_sum = jnp.sum(grad_probs * probs, axis=-1, keepdims=True)
        grad_scores = (probs * (grad_probs - inner_sum) * score_scale).astype(jnp.bfloat16)
        query_grad = jnp.einsum(
            "rqk,kd->qrd", grad_scores, key_head, preferred_element_type=jnp.float32
        )
        query_grads.append(query_grad.reshape(row_total_count, heads_per_group * HEAD_SIZE))
        key_grads.append(
            jnp.einsum("rqk,qrd->kd", grad_scores, query_head, preferred_element_type=jnp.float32)
        )
    return (
        jnp.concatenate(query_grads, 1),
        jnp.concatenate(key_grads, 1),
        jnp.concatenate(value_grads, 1),
    )


def make_term(width_sides, other_sides):
    down_side, mlp_side, attn_side, qkv_side = width_sides
    mixed_rows, gate_rows, up_rows, context_rows, query_rows, key_rows, value_rows = other_sides

    def grad_term(first_row, row_span):
        pieces = [
            lax.dot_general(
                down_side, mixed_rows, contract_first, preferred_element_type=jnp.float32
            ),
            lax.dot_general(
                mlp_side, gate_rows, contract_first, preferred_element_type=jnp.float32
            ),
            lax.dot_general(mlp_side, up_rows, contract_first, preferred_element_type=jnp.float32),
            lax.dot_general(
                attn_side, context_rows, contract_first, preferred_element_type=jnp.float32
            ),
            lax.dot_general(
                qkv_side, query_rows, contract_first, preferred_element_type=jnp.float32
            ),
            lax.dot_general(qkv_side, key_rows, contract_first, preferred_element_type=jnp.float32),
            lax.dot_general(
                qkv_side, value_rows, contract_first, preferred_element_type=jnp.float32
            ),
        ]
        return jnp.concatenate(pieces, 1)

    return grad_term


def per_device(
    tokens,
    cotangent,
    lengths,
    positions,
    norm_attn,
    w_query,
    w_key,
    w_value,
    w_output,
    norm_mlp,
    w_gate,
    w_up,
    w_down,
):
    row_total_count = tokens.shape[0]
    shard_rows = w_query.shape[0]
    query_width = w_query.shape[1]
    key_width = w_key.shape[1]
    hidden_width = w_gate.shape[1]
    inputs = tokens.astype(jnp.float32)
    valid_rows = (jnp.arange(row_total_count) < lengths[0]).astype(jnp.float32)[:, None]
    cosine_table, sine_table = rope_tables(positions)
    normed_attn = normalize(inputs)
    gain_attn_full, scaled_attn, query_pre, key_unrotated, value_pre = attention_inputs(
        normed_attn, norm_attn, w_query, w_key, w_value
    )
    query_rotated = (
        apply_rotary(
            query_pre.reshape(row_total_count, QUERY_HEADS, HEAD_SIZE), cosine_table, sine_table
        )
        .reshape(row_total_count, query_width)
        .astype(jnp.bfloat16)
    )
    key_rotated = (
        apply_rotary(
            key_unrotated.reshape(row_total_count, KEY_VALUE_HEADS, HEAD_SIZE),
            cosine_table,
            sine_table,
        )
        .reshape(row_total_count, key_width)
        .astype(jnp.bfloat16)
    )
    value_reduced = value_pre.astype(jnp.bfloat16)
    context, log_totals = attend(query_rotated, key_rotated, value_reduced)
    attn_out = lax.dot_general(
        context,
        lax.all_gather(w_output, ("wide", "narrow"), axis=0, tiled=True),
        contract_last,
        preferred_element_type=jnp.float32,
    )
    hidden = inputs + attn_out
    normed_mlp = normalize(hidden)
    gain_mlp_full, scaled_mlp, gate_proj, up_proj = mlp_inputs(normed_mlp, norm_mlp, w_gate, w_up)
    mixed_low = (gate_proj * jax.nn.sigmoid(gate_proj) * up_proj).astype(jnp.bfloat16)
    mlp_out = lax.dot_general(
        mixed_low,
        lax.all_gather(w_down, ("wide", "narrow"), axis=0, tiled=True),
        contract_last,
        preferred_element_type=jnp.float32,
    )
    output = (valid_rows * (hidden + mlp_out)).astype(jnp.bfloat16)
    grad_y = cotangent.astype(jnp.float32) * valid_rows
    grad_y_low = grad_y.astype(jnp.bfloat16)
    grad_cols = grad_y_low
    grad_mixed = jnp.dot(
        grad_cols,
        lax.all_gather(w_down, ("wide", "narrow"), axis=0, tiled=True),
        preferred_element_type=jnp.float32,
    )
    again_values = mlp_inputs(normed_mlp, norm_mlp, w_gate, w_up)
    gate_proj = again_values[2]
    up_proj = again_values[3]
    sigmoid_gate = jax.nn.sigmoid(gate_proj)
    grad_gate = (
        grad_mixed * up_proj * (sigmoid_gate * (1.0 + gate_proj * (1.0 - sigmoid_gate)))
    ).astype(jnp.bfloat16)
    grad_up = (grad_mixed * (gate_proj * sigmoid_gate)).astype(jnp.bfloat16)
    gate_rows = lax.all_gather(w_gate, ("wide", "narrow"), axis=0, tiled=True)
    up_rows = lax.all_gather(w_up, ("wide", "narrow"), axis=0, tiled=True)
    columns = lax.dot_general(
        grad_gate, gate_rows, contract_last, preferred_element_type=jnp.float32
    )
    columns = columns + lax.dot_general(
        grad_up, up_rows, contract_last, preferred_element_type=jnp.float32
    )
    grad_xn2 = columns
    grad_gain_mlp = jnp.sum(grad_xn2 * normed_mlp, axis=0)
    grad_hidden = grad_y + norm_back(grad_xn2 * gain_mlp_full, normed_mlp, hidden)
    grad_attn_low = grad_hidden.astype(jnp.bfloat16)
    grad_cols = grad_attn_low
    grad_context = jnp.dot(
        grad_cols,
        lax.all_gather(w_output, ("wide", "narrow"), axis=0, tiled=True),
        preferred_element_type=jnp.float32,
    )
    grad_context = grad_context.astype(jnp.bfloat16)
    grad_query_rot, gradient_key_rotated, grad_value_sum = attend_back(
        query_rotated, key_rotated, value_reduced, log_totals, grad_context
    )
    grad_query = (
        invert_rotary(
            grad_query_rot.reshape(row_total_count, QUERY_HEADS, HEAD_SIZE),
            cosine_table,
            sine_table,
        )
        .reshape(row_total_count, query_width)
        .astype(jnp.bfloat16)
    )
    grad_key = (
        invert_rotary(
            gradient_key_rotated.reshape(row_total_count, KEY_VALUE_HEADS, HEAD_SIZE),
            cosine_table,
            sine_table,
        )
        .reshape(row_total_count, key_width)
        .astype(jnp.bfloat16)
    )
    grad_value = grad_value_sum.astype(jnp.bfloat16)
    query_rows = lax.all_gather(w_query, ("wide", "narrow"), axis=0, tiled=True)
    key_rows = lax.all_gather(w_key, ("wide", "narrow"), axis=0, tiled=True)
    value_rows = lax.all_gather(w_value, ("wide", "narrow"), axis=0, tiled=True)
    columns = lax.dot_general(
        grad_query, query_rows, contract_last, preferred_element_type=jnp.float32
    )
    columns = columns + lax.dot_general(
        grad_key, key_rows, contract_last, preferred_element_type=jnp.float32
    )
    columns = columns + lax.dot_general(
        grad_value, value_rows, contract_last, preferred_element_type=jnp.float32
    )
    local_term = make_term(
        (grad_y_low, scaled_mlp, grad_attn_low, scaled_attn),
        (mixed_low, grad_gate, grad_up, context, grad_query, grad_key, grad_value),
    )
    all_sums = lax.psum_scatter(
        local_term(jnp.int32(0), lax.axis_size(("wide", "narrow")) * shard_rows),
        ("wide", "narrow"),
        scatter_dimension=0,
        tiled=True,
    )
    edges = [0]
    for width in (
        hidden_width,
        hidden_width,
        hidden_width,
        query_width,
        query_width,
        key_width,
        key_width,
    ):
        edges.append(edges[-1] + width)
    grad_w_down = all_sums[:, edges[0] : edges[1]]
    grad_w_gate = all_sums[:, edges[1] : edges[2]]
    grad_w_up = all_sums[:, edges[2] : edges[3]]
    grad_w_output = all_sums[:, edges[3] : edges[4]]
    grad_w_query = all_sums[:, edges[4] : edges[5]]
    grad_w_key = all_sums[:, edges[5] : edges[6]]
    grad_w_value = all_sums[:, edges[6] : edges[7]]
    grad_gain_attn = jnp.sum(columns * normed_attn, axis=0)
    grad_tokens = grad_hidden + norm_back(columns * gain_attn_full, normed_attn, inputs)
    grad_norm_attn, grad_norm_mlp = (
        lax.psum_scatter(grad_gain_attn, ("wide", "narrow"), scatter_dimension=0, tiled=True),
        lax.psum_scatter(grad_gain_mlp, ("wide", "narrow"), scatter_dimension=0, tiled=True),
    )
    return (
        output,
        grad_tokens,
        grad_norm_attn,
        grad_w_query,
        grad_w_key,
        grad_w_value,
        grad_w_output,
        grad_norm_mlp,
        grad_w_gate,
        grad_w_up,
        grad_w_down,
    )


MESH = pl.DeviceIdType.MESH
ANY = pl.BlockSpec(memory_space=pl.ANY)

CHIPS, CORES = 4, 2

def place():
    w = lax.axis_index("wide"); n = lax.axis_index("narrow")
    return w // CORES, w % CORES, n

def chip_at(c, r):
    xb, yb, rx, ry = c % 2, c // 2, r % 2, r // 2
    return (yb + ry - 2 * yb * ry) * 2 + (xb + rx - 2 * xb * rx)


def remote(src, dst, send, recv, chip, core, z):
    return pltpu.make_async_remote_copy(src_ref=src, dst_ref=dst, send_sem=send, recv_sem=recv,
        device_id={"wide": chip * CORES + core, "narrow": z}, device_id_type=MESH)

def hello(partners):
    barrier = pltpu.get_barrier_semaphore()
    count = 0
    for cond, chip, core, z in partners:
        def sig(chip=chip, core=core, z=z):
            pl.semaphore_signal(barrier, inc=1, device_id={"wide": chip * CORES + core, "narrow": z}, device_id_type=MESH)
        if cond is None:
            sig(); count = count + 1
        else:
            pl.when(cond)(sig); count = count + jnp.where(cond, 1, 0)
    pl.semaphore_wait(barrier, count)

def gather_kernel(nz, wq, wk, wv, wo, gains, wgu, wd, gy, QKV, WO, GAIN, G0, G1, GY,
                  loc, a2a_s, a2a_r, gy_s, gy_r, z_s, z_r, d_s, d_r, p_s, p_r, e_s, e_r):
    c, k, n = place()
    G = (G0, G1); W = (wgu, wd)
    FF = len(G)
    rows = wq.shape[0]
    other = 1 - k
    left, right = n > 0, n < nz - 1
    others = [chip_at(c, r) for r in range(1, CHIPS)]
    hello([(None, cc, k, n) for cc in others] + [(None, c, other, n), (left, c, k, n - 1), (right, c, k, n + 1)])
    kn = k * nz + n
    b = (c * CORES + k) * nz + n
    started = []
    def start(cond, desc):
        if cond is None: desc.start()
        else: pl.when(cond)(lambda: desc.start())
        started.append((cond, desc))
    def recv(cond, desc):
        if cond is None: desc.wait_recv()
        else: pl.when(cond)(lambda: desc.wait_recv())
    def blk(z): return pl.ds(pl.multiple_of(((c * CORES + k) * nz + z) * rows, rows), rows)
    mine = blk(n)
    def mycols(m, cc):
        cols = G[m].shape[-1]
        return W[m].at[:, pl.ds(pl.multiple_of(cc * cols, 128), cols)]
    q, kv = wq.shape[1], wk.shape[1]
    for i, cc in enumerate(others):
        for m in range(FF):
            start(None, remote(mycols(m, cc), G[m].at[c, kn], a2a_s.at[m, i], a2a_r.at[m, i], cc, k, n))
    own = [pltpu.make_async_copy(wq, QKV.at[mine, pl.ds(0, q)], loc.at[0]),
           pltpu.make_async_copy(wk, QKV.at[mine, pl.ds(q, kv)], loc.at[1]),
           pltpu.make_async_copy(wv, QKV.at[mine, pl.ds(q + kv, kv)], loc.at[2]),
           pltpu.make_async_copy(wo, WO.at[mine], loc.at[3]),
           pltpu.make_async_copy(gains, GAIN.at[mine], loc.at[4])]
    ownff = [pltpu.make_async_copy(mycols(m, c), G[m].at[c, kn], loc.at[5 + m]) for m in range(FF)]
    owngy = pltpu.make_async_copy(gy, GY.at[0], loc.at[8])
    for cp in own + ownff + [owngy]: cp.start()
    for cp in own: cp.wait()
    A = (QKV, WO, GAIN)
    def zsend(item, ref, dirn, s):
        cond = (right & (n - s >= 0)) if dirn == 0 else (left & (n + s <= nz - 1))
        z = n + 1 if dirn == 0 else n - 1
        return cond, remote(ref, ref, z_s.at[item, dirn, s], z_r.at[item, dirn, s], c, k, z)
    def zrecv(item, ref, dirn, s):
        cond = (n - s >= 0) if dirn == 0 else (n + s <= nz - 1)
        return cond, remote(ref, ref, z_s.at[item, dirn, s - 1], z_r.at[item, dirn, s - 1], c, k, n)
    def origin(dirn, s):
        o = n - s if dirn == 0 else n + s
        return jnp.clip(o, 0, nz - 1)
    for a in range(3):
        for dirn in range(2):
            start(*zsend(a, A[a].at[mine], dirn, 0))
    for i, cc in enumerate(others):
        start(None, remote(gy, GY.at[1 + i], gy_s.at[i], gy_r.at[i], cc, k, n))
    for s in range(1, nz):
        for dirn in range(2):
            for a in range(3):
                ref = A[a].at[blk(origin(dirn, s))]
                recv(*zrecv(a, ref, dirn, s))
                if s < nz - 1: start(*zsend(a, ref, dirn, s))
    def part(cc, kk): return pl.ds(pl.multiple_of((cc * CORES + kk) * nz * rows, rows), nz * rows)
    for a in range(3):
        for i, cc in enumerate(others):
            start(None, remote(A[a].at[part(c, k)], A[a].at[part(c, k)], p_s.at[a, i], p_r.at[a, i], cc, k, n))
        start(None, remote(A[a].at[part(c, k)], A[a].at[part(c, k)], d_s.at[a, 0], d_r.at[a, 0], c, other, n))
    for m in range(FF):
        ownff[m].wait()
        for i in range(CHIPS - 1):
            remote(G[m].at[c, kn], G[m].at[c, kn], a2a_s.at[m, i], a2a_r.at[m, i], c, k, n).wait_recv()
        ref = G[m].at[:, kn]
        for dirn in range(2): start(*zsend(3 + m, ref, dirn, 0))
        start(None, remote(ref, ref, e_s.at[m, 0, 0], e_r.at[m, 0, 0], c, other, n))
    for s in range(1, nz):
        for dirn in range(2):
            for m in range(FF):
                ref = G[m].at[:, k * nz + origin(dirn, s)]
                cond, d = zrecv(3 + m, ref, dirn, s)
                recv(cond, d)
                if s < nz - 1: start(*zsend(3 + m, ref, dirn, s))
                start(cond, remote(ref, ref, e_s.at[m, dirn, s], e_r.at[m, dirn, s], c, other, n))
    for i in range(CHIPS - 1):
        cc = others[i]
        for a in range(3):
            ref = A[a].at[part(cc, k)]
            remote(ref, ref, p_s.at[a, i], p_r.at[a, i], c, k, n).wait_recv()
            start(None, remote(ref, ref, d_s.at[a, 1 + i], d_r.at[a, 1 + i], c, other, n))
    owngy.wait()
    for i in range(CHIPS - 1):
        remote(gy, GY.at[1 + i], gy_s.at[i], gy_r.at[i], c, k, n).wait_recv()
    for a in range(3):
        for i in range(CHIPS):
            remote(A[a].at[part(c, k)], A[a].at[part(c, k)], d_s.at[a, i], d_r.at[a, i], c, k, n).wait_recv()
    for m in range(FF):
        ref = G[m].at[:, kn]
        remote(ref, ref, e_s.at[m, 0, 0], e_r.at[m, 0, 0], c, k, n).wait_recv()
        for s in range(1, nz):
            for dirn in range(2):
                cond = (n - s >= 0) if dirn == 0 else (n + s <= nz - 1)
                recv(cond, remote(ref, ref, e_s.at[m, dirn, s], e_r.at[m, dirn, s], c, k, n))
    for cond, desc in started:
        if cond is None: desc.wait_send()
        else: pl.when(cond)(lambda desc=desc: desc.wait_send())

def gather_all(nz, wq, wk, wv, wo, gains, wgu, wd, gy):
    D = wq.shape[0] * CHIPS * CORES * nz
    bf = jnp.bfloat16
    def ff(w):
        return jax.ShapeDtypeStruct((CHIPS, CORES * nz, w.shape[0], w.shape[1] // CHIPS), bf)
    dma = pltpu.SemaphoreType.DMA
    return pl.pallas_call(
        functools.partial(gather_kernel, nz),
        out_shape=(jax.ShapeDtypeStruct((D, wq.shape[1] + 2 * wk.shape[1]), bf), jax.ShapeDtypeStruct((D, wo.shape[1]), bf),
                   jax.ShapeDtypeStruct((D, 128), bf), ff(wgu), ff(wd), jax.ShapeDtypeStruct((CHIPS,) + gy.shape, bf)),
        in_specs=[ANY] * 8, out_specs=(ANY,) * 6,
        scratch_shapes=[dma((9,)), dma((3, 3)), dma((3, 3)), dma((3,)), dma((3,)), dma((6, 2, nz)), dma((6, 2, nz)),
                        dma((3, 4)), dma((3, 4)), dma((3, 3)), dma((3, 3)), dma((3, 2, nz)), dma((3, 2, nz))],
        compiler_params=pltpu.CompilerParams(collective_id=0, has_side_effects=True),
        name="gather_all",
    )(wq, wk, wv, wo, gains, wgu, wd, gy)

def mlp_kernel(nz, x, gy, gu_hbm, gd_hbm, gx_parts, mlp_parts, sums,
               xs, gys, gu, gd, mix, ggu, gx, mo, xt, load, ag_s, ag_r, rs_s, rs_r, own, out, core_s, core_r, ready, done):
    c, k, n = place()
    f32, bf16 = jnp.float32, jnp.bfloat16
    slots, width = x.shape
    half = slots // 2
    rows, cols = gd.shape[1:]
    per_tile = nz
    tile = nz * rows
    hello([(None, chip_at(c, r), k, n) for r in (1, 2, 3)] + [(None, c, 1 - k, n)])
    loads = [pltpu.make_async_copy(x, xs.at[0], load.at[0])]
    sends = [remote(x, xs.at[r], ag_s.at[r], ag_r.at[r], chip_at(c, r), k, n) for r in (1, 2)]
    for cp in sends: cp.start()
    loads += [pltpu.make_async_copy(gu_hbm, gu, load.at[1]), pltpu.make_async_copy(gd_hbm, gd, load.at[2]),
              pltpu.make_async_copy(gy, gys, load.at[3])]
    for cp in loads: cp.start()
    relays = [remote(xs.at[1, pl.ds(0, half)], xs.at[3, pl.ds(0, half)], ag_s.at[0], ag_r.at[0], chip_at(c, 2), k, n),
              remote(xs.at[2, pl.ds(half, half)], xs.at[3, pl.ds(half, half)], ag_s.at[3], ag_r.at[3], chip_at(c, 1), k, n)]
    for cp in loads: cp.wait()

    def columns(ref, at, size):
        t = ref[:, :, pl.ds(at, size)]
        return t.reshape(t.shape[0] * t.shape[1], size)

    def some_rows(ref, i):
        t = ref[pl.ds(i * (256 // rows), 256 // rows)]
        return t.reshape(256, t.shape[2])

    def block(r, carry):
        @pl.when(r == 1)
        def _():
            for cp in sends: cp.wait_recv()
            for cp in relays: cp.start()
        @pl.when(r == 3)
        def _():
            for cp in relays: cp.wait_recv()
        def chunk(col, w):
            h = jnp.dot(xs[r], columns(gu, 2 * col, 2 * w), preferred_element_type=f32)
            gm = jnp.dot(gys[r], columns(gd, col, w), preferred_element_type=f32)
            for q in range(w // 128):
                gate, up, g = h[:, 256 * q : 256 * q + 128], h[:, 256 * q + 128 : 256 * q + 256], gm[:, 128 * q : 128 * q + 128]
                sg = 1.0 / (1.0 + jnp.exp(-gate))
                act = gate * sg
                mix[r, :, pl.ds(col + 128 * q, 128)] = (act * up).astype(bf16)
                ggu[r, :, pl.ds(2 * col + 256 * q, 128)] = (g * up * (sg * (1.0 + gate * (1.0 - sg)))).astype(bf16)
                ggu[r, :, pl.ds(2 * col + 256 * q + 128, 128)] = (g * act).astype(bf16)
        def pair(j, carry):
            chunk(pl.multiple_of(j * 256, 256), 256)
            return carry
        lax.fori_loop(0, cols // 256, pair, 0)
        if cols % 256: chunk(cols - 128, 128)
        def back(i, carry):
            at = pl.ds(pl.multiple_of(i * 256, 256), 256)
            gx[r, :, at] = lax.dot_general(ggu[r], some_rows(gu, i), contract_last, preferred_element_type=f32).astype(bf16)
            return carry
        lax.fori_loop(0, width // 256, back, 0)
        @pl.when(r == 0)
        def _(): pltpu.make_async_copy(gx.at[0], gx_parts.at[0], own).start()
        @pl.when(r > 0)
        def _(): remote(gx.at[r], gx_parts.at[r], rs_s.at[r], rs_r.at[r], chip_at(c, r), k, n).start()
        def down(i, carry):
            at = pl.ds(pl.multiple_of(i * 256, 256), 256)
            mo[r, :, at] = lax.dot_general(mix[r], some_rows(gd, i), contract_last, preferred_element_type=f32).astype(bf16)
            return carry
        lax.fori_loop(0, width // 256, down, 0)
        pltpu.make_async_copy(mo.at[r], mlp_parts.at[r], out.at[r]).start()
        return carry
    lax.fori_loop(0, CHIPS, block, 0)

    pl.semaphore_signal(ready, inc=1, device_id={"wide": c * CORES + 1 - k, "narrow": n}, device_id_type=MESH)
    pl.semaphore_wait(ready, 1)
    sent, came = 0, CHIPS * per_tile

    def terms(t, kk, put):
        at = pl.ds(pl.multiple_of((t * CORES + kk) * tile, 128), tile)
        for src, right, ref in ((xs, ggu, gu), (gys, mix, gd)):
            total = ref.shape[-1]
            for r in range(CHIPS):
                xt[:, r * slots : (r + 1) * slots] = src[r, :, at].T
            def one(col, w):
                b = right[:, :, pl.ds(col, w)].reshape(CHIPS * slots, w)
                put(ref, t, col, w, jnp.dot(xt[...], b, preferred_element_type=f32))
            def step(j, carry):
                one(pl.multiple_of(j * 256, 256), 256)
                return carry
            lax.fori_loop(0, total // 256, step, 0)
            if total % 256: one(total - 128, 128)

    def to_core(ref, i, t):
        return remote(ref.at[pl.ds(sent + t * per_tile, per_tile)], ref.at[pl.ds(came + t * per_tile, per_tile)],
                      core_s.at[i, t], core_r.at[i, t], c, 1 - k, n)

    def to_sums(ref, i, t):
        first = 0 if i == 0 else cols
        return pltpu.make_async_copy(ref.at[pl.ds(came + t * per_tile, per_tile)],
                                     sums.at[:, t, :, pl.ds(first, ref.shape[-1])], done.at[i, t])

    def theirs(t, carry):
        def put(ref, t, col, w, v):
            ref[pl.ds(sent + t * per_tile, per_tile), :, pl.ds(col, w)] = v.astype(bf16).reshape(per_tile, rows, w)
        terms(t, 1 - k, put)
        for i, ref in enumerate((gd, gu)): to_core(ref, i, t).start()
        return carry
    lax.fori_loop(0, CHIPS, theirs, 0)

    def ours(t, carry):
        for i, ref in enumerate((gd, gu)): to_core(ref, i, t).wait_recv()
        def put(ref, t, col, w, v):
            here = (pl.ds(came + t * per_tile, per_tile), slice(None), pl.ds(col, w))
            ref[here] = (ref[here].astype(f32) + v.reshape(per_tile, rows, w)).astype(bf16)
        terms(t, k, put)
        for i, ref in enumerate((gd, gu)): to_sums(ref, i, t).start()
        return carry
    lax.fori_loop(0, CHIPS, ours, 0)

    for cp in sends + relays: cp.wait_send()
    pltpu.make_async_copy(gx.at[0], gx_parts.at[0], own).wait()
    for r in range(CHIPS):
        pltpu.make_async_copy(mo.at[r], mlp_parts.at[r], out.at[r]).wait()
    for t in range(CHIPS):
        for i, ref in enumerate((gd, gu)):
            to_core(ref, i, t).wait_send()
            to_sums(ref, i, t).wait()
    for r in (1, 2, 3):
        remote(gx.at[r], gx_parts.at[r], rs_s.at[r], rs_r.at[r], chip_at(c, r), k, n).wait()


def mlp_all(nz, x, gy, gu, gd):
    slots, width = x.shape
    rows, cols = gd.shape[1:]
    bf, dma, vm = jnp.bfloat16, pltpu.SemaphoreType.DMA, pltpu.VMEM
    def blocks(w): return jax.ShapeDtypeStruct((CHIPS, slots, w), bf)
    flops = 2 * 9 * CHIPS * slots * width * cols
    return pl.pallas_call(
        functools.partial(mlp_kernel, nz),
        out_shape=(blocks(width), blocks(width), jax.ShapeDtypeStruct((nz, CHIPS, rows, 3 * cols), bf)),
        in_specs=[ANY] * 4, out_specs=(ANY,) * 3,
        scratch_shapes=[vm((CHIPS, slots, width), bf), vm((CHIPS, slots, width), bf), vm(gu.shape, bf), vm(gd.shape, bf),
                        vm((CHIPS, slots, cols), bf), vm((CHIPS, slots, 2 * cols), bf), vm((CHIPS, slots, width), bf),
                        vm((CHIPS, slots, width), bf), vm((nz * rows, CHIPS * slots), bf), dma((4,)), dma((4,)), dma((4,)), dma((4,)), dma((4,)),
                        dma, dma((4,)), dma((2, 4)), dma((2, 4)), pltpu.SemaphoreType.REGULAR, dma((2, 4))],
        compiler_params=pltpu.CompilerParams(collective_id=1, has_side_effects=True, vmem_limit_bytes=62 << 20),
        cost_estimate=pl.CostEstimate(flops=flops, bytes_accessed=60 << 20, transcendentals=CHIPS * slots * cols),
        name="mlp_all",
    )(x, gy, gu, gd)


PAIR = 2 * HEAD_SIZE
REPEAT = QUERY_HEADS // KEY_VALUE_HEADS
PAIRS = REPEAT // 2


def lane_tables(positions):
    cosine, sine = rope_tables(positions)
    first = jnp.arange(HEAD_SIZE) < HEAD_SIZE // 2
    low, high = jnp.where(first, -sine, 0.0), jnp.where(first, 0.0, sine)
    return jnp.stack([jnp.concatenate([t, t], 1) for t in (cosine, low, high)])


def rotate(u, tables):
    half = HEAD_SIZE // 2
    return u * tables[0] + pltpu.roll(u, PAIR - half, 1) * tables[1] + pltpu.roll(u, half, 1) * tables[2]


def unrotate(g, tables):
    half = HEAD_SIZE // 2
    return g * tables[0] + pltpu.roll(g * tables[2], PAIR - half, 1) + pltpu.roll(g * tables[1], half, 1)


def row_blocks(slots):
    return [(at, min(128, slots - at), at + 128) for at in range(0, slots, 128)]


def causal(s, below, fill):
    clear = s.shape[1] - 128
    last = jnp.where(below, s[:, clear:], fill)
    return jnp.concatenate([s[:, :clear], last], 1) if clear else last


def attend_kernel(q_ref, k_ref, v_ref, tab_ref, qr_ref, k_out, v_out, lse_ref, ctx_ref, ks, vs):
    g = pl.program_id(0)
    f32, bf16 = jnp.float32, jnp.bfloat16
    slots = q_ref.shape[0]
    @pl.when(g == 0)
    def _():
        ks[...] = jnp.zeros_like(ks)
        vs[...] = jnp.zeros_like(vs)
    lane = lax.broadcasted_iota(jnp.int32, (slots, PAIR), 1)
    tables = (tab_ref[0], tab_ref[1], tab_ref[2])
    key, val = rotate(k_ref[...], tables), v_ref[...]
    odd = g % 2 == 1
    for x, own, stack, scale in ((key, k_out, ks, HEAD_SIZE ** -0.5), (val, v_out, vs, 1.0)):
        x = jnp.where(lane < HEAD_SIZE, jnp.where(odd, pltpu.roll(x, HEAD_SIZE, 1), x), 0.0).astype(bf16)
        own[0] = x
        x = x.astype(f32) * scale
        stack[0, 0:slots, :] = x.astype(bf16)
        stack[1, 0:slots, :] = pltpu.roll(x, HEAD_SIZE, 1).astype(bf16)
    for at, size, keys in row_blocks(slots):
        below = lax.broadcasted_iota(jnp.int32, (size, 128), 0) >= lax.broadcasted_iota(jnp.int32, (size, 128), 1)
        lse = jnp.zeros((size, PAIR), f32)
        here = lane[0:size]
        for p in range(PAIRS):
            span = slice(p * PAIR, (p + 1) * PAIR)
            rows = slice(at, at + size)
            q = rotate(q_ref[rows, span], tuple(t[rows] for t in tables)).astype(bf16)
            qr_ref[rows, span] = q
            ctx = jnp.zeros((size, PAIR), f32)
            for h in range(2):
                s = lax.dot_general(q, ks[h, 0:keys, :], contract_last, preferred_element_type=f32)
                s = causal(s, below, masked_score)
                peak = jnp.max(s, axis=-1, keepdims=True)
                e = jnp.exp(s - peak)
                total = jnp.sum(e, axis=-1, keepdims=True)
                lse = jnp.where(here == 2 * p + h, peak + jnp.log(total), lse)
                probs = (e * (1.0 / total)).astype(bf16)
                ctx = ctx + jnp.dot(probs, vs[h, 0:keys, :], preferred_element_type=f32)
            ctx_ref[rows, span] = ctx.astype(bf16)
        lse_ref[0, at : at + size, :] = lse


def attend_all(qkv, tables):
    slots = qkv.shape[0]
    wide = REPEAT * HEAD_SIZE
    first = QUERY_HEADS * HEAD_SIZE // PAIR
    bf16 = jnp.bfloat16
    keys = -(-slots // 128) * 128
    shape = jax.ShapeDtypeStruct
    per_head = pl.BlockSpec((1, slots, PAIR), lambda g: (g, 0, 0))
    wide_spec = pl.BlockSpec((slots, wide), lambda g: (0, g))
    return pl.pallas_call(
        attend_kernel,
        grid=(KEY_VALUE_HEADS,),
        out_shape=(shape((slots, QUERY_HEADS * HEAD_SIZE), bf16), shape((KEY_VALUE_HEADS, slots, PAIR), bf16),
                   shape((KEY_VALUE_HEADS, slots, PAIR), bf16), shape((KEY_VALUE_HEADS, slots, PAIR), jnp.float32),
                   shape((slots, QUERY_HEADS * HEAD_SIZE), bf16)),
        in_specs=[wide_spec, pl.BlockSpec((slots, PAIR), lambda g: (0, first + g // 2)),
                  pl.BlockSpec((slots, PAIR), lambda g: (0, first + KEY_VALUE_HEADS // 2 + g // 2)),
                  pl.BlockSpec((3, slots, PAIR), lambda g: (0, 0, 0))],
        out_specs=(wide_spec, per_head, per_head, per_head, wide_spec),
        scratch_shapes=[pltpu.VMEM((2, keys, PAIR), bf16), pltpu.VMEM((2, keys, PAIR), bf16)],
        compiler_params=pltpu.CompilerParams(vmem_limit_bytes=32 << 20),
        name="attend",
    )(qkv, qkv, qkv, tables)


def attend_back_kernel(q_ref, k_ref, v_ref, lse_ref, gc_ref, tab_ref, part, gq_ref, gk_ref, gv_ref, parts,
                       ks, kt, vt, ds, pr, qs, gs, loc, s_s, s_r):
    g = pl.program_id(0)
    c, k, n = place()
    copies = [pltpu.make_async_copy(part.at[0], parts.at[0], loc)]
    copies += [remote(part.at[r], parts.at[r], s_s.at[r - 1], s_r.at[r - 1], chip_at(c, r), k, n) for r in (1, 2, 3)]
    @pl.when(g == 0)
    def _():
        hello([(None, chip_at(c, r), k, n) for r in (1, 2, 3)])
        for cp in copies: cp.start()
    f32, bf16 = jnp.float32, jnp.bfloat16
    slots = q_ref.shape[0]
    scale = HEAD_SIZE ** -0.5
    @pl.when(g == 0)
    def _():
        for ref in (ks, kt, vt, ds, pr): ref[...] = jnp.zeros_like(ref)
    lane = lax.broadcasted_iota(jnp.int32, (slots, PAIR), 1)
    tables = (tab_ref[0], tab_ref[1], tab_ref[2])
    key, val = k_ref[0].astype(f32), v_ref[0].astype(f32)
    for stack, x in ((ks, key * scale), (kt, key), (vt, val)):
        stack[0, 0:slots, :] = x.astype(bf16)
        stack[1, 0:slots, :] = pltpu.roll(x, HEAD_SIZE, 1).astype(bf16)
    for at, size, keys in row_blocks(slots):
        rows = slice(at, at + size)
        below = lax.broadcasted_iota(jnp.int32, (size, 128), 0) >= lax.broadcasted_iota(jnp.int32, (size, 128), 1)
        lse = lse_ref[0, rows, :]
        for p in range(PAIRS):
            span = slice(p * PAIR, (p + 1) * PAIR)
            deep = slice(p * slots + at, p * slots + at + size)
            q, gc = q_ref[rows, span], gc_ref[rows, span]
            qs[deep, :] = q
            gs[deep, :] = gc
            gq = jnp.zeros((size, PAIR), f32)
            for h in range(2):
                s = lax.dot_general(q, ks[h, 0:keys, :], contract_last, preferred_element_type=f32)
                e = jnp.exp(s - lse[:, 2 * p + h : 2 * p + h + 1])
                probs = causal(e, below, 0.0)
                pr[h, deep, 0:keys] = probs.astype(bf16)
                gp = lax.dot_general(gc, vt[h, 0:keys, :], contract_last, preferred_element_type=f32)
                inner = jnp.sum(gp * probs, axis=-1, keepdims=True)
                grad = (probs * (gp - inner) * scale).astype(bf16)
                ds[h, deep, 0:keys] = grad
                gq = gq + jnp.dot(grad, kt[h, 0:keys, :], preferred_element_type=f32)
            gq_ref[rows, span] = unrotate(gq, tuple(t[rows] for t in tables)).astype(bf16)
    for src, right, out, turn in ((ds, qs, gk_ref, True), (pr, gs, gv_ref, False)):
        lo, hi = (
            lax.dot_general(src[h], right[...], contract_first, preferred_element_type=f32)[0:slots] for h in range(2)
        )
        x = jnp.where(lane < HEAD_SIZE, lo + pltpu.roll(hi, HEAD_SIZE, 1), 0.0)
        if turn: x = unrotate(x, tables)
        @pl.when(g % 2 == 0)
        def _(): out[...] = x
        @pl.when(g % 2 == 1)
        def _(): out[...] = jnp.where(lane < HEAD_SIZE, out[...], pltpu.roll(x, HEAD_SIZE, 1))
    @pl.when(g == KEY_VALUE_HEADS - 1)
    def _():
        for cp in copies: cp.wait()


def attend_back_all(q, k, v, lse, grad_context, tables, part):
    slots = q.shape[0]
    wide = REPEAT * HEAD_SIZE
    bf16, f32, vm = jnp.bfloat16, jnp.float32, pltpu.VMEM
    keys = -(-slots // 128) * 128
    shape = jax.ShapeDtypeStruct
    per_head = pl.BlockSpec((1, slots, PAIR), lambda g: (g, 0, 0))
    wide_spec = pl.BlockSpec((slots, wide), lambda g: (0, g))
    two = pl.BlockSpec((slots, PAIR), lambda g: (0, g // 2))
    return pl.pallas_call(
        attend_back_kernel,
        grid=(KEY_VALUE_HEADS,),
        out_shape=(shape((slots, QUERY_HEADS * HEAD_SIZE), bf16), shape((slots, KEY_VALUE_HEADS * HEAD_SIZE), f32),
                   shape((slots, KEY_VALUE_HEADS * HEAD_SIZE), f32), shape(part.shape, part.dtype)),
        in_specs=[wide_spec, per_head, per_head, per_head, wide_spec, pl.BlockSpec((3, slots, PAIR), lambda g: (0, 0, 0)), ANY],
        out_specs=(wide_spec, two, two, ANY),
        scratch_shapes=[vm((2, keys, PAIR), bf16)] * 3 + [vm((2, PAIRS * slots, keys), bf16)] * 2 + [vm((PAIRS * slots, PAIR), bf16)] * 2
        + [pltpu.SemaphoreType.DMA, pltpu.SemaphoreType.DMA((3,)), pltpu.SemaphoreType.DMA((3,))],
        compiler_params=pltpu.CompilerParams(collective_id=2, has_side_effects=True, vmem_limit_bytes=40 << 20),
        name="attend_back",
    )(q, k, v, lse, grad_context, tables, part)


def add_into(dst, *srcs):
    rows = dst.shape[0]
    step = 16
    def body(i, carry):
        at = pl.ds(pl.multiple_of(i * step, step), step)
        total = dst[at, :].astype(jnp.float32)
        for s in srcs: total = total + s[at, :].astype(jnp.float32)
        dst[at, :] = total.astype(dst.dtype)
        return carry
    lax.fori_loop(0, rows // step, body, 0)


def reduce_kernel(nz, items, *refs):
    terms, ff = refs[:items], refs[items]
    outs, ff_out = refs[items + 1 : 2 * items + 1], refs[2 * items + 1]
    bufs = refs[2 * items + 2 :]
    took, away, zbuf = bufs[:items], bufs[items : 2 * items], bufs[2 * items : 3 * items]
    core_s, core_r, half_s, half_r, main_s, main_r, z_s, z_r, ff_s, ff_r, loc = bufs[3 * items :]
    c, k, n = place()
    left, right = n > 0, n < nz - 1
    cx, cy, cd = (chip_at(c, r) for r in (1, 2, 3))
    hello([(None, cc, k, n) for cc in (cx, cy, cd)] + [(None, c, 1 - k, n), (left, c, k, n - 1), (right, c, k, n + 1)])
    rows = ff.shape[1]
    part = nz * rows
    half = part // 2
    top, low = pl.ds(0, half), pl.ds(half, half)
    def arrive(a, at, size): return zbuf[a].at[pl.ds(at, size)]
    own = [pltpu.make_async_copy(terms[a].at[:, k], away[a], loc.at[a]) for a in range(items)]
    swap = [remote(terms[a].at[:, 1 - k], took[a], core_s.at[a], core_r.at[a], c, 1 - k, n) for a in range(items)]
    for cp in own + swap: cp.start()
    cross = [[remote(away[a].at[cd, top], arrive(a, 2 * part, half), half_s.at[a, 0], half_r.at[a, 0], cx, k, n),
              remote(away[a].at[cd, low], arrive(a, 2 * part + half, half), half_s.at[a, 1], half_r.at[a, 1], cy, k, n)]
             for a in range(items)]
    main = [[remote(away[a].at[cx, top], arrive(a, 0, half), main_s.at[a, 0], main_r.at[a, 0], cx, k, n),
             remote(away[a].at[cy, low], arrive(a, part + half, half), main_s.at[a, 1], main_r.at[a, 1], cy, k, n),
             remote(away[a].at[cx, low], arrive(a, half, half), main_s.at[a, 2], main_r.at[a, 2], cx, k, n),
             remote(away[a].at[cy, top], arrive(a, part, half), main_s.at[a, 3], main_r.at[a, 3], cy, k, n)]
            for a in range(items)]

    def cores(a):
        own[a].wait()
        swap[a].wait_recv()
        add_into(away[a].at[cd], took[a].at[cd])
        for cp in cross[a]: cp.start()
        for cc in (cx, cy, c): add_into(away[a].at[cc], took[a].at[cc])

    def relay(a):
        cross[a][0].wait_recv()
        add_into(away[a].at[cy, top], arrive(a, 2 * part, half))
        main[a][3].start()
        cross[a][1].wait_recv()
        add_into(away[a].at[cx, low], arrive(a, 2 * part + half, half))
        for i in (2, 0, 1): main[a][i].start()

    def mine(a):
        for cp in main[a]: cp.wait_recv()
        add_into(away[a].at[c], arrive(a, 0, part), arrive(a, part, part))

    def slot(a, way, j): return arrive(a, pl.multiple_of(2 * part + 2 * half + (way * nz + j) * rows, rows), rows)
    def piece(a, j): return away[a].at[c, pl.ds(pl.multiple_of(j * rows, rows), rows)]
    def hop(a, way, j):
        return remote(piece(a, j), slot(a, way, j), z_s.at[a, way, j], z_r.at[a, way, j], c, k, n + 1 if way == 0 else n - 1)

    def along(some):
        for t in range(nz):
            for way in range(2):
                hops = n if way == 0 else nz - 1 - n
                j = jnp.clip(n + nz - 1 - t if way == 0 else t - hops, 0, nz - 1)
                for a in some:
                    @pl.when((hops > 0) & (t >= hops))
                    def _():
                        hop(a, way, j).wait_recv()
                        add_into(piece(a, j), slot(a, way, j))
                    @pl.when((t >= hops) & (j != n))
                    def _(): hop(a, way, j).start()
        done = [pltpu.make_async_copy(piece(a, n), outs[a], loc.at[a]) for a in some]
        for cp in done: cp.start()
        return done

    stores = []
    for a in range(items): cores(a)
    for a in range(items): relay(a)
    mine(0)
    stores += along([0])
    for a in range(1, items): mine(a)
    swaps = [pltpu.make_async_copy(ff.at[c], ff_out.at[c], loc.at[items])]
    for r, cc in enumerate((cx, cy, cd)):
        swaps.append(remote(ff.at[cc], ff_out.at[c], ff_s.at[r], ff_r.at[r], cc, k, n))
    for cp in swaps: cp.start()
    stores += along(list(range(1, items)))
    for cp in stores: cp.wait()
    for cp in swaps: cp.wait()
    for a in range(items):
        swap[a].wait_send()
        for cp in cross[a] + main[a]: cp.wait_send()
        for j in range(nz):
            for way in range(2):
                @pl.when(n < j if way == 0 else n > j)
                def _(): hop(a, way, j).wait_send()


def reduce_all(nz, terms, ff, cid):
    dma, vm = pltpu.SemaphoreType.DMA, pltpu.VMEM
    m = len(terms)
    rows = ff.shape[1]
    part = nz * rows
    shape = jax.ShapeDtypeStruct
    terms = [t.reshape(CHIPS, CORES, part, t.shape[-1]) for t in terms]
    blocks = [vm((CHIPS, part, t.shape[-1]), t.dtype) for t in terms]
    return pl.pallas_call(
        functools.partial(reduce_kernel, nz, m),
        out_shape=tuple(shape((rows, t.shape[-1]), t.dtype) for t in terms) + (shape(ff.shape, ff.dtype),),
        in_specs=[ANY] * (m + 1), out_specs=(ANY,) * (m + 1),
        scratch_shapes=blocks + blocks + [vm((3 * part + 2 * nz * rows, t.shape[-1]), t.dtype) for t in terms]
        + [dma((m,)), dma((m,)), dma((m, 2)), dma((m, 2)), dma((m, 4)), dma((m, 4)), dma((m, 2, nz)), dma((m, 2, nz)),
           dma((3,)), dma((3,)), dma((m + 1,))],
        compiler_params=pltpu.CompilerParams(collective_id=cid, has_side_effects=True, vmem_limit_bytes=60 << 20),
        name="reduce_all",
    )(*terms, ff)


def fits(mesh):
    return mesh.shape["wide"] == CHIPS * CORES


def fast_device(
    nz,
    tokens,
    cotangent,
    lengths,
    positions,
    norm_attn,
    w_query,
    w_key,
    w_value,
    w_output,
    norm_mlp,
    w_gate,
    w_up,
    w_down,
):
    f32, bf16 = jnp.float32, jnp.bfloat16
    c, k, n = place()
    slots, width = tokens.shape
    rows = w_query.shape[0]
    query_width, key_width = w_query.shape[1], w_key.shape[1]
    cols = w_gate.shape[1] // CHIPS
    inputs = tokens.astype(f32)
    valid_rows = (jnp.arange(slots) < lengths[0]).astype(f32)[:, None]
    tables = lane_tables(positions)
    grad_y = cotangent.astype(f32) * valid_rows
    grad_y_low = grad_y.astype(bf16)
    gains = jnp.zeros((rows, 128), bf16).at[:, 0].set(norm_attn).at[:, 1].set(norm_mlp)
    chunks = (rows, w_gate.shape[1] // 128, 128)
    w_gate_up = jnp.stack([w_gate.reshape(chunks), w_up.reshape(chunks)], 2).reshape(rows, 2 * w_gate.shape[1])
    w_qkv, w_out, gain_cols, ff_gate_up, ff_down, gy_all = gather_all(
        nz, w_query, w_key, w_value, w_output, gains, w_gate_up, w_down, grad_y_low
    )
    ff_gate_up, ff_down = (w.reshape(-1, rows, w.shape[-1]) for w in (ff_gate_up, ff_down))
    gain_attn = gain_cols[:, 0].astype(f32)
    gain_mlp = gain_cols[:, 1].astype(f32)

    normed_attn = normalize(inputs)
    scaled_attn = (normed_attn * gain_attn).astype(bf16)
    qkv = jnp.dot(scaled_attn, w_qkv, preferred_element_type=f32)
    query_rotated, key_rotated, value_reduced, log_totals, context = attend_all(qkv, tables)
    hidden = inputs + lax.dot_general(context, w_out, contract_last, preferred_element_type=f32)
    normed_mlp = normalize(hidden)
    scaled_mlp = (normed_mlp * gain_mlp).astype(bf16)

    grad_x_parts, mlp_part, ff_sums = mlp_all(nz, scaled_mlp, gy_all, ff_gate_up, ff_down)
    grad_xn2 = jnp.sum(grad_x_parts.astype(f32), axis=0)
    grad_gain_mlp = jnp.sum(grad_xn2 * normed_mlp, axis=0)
    grad_hidden = grad_y + norm_back(grad_xn2 * gain_mlp, normed_mlp, hidden)
    grad_attn_low = grad_hidden.astype(bf16)
    grad_context = jnp.dot(grad_attn_low, w_out, preferred_element_type=f32).astype(bf16)
    grad_query, grad_key, grad_value, mlp_parts = attend_back_all(
        query_rotated, key_rotated, value_reduced, log_totals, grad_context, tables, mlp_part
    )
    output = (valid_rows * (hidden + jnp.sum(mlp_parts.astype(f32), axis=0))).astype(bf16)
    grad_qkv = jnp.concatenate([grad_query, grad_key.astype(bf16), grad_value.astype(bf16)], 1)
    grad_xn1 = lax.dot_general(grad_qkv, w_qkv, contract_last, preferred_element_type=f32)
    grad_gain_attn = jnp.sum(grad_xn1 * normed_attn, axis=0)
    grad_tokens = grad_hidden + norm_back(grad_xn1 * gain_attn, normed_attn, inputs)

    def over_rows(left, right):
        return lax.dot_general(left, right, contract_first, preferred_element_type=f32)

    ff_sums = lax.psum_scatter(ff_sums, "narrow", scatter_dimension=0, tiled=True)
    gain_terms = jnp.zeros((width, 128), f32).at[:, 0].set(grad_gain_attn).at[:, 1].set(grad_gain_mlp)
    grad_w_output, grad_qkv_rows, gain_sums, ff_sums = reduce_all(
        nz,
        [
            over_rows(grad_attn_low, context).astype(bf16),
            over_rows(scaled_attn, grad_qkv).astype(bf16),
            gain_terms.astype(bf16),
        ],
        ff_sums.reshape(CHIPS, rows, 3 * cols),
        3,
    )
    grad_w_down = jnp.swapaxes(ff_sums[:, :, :cols], 0, 1).reshape(rows, CHIPS * cols).astype(f32)
    grad_gate_up = jnp.swapaxes(ff_sums[:, :, cols:], 0, 1).reshape(rows, CHIPS * cols // 128, 2, 128).astype(f32)
    grad_w_gate = grad_gate_up[:, :, 0].reshape(rows, CHIPS * cols)
    grad_w_up = grad_gate_up[:, :, 1].reshape(rows, CHIPS * cols)
    grad_w_output = grad_w_output.astype(f32)
    grad_w_query = grad_qkv_rows[:, :query_width].astype(f32)
    grad_w_key = grad_qkv_rows[:, query_width : query_width + key_width].astype(f32)
    grad_w_value = grad_qkv_rows[:, query_width + key_width :].astype(f32)
    grad_norm_attn, grad_norm_mlp = gain_sums[:, 0].astype(f32), gain_sums[:, 1].astype(f32)
    return (
        output,
        grad_tokens,
        grad_norm_attn,
        grad_w_query,
        grad_w_key,
        grad_w_value,
        grad_w_output,
        grad_norm_mlp,
        grad_w_gate,
        grad_w_up,
        grad_w_down,
    )


def solution(mesh):
    in_specs = (
        P(("wide", "narrow"), None),
        P(("wide", "narrow"), None),
        P(("wide", "narrow")),
        P(("wide", "narrow")),
        P(("wide", "narrow")),
        P(("wide", "narrow"), None),
        P(("wide", "narrow"), None),
        P(("wide", "narrow"), None),
        P(("wide", "narrow"), None),
        P(("wide", "narrow")),
        P(("wide", "narrow"), None),
        P(("wide", "narrow"), None),
        P(("wide", "narrow"), None),
    )
    out_specs = (
        P(("wide", "narrow"), None),
        P(("wide", "narrow"), None),
        P(("wide", "narrow")),
        P(("wide", "narrow"), None),
        P(("wide", "narrow"), None),
        P(("wide", "narrow"), None),
        P(("wide", "narrow"), None),
        P(("wide", "narrow")),
        P(("wide", "narrow"), None),
        P(("wide", "narrow"), None),
        P(("wide", "narrow"), None),
    )
    body = functools.partial(fast_device, mesh.shape["narrow"]) if fits(mesh) else per_device
    return jax.shard_map(
        body, mesh=mesh, in_specs=in_specs, out_specs=out_specs, check_vma=False
    )
```

```python
import functools
import math

import jax
import jax.numpy as jnp
from jax import lax
from jax.experimental import pallas as pl
from jax.experimental.pallas import tpu as pltpu
from jax.sharding import PartitionSpec as P

QUERY_HEADS = 32
KEY_VALUE_HEADS = 4
HEAD_SIZE = 64


norm_eps = 1e-05
rope_base = 10000.0
masked_score = -1e30
contract_last = (((1,), (1,)), ((), ()))
contract_first = (((0,), (0,)), ((), ()))


def rope_tables(positions):
    half_dim = HEAD_SIZE // 2
    inv_freq = jnp.exp(
        -math.log(rope_base) * jnp.arange(half_dim, dtype=jnp.float32) * 2.0 / HEAD_SIZE
    )
    angles = positions.astype(jnp.float32)[..., None] * inv_freq
    cosine = jnp.cos(angles)
    sine_part = jnp.sin(angles)
    return (jnp.concatenate([cosine, cosine], -1), jnp.concatenate([sine_part, sine_part], -1))


def apply_rotary(values, cosine_table, sine_table):
    half_dim = values.shape[-1] // 2
    turned = jnp.concatenate([-values[..., half_dim:], values[..., :half_dim]], -1)
    return values * cosine_table[..., None, :] + turned * sine_table[..., None, :]


def invert_rotary(grad_rows, cosine_table, sine_table):
    half_dim = grad_rows.shape[-1] // 2
    with_cos = grad_rows * cosine_table[..., None, :]
    with_sin = grad_rows * sine_table[..., None, :]
    return with_cos + jnp.concatenate([with_sin[..., half_dim:], -with_sin[..., :half_dim]], -1)


def normalize(values):
    return values * lax.rsqrt(jnp.mean(values * values, axis=-1, keepdims=True) + norm_eps)


def norm_back(grad_hat, normed, values):
    row_scale = lax.rsqrt(jnp.mean(values * values, axis=-1, keepdims=True) + norm_eps)
    return row_scale * (grad_hat - normed * jnp.mean(grad_hat * normed, axis=-1, keepdims=True))


def attention_inputs(normed, norm_attn, w_query, w_key, w_value):
    gain_piece = lax.all_gather(norm_attn, ("wide", "narrow"), axis=0, tiled=True)
    query_rows = lax.all_gather(w_query, ("wide", "narrow"), axis=0, tiled=True)
    key_rows = lax.all_gather(w_key, ("wide", "narrow"), axis=0, tiled=True)
    value_rows = lax.all_gather(w_value, ("wide", "narrow"), axis=0, tiled=True)
    gain_float = gain_piece.astype(jnp.float32)
    columns = (normed * gain_float).astype(jnp.bfloat16)
    query_sum = jnp.dot(columns, query_rows, preferred_element_type=jnp.float32)
    key_sum = jnp.dot(columns, key_rows, preferred_element_type=jnp.float32)
    value_sum = jnp.dot(columns, value_rows, preferred_element_type=jnp.float32)
    return (gain_float, columns, query_sum, key_sum, value_sum)


def mlp_inputs(normed, norm_mlp, w_gate, w_up):
    gain_piece = lax.all_gather(norm_mlp, ("wide", "narrow"), axis=0, tiled=True)
    gate_rows = lax.all_gather(w_gate, ("wide", "narrow"), axis=0, tiled=True)
    up_rows = lax.all_gather(w_up, ("wide", "narrow"), axis=0, tiled=True)
    gain_float = gain_piece.astype(jnp.float32)
    columns = (normed * gain_float).astype(jnp.bfloat16)
    gate_sum = jnp.dot(columns, gate_rows, preferred_element_type=jnp.float32)
    up_sum = jnp.dot(columns, up_rows, preferred_element_type=jnp.float32)
    return (gain_float, columns, gate_sum, up_sum)


def head_slices(query_rotated, key_rotated, value_reduced, shared_key_head):
    row_total_count = query_rotated.shape[0]
    heads_per_group = QUERY_HEADS // KEY_VALUE_HEADS
    query_head = query_rotated[
        :,
        shared_key_head
        * heads_per_group
        * HEAD_SIZE : (shared_key_head + 1)
        * heads_per_group
        * HEAD_SIZE,
    ].reshape(row_total_count, heads_per_group, HEAD_SIZE)
    key_head = key_rotated[:, shared_key_head * HEAD_SIZE : (shared_key_head + 1) * HEAD_SIZE]
    value_head = value_reduced[:, shared_key_head * HEAD_SIZE : (shared_key_head + 1) * HEAD_SIZE]
    return (query_head, key_head, value_head)


def head_scores(query_head, key_head):
    row_total_count = query_head.shape[0]
    causal = jnp.arange(row_total_count)[:, None] >= jnp.arange(row_total_count)[None, :]
    raw_scores = jnp.einsum("qrd,kd->rqk", query_head, key_head, preferred_element_type=jnp.float32)
    return jnp.where(causal, raw_scores * HEAD_SIZE ** (-0.5), masked_score)


def attend(query_rotated, key_rotated, value_reduced):
    row_total_count = query_rotated.shape[0]
    heads_per_group = QUERY_HEADS // KEY_VALUE_HEADS
    contexts = []
    log_totals = []
    for shared_key_head in range(KEY_VALUE_HEADS):
        query_head, key_head, value_head = head_slices(
            query_rotated, key_rotated, value_reduced, shared_key_head
        )
        scores = head_scores(query_head, key_head)
        row_peak = jnp.max(scores, axis=-1, keepdims=True)
        exp_scores = jnp.exp(scores - row_peak)
        row_total = jnp.sum(exp_scores, axis=-1, keepdims=True)
        probs = exp_scores / row_total
        context_head = jnp.einsum(
            "rqk,kd->qrd",
            probs.astype(jnp.bfloat16),
            value_head,
            preferred_element_type=jnp.float32,
        )
        contexts.append(context_head.reshape(row_total_count, heads_per_group * HEAD_SIZE))
        log_totals.append(row_peak + jnp.log(row_total))
    return (jnp.concatenate(contexts, 1).astype(jnp.bfloat16), log_totals)


def attend_back(query_rotated, key_rotated, value_reduced, log_totals, grad_context):
    row_total_count = query_rotated.shape[0]
    heads_per_group = QUERY_HEADS // KEY_VALUE_HEADS
    score_scale = HEAD_SIZE ** (-0.5)
    query_grads = []
    key_grads = []
    value_grads = []
    for shared_key_head in range(KEY_VALUE_HEADS):
        query_head, key_head, value_head = head_slices(
            query_rotated, key_rotated, value_reduced, shared_key_head
        )
        scores = head_scores(query_head, key_head)
        probs = jnp.exp(scores - log_totals[shared_key_head])
        probs_low = probs.astype(jnp.bfloat16)
        grad_head = grad_context[
            :,
            shared_key_head
            * heads_per_group
            * HEAD_SIZE : (shared_key_head + 1)
            * heads_per_group
            * HEAD_SIZE,
        ].reshape(row_total_count, heads_per_group, HEAD_SIZE)
        grad_probs = jnp.einsum(
            "qrd,kd->rqk", grad_head, value_head, preferred_element_type=jnp.float32
        )
        value_grads.append(
            jnp.einsum("rqk,qrd->kd", probs_low, grad_head, preferred_element_type=jnp.float32)
        )
        inner_sum = jnp.sum(grad_probs * probs, axis=-1, keepdims=True)
        grad_scores = (probs * (grad_probs - inner_sum) * score_scale).astype(jnp.bfloat16)
        query_grad = jnp.einsum(
            "rqk,kd->qrd", grad_scores, key_head, preferred_element_type=jnp.float32
        )
        query_grads.append(query_grad.reshape(row_total_count, heads_per_group * HEAD_SIZE))
        key_grads.append(
            jnp.einsum("rqk,qrd->kd", grad_scores, query_head, preferred_element_type=jnp.float32)
        )
    return (
        jnp.concatenate(query_grads, 1),
        jnp.concatenate(key_grads, 1),
        jnp.concatenate(value_grads, 1),
    )


def make_term(width_sides, other_sides):
    down_side, mlp_side, attn_side, qkv_side = width_sides
    mixed_rows, gate_rows, up_rows, context_rows, query_rows, key_rows, value_rows = other_sides

    def grad_term(first_row, row_span):
        pieces = [
            lax.dot_general(
                down_side, mixed_rows, contract_first, preferred_element_type=jnp.float32
            ),
            lax.dot_general(
                mlp_side, gate_rows, contract_first, preferred_element_type=jnp.float32
            ),
            lax.dot_general(mlp_side, up_rows, contract_first, preferred_element_type=jnp.float32),
            lax.dot_general(
                attn_side, context_rows, contract_first, preferred_element_type=jnp.float32
            ),
            lax.dot_general(
                qkv_side, query_rows, contract_first, preferred_element_type=jnp.float32
            ),
            lax.dot_general(qkv_side, key_rows, contract_first, preferred_element_type=jnp.float32),
            lax.dot_general(
                qkv_side, value_rows, contract_first, preferred_element_type=jnp.float32
            ),
        ]
        return jnp.concatenate(pieces, 1)

    return grad_term


def per_device(
    tokens,
    cotangent,
    lengths,
    positions,
    norm_attn,
    w_query,
    w_key,
    w_value,
    w_output,
    norm_mlp,
    w_gate,
    w_up,
    w_down,
):
    row_total_count = tokens.shape[0]
    shard_rows = w_query.shape[0]
    query_width = w_query.shape[1]
    key_width = w_key.shape[1]
    hidden_width = w_gate.shape[1]
    inputs = tokens.astype(jnp.float32)
    valid_rows = (jnp.arange(row_total_count) < lengths[0]).astype(jnp.float32)[:, None]
    cosine_table, sine_table = rope_tables(positions)
    normed_attn = normalize(inputs)
    gain_attn_full, scaled_attn, query_pre, key_unrotated, value_pre = attention_inputs(
        normed_attn, norm_attn, w_query, w_key, w_value
    )
    query_rotated = (
        apply_rotary(
            query_pre.reshape(row_total_count, QUERY_HEADS, HEAD_SIZE), cosine_table, sine_table
        )
        .reshape(row_total_count, query_width)
        .astype(jnp.bfloat16)
    )
    key_rotated = (
        apply_rotary(
            key_unrotated.reshape(row_total_count, KEY_VALUE_HEADS, HEAD_SIZE),
            cosine_table,
            sine_table,
        )
        .reshape(row_total_count, key_width)
        .astype(jnp.bfloat16)
    )
    value_reduced = value_pre.astype(jnp.bfloat16)
    context, log_totals = attend(query_rotated, key_rotated, value_reduced)
    attn_out = lax.dot_general(
        context,
        lax.all_gather(w_output, ("wide", "narrow"), axis=0, tiled=True),
        contract_last,
        preferred_element_type=jnp.float32,
    )
    hidden = inputs + attn_out
    normed_mlp = normalize(hidden)
    gain_mlp_full, scaled_mlp, gate_proj, up_proj = mlp_inputs(normed_mlp, norm_mlp, w_gate, w_up)
    mixed_low = (gate_proj * jax.nn.sigmoid(gate_proj) * up_proj).astype(jnp.bfloat16)
    mlp_out = lax.dot_general(
        mixed_low,
        lax.all_gather(w_down, ("wide", "narrow"), axis=0, tiled=True),
        contract_last,
        preferred_element_type=jnp.float32,
    )
    output = (valid_rows * (hidden + mlp_out)).astype(jnp.bfloat16)
    grad_y = cotangent.astype(jnp.float32) * valid_rows
    grad_y_low = grad_y.astype(jnp.bfloat16)
    grad_cols = grad_y_low
    grad_mixed = jnp.dot(
        grad_cols,
        lax.all_gather(w_down, ("wide", "narrow"), axis=0, tiled=True),
        preferred_element_type=jnp.float32,
    )
    again_values = mlp_inputs(normed_mlp, norm_mlp, w_gate, w_up)
    gate_proj = again_values[2]
    up_proj = again_values[3]
    sigmoid_gate = jax.nn.sigmoid(gate_proj)
    grad_gate = (
        grad_mixed * up_proj * (sigmoid_gate * (1.0 + gate_proj * (1.0 - sigmoid_gate)))
    ).astype(jnp.bfloat16)
    grad_up = (grad_mixed * (gate_proj * sigmoid_gate)).astype(jnp.bfloat16)
    gate_rows = lax.all_gather(w_gate, ("wide", "narrow"), axis=0, tiled=True)
    up_rows = lax.all_gather(w_up, ("wide", "narrow"), axis=0, tiled=True)
    columns = lax.dot_general(
        grad_gate, gate_rows, contract_last, preferred_element_type=jnp.float32
    )
    columns = columns + lax.dot_general(
        grad_up, up_rows, contract_last, preferred_element_type=jnp.float32
    )
    grad_xn2 = columns
    grad_gain_mlp = jnp.sum(grad_xn2 * normed_mlp, axis=0)
    grad_hidden = grad_y + norm_back(grad_xn2 * gain_mlp_full, normed_mlp, hidden)
    grad_attn_low = grad_hidden.astype(jnp.bfloat16)
    grad_cols = grad_attn_low
    grad_context = jnp.dot(
        grad_cols,
        lax.all_gather(w_output, ("wide", "narrow"), axis=0, tiled=True),
        preferred_element_type=jnp.float32,
    )
    grad_context = grad_context.astype(jnp.bfloat16)
    grad_query_rot, gradient_key_rotated, grad_value_sum = attend_back(
        query_rotated, key_rotated, value_reduced, log_totals, grad_context
    )
    grad_query = (
        invert_rotary(
            grad_query_rot.reshape(row_total_count, QUERY_HEADS, HEAD_SIZE),
            cosine_table,
            sine_table,
        )
        .reshape(row_total_count, query_width)
        .astype(jnp.bfloat16)
    )
    grad_key = (
        invert_rotary(
            gradient_key_rotated.reshape(row_total_count, KEY_VALUE_HEADS, HEAD_SIZE),
            cosine_table,
            sine_table,
        )
        .reshape(row_total_count, key_width)
        .astype(jnp.bfloat16)
    )
    grad_value = grad_value_sum.astype(jnp.bfloat16)
    query_rows = lax.all_gather(w_query, ("wide", "narrow"), axis=0, tiled=True)
    key_rows = lax.all_gather(w_key, ("wide", "narrow"), axis=0, tiled=True)
    value_rows = lax.all_gather(w_value, ("wide", "narrow"), axis=0, tiled=True)
    columns = lax.dot_general(
        grad_query, query_rows, contract_last, preferred_element_type=jnp.float32
    )
    columns = columns + lax.dot_general(
        grad_key, key_rows, contract_last, preferred_element_type=jnp.float32
    )
    columns = columns + lax.dot_general(
        grad_value, value_rows, contract_last, preferred_element_type=jnp.float32
    )
    local_term = make_term(
        (grad_y_low, scaled_mlp, grad_attn_low, scaled_attn),
        (mixed_low, grad_gate, grad_up, context, grad_query, grad_key, grad_value),
    )
    all_sums = lax.psum_scatter(
        local_term(jnp.int32(0), lax.axis_size(("wide", "narrow")) * shard_rows),
        ("wide", "narrow"),
        scatter_dimension=0,
        tiled=True,
    )
    edges = [0]
    for width in (
        hidden_width,
        hidden_width,
        hidden_width,
        query_width,
        query_width,
        key_width,
        key_width,
    ):
        edges.append(edges[-1] + width)
    grad_w_down = all_sums[:, edges[0] : edges[1]]
    grad_w_gate = all_sums[:, edges[1] : edges[2]]
    grad_w_up = all_sums[:, edges[2] : edges[3]]
    grad_w_output = all_sums[:, edges[3] : edges[4]]
    grad_w_query = all_sums[:, edges[4] : edges[5]]
    grad_w_key = all_sums[:, edges[5] : edges[6]]
    grad_w_value = all_sums[:, edges[6] : edges[7]]
    grad_gain_attn = jnp.sum(columns * normed_attn, axis=0)
    grad_tokens = grad_hidden + norm_back(columns * gain_attn_full, normed_attn, inputs)
    grad_norm_attn, grad_norm_mlp = (
        lax.psum_scatter(grad_gain_attn, ("wide", "narrow"), scatter_dimension=0, tiled=True),
        lax.psum_scatter(grad_gain_mlp, ("wide", "narrow"), scatter_dimension=0, tiled=True),
    )
    return (
        output,
        grad_tokens,
        grad_norm_attn,
        grad_w_query,
        grad_w_key,
        grad_w_value,
        grad_w_output,
        grad_norm_mlp,
        grad_w_gate,
        grad_w_up,
        grad_w_down,
    )


MESH = pl.DeviceIdType.MESH
ANY = pl.BlockSpec(memory_space=pl.ANY)

CHIPS, CORES = 4, 2

def place():
    w = lax.axis_index("wide"); n = lax.axis_index("narrow")
    return w // CORES, w % CORES, n

def chip_at(c, r):
    xb, yb, rx, ry = c % 2, c // 2, r % 2, r // 2
    return (yb + ry - 2 * yb * ry) * 2 + (xb + rx - 2 * xb * rx)


def remote(src, dst, send, recv, chip, core, z):
    return pltpu.make_async_remote_copy(src_ref=src, dst_ref=dst, send_sem=send, recv_sem=recv,
        device_id={"wide": chip * CORES + core, "narrow": z}, device_id_type=MESH)

def hello(partners):
    barrier = pltpu.get_barrier_semaphore()
    count = 0
    for cond, chip, core, z in partners:
        def sig(chip=chip, core=core, z=z):
            pl.semaphore_signal(barrier, inc=1, device_id={"wide": chip * CORES + core, "narrow": z}, device_id_type=MESH)
        if cond is None:
            sig(); count = count + 1
        else:
            pl.when(cond)(sig); count = count + jnp.where(cond, 1, 0)
    pl.semaphore_wait(barrier, count)

class Line:
    def __init__(self, nz, at, refs, send, recv, place_of):
        self.nz, self.at, self.refs, self.send, self.recv, self.place_of = nz, at, refs, send, recv, place_of

    def _copy(self, a, way, s, origin):
        c, k, n = self.at
        ref = self.place_of(self.refs[a], origin)
        return remote(ref, ref, self.send.at[a, way, s], self.recv.at[a, way, s], c, k, n + 1 if way == 0 else n - 1)

    def _origin(self, way, s):
        n = self.at[2]
        o = n - s if way == 0 else n + s
        return (n >= s) if way == 0 else (n + s <= self.nz - 1), jnp.clip(o, 0, self.nz - 1)

    def _sends(self, way, s):
        n = self.at[2]
        return self._origin(way, s)[0] & ((n < self.nz - 1) if way == 0 else (n > 0))

    def start(self, a, s, way):
        @pl.when(self._sends(way, s))
        def _(): self._copy(a, way, s, self._origin(way, s)[1]).start()

    def step(self, a, s, then=None):
        for way in range(2):
            came, origin = self._origin(way, s)
            @pl.when(came)
            def _(): self._copy(a, way, s - 1, origin).wait_recv()
            if s < self.nz - 1: self.start(a, s, way)
            if then is not None:
                @pl.when(came)
                def _(): then(origin)

    def finish(self, a):
        for s in range(self.nz - 1):
            for way in range(2):
                @pl.when(self._sends(way, s))
                def _(): self._copy(a, way, s, self._origin(way, s)[1]).wait_send()


def gather_kernel(nz, wq, wk, wv, wo, gains, wg, wu, wd, qkv, out, gain, gu, gd,
                  loc, sw_s, sw_r, z_s, z_r, f_s, f_r, p_s, p_r, h_s, h_r, d_s, d_r, e_s, e_r):
    c, k, n = at = place()
    rows, q = wq.shape
    kv = wk.shape[1]
    cols = gd.shape[-1]
    part = nz * rows
    half = part // 2
    kn = k * nz + n
    cx, cy, cd = (chip_at(c, r) for r in (1, 2, 3))
    hello([(None, cc, k, n) for cc in (cx, cy, cd)] + [(None, c, 1 - k, n), (n > 0, c, k, n - 1), (n < nz - 1, c, k, n + 1)])

    def mycols(w, cc): return w.at[:, pl.ds(pl.multiple_of(cc * cols, 128), cols)]
    def landing(i, cc): return gd.at[cc] if i == 2 else gu.at[cc, kn, :, pl.ds(i * cols, cols)]
    whole = (qkv, out, gain)
    def block(ref, z): return ref.at[pl.ds(pl.multiple_of(((c * CORES + k) * nz + z) * rows, rows), rows)]
    own = [pltpu.make_async_copy(wq, block(qkv, n).at[:, pl.ds(0, q)], loc.at[0]),
           pltpu.make_async_copy(wk, block(qkv, n).at[:, pl.ds(q, kv)], loc.at[1]),
           pltpu.make_async_copy(wv, block(qkv, n).at[:, pl.ds(q + kv, kv)], loc.at[2]),
           pltpu.make_async_copy(wo, block(out, n), loc.at[3]), pltpu.make_async_copy(gains, block(gain, n), loc.at[4])]
    ownff = [pltpu.make_async_copy(mycols(w, c), landing(i, c), loc.at[5 + i]) for i, w in enumerate((wg, wu, wd))]
    for cp in own + ownff: cp.start()
    swap = [[remote(mycols(w, cc), landing(i, c), sw_s.at[i, r], sw_r.at[i, r], cc, k, n) for r, cc in enumerate((cx, cy, cd))]
            for i, w in enumerate((wg, wu, wd))]
    for i in range(3):
        for cp in swap[i]: cp.start()
    for cp in own: cp.wait()

    line = Line(nz, at, whole, z_s, z_r, block)
    for a in range(3):
        for way in range(2): line.start(a, 0, way)

    def span(ref, cc, first, size):
        return ref.at[pl.ds(pl.multiple_of((cc * CORES + k) * part, part) + first, size)]
    plane = [[remote(span(ref, c, 0, part), span(ref, c, 0, part), p_s.at[a, r], p_r.at[a, r], cc, k, n) for r, cc in enumerate((cx, cy))]
             for a, ref in enumerate(whole)]
    across = [[remote(span(ref, cx, 0, half), span(ref, cx, 0, half), h_s.at[a, 0], h_r.at[a, 0], cy, k, n),
               remote(span(ref, cy, half, half), span(ref, cy, half, half), h_s.at[a, 1], h_r.at[a, 1], cx, k, n)]
              for a, ref in enumerate(whole)]
    cores = [[remote(span(ref, cc, 0, part), span(ref, cc, 0, part), d_s.at[a, r], d_r.at[a, r], c, 1 - k, n)
              for r, cc in enumerate((c, cx, cy, cd))] for a, ref in enumerate(whole)]

    def plane_start(a):
        for cp in plane[a] + cores[a][:1]: cp.start()
    def plane_next(a):
        for i in range(2):
            plane[a][i].wait_recv()
            across[a][i].start()
            cores[a][1 + i].start()
    def plane_last(a):
        for cp in across[a]: cp.wait_recv()
        cores[a][3].start()

    for s in range(1, nz):
        for a in range(3):
            line.step(a, s)
            if s == nz - 1: plane_start(a)

    ff = Line(nz, at, (gu,), f_s, f_r, lambda ref, z: ref.at[:, k * nz + z])
    def twin(z):
        ref = gu.at[:, k * nz + z]
        return remote(ref, ref, e_s.at[z], e_r.at[z], c, 1 - k, n)
    for i in range(2):
        ownff[i].wait()
        for cp in swap[i]: cp.wait_recv()
    for way in range(2): ff.start(0, 0, way)
    twin(n).start()
    plane_next(0)
    ff.step(0, 1, lambda z: twin(z).start())
    for a in (1, 2): plane_next(a)
    ff.step(0, 2, lambda z: twin(z).start())
    for a in range(3): plane_last(a)
    ownff[2].wait()
    for cp in swap[2]: cp.wait_recv()
    for s in range(3, nz): ff.step(0, s, lambda z: twin(z).start())
    for a in range(3):
        for cp in cores[a]: cp.wait_recv()
    for z in range(nz): twin(z).wait()
    for i in range(3):
        for cp in swap[i]: cp.wait_send()
    for a in range(3):
        line.finish(a)
        for cp in plane[a] + across[a] + cores[a]: cp.wait_send()
    ff.finish(0)


def gather_all(nz, wq, wk, wv, wo, gains, wg, wu, wd):
    rows = wq.shape[0]
    width = rows * CHIPS * CORES * nz
    cols = wg.shape[1] // CHIPS
    bf = jnp.bfloat16
    shape = jax.ShapeDtypeStruct
    dma = pltpu.SemaphoreType.DMA
    return pl.pallas_call(
        functools.partial(gather_kernel, nz),
        out_shape=(shape((width, wq.shape[1] + 2 * wk.shape[1]), bf), shape((width, wo.shape[1]), bf), shape((width, gains.shape[1]), bf),
                   shape((CHIPS, CORES * nz, rows, 2 * cols), bf), shape((CHIPS, rows, cols), bf)),
        in_specs=[ANY] * 8, out_specs=(ANY,) * 5,
        scratch_shapes=[dma((8,)), dma((3, 3)), dma((3, 3)), dma((3, 2, nz)), dma((3, 2, nz)), dma((1, 2, nz)), dma((1, 2, nz)),
                        dma((3, 2)), dma((3, 2)), dma((3, 2)), dma((3, 2)), dma((3, 4)), dma((3, 4)), dma((nz,)), dma((nz,))],
        compiler_params=pltpu.CompilerParams(collective_id=0, has_side_effects=True),
        name="gather_all",
    )(wq, wk, wv, wo, gains, wg, wu, wd)


HALVES = ((0, 0), (0, 1), (1, 0), (2, 0), (1, 1), (2, 1), (3, 0), (3, 1))


def mlp_kernel(nz, x, gy, gu_hbm, gd_hbm, gx_parts, mlp_parts, mlp_cross, sums,
               xs, gys, gu, gd, mix, ggu, gx, mo, xt, load, ag_s, ag_r, rs_s, rs_r, mo_s, mo_r, out, core_s, core_r, ready, done):
    c, k, n = place()
    f32, bf16 = jnp.float32, jnp.bfloat16
    slots, width = x.shape
    half = slots // 2
    rows, cols = gd.shape[1:]
    per_tile = nz
    tile = nz * rows
    hello([(None, chip_at(c, r), k, n) for r in (1, 2, 3)] + [(None, c, 1 - k, n)])
    def half_of(ref, h): return ref.at[pl.ds(h * half, half)]
    index = {place_: i for i, place_ in enumerate(HALVES)}
    sends = {}
    for h in range(2):
        for r in (1, 2):
            i = index[r, h]
            sends[i] = remote(half_of(x, h), xs.at[i], ag_s.at[i], ag_r.at[i], chip_at(c, r), k, n)
            sends[i].start()
    loads = [pltpu.make_async_copy(half_of(x, h), xs.at[h], load.at[h]) for h in range(2)]
    loads += [pltpu.make_async_copy(half_of(gy.at[r], h), gys.at[i], load.at[2 + i]) for i, (r, h) in enumerate(HALVES)]
    for cp in loads: cp.start()
    def weights(col, w, j):
        return [pltpu.make_async_copy(a.at[:, :, pl.ds(first + col, w)], b.at[:, :, pl.ds(first + col, w)], load.at[10 + 3 * j + i])
                for i, (a, b, first) in enumerate(((gu_hbm, gu, 0), (gu_hbm, gu, cols), (gd_hbm, gd, 0)))]
    for j in range(-(-cols // 256)):
        for cp in weights(j * 256, min(256, cols - j * 256), j): cp.start()
    relays = {index[3, 0]: (index[1, 0], 2), index[3, 1]: (index[2, 1], 1)}
    relays = {i: remote(xs.at[j], xs.at[i], ag_s.at[i], ag_r.at[i], chip_at(c, r), k, n) for i, (j, r) in relays.items()}
    for cp in loads: cp.wait()

    def columns(ref, at, size):
        t = ref[:, :, pl.ds(at, size)]
        return t.reshape(t.shape[0] * t.shape[1], size)

    def some_rows(ref, i):
        t = ref[pl.ds(i * (256 // rows), 256 // rows)]
        return t.reshape(256, t.shape[2])

    def to_owner(src, dst, i, s_s, s_r):
        r, h = HALVES[i]
        return remote(src.at[i], half_of(dst.at[r], h), s_s.at[i], s_r.at[i], chip_at(c, r), k, n)

    def kept(src, dst, i, j):
        return pltpu.make_async_copy(src.at[i], half_of(dst, HALVES[i][1]), out.at[j])

    def block(r, carry):
        two = pl.ds(2 * r, 2)
        for t in (1, 2):
            @pl.when(r == t)
            def _():
                for i in (2 * t, 2 * t + 1): sends[i].wait_recv()
                relays[{1: index[3, 0], 2: index[3, 1]}[t]].start()
        @pl.when(r == 3)
        def _():
            for cp in relays.values(): cp.wait_recv()
        def both(ref): return ref[two].reshape(slots, ref.shape[2])
        def put(ref, at, v): ref[two, :, at] = v.astype(bf16).reshape(2, half, v.shape[1])
        def chunk(col, w, j):
            @pl.when(r == 0)
            def _():
                for cp in weights(col, w, j): cp.wait()
            tokens = both(xs)
            hg = jnp.dot(tokens, columns(gu, col, w), preferred_element_type=f32)
            hu = jnp.dot(tokens, columns(gu, cols + col, w), preferred_element_type=f32)
            gm = jnp.dot(both(gys), columns(gd, col, w), preferred_element_type=f32)
            for q in range(w // 128):
                gate, up, g = (t[:, 128 * q : 128 * q + 128] for t in (hg, hu, gm))
                sg = 1.0 / (1.0 + jnp.exp(-gate))
                act = gate * sg
                put(mix, pl.ds(col + 128 * q, 128), act * up)
                put(ggu, pl.ds(col + 128 * q, 128), g * up * (sg * (1.0 + gate * (1.0 - sg))))
                put(ggu, pl.ds(cols + col + 128 * q, 128), g * act)
        def pair(j, carry):
            chunk(pl.multiple_of(j * 256, 256), 256, j)
            return carry
        lax.fori_loop(0, cols // 256, pair, 0)
        if cols % 256: chunk(cols // 256 * 256, cols % 256, cols // 256)
        def back(i, carry):
            at = pl.ds(pl.multiple_of(i * 256, 256), 256)
            put(gx, at, lax.dot_general(both(ggu), some_rows(gu, i), contract_last, preferred_element_type=f32))
            return carry
        lax.fori_loop(0, width // 256, back, 0)
        for t in range(CHIPS):
            @pl.when(r == t)
            def _():
                for i in (2 * t, 2 * t + 1):
                    (to_owner(gx, gx_parts, i, rs_s, rs_r) if t else kept(gx, gx_parts.at[0], i, i)).start()
        def down(i, carry):
            at = pl.ds(pl.multiple_of(i * 256, 256), 256)
            put(mo, at, lax.dot_general(both(mix), some_rows(gd, i), contract_last, preferred_element_type=f32))
            return carry
        lax.fori_loop(0, width // 256, down, 0)
        for t in range(CHIPS):
            @pl.when(r == t)
            def _():
                for i in (2 * t, 2 * t + 1):
                    (kept(mo, mlp_parts.at[0], i, 2 + i) if t == 0 else kept(mo, mlp_cross, i, i - 2) if t == 3
                     else to_owner(mo, mlp_parts, i, mo_s, mo_r)).start()
        return carry
    lax.fori_loop(0, CHIPS, block, 0)

    pl.semaphore_signal(ready, inc=1, device_id={"wide": c * CORES + 1 - k, "narrow": n}, device_id_type=MESH)
    pl.semaphore_wait(ready, 1)
    sent, came = pl.ds(0, CHIPS * nz), pl.ds(CHIPS * nz, CHIPS * nz)
    pairs = ((gys, mix, gd), (xs, ggu, gu))

    def tiles(total): return [(t * 256, min(256, total - t * 256)) for t in range(-(-total // 256))]

    def to_core(i, col, w, sem):
        ref = pairs[i][2]
        return remote(ref.at[sent, :, pl.ds(col, w)], ref.at[came, :, pl.ds(col, w)], core_s.at[sem], core_r.at[sem], c, 1 - k, n)

    def to_sums(i, t, sem):
        ref = pairs[i][2]
        return pltpu.make_async_copy(ref.at[pl.ds(CHIPS * nz + t * nz, nz)], sums.at[:, t, :, pl.ds(i * cols, ref.shape[-1])], done.at[sem])

    def each(i, body):
        total, base = pairs[i][2].shape[-1], 0 if i == 0 else len(tiles(cols))
        def step(j, carry):
            body(pl.multiple_of(j * 256, 256), 256, base + j)
            return carry
        lax.fori_loop(0, total // 256, step, 0)
        if total % 256: body(total // 256 * 256, total % 256, base + total // 256)

    def terms(i, kk, use):
        src, right, ref = pairs[i]
        for t in range(CHIPS):
            at = pl.ds(pl.multiple_of((t * CORES + kk) * tile, 128), tile)
            for r in range(CHIPS):
                xt[t * tile : (t + 1) * tile, r * slots : (r + 1) * slots] = src[2 * r : 2 * r + 2, :, at].reshape(slots, tile).T
        def body(col, w, sem):
            b = right[:, :, pl.ds(col, w)].reshape(CHIPS * slots, w)
            use(i, col, w, sem, jnp.dot(xt[...], b, preferred_element_type=f32).reshape(CHIPS * nz, rows, w))
        each(i, body)

    def theirs(i, col, w, sem, v):
        pairs[i][2][sent, :, pl.ds(col, w)] = v.astype(bf16)
        to_core(i, col, w, sem).start()

    def ours(i, col, w, sem, v):
        to_core(i, col, w, sem).wait_recv()
        ref = pairs[i][2]
        here = (came, slice(None), pl.ds(col, w))
        ref[here] = (ref[here].astype(f32) + v).astype(bf16)

    for i in range(2): terms(i, 1 - k, theirs)
    for i in range(2):
        terms(i, k, ours)
        for t in range(CHIPS): to_sums(i, t, i * CHIPS + t).start()

    for cp in (*sends.values(), *relays.values()): cp.wait_send()
    for i in range(2):
        kept(gx, gx_parts.at[0], i, i).wait()
        kept(mo, mlp_parts.at[0], i, 2 + i).wait()
        kept(mo, mlp_cross, 6 + i, 4 + i).wait()
    for i in range(2):
        each(i, lambda col, w, sem: to_core(i, col, w, sem).wait_send())
        for t in range(CHIPS): to_sums(i, t, i * CHIPS + t).wait()
    for i in range(2, 6): to_owner(mo, mlp_parts, i, mo_s, mo_r).wait()
    for i in range(2, 8): to_owner(gx, gx_parts, i, rs_s, rs_r).wait()


def mlp_all(nz, x, gy, gu, gd):
    slots, width = x.shape
    rows, cols = gd.shape[1:]
    bf, dma, vm = jnp.bfloat16, pltpu.SemaphoreType.DMA, pltpu.VMEM
    def blocks(w): return jax.ShapeDtypeStruct((CHIPS, slots, w), bf)
    def halves(w): return vm((2 * CHIPS, slots // 2, w), bf)
    tiles = -(-cols // 256)
    flops = 2 * 9 * CHIPS * slots * width * cols
    return pl.pallas_call(
        functools.partial(mlp_kernel, nz),
        out_shape=(blocks(width), jax.ShapeDtypeStruct((3, slots, width), bf), jax.ShapeDtypeStruct((slots, width), bf), jax.ShapeDtypeStruct((nz, CHIPS, rows, 3 * cols), bf)),
        in_specs=[ANY] * 4, out_specs=(ANY,) * 4,
        scratch_shapes=[halves(width), halves(width), vm(gu.shape, bf), vm(gd.shape, bf), halves(cols), halves(2 * cols), halves(width),
                        halves(width), vm((CHIPS * nz * rows, CHIPS * slots), bf), dma((10 + 3 * tiles,)), dma((8,)), dma((8,)), dma((8,)), dma((8,)),
                        dma((8,)), dma((8,)), dma((6,)), dma((3 * tiles,)), dma((3 * tiles,)), pltpu.SemaphoreType.REGULAR, dma((8,))],
        compiler_params=pltpu.CompilerParams(collective_id=1, has_side_effects=True, vmem_limit_bytes=62 << 20),
        cost_estimate=pl.CostEstimate(flops=flops, bytes_accessed=60 << 20, transcendentals=CHIPS * slots * cols),
        name="mlp_all",
    )(x, gy, gu, gd)


PAIR = 2 * HEAD_SIZE
REPEAT = QUERY_HEADS // KEY_VALUE_HEADS
PAIRS = REPEAT // 2


def lane_tables(positions):
    cosine, sine = rope_tables(positions)
    first = jnp.arange(HEAD_SIZE) < HEAD_SIZE // 2
    low, high = jnp.where(first, -sine, 0.0), jnp.where(first, 0.0, sine)
    return jnp.stack([jnp.concatenate([t, t], 1) for t in (cosine, low, high)])


def rotate(u, tables):
    half = HEAD_SIZE // 2
    return u * tables[0] + pltpu.roll(u, PAIR - half, 1) * tables[1] + pltpu.roll(u, half, 1) * tables[2]


def unrotate(g, tables):
    half = HEAD_SIZE // 2
    return g * tables[0] + pltpu.roll(g * tables[2], PAIR - half, 1) + pltpu.roll(g * tables[1], half, 1)


def row_blocks(slots):
    return [(at, min(128, slots - at), at + 128) for at in range(0, slots, 128)]


def causal(s, below, fill):
    clear = s.shape[1] - 128
    last = jnp.where(below, s[:, clear:], fill)
    return jnp.concatenate([s[:, :clear], last], 1) if clear else last


def attend_kernel(nz, q_ref, k_ref, v_ref, tab_ref, gy, gd_own, qr_ref, k_out, v_out, lse_ref, ctx_ref, gys, gd, ks, vs,
                  loc, g_s, g_r, h_s, h_r, f_s, f_r, e_s, e_r):
    g = pl.program_id(0)
    f32, bf16 = jnp.float32, jnp.bfloat16
    slots = q_ref.shape[0]
    c, k, n = at = place()
    mine = [pltpu.make_async_copy(gd_own, gd.at[:, k * nz + n], loc.at[0]), pltpu.make_async_copy(gy, gys.at[0], loc.at[1])]
    line = Line(nz, at, (gd,), f_s, f_r, lambda ref, z: ref.at[:, k * nz + z])
    half = slots // 2
    sends = [remote(gy, gys.at[r], g_s.at[r], g_r.at[r], chip_at(c, r), k, n) for r in (1, 2)]
    relays = [remote(gys.at[1, pl.ds(0, half)], gys.at[3, pl.ds(0, half)], h_s.at[0], h_r.at[0], chip_at(c, 2), k, n),
              remote(gys.at[2, pl.ds(half, half)], gys.at[3, pl.ds(half, half)], h_s.at[1], h_r.at[1], chip_at(c, 1), k, n)]
    def twin(z):
        ref = gd.at[:, k * nz + z]
        return remote(ref, ref, e_s.at[z], e_r.at[z], c, 1 - k, n)
    @pl.when(g == 0)
    def _():
        hello([(None, chip_at(c, r), k, n) for r in (1, 2)]
              + [(None, c, 1 - k, n), (n > 0, c, k, n - 1), (n < nz - 1, c, k, n + 1)])
        for cp in mine + sends: cp.start()
        mine[0].wait()
        for way in range(2): line.start(0, 0, way)
        twin(n).start()
    @pl.when(g == KEY_VALUE_HEADS - 1)
    def _():
        line.step(0, 1, lambda z: twin(z).start())
    @pl.when(g == 0)
    def _():
        ks[...] = jnp.zeros_like(ks)
        vs[...] = jnp.zeros_like(vs)
    lane = lax.broadcasted_iota(jnp.int32, (slots, PAIR), 1)
    tables = (tab_ref[0], tab_ref[1], tab_ref[2])
    key, val = rotate(k_ref[...], tables), v_ref[...]
    odd = g % 2 == 1
    for x, own, stack, scale in ((key, k_out, ks, HEAD_SIZE ** -0.5), (val, v_out, vs, 1.0)):
        x = jnp.where(lane < HEAD_SIZE, jnp.where(odd, pltpu.roll(x, HEAD_SIZE, 1), x), 0.0).astype(bf16)
        own[0] = x
        x = x.astype(f32) * scale
        stack[0, 0:slots, :] = x.astype(bf16)
        stack[1, 0:slots, :] = pltpu.roll(x, HEAD_SIZE, 1).astype(bf16)
    for start, size, keys in row_blocks(slots):
        below = lax.broadcasted_iota(jnp.int32, (size, 128), 0) >= lax.broadcasted_iota(jnp.int32, (size, 128), 1)
        lse = jnp.zeros((size, PAIR), f32)
        here = lane[0:size]
        for p in range(PAIRS):
            span = slice(p * PAIR, (p + 1) * PAIR)
            rows = slice(start, start + size)
            q = rotate(q_ref[rows, span], tuple(t[rows] for t in tables)).astype(bf16)
            qr_ref[rows, span] = q
            ctx = jnp.zeros((size, PAIR), f32)
            for h in range(2):
                s = lax.dot_general(q, ks[h, 0:keys, :], contract_last, preferred_element_type=f32)
                s = causal(s, below, masked_score)
                peak = jnp.max(s, axis=-1, keepdims=True)
                e = jnp.exp(s - peak)
                total = jnp.sum(e, axis=-1, keepdims=True)
                lse = jnp.where(here == 2 * p + h, peak + jnp.log(total), lse)
                probs = (e * (1.0 / total)).astype(bf16)
                ctx = ctx + jnp.dot(probs, vs[h, 0:keys, :], preferred_element_type=f32)
            ctx_ref[rows, span] = ctx.astype(bf16)
        lse_ref[0, start : start + size, :] = lse
    @pl.when(g == KEY_VALUE_HEADS - 1)
    def _():
        for cp in sends: cp.wait_recv()
        for cp in relays: cp.start()
        for s in range(2, nz): line.step(0, s, lambda z: twin(z).start())
        for cp in relays: cp.wait()
        for z in range(nz): twin(z).wait()
        for cp in sends: cp.wait_send()
        mine[1].wait()
        line.finish(0)


def attend_all(nz, qkv, tables, gy, gd_own):
    slots = qkv.shape[0]
    wide = REPEAT * HEAD_SIZE
    dma = pltpu.SemaphoreType.DMA
    first = QUERY_HEADS * HEAD_SIZE // PAIR
    bf16 = jnp.bfloat16
    keys = -(-slots // 128) * 128
    shape = jax.ShapeDtypeStruct
    per_head = pl.BlockSpec((1, slots, PAIR), lambda g: (g, 0, 0))
    wide_spec = pl.BlockSpec((slots, wide), lambda g: (0, g))
    return pl.pallas_call(
        functools.partial(attend_kernel, nz),
        grid=(KEY_VALUE_HEADS,),
        out_shape=(shape((slots, QUERY_HEADS * HEAD_SIZE), bf16), shape((KEY_VALUE_HEADS, slots, PAIR), bf16),
                   shape((KEY_VALUE_HEADS, slots, PAIR), bf16), shape((KEY_VALUE_HEADS, slots, PAIR), jnp.float32),
                   shape((slots, QUERY_HEADS * HEAD_SIZE), bf16), shape((CHIPS,) + gy.shape, bf16),
                   shape((CHIPS, CORES * nz) + gd_own.shape[1:], bf16)),
        in_specs=[wide_spec, pl.BlockSpec((slots, PAIR), lambda g: (0, first + g // 2)),
                  pl.BlockSpec((slots, PAIR), lambda g: (0, first + KEY_VALUE_HEADS // 2 + g // 2)),
                  pl.BlockSpec((3, slots, PAIR), lambda g: (0, 0, 0)), ANY, ANY],
        out_specs=(wide_spec, per_head, per_head, per_head, wide_spec, ANY, ANY),
        scratch_shapes=[pltpu.VMEM((2, keys, PAIR), bf16), pltpu.VMEM((2, keys, PAIR), bf16),
                        dma((2,)), dma((3,)), dma((3,)), dma((2,)), dma((2,)), dma((1, 2, nz)), dma((1, 2, nz)), dma((nz,)), dma((nz,))],
        compiler_params=pltpu.CompilerParams(collective_id=4, has_side_effects=True, vmem_limit_bytes=32 << 20),
        name="attend",
    )(qkv, qkv, qkv, tables, gy, gd_own)


def attend_back_kernel(q_ref, k_ref, v_ref, lse_ref, gc_ref, tab_ref, part, gq_ref, gk_ref, gv_ref, crossed,
                       ks, kt, vt, ds, pr, qs, gs, s_s, s_r):
    g = pl.program_id(0)
    c, k, n = place()
    copy = remote(part, crossed, s_s, s_r, chip_at(c, 3), k, n)
    @pl.when(g == 0)
    def _():
        hello([(None, chip_at(c, 3), k, n)])
        copy.start()
    f32, bf16 = jnp.float32, jnp.bfloat16
    slots = q_ref.shape[0]
    scale = HEAD_SIZE ** -0.5
    @pl.when(g == 0)
    def _():
        for ref in (ks, kt, vt, ds, pr): ref[...] = jnp.zeros_like(ref)
    lane = lax.broadcasted_iota(jnp.int32, (slots, PAIR), 1)
    tables = (tab_ref[0], tab_ref[1], tab_ref[2])
    key, val = k_ref[0].astype(f32), v_ref[0].astype(f32)
    for stack, x in ((ks, key * scale), (kt, key), (vt, val)):
        stack[0, 0:slots, :] = x.astype(bf16)
        stack[1, 0:slots, :] = pltpu.roll(x, HEAD_SIZE, 1).astype(bf16)
    for at, size, keys in row_blocks(slots):
        rows = slice(at, at + size)
        below = lax.broadcasted_iota(jnp.int32, (size, 128), 0) >= lax.broadcasted_iota(jnp.int32, (size, 128), 1)
        lse = lse_ref[0, rows, :]
        for p in range(PAIRS):
            span = slice(p * PAIR, (p + 1) * PAIR)
            deep = slice(p * slots + at, p * slots + at + size)
            q, gc = q_ref[rows, span], gc_ref[rows, span]
            qs[deep, :] = q
            gs[deep, :] = gc
            gq = jnp.zeros((size, PAIR), f32)
            for h in range(2):
                s = lax.dot_general(q, ks[h, 0:keys, :], contract_last, preferred_element_type=f32)
                e = jnp.exp(s - lse[:, 2 * p + h : 2 * p + h + 1])
                probs = causal(e, below, 0.0)
                pr[h, deep, 0:keys] = probs.astype(bf16)
                gp = lax.dot_general(gc, vt[h, 0:keys, :], contract_last, preferred_element_type=f32)
                inner = jnp.sum(gp * probs, axis=-1, keepdims=True)
                grad = (probs * (gp - inner) * scale).astype(bf16)
                ds[h, deep, 0:keys] = grad
                gq = gq + jnp.dot(grad, kt[h, 0:keys, :], preferred_element_type=f32)
            gq_ref[rows, span] = unrotate(gq, tuple(t[rows] for t in tables)).astype(bf16)
    for src, right, out, turn in ((ds, qs, gk_ref, True), (pr, gs, gv_ref, False)):
        lo, hi = (
            lax.dot_general(src[h], right[...], contract_first, preferred_element_type=f32)[0:slots] for h in range(2)
        )
        x = jnp.where(lane < HEAD_SIZE, lo + pltpu.roll(hi, HEAD_SIZE, 1), 0.0)
        if turn: x = unrotate(x, tables)
        @pl.when(g % 2 == 0)
        def _(): out[...] = x
        @pl.when(g % 2 == 1)
        def _(): out[...] = jnp.where(lane < HEAD_SIZE, out[...], pltpu.roll(x, HEAD_SIZE, 1))
    @pl.when(g == KEY_VALUE_HEADS - 1)
    def _(): copy.wait()


def attend_back_all(q, k, v, lse, grad_context, tables, part):
    slots = q.shape[0]
    wide = REPEAT * HEAD_SIZE
    bf16, f32, vm = jnp.bfloat16, jnp.float32, pltpu.VMEM
    keys = -(-slots // 128) * 128
    shape = jax.ShapeDtypeStruct
    per_head = pl.BlockSpec((1, slots, PAIR), lambda g: (g, 0, 0))
    wide_spec = pl.BlockSpec((slots, wide), lambda g: (0, g))
    two = pl.BlockSpec((slots, PAIR), lambda g: (0, g // 2))
    return pl.pallas_call(
        attend_back_kernel,
        grid=(KEY_VALUE_HEADS,),
        out_shape=(shape((slots, QUERY_HEADS * HEAD_SIZE), bf16), shape((slots, KEY_VALUE_HEADS * HEAD_SIZE), f32),
                   shape((slots, KEY_VALUE_HEADS * HEAD_SIZE), f32), shape(part.shape, part.dtype)),
        in_specs=[wide_spec, per_head, per_head, per_head, wide_spec, pl.BlockSpec((3, slots, PAIR), lambda g: (0, 0, 0)), ANY],
        out_specs=(wide_spec, two, two, ANY),
        scratch_shapes=[vm((2, keys, PAIR), bf16)] * 3 + [vm((2, PAIRS * slots, keys), bf16)] * 2 + [vm((PAIRS * slots, PAIR), bf16)] * 2
        + [pltpu.SemaphoreType.DMA] * 2,
        compiler_params=pltpu.CompilerParams(collective_id=2, has_side_effects=True, vmem_limit_bytes=40 << 20),
        name="attend_back",
    )(q, k, v, lse, grad_context, tables, part)


def add_into(dst, *srcs):
    rows = dst.shape[0]
    step = 16
    def body(i, carry):
        at = pl.ds(pl.multiple_of(i * step, step), step)
        total = dst[at, :].astype(jnp.float32)
        for s in srcs: total = total + s[at, :].astype(jnp.float32)
        dst[at, :] = total.astype(dst.dtype)
        return carry
    lax.fori_loop(0, rows // step, body, 0)


def reduce_kernel(nz, items, *refs):
    terms, outs, bufs = refs[:items], refs[items : 2 * items], refs[2 * items :]
    took, away, zbuf = bufs[:items], bufs[items : 2 * items], bufs[2 * items : 3 * items]
    core_s, core_r, half_s, half_r, main_s, main_r, z_s, z_r, loc = bufs[3 * items :]
    c, k, n = place()
    left, right = n > 0, n < nz - 1
    cx, cy, cd = (chip_at(c, r) for r in (1, 2, 3))
    hello([(None, cc, k, n) for cc in (cx, cy, cd)] + [(None, c, 1 - k, n), (left, c, k, n - 1), (right, c, k, n + 1)])
    rows = outs[0].shape[0]
    part = nz * rows
    half = part // 2
    top, low = pl.ds(0, half), pl.ds(half, half)
    def arrive(a, at, size): return zbuf[a].at[pl.ds(at, size)]
    own = [pltpu.make_async_copy(terms[a].at[:, k], away[a], loc.at[a]) for a in range(items)]
    swap = [remote(terms[a].at[:, 1 - k], took[a], core_s.at[a], core_r.at[a], c, 1 - k, n) for a in range(items)]
    for cp in own + swap: cp.start()
    cross = [[remote(away[a].at[cd, top], arrive(a, 2 * part, half), half_s.at[a, 0], half_r.at[a, 0], cx, k, n),
              remote(away[a].at[cd, low], arrive(a, 2 * part + half, half), half_s.at[a, 1], half_r.at[a, 1], cy, k, n)]
             for a in range(items)]
    main = [[remote(away[a].at[cx, top], arrive(a, 0, half), main_s.at[a, 0], main_r.at[a, 0], cx, k, n),
             remote(away[a].at[cy, low], arrive(a, part + half, half), main_s.at[a, 1], main_r.at[a, 1], cy, k, n),
             remote(away[a].at[cx, low], arrive(a, half, half), main_s.at[a, 2], main_r.at[a, 2], cx, k, n),
             remote(away[a].at[cy, top], arrive(a, part, half), main_s.at[a, 3], main_r.at[a, 3], cy, k, n)]
            for a in range(items)]

    def cores(a):
        own[a].wait()
        swap[a].wait_recv()
        add_into(away[a].at[cd], took[a].at[cd])
        for cp in cross[a]: cp.start()
        for cc in (cx, cy, c): add_into(away[a].at[cc], took[a].at[cc])

    def relay(a):
        cross[a][0].wait_recv()
        add_into(away[a].at[cy, top], arrive(a, 2 * part, half))
        main[a][3].start()
        cross[a][1].wait_recv()
        add_into(away[a].at[cx, low], arrive(a, 2 * part + half, half))
        for i in (2, 0, 1): main[a][i].start()

    def mine(a):
        for cp in main[a]: cp.wait_recv()
        add_into(away[a].at[c], arrive(a, 0, part), arrive(a, part, part))

    def slot(a, way, j): return arrive(a, pl.multiple_of(2 * part + 2 * half + (way * nz + j) * rows, rows), rows)
    def piece(a, j): return away[a].at[c, pl.ds(pl.multiple_of(j * rows, rows), rows)]
    def hop(a, way, j):
        return remote(piece(a, j), slot(a, way, j), z_s.at[a, way, j], z_r.at[a, way, j], c, k, n + 1 if way == 0 else n - 1)

    def along(some):
        for t in range(nz):
            for way in range(2):
                hops = n if way == 0 else nz - 1 - n
                j = jnp.clip(n + nz - 1 - t if way == 0 else t - hops, 0, nz - 1)
                for a in some:
                    @pl.when((hops > 0) & (t >= hops))
                    def _():
                        hop(a, way, j).wait_recv()
                        add_into(piece(a, j), slot(a, way, j))
                    @pl.when((t >= hops) & (j != n))
                    def _(): hop(a, way, j).start()
        done = [pltpu.make_async_copy(piece(a, n), outs[a], loc.at[a]) for a in some]
        for cp in done: cp.start()
        return done

    stores = []
    for a in range(items): cores(a)
    for a in range(items): relay(a)
    mine(0)
    stores += along([0])
    for a in range(1, items): mine(a)
    stores += along(list(range(1, items)))
    for cp in stores: cp.wait()
    for a in range(items):
        swap[a].wait_send()
        for cp in cross[a] + main[a]: cp.wait_send()
        for j in range(nz):
            for way in range(2):
                @pl.when(n < j if way == 0 else n > j)
                def _(): hop(a, way, j).wait_send()


def reduce_all(nz, terms, cid):
    dma, vm = pltpu.SemaphoreType.DMA, pltpu.VMEM
    m = len(terms)
    part = terms[0].shape[0] // (CHIPS * CORES)
    rows = part // nz
    shape = jax.ShapeDtypeStruct
    terms = [t.reshape(CHIPS, CORES, part, t.shape[-1]) for t in terms]
    blocks = [vm((CHIPS, part, t.shape[-1]), t.dtype) for t in terms]
    return pl.pallas_call(
        functools.partial(reduce_kernel, nz, m),
        out_shape=tuple(shape((rows, t.shape[-1]), t.dtype) for t in terms),
        in_specs=[ANY] * m, out_specs=(ANY,) * m,
        scratch_shapes=blocks + blocks + [vm((3 * part + 2 * nz * rows, t.shape[-1]), t.dtype) for t in terms]
        + [dma((m,)), dma((m,)), dma((m, 2)), dma((m, 2)), dma((m, 4)), dma((m, 4)), dma((m, 2, nz)), dma((m, 2, nz)), dma((m,))],
        compiler_params=pltpu.CompilerParams(collective_id=cid, has_side_effects=True, vmem_limit_bytes=60 << 20),
        name="reduce_all",
    )(*terms)


def spread_kernel(src, *refs):
    outs, (s_s, s_r, loc) = refs[:3], refs[3:]
    c, k, n = place()
    cols = src.shape[-1] // 3
    hello([(None, chip_at(c, r), k, n) for r in (1, 2, 3)])
    at = pl.ds(pl.multiple_of(c * cols, 128), cols)
    cps = []
    for m in range(3):
        cps.append(pltpu.make_async_copy(src.at[c, :, pl.ds(m * cols, cols)], outs[m].at[:, at], loc.at[m]))
        for r in (1, 2, 3):
            cc = chip_at(c, r)
            cps.append(remote(src.at[cc, :, pl.ds(m * cols, cols)], outs[m].at[:, at], s_s.at[m, r - 1], s_r.at[m, r - 1], cc, k, n))
    for cp in cps: cp.start()
    for cp in cps: cp.wait()


def spread(src, cid):
    dma = pltpu.SemaphoreType.DMA
    rows, cols = src.shape[1], src.shape[2] // 3
    return pl.pallas_call(
        spread_kernel,
        out_shape=(jax.ShapeDtypeStruct((rows, CHIPS * cols), src.dtype),) * 3, in_specs=[ANY], out_specs=(ANY,) * 3,
        scratch_shapes=[dma((3, 3)), dma((3, 3)), dma((3,))],
        compiler_params=pltpu.CompilerParams(collective_id=cid, has_side_effects=True),
        name="spread",
    )(src)


def fits(mesh):
    return mesh.shape["wide"] == CHIPS * CORES


def fast_device(
    nz,
    tokens,
    cotangent,
    lengths,
    positions,
    norm_attn,
    w_query,
    w_key,
    w_value,
    w_output,
    norm_mlp,
    w_gate,
    w_up,
    w_down,
):
    f32, bf16 = jnp.float32, jnp.bfloat16
    c, k, n = place()
    slots, width = tokens.shape
    rows = w_query.shape[0]
    query_width, key_width = w_query.shape[1], w_key.shape[1]
    cols = w_gate.shape[1] // CHIPS
    inputs = tokens.astype(f32)
    valid_rows = (jnp.arange(slots) < lengths[0]).astype(f32)[:, None]
    tables = lane_tables(positions)
    grad_y = cotangent.astype(f32) * valid_rows
    grad_y_low = grad_y.astype(bf16)
    gains = jnp.zeros((rows, 128), bf16).at[:, 0].set(norm_attn).at[:, 1].set(norm_mlp)
    w_qkv, w_out, gain_cols, ff_gate_up, ff_down = gather_all(
        nz, w_query, w_key, w_value, w_output, gains, w_gate, w_up, w_down
    )
    gain_attn = gain_cols[:, 0].astype(f32)
    gain_mlp = gain_cols[:, 1].astype(f32)

    normed_attn = normalize(inputs)
    scaled_attn = (normed_attn * gain_attn).astype(bf16)
    qkv = jnp.dot(scaled_attn, w_qkv, preferred_element_type=f32)
    query_rotated, key_rotated, value_reduced, log_totals, context, gy_all, ff_down = attend_all(
        nz, qkv, tables, grad_y_low, ff_down
    )
    ff_gate_up, ff_down = (w.reshape(-1, rows, w.shape[-1]) for w in (ff_gate_up, ff_down))
    hidden = inputs + lax.dot_general(context, w_out, contract_last, preferred_element_type=f32)
    normed_mlp = normalize(hidden)
    scaled_mlp = (normed_mlp * gain_mlp).astype(bf16)

    grad_x_parts, mlp_parts, mlp_cross, ff_sums = mlp_all(nz, scaled_mlp, gy_all, ff_gate_up, ff_down)
    grad_xn2 = jnp.sum(grad_x_parts.astype(f32), axis=0)
    grad_gain_mlp = jnp.sum(grad_xn2 * normed_mlp, axis=0)
    grad_hidden = grad_y + norm_back(grad_xn2 * gain_mlp, normed_mlp, hidden)
    grad_attn_low = grad_hidden.astype(bf16)
    grad_context = jnp.dot(grad_attn_low, w_out, preferred_element_type=f32).astype(bf16)
    grad_query, grad_key, grad_value, mlp_crossed = attend_back_all(
        query_rotated, key_rotated, value_reduced, log_totals, grad_context, tables, mlp_cross
    )
    output = (valid_rows * (hidden + jnp.sum(mlp_parts.astype(f32), axis=0) + mlp_crossed.astype(f32))).astype(bf16)
    grad_qkv = jnp.concatenate([grad_query, grad_key.astype(bf16), grad_value.astype(bf16)], 1)
    grad_xn1 = lax.dot_general(grad_qkv, w_qkv, contract_last, preferred_element_type=f32)
    grad_gain_attn = jnp.sum(grad_xn1 * normed_attn, axis=0)
    grad_tokens = grad_hidden + norm_back(grad_xn1 * gain_attn, normed_attn, inputs)

    def over_rows(left, right):
        return lax.dot_general(left, right, contract_first, preferred_element_type=f32)

    ff_sums = lax.psum_scatter(ff_sums, "narrow", scatter_dimension=0, tiled=True)
    gain_terms = jnp.zeros((width, 128), f32).at[:, 0].set(grad_gain_attn).at[:, 1].set(grad_gain_mlp)
    grad_w_output, grad_qkv_rows, gain_sums = reduce_all(
        nz,
        [
            over_rows(grad_attn_low, context).astype(bf16),
            over_rows(scaled_attn, grad_qkv).astype(bf16),
            gain_terms.astype(bf16),
        ],
        3,
    )
    grad_w_down, grad_w_gate, grad_w_up = (g.astype(f32) for g in spread(ff_sums.reshape(CHIPS, rows, 3 * cols), 5))
    grad_w_output = grad_w_output.astype(f32)
    grad_w_query = grad_qkv_rows[:, :query_width].astype(f32)
    grad_w_key = grad_qkv_rows[:, query_width : query_width + key_width].astype(f32)
    grad_w_value = grad_qkv_rows[:, query_width + key_width :].astype(f32)
    grad_norm_attn, grad_norm_mlp = gain_sums[:, 0].astype(f32), gain_sums[:, 1].astype(f32)
    return (
        output,
        grad_tokens,
        grad_norm_attn,
        grad_w_query,
        grad_w_key,
        grad_w_value,
        grad_w_output,
        grad_norm_mlp,
        grad_w_gate,
        grad_w_up,
        grad_w_down,
    )


def solution(mesh):
    in_specs = (
        P(("wide", "narrow"), None),
        P(("wide", "narrow"), None),
        P(("wide", "narrow")),
        P(("wide", "narrow")),
        P(("wide", "narrow")),
        P(("wide", "narrow"), None),
        P(("wide", "narrow"), None),
        P(("wide", "narrow"), None),
        P(("wide", "narrow"), None),
        P(("wide", "narrow")),
        P(("wide", "narrow"), None),
        P(("wide", "narrow"), None),
        P(("wide", "narrow"), None),
    )
    out_specs = (
        P(("wide", "narrow"), None),
        P(("wide", "narrow"), None),
        P(("wide", "narrow")),
        P(("wide", "narrow"), None),
        P(("wide", "narrow"), None),
        P(("wide", "narrow"), None),
        P(("wide", "narrow"), None),
        P(("wide", "narrow")),
        P(("wide", "narrow"), None),
        P(("wide", "narrow"), None),
        P(("wide", "narrow"), None),
    )
    body = functools.partial(fast_device, mesh.shape["narrow"]) if fits(mesh) else per_device
    return jax.shard_map(
        body, mesh=mesh, in_specs=in_specs, out_specs=out_specs, check_vma=False
    )
```

```python
import functools
import math

import jax
import jax.numpy as jnp
from jax import lax
from jax.experimental import pallas as pl
from jax.experimental.pallas import tpu as pltpu
from jax.sharding import PartitionSpec as P

QUERY_HEADS = 32
KEY_VALUE_HEADS = 4
HEAD_SIZE = 64


norm_eps = 1e-05
rope_base = 10000.0
masked_score = -1e30
contract_last = (((1,), (1,)), ((), ()))
contract_first = (((0,), (0,)), ((), ()))


def rope_tables(positions):
    half_dim = HEAD_SIZE // 2
    inv_freq = jnp.exp(
        -math.log(rope_base) * jnp.arange(half_dim, dtype=jnp.float32) * 2.0 / HEAD_SIZE
    )
    angles = positions.astype(jnp.float32)[..., None] * inv_freq
    cosine = jnp.cos(angles)
    sine_part = jnp.sin(angles)
    return (jnp.concatenate([cosine, cosine], -1), jnp.concatenate([sine_part, sine_part], -1))


def apply_rotary(values, cosine_table, sine_table):
    half_dim = values.shape[-1] // 2
    turned = jnp.concatenate([-values[..., half_dim:], values[..., :half_dim]], -1)
    return values * cosine_table[..., None, :] + turned * sine_table[..., None, :]


def invert_rotary(grad_rows, cosine_table, sine_table):
    half_dim = grad_rows.shape[-1] // 2
    with_cos = grad_rows * cosine_table[..., None, :]
    with_sin = grad_rows * sine_table[..., None, :]
    return with_cos + jnp.concatenate([with_sin[..., half_dim:], -with_sin[..., :half_dim]], -1)


def normalize(values):
    return values * lax.rsqrt(jnp.mean(values * values, axis=-1, keepdims=True) + norm_eps)


def norm_back(grad_hat, normed, values):
    row_scale = lax.rsqrt(jnp.mean(values * values, axis=-1, keepdims=True) + norm_eps)
    return row_scale * (grad_hat - normed * jnp.mean(grad_hat * normed, axis=-1, keepdims=True))


def attention_inputs(normed, norm_attn, w_query, w_key, w_value):
    gain_piece = lax.all_gather(norm_attn, ("wide", "narrow"), axis=0, tiled=True)
    query_rows = lax.all_gather(w_query, ("wide", "narrow"), axis=0, tiled=True)
    key_rows = lax.all_gather(w_key, ("wide", "narrow"), axis=0, tiled=True)
    value_rows = lax.all_gather(w_value, ("wide", "narrow"), axis=0, tiled=True)
    gain_float = gain_piece.astype(jnp.float32)
    columns = (normed * gain_float).astype(jnp.bfloat16)
    query_sum = jnp.dot(columns, query_rows, preferred_element_type=jnp.float32)
    key_sum = jnp.dot(columns, key_rows, preferred_element_type=jnp.float32)
    value_sum = jnp.dot(columns, value_rows, preferred_element_type=jnp.float32)
    return (gain_float, columns, query_sum, key_sum, value_sum)


def mlp_inputs(normed, norm_mlp, w_gate, w_up):
    gain_piece = lax.all_gather(norm_mlp, ("wide", "narrow"), axis=0, tiled=True)
    gate_rows = lax.all_gather(w_gate, ("wide", "narrow"), axis=0, tiled=True)
    up_rows = lax.all_gather(w_up, ("wide", "narrow"), axis=0, tiled=True)
    gain_float = gain_piece.astype(jnp.float32)
    columns = (normed * gain_float).astype(jnp.bfloat16)
    gate_sum = jnp.dot(columns, gate_rows, preferred_element_type=jnp.float32)
    up_sum = jnp.dot(columns, up_rows, preferred_element_type=jnp.float32)
    return (gain_float, columns, gate_sum, up_sum)


def head_slices(query_rotated, key_rotated, value_reduced, shared_key_head):
    row_total_count = query_rotated.shape[0]
    heads_per_group = QUERY_HEADS // KEY_VALUE_HEADS
    query_head = query_rotated[
        :,
        shared_key_head
        * heads_per_group
        * HEAD_SIZE : (shared_key_head + 1)
        * heads_per_group
        * HEAD_SIZE,
    ].reshape(row_total_count, heads_per_group, HEAD_SIZE)
    key_head = key_rotated[:, shared_key_head * HEAD_SIZE : (shared_key_head + 1) * HEAD_SIZE]
    value_head = value_reduced[:, shared_key_head * HEAD_SIZE : (shared_key_head + 1) * HEAD_SIZE]
    return (query_head, key_head, value_head)


def head_scores(query_head, key_head):
    row_total_count = query_head.shape[0]
    causal = jnp.arange(row_total_count)[:, None] >= jnp.arange(row_total_count)[None, :]
    raw_scores = jnp.einsum("qrd,kd->rqk", query_head, key_head, preferred_element_type=jnp.float32)
    return jnp.where(causal, raw_scores * HEAD_SIZE ** (-0.5), masked_score)


def attend(query_rotated, key_rotated, value_reduced):
    row_total_count = query_rotated.shape[0]
    heads_per_group = QUERY_HEADS // KEY_VALUE_HEADS
    contexts = []
    log_totals = []
    for shared_key_head in range(KEY_VALUE_HEADS):
        query_head, key_head, value_head = head_slices(
            query_rotated, key_rotated, value_reduced, shared_key_head
        )
        scores = head_scores(query_head, key_head)
        row_peak = jnp.max(scores, axis=-1, keepdims=True)
        exp_scores = jnp.exp(scores - row_peak)
        row_total = jnp.sum(exp_scores, axis=-1, keepdims=True)
        probs = exp_scores / row_total
        context_head = jnp.einsum(
            "rqk,kd->qrd",
            probs.astype(jnp.bfloat16),
            value_head,
            preferred_element_type=jnp.float32,
        )
        contexts.append(context_head.reshape(row_total_count, heads_per_group * HEAD_SIZE))
        log_totals.append(row_peak + jnp.log(row_total))
    return (jnp.concatenate(contexts, 1).astype(jnp.bfloat16), log_totals)


def attend_back(query_rotated, key_rotated, value_reduced, log_totals, grad_context):
    row_total_count = query_rotated.shape[0]
    heads_per_group = QUERY_HEADS // KEY_VALUE_HEADS
    score_scale = HEAD_SIZE ** (-0.5)
    query_grads = []
    key_grads = []
    value_grads = []
    for shared_key_head in range(KEY_VALUE_HEADS):
        query_head, key_head, value_head = head_slices(
            query_rotated, key_rotated, value_reduced, shared_key_head
        )
        scores = head_scores(query_head, key_head)
        probs = jnp.exp(scores - log_totals[shared_key_head])
        probs_low = probs.astype(jnp.bfloat16)
        grad_head = grad_context[
            :,
            shared_key_head
            * heads_per_group
            * HEAD_SIZE : (shared_key_head + 1)
            * heads_per_group
            * HEAD_SIZE,
        ].reshape(row_total_count, heads_per_group, HEAD_SIZE)
        grad_probs = jnp.einsum(
            "qrd,kd->rqk", grad_head, value_head, preferred_element_type=jnp.float32
        )
        value_grads.append(
            jnp.einsum("rqk,qrd->kd", probs_low, grad_head, preferred_element_type=jnp.float32)
        )
        inner_sum = jnp.sum(grad_probs * probs, axis=-1, keepdims=True)
        grad_scores = (probs * (grad_probs - inner_sum) * score_scale).astype(jnp.bfloat16)
        query_grad = jnp.einsum(
            "rqk,kd->qrd", grad_scores, key_head, preferred_element_type=jnp.float32
        )
        query_grads.append(query_grad.reshape(row_total_count, heads_per_group * HEAD_SIZE))
        key_grads.append(
            jnp.einsum("rqk,qrd->kd", grad_scores, query_head, preferred_element_type=jnp.float32)
        )
    return (
        jnp.concatenate(query_grads, 1),
        jnp.concatenate(key_grads, 1),
        jnp.concatenate(value_grads, 1),
    )


def make_term(width_sides, other_sides):
    down_side, mlp_side, attn_side, qkv_side = width_sides
    mixed_rows, gate_rows, up_rows, context_rows, query_rows, key_rows, value_rows = other_sides

    def grad_term(first_row, row_span):
        pieces = [
            lax.dot_general(
                down_side, mixed_rows, contract_first, preferred_element_type=jnp.float32
            ),
            lax.dot_general(
                mlp_side, gate_rows, contract_first, preferred_element_type=jnp.float32
            ),
            lax.dot_general(mlp_side, up_rows, contract_first, preferred_element_type=jnp.float32),
            lax.dot_general(
                attn_side, context_rows, contract_first, preferred_element_type=jnp.float32
            ),
            lax.dot_general(
                qkv_side, query_rows, contract_first, preferred_element_type=jnp.float32
            ),
            lax.dot_general(qkv_side, key_rows, contract_first, preferred_element_type=jnp.float32),
            lax.dot_general(
                qkv_side, value_rows, contract_first, preferred_element_type=jnp.float32
            ),
        ]
        return jnp.concatenate(pieces, 1)

    return grad_term


def per_device(
    tokens,
    cotangent,
    lengths,
    positions,
    norm_attn,
    w_query,
    w_key,
    w_value,
    w_output,
    norm_mlp,
    w_gate,
    w_up,
    w_down,
):
    row_total_count = tokens.shape[0]
    shard_rows = w_query.shape[0]
    query_width = w_query.shape[1]
    key_width = w_key.shape[1]
    hidden_width = w_gate.shape[1]
    inputs = tokens.astype(jnp.float32)
    valid_rows = (jnp.arange(row_total_count) < lengths[0]).astype(jnp.float32)[:, None]
    cosine_table, sine_table = rope_tables(positions)
    normed_attn = normalize(inputs)
    gain_attn_full, scaled_attn, query_pre, key_unrotated, value_pre = attention_inputs(
        normed_attn, norm_attn, w_query, w_key, w_value
    )
    query_rotated = (
        apply_rotary(
            query_pre.reshape(row_total_count, QUERY_HEADS, HEAD_SIZE), cosine_table, sine_table
        )
        .reshape(row_total_count, query_width)
        .astype(jnp.bfloat16)
    )
    key_rotated = (
        apply_rotary(
            key_unrotated.reshape(row_total_count, KEY_VALUE_HEADS, HEAD_SIZE),
            cosine_table,
            sine_table,
        )
        .reshape(row_total_count, key_width)
        .astype(jnp.bfloat16)
    )
    value_reduced = value_pre.astype(jnp.bfloat16)
    context, log_totals = attend(query_rotated, key_rotated, value_reduced)
    attn_out = lax.dot_general(
        context,
        lax.all_gather(w_output, ("wide", "narrow"), axis=0, tiled=True),
        contract_last,
        preferred_element_type=jnp.float32,
    )
    hidden = inputs + attn_out
    normed_mlp = normalize(hidden)
    gain_mlp_full, scaled_mlp, gate_proj, up_proj = mlp_inputs(normed_mlp, norm_mlp, w_gate, w_up)
    mixed_low = (gate_proj * jax.nn.sigmoid(gate_proj) * up_proj).astype(jnp.bfloat16)
    mlp_out = lax.dot_general(
        mixed_low,
        lax.all_gather(w_down, ("wide", "narrow"), axis=0, tiled=True),
        contract_last,
        preferred_element_type=jnp.float32,
    )
    output = (valid_rows * (hidden + mlp_out)).astype(jnp.bfloat16)
    grad_y = cotangent.astype(jnp.float32) * valid_rows
    grad_y_low = grad_y.astype(jnp.bfloat16)
    grad_cols = grad_y_low
    grad_mixed = jnp.dot(
        grad_cols,
        lax.all_gather(w_down, ("wide", "narrow"), axis=0, tiled=True),
        preferred_element_type=jnp.float32,
    )
    again_values = mlp_inputs(normed_mlp, norm_mlp, w_gate, w_up)
    gate_proj = again_values[2]
    up_proj = again_values[3]
    sigmoid_gate = jax.nn.sigmoid(gate_proj)
    grad_gate = (
        grad_mixed * up_proj * (sigmoid_gate * (1.0 + gate_proj * (1.0 - sigmoid_gate)))
    ).astype(jnp.bfloat16)
    grad_up = (grad_mixed * (gate_proj * sigmoid_gate)).astype(jnp.bfloat16)
    gate_rows = lax.all_gather(w_gate, ("wide", "narrow"), axis=0, tiled=True)
    up_rows = lax.all_gather(w_up, ("wide", "narrow"), axis=0, tiled=True)
    columns = lax.dot_general(
        grad_gate, gate_rows, contract_last, preferred_element_type=jnp.float32
    )
    columns = columns + lax.dot_general(
        grad_up, up_rows, contract_last, preferred_element_type=jnp.float32
    )
    grad_xn2 = columns
    grad_gain_mlp = jnp.sum(grad_xn2 * normed_mlp, axis=0)
    grad_hidden = grad_y + norm_back(grad_xn2 * gain_mlp_full, normed_mlp, hidden)
    grad_attn_low = grad_hidden.astype(jnp.bfloat16)
    grad_cols = grad_attn_low
    grad_context = jnp.dot(
        grad_cols,
        lax.all_gather(w_output, ("wide", "narrow"), axis=0, tiled=True),
        preferred_element_type=jnp.float32,
    )
    grad_context = grad_context.astype(jnp.bfloat16)
    grad_query_rot, gradient_key_rotated, grad_value_sum = attend_back(
        query_rotated, key_rotated, value_reduced, log_totals, grad_context
    )
    grad_query = (
        invert_rotary(
            grad_query_rot.reshape(row_total_count, QUERY_HEADS, HEAD_SIZE),
            cosine_table,
            sine_table,
        )
        .reshape(row_total_count, query_width)
        .astype(jnp.bfloat16)
    )
    grad_key = (
        invert_rotary(
            gradient_key_rotated.reshape(row_total_count, KEY_VALUE_HEADS, HEAD_SIZE),
            cosine_table,
            sine_table,
        )
        .reshape(row_total_count, key_width)
        .astype(jnp.bfloat16)
    )
    grad_value = grad_value_sum.astype(jnp.bfloat16)
    query_rows = lax.all_gather(w_query, ("wide", "narrow"), axis=0, tiled=True)
    key_rows = lax.all_gather(w_key, ("wide", "narrow"), axis=0, tiled=True)
    value_rows = lax.all_gather(w_value, ("wide", "narrow"), axis=0, tiled=True)
    columns = lax.dot_general(
        grad_query, query_rows, contract_last, preferred_element_type=jnp.float32
    )
    columns = columns + lax.dot_general(
        grad_key, key_rows, contract_last, preferred_element_type=jnp.float32
    )
    columns = columns + lax.dot_general(
        grad_value, value_rows, contract_last, preferred_element_type=jnp.float32
    )
    local_term = make_term(
        (grad_y_low, scaled_mlp, grad_attn_low, scaled_attn),
        (mixed_low, grad_gate, grad_up, context, grad_query, grad_key, grad_value),
    )
    all_sums = lax.psum_scatter(
        local_term(jnp.int32(0), lax.axis_size(("wide", "narrow")) * shard_rows),
        ("wide", "narrow"),
        scatter_dimension=0,
        tiled=True,
    )
    edges = [0]
    for width in (
        hidden_width,
        hidden_width,
        hidden_width,
        query_width,
        query_width,
        key_width,
        key_width,
    ):
        edges.append(edges[-1] + width)
    grad_w_down = all_sums[:, edges[0] : edges[1]]
    grad_w_gate = all_sums[:, edges[1] : edges[2]]
    grad_w_up = all_sums[:, edges[2] : edges[3]]
    grad_w_output = all_sums[:, edges[3] : edges[4]]
    grad_w_query = all_sums[:, edges[4] : edges[5]]
    grad_w_key = all_sums[:, edges[5] : edges[6]]
    grad_w_value = all_sums[:, edges[6] : edges[7]]
    grad_gain_attn = jnp.sum(columns * normed_attn, axis=0)
    grad_tokens = grad_hidden + norm_back(columns * gain_attn_full, normed_attn, inputs)
    grad_norm_attn, grad_norm_mlp = (
        lax.psum_scatter(grad_gain_attn, ("wide", "narrow"), scatter_dimension=0, tiled=True),
        lax.psum_scatter(grad_gain_mlp, ("wide", "narrow"), scatter_dimension=0, tiled=True),
    )
    return (
        output,
        grad_tokens,
        grad_norm_attn,
        grad_w_query,
        grad_w_key,
        grad_w_value,
        grad_w_output,
        grad_norm_mlp,
        grad_w_gate,
        grad_w_up,
        grad_w_down,
    )


MESH = pl.DeviceIdType.MESH
ANY = pl.BlockSpec(memory_space=pl.ANY)

CHIPS, CORES = 4, 2

def place():
    w = lax.axis_index("wide"); n = lax.axis_index("narrow")
    return w // CORES, w % CORES, n

def chip_at(c, r):
    xb, yb, rx, ry = c % 2, c // 2, r % 2, r // 2
    return (yb + ry - 2 * yb * ry) * 2 + (xb + rx - 2 * xb * rx)


def remote(src, dst, send, recv, chip, core, z):
    return pltpu.make_async_remote_copy(src_ref=src, dst_ref=dst, send_sem=send, recv_sem=recv,
        device_id={"wide": chip * CORES + core, "narrow": z}, device_id_type=MESH)

def hello(partners):
    barrier = pltpu.get_barrier_semaphore()
    count = 0
    for cond, chip, core, z in partners:
        def sig(chip=chip, core=core, z=z):
            pl.semaphore_signal(barrier, inc=1, device_id={"wide": chip * CORES + core, "narrow": z}, device_id_type=MESH)
        if cond is None:
            sig(); count = count + 1
        else:
            pl.when(cond)(sig); count = count + jnp.where(cond, 1, 0)
    pl.semaphore_wait(barrier, count)

class Line:
    def __init__(self, nz, at, refs, send, recv, place_of):
        self.nz, self.at, self.refs, self.send, self.recv, self.place_of = nz, at, refs, send, recv, place_of

    def _copy(self, a, way, s, origin):
        c, k, n = self.at
        ref = self.place_of(self.refs[a], origin)
        return remote(ref, ref, self.send.at[a, way, s], self.recv.at[a, way, s], c, k, n + 1 if way == 0 else n - 1)

    def _origin(self, way, s):
        n = self.at[2]
        o = n - s if way == 0 else n + s
        return (n >= s) if way == 0 else (n + s <= self.nz - 1), jnp.clip(o, 0, self.nz - 1)

    def _sends(self, way, s):
        n = self.at[2]
        return self._origin(way, s)[0] & ((n < self.nz - 1) if way == 0 else (n > 0))

    def start(self, a, s, way):
        @pl.when(self._sends(way, s))
        def _(): self._copy(a, way, s, self._origin(way, s)[1]).start()

    def step(self, a, s, then=None):
        for way in range(2):
            came, origin = self._origin(way, s)
            @pl.when(came)
            def _(): self._copy(a, way, s - 1, origin).wait_recv()
            if s < self.nz - 1: self.start(a, s, way)
            if then is not None:
                @pl.when(came)
                def _(): then(origin)

    def finish(self, a):
        for s in range(self.nz - 1):
            for way in range(2):
                @pl.when(self._sends(way, s))
                def _(): self._copy(a, way, s, self._origin(way, s)[1]).wait_send()


def gather_kernel(nz, wq, wk, wv, wo, gains, wg, wu, wd, qkv, out, gain, gu, gd,
                  loc, sw_s, sw_r, z_s, z_r, f_s, f_r, p_s, p_r, h_s, h_r, d_s, d_r, e_s, e_r):
    c, k, n = at = place()
    rows, q = wq.shape
    kv = wk.shape[1]
    cols = gd.shape[-1]
    part = nz * rows
    half = part // 2
    kn = k * nz + n
    cx, cy, cd = (chip_at(c, r) for r in (1, 2, 3))
    hello([(None, cc, k, n) for cc in (cx, cy, cd)] + [(None, c, 1 - k, n), (n > 0, c, k, n - 1), (n < nz - 1, c, k, n + 1)])

    def mycols(w, cc): return w.at[:, pl.ds(pl.multiple_of(cc * cols, 128), cols)]
    def landing(i, cc): return gd.at[cc] if i == 2 else gu.at[cc, kn, :, pl.ds(i * cols, cols)]
    whole = (qkv, out, gain)
    def block(ref, z): return ref.at[pl.ds(pl.multiple_of(((c * CORES + k) * nz + z) * rows, rows), rows)]
    own = [pltpu.make_async_copy(wq, block(qkv, n).at[:, pl.ds(0, q)], loc.at[0]),
           pltpu.make_async_copy(wk, block(qkv, n).at[:, pl.ds(q, kv)], loc.at[1]),
           pltpu.make_async_copy(wv, block(qkv, n).at[:, pl.ds(q + kv, kv)], loc.at[2]),
           pltpu.make_async_copy(wo, block(out, n), loc.at[3]), pltpu.make_async_copy(gains, block(gain, n), loc.at[4])]
    ownff = [pltpu.make_async_copy(mycols(w, c), landing(i, c), loc.at[5 + i]) for i, w in enumerate((wg, wu, wd))]
    for cp in own + ownff: cp.start()
    swap = [[remote(mycols(w, cc), landing(i, c), sw_s.at[i, r], sw_r.at[i, r], cc, k, n) for r, cc in enumerate((cx, cy, cd))]
            for i, w in enumerate((wg, wu, wd))]
    for i in range(3):
        for cp in swap[i]: cp.start()
    for cp in own: cp.wait()

    line = Line(nz, at, whole, z_s, z_r, block)
    for a in range(3):
        for way in range(2): line.start(a, 0, way)

    def span(ref, cc, first, size):
        return ref.at[pl.ds(pl.multiple_of((cc * CORES + k) * part, part) + first, size)]
    plane = [[remote(span(ref, c, 0, part), span(ref, c, 0, part), p_s.at[a, r], p_r.at[a, r], cc, k, n) for r, cc in enumerate((cx, cy))]
             for a, ref in enumerate(whole)]
    across = [[remote(span(ref, cx, 0, half), span(ref, cx, 0, half), h_s.at[a, 0], h_r.at[a, 0], cy, k, n),
               remote(span(ref, cy, half, half), span(ref, cy, half, half), h_s.at[a, 1], h_r.at[a, 1], cx, k, n)]
              for a, ref in enumerate(whole)]
    cores = [[remote(span(ref, cc, 0, part), span(ref, cc, 0, part), d_s.at[a, r], d_r.at[a, r], c, 1 - k, n)
              for r, cc in enumerate((c, cx, cy, cd))] for a, ref in enumerate(whole)]

    def plane_start(a):
        for cp in plane[a] + cores[a][:1]: cp.start()
    def plane_next(a):
        for i in range(2):
            plane[a][i].wait_recv()
            across[a][i].start()
            cores[a][1 + i].start()
    def plane_last(a):
        for cp in across[a]: cp.wait_recv()
        cores[a][3].start()

    for s in range(1, nz):
        for a in range(3):
            line.step(a, s)
            if s == nz - 1: plane_start(a)

    ff = Line(nz, at, (gu,), f_s, f_r, lambda ref, z: ref.at[:, k * nz + z])
    def twin(z):
        ref = gu.at[:, k * nz + z]
        return remote(ref, ref, e_s.at[z], e_r.at[z], c, 1 - k, n)
    for i in range(2):
        ownff[i].wait()
        for cp in swap[i]: cp.wait_recv()
    for way in range(2): ff.start(0, 0, way)
    twin(n).start()
    plane_next(0)
    ff.step(0, 1, lambda z: twin(z).start())
    for a in (1, 2): plane_next(a)
    ff.step(0, 2, lambda z: twin(z).start())
    for a in range(3): plane_last(a)
    ownff[2].wait()
    for cp in swap[2]: cp.wait_recv()
    for s in range(3, nz): ff.step(0, s, lambda z: twin(z).start())
    for a in range(3):
        for cp in cores[a]: cp.wait_recv()
    for z in range(nz): twin(z).wait()
    for i in range(3):
        for cp in swap[i]: cp.wait_send()
    for a in range(3):
        line.finish(a)
        for cp in plane[a] + across[a] + cores[a]: cp.wait_send()
    ff.finish(0)


def gather_all(nz, wq, wk, wv, wo, gains, wg, wu, wd):
    rows = wq.shape[0]
    width = rows * CHIPS * CORES * nz
    cols = wg.shape[1] // CHIPS
    bf = jnp.bfloat16
    shape = jax.ShapeDtypeStruct
    dma = pltpu.SemaphoreType.DMA
    return pl.pallas_call(
        functools.partial(gather_kernel, nz),
        out_shape=(shape((width, wq.shape[1] + 2 * wk.shape[1]), bf), shape((width, wo.shape[1]), bf), shape((width, gains.shape[1]), bf),
                   shape((CHIPS, CORES * nz, rows, 2 * cols), bf), shape((CHIPS, rows, cols), bf)),
        in_specs=[ANY] * 8, out_specs=(ANY,) * 5,
        scratch_shapes=[dma((8,)), dma((3, 3)), dma((3, 3)), dma((3, 2, nz)), dma((3, 2, nz)), dma((1, 2, nz)), dma((1, 2, nz)),
                        dma((3, 2)), dma((3, 2)), dma((3, 2)), dma((3, 2)), dma((3, 4)), dma((3, 4)), dma((nz,)), dma((nz,))],
        compiler_params=pltpu.CompilerParams(collective_id=0, has_side_effects=True),
        name="gather_all",
    )(wq, wk, wv, wo, gains, wg, wu, wd)


def add_into(dst, *srcs):
    rows = dst.shape[0]
    step = 16
    def body(i, carry):
        at = pl.ds(pl.multiple_of(i * step, step), step)
        total = dst[at, :].astype(jnp.float32)
        for s in srcs: total = total + s[at, :].astype(jnp.float32)
        dst[at, :] = total.astype(dst.dtype)
        return carry
    lax.fori_loop(0, rows // step, body, 0)


HALVES = ((0, 0), (0, 1), (1, 0), (2, 0), (1, 1), (2, 1), (3, 0), (3, 1))


def mlp_kernel(nz, x, gy, gu_hbm, gd_hbm, gx_parts, mlp_parts, mlp_cross, down_sums, sums,
               xs, gys, gu, gd, mix, ggu, gx, mo, xt, zin, load, ag_s, ag_r, rs_s, rs_r, mo_s, mo_r, out, core_s, core_r, ready, done, z_s, z_r):
    c, k, n = place()
    f32, bf16 = jnp.float32, jnp.bfloat16
    slots, width = x.shape
    half = slots // 2
    rows, cols = gd.shape[2:]
    tile = nz * rows
    hello([(None, chip_at(c, r), k, n) for r in (1, 2, 3)]
          + [(None, c, 1 - k, n), (n > 0, c, k, n - 1), (n < nz - 1, c, k, n + 1)])
    def half_of(ref, h): return ref.at[pl.ds(h * half, half)]
    index = {place_: i for i, place_ in enumerate(HALVES)}
    sends = {}
    for h in range(2):
        for r in (1, 2):
            i = index[r, h]
            sends[i] = remote(half_of(x, h), xs.at[i], ag_s.at[i], ag_r.at[i], chip_at(c, r), k, n)
            if h == 0: sends[i].start()
    loads = [pltpu.make_async_copy(half_of(x, h), xs.at[h], load.at[h]) for h in range(2)]
    loads += [pltpu.make_async_copy(half_of(gy.at[r], h), gys.at[i], load.at[2 + i]) for i, (r, h) in enumerate(HALVES)]
    for cp in loads: cp.start()
    def weights(col, w, j):
        return [pltpu.make_async_copy(a.at[:, :, :, pl.ds(first + col, w)], b.at[:, :, :, pl.ds(first + col, w)], load.at[10 + 3 * j + i])
                for i, (a, b, first) in enumerate(((gu_hbm, gu, 0), (gu_hbm, gu, cols), (gd_hbm, gd, 0)))]
    for j in range(-(-cols // 256)):
        for cp in weights(j * 256, min(256, cols - j * 256), j): cp.start()
    relays = {index[3, 0]: (index[1, 0], 2), index[3, 1]: (index[2, 1], 1)}
    relays = {i: remote(xs.at[j], xs.at[i], ag_s.at[i], ag_r.at[i], chip_at(c, r), k, n) for i, (j, r) in relays.items()}
    for cp in loads: cp.wait()

    def columns(ref, at, size):
        return ref[:, :, :, pl.ds(at, size)].reshape(width, size)

    def some_rows(ref, i): return ref[i].reshape(tile, ref.shape[3])

    def to_owner(src, dst, i, s_s, s_r):
        r, h = HALVES[i]
        return remote(src.at[i], half_of(dst.at[r], h), s_s.at[i], s_r.at[i], chip_at(c, r), k, n)

    def kept(src, dst, i, j):
        return pltpu.make_async_copy(src.at[i], half_of(dst, HALVES[i][1]), out.at[j])

    def block(r, carry):
        two = pl.ds(2 * r, 2)
        @pl.when(r == 1)
        def _():
            for i in (2, 3): sends[i].wait_recv()
            relays[index[3, 0]].start()
        @pl.when(r == 3)
        def _():
            for cp in relays.values(): cp.wait_recv()
        def both(ref): return ref[two].reshape(slots, ref.shape[2])
        def put(ref, at, v): ref[two, :, at] = v.astype(bf16).reshape(2, half, v.shape[1])
        def chunk(col, w, j):
            @pl.when(r == 0)
            def _():
                for cp in weights(col, w, j): cp.wait()
            tokens = both(xs)
            hg = jnp.dot(tokens, columns(gu, col, w), preferred_element_type=f32)
            hu = jnp.dot(tokens, columns(gu, cols + col, w), preferred_element_type=f32)
            gm = jnp.dot(both(gys), columns(gd, col, w), preferred_element_type=f32)
            for q in range(w // 128):
                gate, up, g = (t[:, 128 * q : 128 * q + 128] for t in (hg, hu, gm))
                sg = 1.0 / (1.0 + jnp.exp(-gate))
                act = gate * sg
                put(mix, pl.ds(col + 128 * q, 128), act * up)
                put(ggu, pl.ds(col + 128 * q, 128), g * up * (sg * (1.0 + gate * (1.0 - sg))))
                put(ggu, pl.ds(cols + col + 128 * q, 128), g * act)
        def pair(j, carry):
            chunk(pl.multiple_of(j * 256, 256), 256, j)
            return carry
        lax.fori_loop(0, cols // 256, pair, 0)
        if cols % 256: chunk(cols // 256 * 256, cols % 256, cols // 256)
        @pl.when(r == 0)
        def _():
            for i in (4, 5): sends[i].start()
        @pl.when(r == 1)
        def _():
            for i in (4, 5): sends[i].wait_recv()
            relays[index[3, 1]].start()
        def back(i, carry):
            at = pl.ds(pl.multiple_of(i * tile, 128), tile)
            put(gx, at, lax.dot_general(both(ggu), some_rows(gu, i), contract_last, preferred_element_type=f32))
            return carry
        lax.fori_loop(0, CHIPS * CORES, back, 0)
        for t in range(CHIPS):
            @pl.when(r == t)
            def _():
                for i in (2 * t, 2 * t + 1):
                    (to_owner(gx, gx_parts, i, rs_s, rs_r) if t else kept(gx, gx_parts.at[0], i, i)).start()
        def down(i, carry):
            at = pl.ds(pl.multiple_of(i * tile, 128), tile)
            put(mo, at, lax.dot_general(both(mix), some_rows(gd, i), contract_last, preferred_element_type=f32))
            return carry
        lax.fori_loop(0, CHIPS * CORES, down, 0)
        for t in range(CHIPS):
            @pl.when(r == t)
            def _():
                for i in (2 * t, 2 * t + 1):
                    (kept(mo, mlp_parts.at[0], i, 2 + i) if t == 0 else kept(mo, mlp_cross, i, i - 2) if t == 3
                     else to_owner(mo, mlp_parts, i, mo_s, mo_r)).start()
        return carry
    lax.fori_loop(0, CHIPS, block, 0)

    pl.semaphore_signal(ready, inc=1, device_id={"wide": c * CORES + 1 - k, "narrow": n}, device_id_type=MESH)
    pl.semaphore_wait(ready, 1)
    sent, came = pl.ds(0, CHIPS), pl.ds(CHIPS, CHIPS)
    pairs = ((gys, mix, gd), (xs, ggu, gu))

    def tiles(total): return [(t * 256, min(256, total - t * 256)) for t in range(-(-total // 256))]

    def to_core(i, col, w, sem):
        ref = pairs[i][2]
        return remote(ref.at[sent, :, :, pl.ds(col, w)], ref.at[came, :, :, pl.ds(col, w)], core_s.at[sem], core_r.at[sem], c, 1 - k, n)

    def to_sums(t): return pltpu.make_async_copy(gu.at[CHIPS + t], sums.at[:, t], done.at[t])

    def each(i, body):
        total, base = pairs[i][2].shape[-1], 0 if i == 0 else len(tiles(cols))
        def step(j, carry):
            body(pl.multiple_of(j * 256, 256), 256, base + j)
            return carry
        lax.fori_loop(0, total // 256, step, 0)
        if total % 256: body(total // 256 * 256, total % 256, base + total // 256)

    def terms(i, kk, use):
        src, right, ref = pairs[i]
        for t in range(CHIPS):
            at = pl.ds(pl.multiple_of((t * CORES + kk) * tile, 128), tile)
            for r in range(CHIPS):
                xt[t * tile : (t + 1) * tile, r * slots : (r + 1) * slots] = src[2 * r : 2 * r + 2, :, at].reshape(slots, tile).T
        def body(col, w, sem):
            b = right[:, :, pl.ds(col, w)].reshape(CHIPS * slots, w)
            use(i, col, w, sem, jnp.dot(xt[...], b, preferred_element_type=f32).reshape(CHIPS, nz, rows, w))
        each(i, body)

    def theirs(i, col, w, sem, v):
        pairs[i][2][sent, :, :, pl.ds(col, w)] = v.astype(bf16)
        to_core(i, col, w, sem).start()

    def ours(i, col, w, sem, v):
        to_core(i, col, w, sem).wait_recv()
        ref = pairs[i][2]
        here = (came, slice(None), slice(None), pl.ds(col, w))
        ref[here] = (ref[here].astype(f32) + v).astype(bf16)

    def hop(way, j):
        return remote(gd.at[came, j], zin.at[way, jnp.clip(j - n - 1 if way == 0 else n - 1 - j, 0, nz - 2)],
                      z_s.at[way, j], z_r.at[way, j], c, k, n + 1 if way == 0 else n - 1)

    def along(t):
        for way in range(2):
            hops = n if way == 0 else nz - 1 - n
            j = jnp.clip(n + nz - 1 - t if way == 0 else t - hops, 0, nz - 1)
            @pl.when((hops > 0) & (t >= hops))
            def _():
                hop(way, j).wait_recv()
                for i in range(CHIPS):
                    add_into(gd.at[CHIPS + i, j], zin.at[way, jnp.clip(j - n if way == 0 else n - j, 0, nz - 2), i])
            @pl.when((t >= hops) & (j != n))
            def _(): hop(way, j).start()

    terms(0, 1 - k, theirs)
    terms(0, k, ours)
    along(0)
    terms(1, 1 - k, theirs)
    along(1)
    terms(1, k, ours)
    for t in range(CHIPS): to_sums(t).start()
    for t in range(2, nz): along(t)
    own_down = pltpu.make_async_copy(gd.at[came, n], down_sums, done.at[CHIPS])
    own_down.start()

    for cp in (*sends.values(), *relays.values()): cp.wait_send()
    for i in range(2):
        kept(gx, gx_parts.at[0], i, i).wait()
        kept(mo, mlp_parts.at[0], i, 2 + i).wait()
        kept(mo, mlp_cross, 6 + i, 4 + i).wait()
    for i in range(2): each(i, lambda col, w, sem: to_core(i, col, w, sem).wait_send())
    for t in range(CHIPS): to_sums(t).wait()
    for j in range(nz):
        for way in range(2):
            @pl.when(n < j if way == 0 else n > j)
            def _(): hop(way, j).wait_send()
    own_down.wait()
    for i in range(2, 6): to_owner(mo, mlp_parts, i, mo_s, mo_r).wait()
    for i in range(2, 8): to_owner(gx, gx_parts, i, rs_s, rs_r).wait()


def mlp_all(nz, x, gy, gu, gd):
    slots, width = x.shape
    rows, cols = gd.shape[2:]
    bf, dma, vm = jnp.bfloat16, pltpu.SemaphoreType.DMA, pltpu.VMEM
    def blocks(w): return jax.ShapeDtypeStruct((CHIPS, slots, w), bf)
    def halves(w): return vm((2 * CHIPS, slots // 2, w), bf)
    tiles = -(-cols // 256)
    flops = 2 * 9 * CHIPS * slots * width * cols
    return pl.pallas_call(
        functools.partial(mlp_kernel, nz),
        out_shape=(blocks(width), jax.ShapeDtypeStruct((3, slots, width), bf), jax.ShapeDtypeStruct((slots, width), bf),
                   jax.ShapeDtypeStruct((CHIPS, rows, cols), bf), jax.ShapeDtypeStruct((nz, CHIPS, rows, 2 * cols), bf)),
        in_specs=[ANY] * 4, out_specs=(ANY,) * 5,
        scratch_shapes=[halves(width), halves(width), vm(gu.shape, bf), vm(gd.shape, bf), halves(cols), halves(2 * cols), halves(width),
                        halves(width), vm((CHIPS * nz * rows, CHIPS * slots), bf), vm((2, nz - 1, CHIPS, rows, cols), bf), dma((10 + 3 * tiles,)), dma((8,)), dma((8,)), dma((8,)), dma((8,)),
                        dma((8,)), dma((8,)), dma((6,)), dma((3 * tiles,)), dma((3 * tiles,)), pltpu.SemaphoreType.REGULAR, dma((CHIPS + 1,)), dma((2, nz)), dma((2, nz))],
        compiler_params=pltpu.CompilerParams(collective_id=1, has_side_effects=True, vmem_limit_bytes=62 << 20),
        cost_estimate=pl.CostEstimate(flops=flops, bytes_accessed=60 << 20, transcendentals=CHIPS * slots * cols),
        name="mlp_all",
    )(x, gy, gu, gd)


PAIR = 2 * HEAD_SIZE
REPEAT = QUERY_HEADS // KEY_VALUE_HEADS
PAIRS = REPEAT // 2


def lane_tables(positions):
    cosine, sine = rope_tables(positions)
    first = jnp.arange(HEAD_SIZE) < HEAD_SIZE // 2
    low, high = jnp.where(first, -sine, 0.0), jnp.where(first, 0.0, sine)
    return jnp.stack([jnp.concatenate([t, t], 1) for t in (cosine, low, high)])


def rotate(u, tables):
    half = HEAD_SIZE // 2
    return u * tables[0] + pltpu.roll(u, PAIR - half, 1) * tables[1] + pltpu.roll(u, half, 1) * tables[2]


def unrotate(g, tables):
    half = HEAD_SIZE // 2
    return g * tables[0] + pltpu.roll(g * tables[2], PAIR - half, 1) + pltpu.roll(g * tables[1], half, 1)


def row_blocks(slots):
    return [(at, min(128, slots - at), at + 128) for at in range(0, slots, 128)]


def causal(s, below, fill):
    clear = s.shape[1] - 128
    last = jnp.where(below, s[:, clear:], fill)
    return jnp.concatenate([s[:, :clear], last], 1) if clear else last


def attend_kernel(nz, q_ref, k_ref, v_ref, tab_ref, gy, gd_own, qr_ref, k_out, v_out, lse_ref, ctx_ref, gys, gd, ks, vs,
                  loc, g_s, g_r, h_s, h_r, f_s, f_r, e_s, e_r):
    g = pl.program_id(0)
    f32, bf16 = jnp.float32, jnp.bfloat16
    slots = q_ref.shape[0]
    c, k, n = at = place()
    mine = [pltpu.make_async_copy(gd_own, gd.at[:, k * nz + n], loc.at[0]), pltpu.make_async_copy(gy, gys.at[0], loc.at[1])]
    line = Line(nz, at, (gd,), f_s, f_r, lambda ref, z: ref.at[:, k * nz + z])
    half = slots // 2
    sends = [remote(gy, gys.at[r], g_s.at[r], g_r.at[r], chip_at(c, r), k, n) for r in (1, 2)]
    relays = [remote(gys.at[1, pl.ds(0, half)], gys.at[3, pl.ds(0, half)], h_s.at[0], h_r.at[0], chip_at(c, 2), k, n),
              remote(gys.at[2, pl.ds(half, half)], gys.at[3, pl.ds(half, half)], h_s.at[1], h_r.at[1], chip_at(c, 1), k, n)]
    def twin(z):
        ref = gd.at[:, k * nz + z]
        return remote(ref, ref, e_s.at[z], e_r.at[z], c, 1 - k, n)
    @pl.when(g == 0)
    def _():
        hello([(None, chip_at(c, r), k, n) for r in (1, 2)]
              + [(None, c, 1 - k, n), (n > 0, c, k, n - 1), (n < nz - 1, c, k, n + 1)])
        for cp in mine + sends: cp.start()
        mine[0].wait()
        for way in range(2): line.start(0, 0, way)
        twin(n).start()
    @pl.when(g == KEY_VALUE_HEADS - 1)
    def _():
        line.step(0, 1, lambda z: twin(z).start())
    @pl.when(g == 0)
    def _():
        ks[...] = jnp.zeros_like(ks)
        vs[...] = jnp.zeros_like(vs)
    lane = lax.broadcasted_iota(jnp.int32, (slots, PAIR), 1)
    tables = (tab_ref[0], tab_ref[1], tab_ref[2])
    key, val = rotate(k_ref[...], tables), v_ref[...]
    odd = g % 2 == 1
    for x, own, stack, scale in ((key, k_out, ks, HEAD_SIZE ** -0.5), (val, v_out, vs, 1.0)):
        x = jnp.where(lane < HEAD_SIZE, jnp.where(odd, pltpu.roll(x, HEAD_SIZE, 1), x), 0.0).astype(bf16)
        own[0] = x
        x = x.astype(f32) * scale
        stack[0, 0:slots, :] = x.astype(bf16)
        stack[1, 0:slots, :] = pltpu.roll(x, HEAD_SIZE, 1).astype(bf16)
    for start, size, keys in row_blocks(slots):
        below = lax.broadcasted_iota(jnp.int32, (size, 128), 0) >= lax.broadcasted_iota(jnp.int32, (size, 128), 1)
        lse = jnp.zeros((size, PAIR), f32)
        here = lane[0:size]
        for p in range(PAIRS):
            span = slice(p * PAIR, (p + 1) * PAIR)
            rows = slice(start, start + size)
            q = rotate(q_ref[rows, span], tuple(t[rows] for t in tables)).astype(bf16)
            qr_ref[rows, span] = q
            ctx = jnp.zeros((size, PAIR), f32)
            for h in range(2):
                s = lax.dot_general(q, ks[h, 0:keys, :], contract_last, preferred_element_type=f32)
                s = causal(s, below, masked_score)
                peak = jnp.max(s, axis=-1, keepdims=True)
                e = jnp.exp(s - peak)
                total = jnp.sum(e, axis=-1, keepdims=True)
                lse = jnp.where(here == 2 * p + h, peak + jnp.log(total), lse)
                probs = (e * (1.0 / total)).astype(bf16)
                ctx = ctx + jnp.dot(probs, vs[h, 0:keys, :], preferred_element_type=f32)
            ctx_ref[rows, span] = ctx.astype(bf16)
        lse_ref[0, start : start + size, :] = lse
    @pl.when(g == KEY_VALUE_HEADS - 1)
    def _():
        for cp in sends: cp.wait_recv()
        for cp in relays: cp.start()
        for s in range(2, nz): line.step(0, s, lambda z: twin(z).start())
        for cp in relays: cp.wait()
        for z in range(nz): twin(z).wait()
        for cp in sends: cp.wait_send()
        mine[1].wait()
        line.finish(0)


def attend_all(nz, qkv, tables, gy, gd_own):
    slots = qkv.shape[0]
    wide = REPEAT * HEAD_SIZE
    dma = pltpu.SemaphoreType.DMA
    first = QUERY_HEADS * HEAD_SIZE // PAIR
    bf16 = jnp.bfloat16
    keys = -(-slots // 128) * 128
    shape = jax.ShapeDtypeStruct
    per_head = pl.BlockSpec((1, slots, PAIR), lambda g: (g, 0, 0))
    wide_spec = pl.BlockSpec((slots, wide), lambda g: (0, g))
    return pl.pallas_call(
        functools.partial(attend_kernel, nz),
        grid=(KEY_VALUE_HEADS,),
        out_shape=(shape((slots, QUERY_HEADS * HEAD_SIZE), bf16), shape((KEY_VALUE_HEADS, slots, PAIR), bf16),
                   shape((KEY_VALUE_HEADS, slots, PAIR), bf16), shape((KEY_VALUE_HEADS, slots, PAIR), jnp.float32),
                   shape((slots, QUERY_HEADS * HEAD_SIZE), bf16), shape((CHIPS,) + gy.shape, bf16),
                   shape((CHIPS, CORES * nz) + gd_own.shape[1:], bf16)),
        in_specs=[wide_spec, pl.BlockSpec((slots, PAIR), lambda g: (0, first + g // 2)),
                  pl.BlockSpec((slots, PAIR), lambda g: (0, first + KEY_VALUE_HEADS // 2 + g // 2)),
                  pl.BlockSpec((3, slots, PAIR), lambda g: (0, 0, 0)), ANY, ANY],
        out_specs=(wide_spec, per_head, per_head, per_head, wide_spec, ANY, ANY),
        scratch_shapes=[pltpu.VMEM((2, keys, PAIR), bf16), pltpu.VMEM((2, keys, PAIR), bf16),
                        dma((2,)), dma((3,)), dma((3,)), dma((2,)), dma((2,)), dma((1, 2, nz)), dma((1, 2, nz)), dma((nz,)), dma((nz,))],
        compiler_params=pltpu.CompilerParams(collective_id=4, has_side_effects=True, vmem_limit_bytes=32 << 20),
        name="attend",
    )(qkv, qkv, qkv, tables, gy, gd_own)


def attend_back_kernel(q_ref, k_ref, v_ref, lse_ref, gc_ref, tab_ref, part, gq_ref, gk_ref, gv_ref, crossed,
                       ks, kt, vt, ds, pr, qs, gs, s_s, s_r):
    g = pl.program_id(0)
    c, k, n = place()
    copy = remote(part, crossed, s_s, s_r, chip_at(c, 3), k, n)
    @pl.when(g == 0)
    def _():
        hello([(None, chip_at(c, 3), k, n)])
        copy.start()
    f32, bf16 = jnp.float32, jnp.bfloat16
    slots = q_ref.shape[0]
    scale = HEAD_SIZE ** -0.5
    @pl.when(g == 0)
    def _():
        for ref in (ks, kt, vt, ds, pr): ref[...] = jnp.zeros_like(ref)
    lane = lax.broadcasted_iota(jnp.int32, (slots, PAIR), 1)
    tables = (tab_ref[0], tab_ref[1], tab_ref[2])
    key, val = k_ref[0].astype(f32), v_ref[0].astype(f32)
    for stack, x in ((ks, key * scale), (kt, key), (vt, val)):
        stack[0, 0:slots, :] = x.astype(bf16)
        stack[1, 0:slots, :] = pltpu.roll(x, HEAD_SIZE, 1).astype(bf16)
    for at, size, keys in row_blocks(slots):
        rows = slice(at, at + size)
        below = lax.broadcasted_iota(jnp.int32, (size, 128), 0) >= lax.broadcasted_iota(jnp.int32, (size, 128), 1)
        lse = lse_ref[0, rows, :]
        for p in range(PAIRS):
            span = slice(p * PAIR, (p + 1) * PAIR)
            deep = slice(p * slots + at, p * slots + at + size)
            q, gc = q_ref[rows, span], gc_ref[rows, span]
            qs[deep, :] = q
            gs[deep, :] = gc
            gq = jnp.zeros((size, PAIR), f32)
            for h in range(2):
                s = lax.dot_general(q, ks[h, 0:keys, :], contract_last, preferred_element_type=f32)
                e = jnp.exp(s - lse[:, 2 * p + h : 2 * p + h + 1])
                probs = causal(e, below, 0.0)
                pr[h, deep, 0:keys] = probs.astype(bf16)
                gp = lax.dot_general(gc, vt[h, 0:keys, :], contract_last, preferred_element_type=f32)
                inner = jnp.sum(gp * probs, axis=-1, keepdims=True)
                grad = (probs * (gp - inner) * scale).astype(bf16)
                ds[h, deep, 0:keys] = grad
                gq = gq + jnp.dot(grad, kt[h, 0:keys, :], preferred_element_type=f32)
            gq_ref[rows, span] = unrotate(gq, tuple(t[rows] for t in tables)).astype(bf16)
    for src, right, out, turn in ((ds, qs, gk_ref, True), (pr, gs, gv_ref, False)):
        lo, hi = (
            lax.dot_general(src[h], right[...], contract_first, preferred_element_type=f32)[0:slots] for h in range(2)
        )
        x = jnp.where(lane < HEAD_SIZE, lo + pltpu.roll(hi, HEAD_SIZE, 1), 0.0)
        if turn: x = unrotate(x, tables)
        @pl.when(g % 2 == 0)
        def _(): out[...] = x
        @pl.when(g % 2 == 1)
        def _(): out[...] = jnp.where(lane < HEAD_SIZE, out[...], pltpu.roll(x, HEAD_SIZE, 1))
    @pl.when(g == KEY_VALUE_HEADS - 1)
    def _(): copy.wait()


def attend_back_all(q, k, v, lse, grad_context, tables, part):
    slots = q.shape[0]
    wide = REPEAT * HEAD_SIZE
    bf16, f32, vm = jnp.bfloat16, jnp.float32, pltpu.VMEM
    keys = -(-slots // 128) * 128
    shape = jax.ShapeDtypeStruct
    per_head = pl.BlockSpec((1, slots, PAIR), lambda g: (g, 0, 0))
    wide_spec = pl.BlockSpec((slots, wide), lambda g: (0, g))
    two = pl.BlockSpec((slots, PAIR), lambda g: (0, g // 2))
    return pl.pallas_call(
        attend_back_kernel,
        grid=(KEY_VALUE_HEADS,),
        out_shape=(shape((slots, QUERY_HEADS * HEAD_SIZE), bf16), shape((slots, KEY_VALUE_HEADS * HEAD_SIZE), f32),
                   shape((slots, KEY_VALUE_HEADS * HEAD_SIZE), f32), shape(part.shape, part.dtype)),
        in_specs=[wide_spec, per_head, per_head, per_head, wide_spec, pl.BlockSpec((3, slots, PAIR), lambda g: (0, 0, 0)), ANY],
        out_specs=(wide_spec, two, two, ANY),
        scratch_shapes=[vm((2, keys, PAIR), bf16)] * 3 + [vm((2, PAIRS * slots, keys), bf16)] * 2 + [vm((PAIRS * slots, PAIR), bf16)] * 2
        + [pltpu.SemaphoreType.DMA] * 2,
        compiler_params=pltpu.CompilerParams(collective_id=2, has_side_effects=True, vmem_limit_bytes=40 << 20),
        name="attend_back",
    )(q, k, v, lse, grad_context, tables, part)


class Many:
    def __init__(self, copies): self.copies = copies
    def start(self):
        for cp in self.copies: cp.start()
    def wait(self):
        for cp in self.copies: cp.wait()


def columns_home(src, outs, c, k, n, send, recv, loc):
    cols = src.shape[-1] // len(outs)
    at = pl.ds(pl.multiple_of(c * cols, 128), cols)
    local, away = [], []
    for m, out in enumerate(outs):
        local.append(pltpu.make_async_copy(src.at[c, :, pl.ds(m * cols, cols)], out.at[:, at], loc))
        for r in (1, 2, 3):
            cc = chip_at(c, r)
            away.append(remote(src.at[cc, :, pl.ds(m * cols, cols)], out.at[:, at], send.at[m, r - 1], recv.at[m, r - 1], cc, k, n))
    return away + [Many(local)]


def gradient_kernel(nz, gal_hbm, ctx_hbm, xn_hbm, gq_hbm, wq_hbm, tok_hbm, gh_hbm, down, gain, gain_mlp,
                    out0, out1, out2, grad_tokens, down_out,
                    took0, took1, took2, away0, away1, away2, zbuf0, zbuf1, zbuf2, gal, ctx, xn, gq, wq, tok, gh, gx, xt, gain_row,
                    core_s, core_r, half_s, half_r, main_s, main_r, z_s, z_r, ff_s, ff_r, load, loc):
    f32, bf16 = jnp.float32, jnp.bfloat16
    items = 3
    outs, took, away, zbuf = (out0, out1, out2), (took0, took1, took2), (away0, away1, away2), (zbuf0, zbuf1, zbuf2)
    c, k, n = place()
    left, right = n > 0, n < nz - 1
    cx, cy, cd = (chip_at(c, r) for r in (1, 2, 3))
    loads = [pltpu.make_async_copy(a, b, load.at[i]) for i, (a, b) in enumerate(
        ((gal_hbm, gal), (ctx_hbm, ctx), (xn_hbm, xn), (gq_hbm, gq), (wq_hbm, wq), (tok_hbm, tok), (gh_hbm, gh)))]
    for cp in loads: cp.start()
    hello([(None, cc, k, n) for cc in (cx, cy, cd)] + [(None, c, 1 - k, n), (left, c, k, n - 1), (right, c, k, n + 1)])
    slots, width = gal.shape
    rows = outs[0].shape[0]
    part = nz * rows
    half = part // 2
    top, low = pl.ds(0, half), pl.ds(half, half)
    def arrive(a, at, size): return zbuf[a].at[pl.ds(at, size)]
    swap = [remote(away[a], took[a], core_s.at[a], core_r.at[a], c, 1 - k, n) for a in range(items)]
    cross = [[remote(took[a].at[cd, top], arrive(a, 2 * part, half), half_s.at[a, 0], half_r.at[a, 0], cx, k, n),
              remote(took[a].at[cd, low], arrive(a, 2 * part + half, half), half_s.at[a, 1], half_r.at[a, 1], cy, k, n)]
             for a in range(items)]
    main = [[remote(took[a].at[cx, top], arrive(a, 0, half), main_s.at[a, 0], main_r.at[a, 0], cx, k, n),
             remote(took[a].at[cy, low], arrive(a, part + half, half), main_s.at[a, 1], main_r.at[a, 1], cy, k, n),
             remote(took[a].at[cx, low], arrive(a, half, half), main_s.at[a, 2], main_r.at[a, 2], cx, k, n),
             remote(took[a].at[cy, top], arrive(a, part, half), main_s.at[a, 3], main_r.at[a, 3], cy, k, n)]
            for a in range(items)]

    def products(left_side, right_side, kk, put):
        for t in range(CHIPS):
            at = pl.ds(pl.multiple_of((t * CORES + kk) * part, 128), part)
            xt[t * part : (t + 1) * part, :] = left_side[:, at].T
        def step(j, carry):
            at = pl.ds(pl.multiple_of(j * 256, 256), 256)
            put(at, jnp.dot(xt[...], right_side[:, at], preferred_element_type=f32).reshape(CHIPS, part, 256))
            return carry
        lax.fori_loop(0, right_side.shape[1] // 256, step, 0)

    def theirs(a, left_side, right_side):
        def put(at, v): away[a][:, :, at] = v.astype(bf16)
        products(left_side, right_side, 1 - k, put)
        swap[a].start()

    def ours(a, left_side, right_side):
        swap[a].wait_recv()
        def put(at, v): took[a][:, :, at] = (took[a][:, :, at].astype(f32) + v).astype(bf16)
        products(left_side, right_side, k, put)
        for cp in cross[a]: cp.start()

    def input_gradient():
        loads[4].wait()
        def step(j, carry):
            at = pl.ds(pl.multiple_of(j * 256, 256), 256)
            gx[:, at] = lax.dot_general(gq[...], wq[at, :], contract_last, preferred_element_type=f32)
            return carry
        lax.fori_loop(0, width // 256, step, 0)

    def input_norm():
        for cp in loads[5:]: cp.wait()
        def step(j, total):
            at = pl.ds(pl.multiple_of(j * 16, 16), 16)
            x, g = tok[at, :].astype(f32), gx[at, :]
            scale = lax.rsqrt(jnp.mean(x * x, axis=-1, keepdims=True) + norm_eps)
            hat = x * scale
            g1 = g * gain[...]
            gh[at, :] = gh[at, :] + scale * (g1 - hat * jnp.mean(g1 * hat, axis=-1, keepdims=True))
            t = g * hat
            return total + t[0:8] + t[8:16]
        total = lax.fori_loop(0, slots // 16, step, jnp.zeros((8, width), f32))
        return jnp.sum(total, axis=0, keepdims=True)

    def gains_swap(of_attn):
        row = lax.broadcasted_iota(jnp.int32, (128, part), 0)
        def columns_of(t, kk):
            at = pl.ds(pl.multiple_of((t * CORES + kk) * part, 128), part)
            return jnp.where(row == 0, gain_row[0:1, at], jnp.where(row == 1, gain_mlp[0:1, at], 0.0)).T
        gain_row[0:1, :] = of_attn
        for t in range(CHIPS): away[2][t] = columns_of(t, 1 - k).astype(bf16)
        swap[2].start()
        swap[2].wait_recv()
        for t in range(CHIPS): took[2][t] = (took[2][t].astype(f32) + columns_of(t, k)).astype(bf16)
        for cp in cross[2]: cp.start()

    def relay(a):
        cross[a][0].wait_recv()
        add_into(took[a].at[cy, top], arrive(a, 2 * part, half))
        main[a][3].start()
        cross[a][1].wait_recv()
        add_into(took[a].at[cx, low], arrive(a, 2 * part + half, half))
        for i in (2, 0, 1): main[a][i].start()

    def mine(a):
        for cp in main[a]: cp.wait_recv()
        add_into(took[a].at[c], arrive(a, 0, part), arrive(a, part, part))

    def slot(a, way, j): return arrive(a, pl.multiple_of(2 * part + 2 * half + (way * nz + j) * rows, rows), rows)
    def piece(a, j): return took[a].at[c, pl.ds(pl.multiple_of(j * rows, rows), rows)]
    def hop(a, way, j):
        return remote(piece(a, j), slot(a, way, j), z_s.at[a, way, j], z_r.at[a, way, j], c, k, n + 1 if way == 0 else n - 1)

    def along(some):
        for t in range(nz):
            for way in range(2):
                hops = n if way == 0 else nz - 1 - n
                j = jnp.clip(n + nz - 1 - t if way == 0 else t - hops, 0, nz - 1)
                for a in some:
                    @pl.when((hops > 0) & (t >= hops))
                    def _():
                        hop(a, way, j).wait_recv()
                        add_into(piece(a, j), slot(a, way, j))
                    @pl.when((t >= hops) & (j != n))
                    def _(): hop(a, way, j).start()
        done = [pltpu.make_async_copy(piece(a, n), outs[a], loc.at[a]) for a in some]
        for cp in done: cp.start()
        return done

    for cp in loads[:2]: cp.wait()
    theirs(0, gal, ctx)
    for cp in loads[2:4]: cp.wait()
    theirs(1, xn, gq)
    ours(0, gal, ctx)
    ours(1, xn, gq)
    input_gradient()
    relay(0)
    gains_swap(input_norm())
    stores = [pltpu.make_async_copy(gh, grad_tokens, loc.at[items])]
    stores[0].start()
    for a in range(1, items): relay(a)
    mine(0)
    stores += along([0])
    for a in range(1, items): mine(a)
    copies = columns_home(down, (down_out,), c, k, n, ff_s, ff_r, loc.at[items + 1])
    for cp in copies: cp.start()
    stores += along(list(range(1, items)))
    for cp in stores + copies: cp.wait()
    for a in range(items):
        swap[a].wait_send()
        for cp in cross[a] + main[a]: cp.wait_send()
        for j in range(nz):
            for way in range(2):
                @pl.when(n < j if way == 0 else n > j)
                def _(): hop(a, way, j).wait_send()


def gradient_all(nz, gal, ctx, xn, gq, wq, tokens, grad_hidden, down, gain, gain_mlp, cid):
    dma, vm = pltpu.SemaphoreType.DMA, pltpu.VMEM
    bf16, f32 = jnp.bfloat16, jnp.float32
    slots, width = gal.shape
    m = 3
    part = width // (CHIPS * CORES)
    rows = part // nz
    widths = (ctx.shape[1], gq.shape[1], 128)
    shape = jax.ShapeDtypeStruct
    blocks = [vm((CHIPS, part, w), bf16) for w in widths]
    row = pl.BlockSpec((1, width), lambda: (0, 0))
    return pl.pallas_call(
        functools.partial(gradient_kernel, nz),
        out_shape=tuple(shape((rows, w), bf16) for w in widths) + (shape((slots, width), f32), shape((rows, CHIPS * down.shape[2]), bf16)),
        in_specs=[ANY] * 8 + [row, row], out_specs=(ANY,) * (m + 2),
        scratch_shapes=blocks + blocks + [vm((3 * part + 2 * nz * rows, w), bf16) for w in widths]
        + [vm(gal.shape, bf16), vm(ctx.shape, bf16), vm(xn.shape, bf16), vm(gq.shape, bf16), vm(wq.shape, bf16), vm(tokens.shape, bf16),
           vm((slots, width), f32), vm((slots, width), f32), vm((CHIPS * part, slots), bf16), vm((8, width), f32)]
        + [dma((m,)), dma((m,)), dma((m, 2)), dma((m, 2)), dma((m, 4)), dma((m, 4)), dma((m, 2, nz)), dma((m, 2, nz)), dma((1, 3)), dma((1, 3)), dma((7,)), dma((m + 2,))],
        compiler_params=pltpu.CompilerParams(collective_id=cid, has_side_effects=True, vmem_limit_bytes=62 << 20),
        name="gradient_all",
    )(gal, ctx, xn, gq, wq, tokens, grad_hidden, down, gain, gain_mlp)


def spread_kernel(parts, src, *refs):
    outs, (s_s, s_r, loc) = refs[:parts], refs[parts:]
    c, k, n = place()
    hello([(None, chip_at(c, r), k, n) for r in (1, 2, 3)])
    cps = columns_home(src, outs, c, k, n, s_s, s_r, loc)
    for cp in cps: cp.start()
    for cp in cps: cp.wait()


def spread(src, parts, cid):
    dma = pltpu.SemaphoreType.DMA
    rows, cols = src.shape[1], src.shape[2] // parts
    return pl.pallas_call(
        functools.partial(spread_kernel, parts),
        out_shape=(jax.ShapeDtypeStruct((rows, CHIPS * cols), src.dtype),) * parts, in_specs=[ANY], out_specs=(ANY,) * parts,
        scratch_shapes=[dma((parts, 3)), dma((parts, 3)), dma],
        compiler_params=pltpu.CompilerParams(collective_id=cid, has_side_effects=True),
        name="spread",
    )(src)


def fits(mesh):
    return mesh.shape["wide"] == CHIPS * CORES


def fast_device(
    nz,
    tokens,
    cotangent,
    lengths,
    positions,
    norm_attn,
    w_query,
    w_key,
    w_value,
    w_output,
    norm_mlp,
    w_gate,
    w_up,
    w_down,
):
    f32, bf16 = jnp.float32, jnp.bfloat16
    c, k, n = place()
    slots, width = tokens.shape
    rows = w_query.shape[0]
    query_width, key_width = w_query.shape[1], w_key.shape[1]
    cols = w_gate.shape[1] // CHIPS
    inputs = tokens.astype(f32)
    valid_rows = (jnp.arange(slots) < lengths[0]).astype(f32)[:, None]
    tables = lane_tables(positions)
    grad_y = cotangent.astype(f32) * valid_rows
    grad_y_low = grad_y.astype(bf16)
    gains = jnp.zeros((rows, 128), bf16).at[:, 0].set(norm_attn).at[:, 1].set(norm_mlp)
    w_qkv, w_out, gain_cols, ff_gate_up, ff_down = gather_all(
        nz, w_query, w_key, w_value, w_output, gains, w_gate, w_up, w_down
    )
    gain_attn = gain_cols[:, 0].astype(f32)
    gain_mlp = gain_cols[:, 1].astype(f32)

    normed_attn = normalize(inputs)
    scaled_attn = (normed_attn * gain_attn).astype(bf16)
    qkv = jnp.dot(scaled_attn, w_qkv, preferred_element_type=f32)
    query_rotated, key_rotated, value_reduced, log_totals, context, gy_all, ff_down = attend_all(
        nz, qkv, tables, grad_y_low, ff_down
    )
    ff_gate_up, ff_down = (w.reshape(CHIPS * CORES, nz, rows, w.shape[-1]) for w in (ff_gate_up, ff_down))
    hidden = inputs + lax.dot_general(context, w_out, contract_last, preferred_element_type=f32)
    normed_mlp = normalize(hidden)
    scaled_mlp = (normed_mlp * gain_mlp).astype(bf16)

    grad_x_parts, mlp_parts, mlp_cross, down_sums, ff_sums = mlp_all(nz, scaled_mlp, gy_all, ff_gate_up, ff_down)
    grad_xn2 = jnp.sum(grad_x_parts.astype(f32), axis=0)
    grad_gain_mlp = jnp.sum(grad_xn2 * normed_mlp, axis=0)
    grad_hidden = grad_y + norm_back(grad_xn2 * gain_mlp, normed_mlp, hidden)
    grad_attn_low = grad_hidden.astype(bf16)
    grad_context = jnp.dot(grad_attn_low, w_out, preferred_element_type=f32).astype(bf16)
    grad_query, grad_key, grad_value, mlp_crossed = attend_back_all(
        query_rotated, key_rotated, value_reduced, log_totals, grad_context, tables, mlp_cross
    )
    output = (valid_rows * (hidden + jnp.sum(mlp_parts.astype(f32), axis=0) + mlp_crossed.astype(f32))).astype(bf16)
    grad_qkv = jnp.concatenate([grad_query, grad_key.astype(bf16), grad_value.astype(bf16)], 1)
    ff_sums = lax.psum_scatter(ff_sums, "narrow", scatter_dimension=0, tiled=True)
    grad_w_output, grad_qkv_rows, gain_sums, grad_tokens, grad_w_down = gradient_all(
        nz, grad_attn_low, context, scaled_attn, grad_qkv, w_qkv, tokens, grad_hidden, down_sums, gain_attn[None], grad_gain_mlp[None], 3
    )
    grad_w_gate, grad_w_up = (g.astype(f32) for g in spread(ff_sums.reshape(CHIPS, rows, 2 * cols), 2, 5))
    grad_w_down = grad_w_down.astype(f32)
    grad_w_output = grad_w_output.astype(f32)
    grad_w_query = grad_qkv_rows[:, :query_width].astype(f32)
    grad_w_key = grad_qkv_rows[:, query_width : query_width + key_width].astype(f32)
    grad_w_value = grad_qkv_rows[:, query_width + key_width :].astype(f32)
    grad_norm_attn, grad_norm_mlp = gain_sums[:, 0].astype(f32), gain_sums[:, 1].astype(f32)
    return (
        output,
        grad_tokens,
        grad_norm_attn,
        grad_w_query,
        grad_w_key,
        grad_w_value,
        grad_w_output,
        grad_norm_mlp,
        grad_w_gate,
        grad_w_up,
        grad_w_down,
    )


def solution(mesh):
    in_specs = (
        P(("wide", "narrow"), None),
        P(("wide", "narrow"), None),
        P(("wide", "narrow")),
        P(("wide", "narrow")),
        P(("wide", "narrow")),
        P(("wide", "narrow"), None),
        P(("wide", "narrow"), None),
        P(("wide", "narrow"), None),
        P(("wide", "narrow"), None),
        P(("wide", "narrow")),
        P(("wide", "narrow"), None),
        P(("wide", "narrow"), None),
        P(("wide", "narrow"), None),
    )
    out_specs = (
        P(("wide", "narrow"), None),
        P(("wide", "narrow"), None),
        P(("wide", "narrow")),
        P(("wide", "narrow"), None),
        P(("wide", "narrow"), None),
        P(("wide", "narrow"), None),
        P(("wide", "narrow"), None),
        P(("wide", "narrow")),
        P(("wide", "narrow"), None),
        P(("wide", "narrow"), None),
        P(("wide", "narrow"), None),
    )
    body = functools.partial(fast_device, mesh.shape["narrow"]) if fits(mesh) else per_device
    return jax.shard_map(
        body, mesh=mesh, in_specs=in_specs, out_specs=out_specs, check_vma=False
    )
```

```python
import functools
import math

import jax
import jax.numpy as jnp
from jax import lax
from jax.experimental import pallas as pl
from jax.experimental.pallas import tpu as pltpu
from jax.sharding import PartitionSpec as P

QUERY_HEADS = 32
KEY_VALUE_HEADS = 4
HEAD_SIZE = 64


norm_eps = 1e-05
rope_base = 10000.0
masked_score = -1e30
contract_last = (((1,), (1,)), ((), ()))
contract_first = (((0,), (0,)), ((), ()))


def rope_tables(positions):
    half_dim = HEAD_SIZE // 2
    inv_freq = jnp.exp(
        -math.log(rope_base) * jnp.arange(half_dim, dtype=jnp.float32) * 2.0 / HEAD_SIZE
    )
    angles = positions.astype(jnp.float32)[..., None] * inv_freq
    cosine = jnp.cos(angles)
    sine_part = jnp.sin(angles)
    return (jnp.concatenate([cosine, cosine], -1), jnp.concatenate([sine_part, sine_part], -1))


def apply_rotary(values, cosine_table, sine_table):
    half_dim = values.shape[-1] // 2
    turned = jnp.concatenate([-values[..., half_dim:], values[..., :half_dim]], -1)
    return values * cosine_table[..., None, :] + turned * sine_table[..., None, :]


def invert_rotary(grad_rows, cosine_table, sine_table):
    half_dim = grad_rows.shape[-1] // 2
    with_cos = grad_rows * cosine_table[..., None, :]
    with_sin = grad_rows * sine_table[..., None, :]
    return with_cos + jnp.concatenate([with_sin[..., half_dim:], -with_sin[..., :half_dim]], -1)


def normalize(values):
    return values * lax.rsqrt(jnp.mean(values * values, axis=-1, keepdims=True) + norm_eps)


def norm_back(grad_hat, normed, values):
    row_scale = lax.rsqrt(jnp.mean(values * values, axis=-1, keepdims=True) + norm_eps)
    return row_scale * (grad_hat - normed * jnp.mean(grad_hat * normed, axis=-1, keepdims=True))


def attention_inputs(normed, norm_attn, w_query, w_key, w_value):
    gain_piece = lax.all_gather(norm_attn, ("wide", "narrow"), axis=0, tiled=True)
    query_rows = lax.all_gather(w_query, ("wide", "narrow"), axis=0, tiled=True)
    key_rows = lax.all_gather(w_key, ("wide", "narrow"), axis=0, tiled=True)
    value_rows = lax.all_gather(w_value, ("wide", "narrow"), axis=0, tiled=True)
    gain_float = gain_piece.astype(jnp.float32)
    columns = (normed * gain_float).astype(jnp.bfloat16)
    query_sum = jnp.dot(columns, query_rows, preferred_element_type=jnp.float32)
    key_sum = jnp.dot(columns, key_rows, preferred_element_type=jnp.float32)
    value_sum = jnp.dot(columns, value_rows, preferred_element_type=jnp.float32)
    return (gain_float, columns, query_sum, key_sum, value_sum)


def mlp_inputs(normed, norm_mlp, w_gate, w_up):
    gain_piece = lax.all_gather(norm_mlp, ("wide", "narrow"), axis=0, tiled=True)
    gate_rows = lax.all_gather(w_gate, ("wide", "narrow"), axis=0, tiled=True)
    up_rows = lax.all_gather(w_up, ("wide", "narrow"), axis=0, tiled=True)
    gain_float = gain_piece.astype(jnp.float32)
    columns = (normed * gain_float).astype(jnp.bfloat16)
    gate_sum = jnp.dot(columns, gate_rows, preferred_element_type=jnp.float32)
    up_sum = jnp.dot(columns, up_rows, preferred_element_type=jnp.float32)
    return (gain_float, columns, gate_sum, up_sum)


def head_slices(query_rotated, key_rotated, value_reduced, shared_key_head):
    row_total_count = query_rotated.shape[0]
    heads_per_group = QUERY_HEADS // KEY_VALUE_HEADS
    query_head = query_rotated[
        :,
        shared_key_head
        * heads_per_group
        * HEAD_SIZE : (shared_key_head + 1)
        * heads_per_group
        * HEAD_SIZE,
    ].reshape(row_total_count, heads_per_group, HEAD_SIZE)
    key_head = key_rotated[:, shared_key_head * HEAD_SIZE : (shared_key_head + 1) * HEAD_SIZE]
    value_head = value_reduced[:, shared_key_head * HEAD_SIZE : (shared_key_head + 1) * HEAD_SIZE]
    return (query_head, key_head, value_head)


def head_scores(query_head, key_head):
    row_total_count = query_head.shape[0]
    causal = jnp.arange(row_total_count)[:, None] >= jnp.arange(row_total_count)[None, :]
    raw_scores = jnp.einsum("qrd,kd->rqk", query_head, key_head, preferred_element_type=jnp.float32)
    return jnp.where(causal, raw_scores * HEAD_SIZE ** (-0.5), masked_score)


def attend(query_rotated, key_rotated, value_reduced):
    row_total_count = query_rotated.shape[0]
    heads_per_group = QUERY_HEADS // KEY_VALUE_HEADS
    contexts = []
    log_totals = []
    for shared_key_head in range(KEY_VALUE_HEADS):
        query_head, key_head, value_head = head_slices(
            query_rotated, key_rotated, value_reduced, shared_key_head
        )
        scores = head_scores(query_head, key_head)
        row_peak = jnp.max(scores, axis=-1, keepdims=True)
        exp_scores = jnp.exp(scores - row_peak)
        row_total = jnp.sum(exp_scores, axis=-1, keepdims=True)
        probs = exp_scores / row_total
        context_head = jnp.einsum(
            "rqk,kd->qrd",
            probs.astype(jnp.bfloat16),
            value_head,
            preferred_element_type=jnp.float32,
        )
        contexts.append(context_head.reshape(row_total_count, heads_per_group * HEAD_SIZE))
        log_totals.append(row_peak + jnp.log(row_total))
    return (jnp.concatenate(contexts, 1).astype(jnp.bfloat16), log_totals)


def attend_back(query_rotated, key_rotated, value_reduced, log_totals, grad_context):
    row_total_count = query_rotated.shape[0]
    heads_per_group = QUERY_HEADS // KEY_VALUE_HEADS
    score_scale = HEAD_SIZE ** (-0.5)
    query_grads = []
    key_grads = []
    value_grads = []
    for shared_key_head in range(KEY_VALUE_HEADS):
        query_head, key_head, value_head = head_slices(
            query_rotated, key_rotated, value_reduced, shared_key_head
        )
        scores = head_scores(query_head, key_head)
        probs = jnp.exp(scores - log_totals[shared_key_head])
        probs_low = probs.astype(jnp.bfloat16)
        grad_head = grad_context[
            :,
            shared_key_head
            * heads_per_group
            * HEAD_SIZE : (shared_key_head + 1)
            * heads_per_group
            * HEAD_SIZE,
        ].reshape(row_total_count, heads_per_group, HEAD_SIZE)
        grad_probs = jnp.einsum(
            "qrd,kd->rqk", grad_head, value_head, preferred_element_type=jnp.float32
        )
        value_grads.append(
            jnp.einsum("rqk,qrd->kd", probs_low, grad_head, preferred_element_type=jnp.float32)
        )
        inner_sum = jnp.sum(grad_probs * probs, axis=-1, keepdims=True)
        grad_scores = (probs * (grad_probs - inner_sum) * score_scale).astype(jnp.bfloat16)
        query_grad = jnp.einsum(
            "rqk,kd->qrd", grad_scores, key_head, preferred_element_type=jnp.float32
        )
        query_grads.append(query_grad.reshape(row_total_count, heads_per_group * HEAD_SIZE))
        key_grads.append(
            jnp.einsum("rqk,qrd->kd", grad_scores, query_head, preferred_element_type=jnp.float32)
        )
    return (
        jnp.concatenate(query_grads, 1),
        jnp.concatenate(key_grads, 1),
        jnp.concatenate(value_grads, 1),
    )


def make_term(width_sides, other_sides):
    down_side, mlp_side, attn_side, qkv_side = width_sides
    mixed_rows, gate_rows, up_rows, context_rows, query_rows, key_rows, value_rows = other_sides

    def grad_term(first_row, row_span):
        pieces = [
            lax.dot_general(
                down_side, mixed_rows, contract_first, preferred_element_type=jnp.float32
            ),
            lax.dot_general(
                mlp_side, gate_rows, contract_first, preferred_element_type=jnp.float32
            ),
            lax.dot_general(mlp_side, up_rows, contract_first, preferred_element_type=jnp.float32),
            lax.dot_general(
                attn_side, context_rows, contract_first, preferred_element_type=jnp.float32
            ),
            lax.dot_general(
                qkv_side, query_rows, contract_first, preferred_element_type=jnp.float32
            ),
            lax.dot_general(qkv_side, key_rows, contract_first, preferred_element_type=jnp.float32),
            lax.dot_general(
                qkv_side, value_rows, contract_first, preferred_element_type=jnp.float32
            ),
        ]
        return jnp.concatenate(pieces, 1)

    return grad_term


def per_device(
    tokens,
    cotangent,
    lengths,
    positions,
    norm_attn,
    w_query,
    w_key,
    w_value,
    w_output,
    norm_mlp,
    w_gate,
    w_up,
    w_down,
):
    row_total_count = tokens.shape[0]
    shard_rows = w_query.shape[0]
    query_width = w_query.shape[1]
    key_width = w_key.shape[1]
    hidden_width = w_gate.shape[1]
    inputs = tokens.astype(jnp.float32)
    valid_rows = (jnp.arange(row_total_count) < lengths[0]).astype(jnp.float32)[:, None]
    cosine_table, sine_table = rope_tables(positions)
    normed_attn = normalize(inputs)
    gain_attn_full, scaled_attn, query_pre, key_unrotated, value_pre = attention_inputs(
        normed_attn, norm_attn, w_query, w_key, w_value
    )
    query_rotated = (
        apply_rotary(
            query_pre.reshape(row_total_count, QUERY_HEADS, HEAD_SIZE), cosine_table, sine_table
        )
        .reshape(row_total_count, query_width)
        .astype(jnp.bfloat16)
    )
    key_rotated = (
        apply_rotary(
            key_unrotated.reshape(row_total_count, KEY_VALUE_HEADS, HEAD_SIZE),
            cosine_table,
            sine_table,
        )
        .reshape(row_total_count, key_width)
        .astype(jnp.bfloat16)
    )
    value_reduced = value_pre.astype(jnp.bfloat16)
    context, log_totals = attend(query_rotated, key_rotated, value_reduced)
    attn_out = lax.dot_general(
        context,
        lax.all_gather(w_output, ("wide", "narrow"), axis=0, tiled=True),
        contract_last,
        preferred_element_type=jnp.float32,
    )
    hidden = inputs + attn_out
    normed_mlp = normalize(hidden)
    gain_mlp_full, scaled_mlp, gate_proj, up_proj = mlp_inputs(normed_mlp, norm_mlp, w_gate, w_up)
    mixed_low = (gate_proj * jax.nn.sigmoid(gate_proj) * up_proj).astype(jnp.bfloat16)
    mlp_out = lax.dot_general(
        mixed_low,
        lax.all_gather(w_down, ("wide", "narrow"), axis=0, tiled=True),
        contract_last,
        preferred_element_type=jnp.float32,
    )
    output = (valid_rows * (hidden + mlp_out)).astype(jnp.bfloat16)
    grad_y = cotangent.astype(jnp.float32) * valid_rows
    grad_y_low = grad_y.astype(jnp.bfloat16)
    grad_cols = grad_y_low
    grad_mixed = jnp.dot(
        grad_cols,
        lax.all_gather(w_down, ("wide", "narrow"), axis=0, tiled=True),
        preferred_element_type=jnp.float32,
    )
    again_values = mlp_inputs(normed_mlp, norm_mlp, w_gate, w_up)
    gate_proj = again_values[2]
    up_proj = again_values[3]
    sigmoid_gate = jax.nn.sigmoid(gate_proj)
    grad_gate = (
        grad_mixed * up_proj * (sigmoid_gate * (1.0 + gate_proj * (1.0 - sigmoid_gate)))
    ).astype(jnp.bfloat16)
    grad_up = (grad_mixed * (gate_proj * sigmoid_gate)).astype(jnp.bfloat16)
    gate_rows = lax.all_gather(w_gate, ("wide", "narrow"), axis=0, tiled=True)
    up_rows = lax.all_gather(w_up, ("wide", "narrow"), axis=0, tiled=True)
    columns = lax.dot_general(
        grad_gate, gate_rows, contract_last, preferred_element_type=jnp.float32
    )
    columns = columns + lax.dot_general(
        grad_up, up_rows, contract_last, preferred_element_type=jnp.float32
    )
    grad_xn2 = columns
    grad_gain_mlp = jnp.sum(grad_xn2 * normed_mlp, axis=0)
    grad_hidden = grad_y + norm_back(grad_xn2 * gain_mlp_full, normed_mlp, hidden)
    grad_attn_low = grad_hidden.astype(jnp.bfloat16)
    grad_cols = grad_attn_low
    grad_context = jnp.dot(
        grad_cols,
        lax.all_gather(w_output, ("wide", "narrow"), axis=0, tiled=True),
        preferred_element_type=jnp.float32,
    )
    grad_context = grad_context.astype(jnp.bfloat16)
    grad_query_rot, gradient_key_rotated, grad_value_sum = attend_back(
        query_rotated, key_rotated, value_reduced, log_totals, grad_context
    )
    grad_query = (
        invert_rotary(
            grad_query_rot.reshape(row_total_count, QUERY_HEADS, HEAD_SIZE),
            cosine_table,
            sine_table,
        )
        .reshape(row_total_count, query_width)
        .astype(jnp.bfloat16)
    )
    grad_key = (
        invert_rotary(
            gradient_key_rotated.reshape(row_total_count, KEY_VALUE_HEADS, HEAD_SIZE),
            cosine_table,
            sine_table,
        )
        .reshape(row_total_count, key_width)
        .astype(jnp.bfloat16)
    )
    grad_value = grad_value_sum.astype(jnp.bfloat16)
    query_rows = lax.all_gather(w_query, ("wide", "narrow"), axis=0, tiled=True)
    key_rows = lax.all_gather(w_key, ("wide", "narrow"), axis=0, tiled=True)
    value_rows = lax.all_gather(w_value, ("wide", "narrow"), axis=0, tiled=True)
    columns = lax.dot_general(
        grad_query, query_rows, contract_last, preferred_element_type=jnp.float32
    )
    columns = columns + lax.dot_general(
        grad_key, key_rows, contract_last, preferred_element_type=jnp.float32
    )
    columns = columns + lax.dot_general(
        grad_value, value_rows, contract_last, preferred_element_type=jnp.float32
    )
    local_term = make_term(
        (grad_y_low, scaled_mlp, grad_attn_low, scaled_attn),
        (mixed_low, grad_gate, grad_up, context, grad_query, grad_key, grad_value),
    )
    all_sums = lax.psum_scatter(
        local_term(jnp.int32(0), lax.axis_size(("wide", "narrow")) * shard_rows),
        ("wide", "narrow"),
        scatter_dimension=0,
        tiled=True,
    )
    edges = [0]
    for width in (
        hidden_width,
        hidden_width,
        hidden_width,
        query_width,
        query_width,
        key_width,
        key_width,
    ):
        edges.append(edges[-1] + width)
    grad_w_down = all_sums[:, edges[0] : edges[1]]
    grad_w_gate = all_sums[:, edges[1] : edges[2]]
    grad_w_up = all_sums[:, edges[2] : edges[3]]
    grad_w_output = all_sums[:, edges[3] : edges[4]]
    grad_w_query = all_sums[:, edges[4] : edges[5]]
    grad_w_key = all_sums[:, edges[5] : edges[6]]
    grad_w_value = all_sums[:, edges[6] : edges[7]]
    grad_gain_attn = jnp.sum(columns * normed_attn, axis=0)
    grad_tokens = grad_hidden + norm_back(columns * gain_attn_full, normed_attn, inputs)
    grad_norm_attn, grad_norm_mlp = (
        lax.psum_scatter(grad_gain_attn, ("wide", "narrow"), scatter_dimension=0, tiled=True),
        lax.psum_scatter(grad_gain_mlp, ("wide", "narrow"), scatter_dimension=0, tiled=True),
    )
    return (
        output,
        grad_tokens,
        grad_norm_attn,
        grad_w_query,
        grad_w_key,
        grad_w_value,
        grad_w_output,
        grad_norm_mlp,
        grad_w_gate,
        grad_w_up,
        grad_w_down,
    )


MESH = pl.DeviceIdType.MESH
ANY = pl.BlockSpec(memory_space=pl.ANY)
VMEM = pl.BlockSpec(memory_space=pltpu.VMEM)

CHIPS, CORES = 4, 2

def place():
    w = lax.axis_index("wide"); n = lax.axis_index("narrow")
    return w // CORES, w % CORES, n

def chip_at(c, r):
    xb, yb, rx, ry = c % 2, c // 2, r % 2, r // 2
    return (yb + ry - 2 * yb * ry) * 2 + (xb + rx - 2 * xb * rx)


def remote(src, dst, send, recv, chip, core, z):
    return pltpu.make_async_remote_copy(src_ref=src, dst_ref=dst, send_sem=send, recv_sem=recv,
        device_id={"wide": chip * CORES + core, "narrow": z}, device_id_type=MESH)

def hello(partners):
    barrier = pltpu.get_barrier_semaphore()
    count = 0
    for cond, chip, core, z in partners:
        def sig(chip=chip, core=core, z=z):
            pl.semaphore_signal(barrier, inc=1, device_id={"wide": chip * CORES + core, "narrow": z}, device_id_type=MESH)
        if cond is None:
            sig(); count = count + 1
        else:
            pl.when(cond)(sig); count = count + jnp.where(cond, 1, 0)
    pl.semaphore_wait(barrier, count)

class Line:
    def __init__(self, nz, at, refs, send, recv, place_of):
        self.nz, self.at, self.refs, self.send, self.recv, self.place_of = nz, at, refs, send, recv, place_of

    def _copy(self, a, way, s, origin):
        c, k, n = self.at
        ref = self.place_of(self.refs[a], origin)
        return remote(ref, ref, self.send.at[a, way, s], self.recv.at[a, way, s], c, k, n + 1 if way == 0 else n - 1)

    def _origin(self, way, s):
        n = self.at[2]
        o = n - s if way == 0 else n + s
        return (n >= s) if way == 0 else (n + s <= self.nz - 1), jnp.clip(o, 0, self.nz - 1)

    def _sends(self, way, s):
        n = self.at[2]
        return self._origin(way, s)[0] & ((n < self.nz - 1) if way == 0 else (n > 0))

    def start(self, a, s, way):
        @pl.when(self._sends(way, s))
        def _(): self._copy(a, way, s, self._origin(way, s)[1]).start()

    def step(self, a, s, then=None):
        for way in range(2):
            came, origin = self._origin(way, s)
            @pl.when(came)
            def _(): self._copy(a, way, s - 1, origin).wait_recv()
            if s < self.nz - 1: self.start(a, s, way)
            if then is not None:
                @pl.when(came)
                def _(): then(origin)

    def finish(self, a):
        for s in range(self.nz - 1):
            for way in range(2):
                @pl.when(self._sends(way, s))
                def _(): self._copy(a, way, s, self._origin(way, s)[1]).wait_send()


def gather_kernel(nz, wq, wk, wv, wo, gains, wg, wu, wd, qkv, out, gain, gu, gd,
                  loc, sw_s, sw_r, z_s, z_r, f_s, f_r, p_s, p_r, h_s, h_r, d_s, d_r, e_s, e_r):
    c, k, n = at = place()
    rows, q = wq.shape
    kv = wk.shape[1]
    cols = gd.shape[-1]
    part = nz * rows
    half = part // 2
    kn = k * nz + n
    cx, cy, cd = (chip_at(c, r) for r in (1, 2, 3))
    hello([(None, cc, k, n) for cc in (cx, cy, cd)] + [(None, c, 1 - k, n), (n > 0, c, k, n - 1), (n < nz - 1, c, k, n + 1)])

    def mycols(w, cc): return w.at[:, pl.ds(pl.multiple_of(cc * cols, 128), cols)]
    def landing(i, cc): return gd.at[cc] if i == 2 else gu.at[cc, kn, :, pl.ds(i * cols, cols)]
    whole = (qkv, out, gain)
    def block(ref, z): return ref.at[pl.ds(pl.multiple_of(((c * CORES + k) * nz + z) * rows, rows), rows)]
    own = [pltpu.make_async_copy(wq, block(qkv, n).at[:, pl.ds(0, q)], loc.at[0]),
           pltpu.make_async_copy(wk, block(qkv, n).at[:, pl.ds(q, kv)], loc.at[1]),
           pltpu.make_async_copy(wv, block(qkv, n).at[:, pl.ds(q + kv, kv)], loc.at[2]),
           pltpu.make_async_copy(wo, block(out, n), loc.at[3]), pltpu.make_async_copy(gains, block(gain, n), loc.at[4])]
    ownff = [pltpu.make_async_copy(mycols(w, c), landing(i, c), loc.at[5 + i]) for i, w in enumerate((wg, wu, wd))]
    for cp in own + ownff: cp.start()
    swap = [[remote(mycols(w, cc), landing(i, c), sw_s.at[i, r], sw_r.at[i, r], cc, k, n) for r, cc in enumerate((cx, cy, cd))]
            for i, w in enumerate((wg, wu, wd))]
    for i in range(3):
        for cp in swap[i]: cp.start()
    for cp in own: cp.wait()

    line = Line(nz, at, whole, z_s, z_r, block)
    for a in range(3):
        for way in range(2): line.start(a, 0, way)

    def span(ref, cc, first, size):
        return ref.at[pl.ds(pl.multiple_of((cc * CORES + k) * part, part) + first, size)]
    plane = [[remote(span(ref, c, 0, part), span(ref, c, 0, part), p_s.at[a, r], p_r.at[a, r], cc, k, n) for r, cc in enumerate((cx, cy))]
             for a, ref in enumerate(whole)]
    across = [[remote(span(ref, cx, 0, half), span(ref, cx, 0, half), h_s.at[a, 0], h_r.at[a, 0], cy, k, n),
               remote(span(ref, cy, half, half), span(ref, cy, half, half), h_s.at[a, 1], h_r.at[a, 1], cx, k, n)]
              for a, ref in enumerate(whole)]
    cores = [[remote(span(ref, cc, 0, part), span(ref, cc, 0, part), d_s.at[a, r], d_r.at[a, r], c, 1 - k, n)
              for r, cc in enumerate((c, cx, cy, cd))] for a, ref in enumerate(whole)]

    def plane_start(a):
        for cp in plane[a] + cores[a][:1]: cp.start()
    def plane_next(a):
        for i in range(2):
            plane[a][i].wait_recv()
            across[a][i].start()
            cores[a][1 + i].start()
    def plane_last(a):
        for cp in across[a]: cp.wait_recv()
        cores[a][3].start()

    for s in range(1, nz):
        for a in range(3):
            line.step(a, s)
            if s == nz - 1: plane_start(a)

    ff = Line(nz, at, (gu,), f_s, f_r, lambda ref, z: ref.at[:, k * nz + z])
    def twin(z):
        ref = gu.at[:, k * nz + z]
        return remote(ref, ref, e_s.at[z], e_r.at[z], c, 1 - k, n)
    for i in range(2):
        ownff[i].wait()
        for cp in swap[i]: cp.wait_recv()
    for way in range(2): ff.start(0, 0, way)
    twin(n).start()
    plane_next(0)
    ff.step(0, 1, lambda z: twin(z).start())
    for a in (1, 2): plane_next(a)
    ff.step(0, 2, lambda z: twin(z).start())
    for a in range(3): plane_last(a)
    ownff[2].wait()
    for cp in swap[2]: cp.wait_recv()
    for s in range(3, nz): ff.step(0, s, lambda z: twin(z).start())
    for a in range(3):
        for cp in cores[a]: cp.wait_recv()
    for z in range(nz): twin(z).wait()
    for i in range(3):
        for cp in swap[i]: cp.wait_send()
    for a in range(3):
        line.finish(a)
        for cp in plane[a] + across[a] + cores[a]: cp.wait_send()
    ff.finish(0)


def gather_all(nz, wq, wk, wv, wo, gains, wg, wu, wd):
    rows = wq.shape[0]
    width = rows * CHIPS * CORES * nz
    cols = wg.shape[1] // CHIPS
    bf = jnp.bfloat16
    shape = jax.ShapeDtypeStruct
    dma = pltpu.SemaphoreType.DMA
    return pl.pallas_call(
        functools.partial(gather_kernel, nz),
        out_shape=(shape((width, wq.shape[1] + 2 * wk.shape[1]), bf), shape((width, wo.shape[1]), bf), shape((width, gains.shape[1]), bf),
                   shape((CHIPS, CORES * nz, rows, 2 * cols), bf), shape((CHIPS, rows, cols), bf)),
        in_specs=[VMEM] * 8, out_specs=(ANY,) * 5,
        scratch_shapes=[dma((8,)), dma((3, 3)), dma((3, 3)), dma((3, 2, nz)), dma((3, 2, nz)), dma((1, 2, nz)), dma((1, 2, nz)),
                        dma((3, 2)), dma((3, 2)), dma((3, 2)), dma((3, 2)), dma((3, 4)), dma((3, 4)), dma((nz,)), dma((nz,))],
        compiler_params=pltpu.CompilerParams(collective_id=0, has_side_effects=True),
        name="gather_all",
    )(wq, wk, wv, wo, gains, wg, wu, wd)


def add_into(dst, *srcs):
    rows = dst.shape[0]
    step = 16
    def body(i, carry):
        at = pl.ds(pl.multiple_of(i * step, step), step)
        total = dst[at, :].astype(jnp.float32)
        for s in srcs: total = total + s[at, :].astype(jnp.float32)
        dst[at, :] = total.astype(dst.dtype)
        return carry
    lax.fori_loop(0, rows // step, body, 0)


HALVES = ((0, 0), (0, 1), (1, 0), (2, 0), (1, 1), (2, 1), (3, 0), (3, 1))


def mlp_kernel(nz, x, gy, gu_hbm, gd_hbm, gx_parts, mlp_parts, mlp_cross, down_sums, sums,
               xs, gys, gu, gd, mix, ggu, gx, mo, xt, zin, load, ag_s, ag_r, rs_s, rs_r, mo_s, mo_r, out, core_s, core_r, ready, done, z_s, z_r):
    c, k, n = place()
    f32, bf16 = jnp.float32, jnp.bfloat16
    slots, width = x.shape
    half = slots // 2
    rows, cols = gd.shape[2:]
    tile = nz * rows
    hello([(None, chip_at(c, r), k, n) for r in (1, 2, 3)]
          + [(None, c, 1 - k, n), (n > 0, c, k, n - 1), (n < nz - 1, c, k, n + 1)])
    def half_of(ref, h): return ref.at[pl.ds(h * half, half)]
    index = {place_: i for i, place_ in enumerate(HALVES)}
    sends = {}
    for h in range(2):
        for r in (1, 2):
            i = index[r, h]
            sends[i] = remote(half_of(x, h), xs.at[i], ag_s.at[i], ag_r.at[i], chip_at(c, r), k, n)
            if h == 0: sends[i].start()
    loads = [pltpu.make_async_copy(half_of(x, h), xs.at[h], load.at[h]) for h in range(2)]
    loads += [pltpu.make_async_copy(half_of(gy.at[r], h), gys.at[i], load.at[2 + i]) for i, (r, h) in enumerate(HALVES)]
    for cp in loads: cp.start()
    def weights(col, w, j):
        return [pltpu.make_async_copy(a.at[:, :, :, pl.ds(first + col, w)], b.at[:, :, :, pl.ds(first + col, w)], load.at[10 + 3 * j + i])
                for i, (a, b, first) in enumerate(((gu_hbm, gu, 0), (gu_hbm, gu, cols), (gd_hbm, gd, 0)))]
    for j in range(-(-cols // 256)):
        for cp in weights(j * 256, min(256, cols - j * 256), j): cp.start()
    relays = {index[3, 0]: (index[1, 0], 2), index[3, 1]: (index[2, 1], 1)}
    relays = {i: remote(xs.at[j], xs.at[i], ag_s.at[i], ag_r.at[i], chip_at(c, r), k, n) for i, (j, r) in relays.items()}
    for cp in loads: cp.wait()

    def columns(ref, at, size):
        return ref[:, :, :, pl.ds(at, size)].reshape(width, size)

    def some_rows(ref, i): return ref[i].reshape(tile, ref.shape[3])

    def to_owner(src, dst, i, s_s, s_r):
        r, h = HALVES[i]
        return remote(src.at[i], half_of(dst.at[r], h), s_s.at[i], s_r.at[i], chip_at(c, r), k, n)

    def kept(src, dst, i, j):
        return pltpu.make_async_copy(src.at[i], half_of(dst, HALVES[i][1]), out.at[j])

    def block(r, carry):
        two = pl.ds(2 * r, 2)
        @pl.when(r == 1)
        def _():
            for i in (2, 3): sends[i].wait_recv()
            relays[index[3, 0]].start()
        @pl.when(r == 3)
        def _():
            for cp in relays.values(): cp.wait_recv()
        def both(ref): return ref[two].reshape(slots, ref.shape[2])
        def put(ref, at, v): ref[two, :, at] = v.astype(bf16).reshape(2, half, v.shape[1])
        def chunk(col, w, j):
            @pl.when(r == 0)
            def _():
                for cp in weights(col, w, j): cp.wait()
            tokens = both(xs)
            hg = jnp.dot(tokens, columns(gu, col, w), preferred_element_type=f32)
            hu = jnp.dot(tokens, columns(gu, cols + col, w), preferred_element_type=f32)
            gm = jnp.dot(both(gys), columns(gd, col, w), preferred_element_type=f32)
            for q in range(w // 128):
                gate, up, g = (t[:, 128 * q : 128 * q + 128] for t in (hg, hu, gm))
                sg = 1.0 / (1.0 + jnp.exp(-gate))
                act = gate * sg
                put(mix, pl.ds(col + 128 * q, 128), act * up)
                put(ggu, pl.ds(col + 128 * q, 128), g * up * (sg * (1.0 + gate * (1.0 - sg))))
                put(ggu, pl.ds(cols + col + 128 * q, 128), g * act)
        def pair(j, carry):
            chunk(pl.multiple_of(j * 256, 256), 256, j)
            return carry
        lax.fori_loop(0, cols // 256, pair, 0)
        if cols % 256: chunk(cols // 256 * 256, cols % 256, cols // 256)
        @pl.when(r == 0)
        def _():
            for i in (4, 5): sends[i].start()
        @pl.when(r == 1)
        def _():
            for i in (4, 5): sends[i].wait_recv()
            relays[index[3, 1]].start()
        def back(i, carry):
            at = pl.ds(pl.multiple_of(i * tile, 128), tile)
            put(gx, at, lax.dot_general(both(ggu), some_rows(gu, i), contract_last, preferred_element_type=f32))
            return carry
        lax.fori_loop(0, CHIPS * CORES, back, 0)
        for t in range(CHIPS):
            @pl.when(r == t)
            def _():
                for i in (2 * t, 2 * t + 1):
                    (to_owner(gx, gx_parts, i, rs_s, rs_r) if t else kept(gx, gx_parts.at[0], i, i)).start()
        def down(i, carry):
            at = pl.ds(pl.multiple_of(i * tile, 128), tile)
            put(mo, at, lax.dot_general(both(mix), some_rows(gd, i), contract_last, preferred_element_type=f32))
            return carry
        lax.fori_loop(0, CHIPS * CORES, down, 0)
        for t in range(CHIPS):
            @pl.when(r == t)
            def _():
                for i in (2 * t, 2 * t + 1):
                    (kept(mo, mlp_parts.at[0], i, 2 + i) if t == 0 else kept(mo, mlp_cross, i, i - 2) if t == 3
                     else to_owner(mo, mlp_parts, i, mo_s, mo_r)).start()
        return carry
    lax.fori_loop(0, CHIPS, block, 0)

    pl.semaphore_signal(ready, inc=1, device_id={"wide": c * CORES + 1 - k, "narrow": n}, device_id_type=MESH)
    pl.semaphore_wait(ready, 1)
    sent, came = pl.ds(0, CHIPS), pl.ds(CHIPS, CHIPS)
    pairs = ((gys, mix, gd), (xs, ggu, gu))

    def tiles(total): return [(t * 256, min(256, total - t * 256)) for t in range(-(-total // 256))]

    def to_core(i, col, w, sem):
        ref = pairs[i][2]
        return remote(ref.at[sent, :, :, pl.ds(col, w)], ref.at[came, :, :, pl.ds(col, w)], core_s.at[sem], core_r.at[sem], c, 1 - k, n)

    def to_sums(t): return pltpu.make_async_copy(gu.at[CHIPS + t], sums.at[:, t], done.at[t])

    def each(i, body):
        total, base = pairs[i][2].shape[-1], 0 if i == 0 else len(tiles(cols))
        def step(j, carry):
            body(pl.multiple_of(j * 256, 256), 256, base + j)
            return carry
        lax.fori_loop(0, total // 256, step, 0)
        if total % 256: body(total // 256 * 256, total % 256, base + total // 256)

    def terms(i, kk, use):
        src, right, ref = pairs[i]
        for t in range(CHIPS):
            at = pl.ds(pl.multiple_of((t * CORES + kk) * tile, 128), tile)
            for r in range(CHIPS):
                xt[t * tile : (t + 1) * tile, r * slots : (r + 1) * slots] = src[2 * r : 2 * r + 2, :, at].reshape(slots, tile).T
        def body(col, w, sem):
            b = right[:, :, pl.ds(col, w)].reshape(CHIPS * slots, w)
            use(i, col, w, sem, jnp.dot(xt[...], b, preferred_element_type=f32).reshape(CHIPS, nz, rows, w))
        each(i, body)

    def theirs(i, col, w, sem, v):
        pairs[i][2][sent, :, :, pl.ds(col, w)] = v.astype(bf16)
        to_core(i, col, w, sem).start()

    def ours(i, col, w, sem, v):
        to_core(i, col, w, sem).wait_recv()
        ref = pairs[i][2]
        here = (came, slice(None), slice(None), pl.ds(col, w))
        ref[here] = (ref[here].astype(f32) + v).astype(bf16)

    def hop(way, j):
        return remote(gd.at[came, j], zin.at[way, jnp.clip(j - n - 1 if way == 0 else n - 1 - j, 0, nz - 2)],
                      z_s.at[way, j], z_r.at[way, j], c, k, n + 1 if way == 0 else n - 1)

    def along(t):
        for way in range(2):
            hops = n if way == 0 else nz - 1 - n
            j = jnp.clip(n + nz - 1 - t if way == 0 else t - hops, 0, nz - 1)
            @pl.when((hops > 0) & (t >= hops))
            def _():
                hop(way, j).wait_recv()
                for i in range(CHIPS):
                    add_into(gd.at[CHIPS + i, j], zin.at[way, jnp.clip(j - n if way == 0 else n - j, 0, nz - 2), i])
            @pl.when((t >= hops) & (j != n))
            def _(): hop(way, j).start()

    terms(0, 1 - k, theirs)
    terms(0, k, ours)
    along(0)
    terms(1, 1 - k, theirs)
    along(1)
    terms(1, k, ours)
    for t in range(CHIPS): to_sums(t).start()
    for t in range(2, nz): along(t)
    own_down = pltpu.make_async_copy(gd.at[came, n], down_sums, done.at[CHIPS])
    own_down.start()

    for cp in (*sends.values(), *relays.values()): cp.wait_send()
    for i in range(2):
        kept(gx, gx_parts.at[0], i, i).wait()
        kept(mo, mlp_parts.at[0], i, 2 + i).wait()
        kept(mo, mlp_cross, 6 + i, 4 + i).wait()
    for i in range(2): each(i, lambda col, w, sem: to_core(i, col, w, sem).wait_send())
    for t in range(CHIPS): to_sums(t).wait()
    for j in range(nz):
        for way in range(2):
            @pl.when(n < j if way == 0 else n > j)
            def _(): hop(way, j).wait_send()
    own_down.wait()
    for i in range(2, 6): to_owner(mo, mlp_parts, i, mo_s, mo_r).wait()
    for i in range(2, 8): to_owner(gx, gx_parts, i, rs_s, rs_r).wait()


def mlp_all(nz, x, gy, gu, gd):
    slots, width = x.shape
    rows, cols = gd.shape[2:]
    bf, dma, vm = jnp.bfloat16, pltpu.SemaphoreType.DMA, pltpu.VMEM
    def blocks(w): return jax.ShapeDtypeStruct((CHIPS, slots, w), bf)
    def halves(w): return vm((2 * CHIPS, slots // 2, w), bf)
    tiles = -(-cols // 256)
    flops = 2 * 9 * CHIPS * slots * width * cols
    return pl.pallas_call(
        functools.partial(mlp_kernel, nz),
        out_shape=(blocks(width), jax.ShapeDtypeStruct((3, slots, width), bf), jax.ShapeDtypeStruct((slots, width), bf),
                   jax.ShapeDtypeStruct((CHIPS, rows, cols), bf), jax.ShapeDtypeStruct((nz, CHIPS, rows, 2 * cols), bf)),
        in_specs=[ANY] * 4, out_specs=(ANY,) * 5,
        scratch_shapes=[halves(width), halves(width), vm(gu.shape, bf), vm(gd.shape, bf), halves(cols), halves(2 * cols), halves(width),
                        halves(width), vm((CHIPS * nz * rows, CHIPS * slots), bf), vm((2, nz - 1, CHIPS, rows, cols), bf), dma((10 + 3 * tiles,)), dma((8,)), dma((8,)), dma((8,)), dma((8,)),
                        dma((8,)), dma((8,)), dma((6,)), dma((3 * tiles,)), dma((3 * tiles,)), pltpu.SemaphoreType.REGULAR, dma((CHIPS + 1,)), dma((2, nz)), dma((2, nz))],
        compiler_params=pltpu.CompilerParams(collective_id=1, has_side_effects=True, vmem_limit_bytes=62 << 20),
        cost_estimate=pl.CostEstimate(flops=flops, bytes_accessed=60 << 20, transcendentals=CHIPS * slots * cols),
        name="mlp_all",
    )(x, gy, gu, gd)


PAIR = 2 * HEAD_SIZE
REPEAT = QUERY_HEADS // KEY_VALUE_HEADS
PAIRS = REPEAT // 2


def lane_tables(positions):
    cosine, sine = rope_tables(positions)
    first = jnp.arange(HEAD_SIZE) < HEAD_SIZE // 2
    low, high = jnp.where(first, -sine, 0.0), jnp.where(first, 0.0, sine)
    return jnp.stack([jnp.concatenate([t, t], 1) for t in (cosine, low, high)])


def rotate(u, tables):
    half = HEAD_SIZE // 2
    return u * tables[0] + pltpu.roll(u, PAIR - half, 1) * tables[1] + pltpu.roll(u, half, 1) * tables[2]


def unrotate(g, tables):
    half = HEAD_SIZE // 2
    return g * tables[0] + pltpu.roll(g * tables[2], PAIR - half, 1) + pltpu.roll(g * tables[1], half, 1)


def row_blocks(slots):
    return [(at, min(128, slots - at), at + 128) for at in range(0, slots, 128)]


def causal(s, below, fill):
    clear = s.shape[1] - 128
    last = jnp.where(below, s[:, clear:], fill)
    return jnp.concatenate([s[:, :clear], last], 1) if clear else last


def scaled(x, gain):
    return (x * lax.rsqrt(jnp.mean(x * x, axis=-1, keepdims=True) + norm_eps) * gain).astype(jnp.bfloat16)


def attend_kernel(nz, tok, gain1, gain2, tab_ref, wq_hbm, wo_hbm, gy, gd_own,
                  qr_ref, k_out, v_out, lse_ref, ctx_ref, xn1, hidden, xn2, gys, gd, ks, vs, wq, wo, qkv,
                  load, loc, g_s, g_r, h_s, h_r, f_s, f_r, e_s, e_r):
    g = pl.program_id(0)
    f32, bf16 = jnp.float32, jnp.bfloat16
    slots, width = tok.shape
    c, k, n = at = place()
    mine = [pltpu.make_async_copy(gd_own, gd.at[:, k * nz + n], loc.at[0]), pltpu.make_async_copy(gy, gys.at[0], loc.at[1])]
    line = Line(nz, at, (gd,), f_s, f_r, lambda ref, z: ref.at[:, k * nz + z])
    half = slots // 2
    sends = [remote(gy, gys.at[r], g_s.at[r - 1], g_r.at[r - 1], chip_at(c, r), k, n) for r in (1, 2)]
    relays = [remote(gys.at[1, pl.ds(0, half)], gys.at[3, pl.ds(0, half)], h_s.at[0], h_r.at[0], chip_at(c, 2), k, n),
              remote(gys.at[2, pl.ds(half, half)], gys.at[3, pl.ds(half, half)], h_s.at[1], h_r.at[1], chip_at(c, 1), k, n)]
    def twin(z):
        ref = gd.at[:, k * nz + z]
        return remote(ref, ref, e_s.at[z], e_r.at[z], c, 1 - k, n)
    def load_q(j):
        at = pl.ds(j * 256 if isinstance(j, int) else pl.multiple_of(j * 256, 256), 256)
        return pltpu.make_async_copy(wq_hbm.at[:, at], wq.at[:, at], load.at[j])
    @pl.when(g == 0)
    def _():
        hello([(None, chip_at(c, r), k, n) for r in (1, 2)]
              + [(None, c, 1 - k, n), (n > 0, c, k, n - 1), (n < nz - 1, c, k, n + 1)])
        for cp in mine + sends: cp.start()
        for j in range(wq.shape[1] // 256): load_q(j).start()
        pltpu.make_async_copy(wo_hbm, wo, loc.at[2]).start()
        mine[0].wait()
        for way in range(2): line.start(0, 0, way)
        twin(n).start()
        def norm(i, carry):
            at = pl.ds(pl.multiple_of(i * 16, 16), 16)
            xn1[at, :] = scaled(tok[at, :].astype(f32), gain1[...])
            return carry
        lax.fori_loop(0, slots // 16, norm, 0)
        def project(j, carry):
            load_q(j).wait()
            at = pl.ds(pl.multiple_of(j * 256, 256), 256)
            qkv[:, at] = jnp.dot(xn1[...], wq[:, at], preferred_element_type=f32)
            return carry
        lax.fori_loop(0, wq.shape[1] // 256, project, 0)
    @pl.when(g == KEY_VALUE_HEADS - 2)
    def _(): line.step(0, 1, lambda z: twin(z).start())
    @pl.when(g == 0)
    def _():
        ks[...] = jnp.zeros_like(ks)
        vs[...] = jnp.zeros_like(vs)
    lane = lax.broadcasted_iota(jnp.int32, (slots, PAIR), 1)
    tables = (tab_ref[0], tab_ref[1], tab_ref[2])
    first = QUERY_HEADS * HEAD_SIZE
    def pair_at(at): return pl.ds(pl.multiple_of(at, PAIR), PAIR)
    key = rotate(qkv[:, pair_at(first + g // 2 * PAIR)], tables)
    val = qkv[:, pair_at(first + KEY_VALUE_HEADS * HEAD_SIZE + g // 2 * PAIR)]
    odd = g % 2 == 1
    for x, own, stack, scale in ((key, k_out, ks, HEAD_SIZE ** -0.5), (val, v_out, vs, 1.0)):
        x = jnp.where(lane < HEAD_SIZE, jnp.where(odd, pltpu.roll(x, HEAD_SIZE, 1), x), 0.0).astype(bf16)
        own[0] = x
        x = x.astype(f32) * scale
        stack[0, 0:slots, :] = x.astype(bf16)
        stack[1, 0:slots, :] = pltpu.roll(x, HEAD_SIZE, 1).astype(bf16)
    for start, size, keys in row_blocks(slots):
        below = lax.broadcasted_iota(jnp.int32, (size, 128), 0) >= lax.broadcasted_iota(jnp.int32, (size, 128), 1)
        lse = jnp.zeros((size, PAIR), f32)
        here = lane[0:size]
        for p in range(PAIRS):
            span = slice(p * PAIR, (p + 1) * PAIR)
            rows = slice(start, start + size)
            q = rotate(qkv[rows, pair_at(g * REPEAT * HEAD_SIZE + p * PAIR)], tuple(t[rows] for t in tables)).astype(bf16)
            qr_ref[rows, span] = q
            ctx = jnp.zeros((size, PAIR), f32)
            for h in range(2):
                s = lax.dot_general(q, ks[h, 0:keys, :], contract_last, preferred_element_type=f32)
                s = causal(s, below, masked_score)
                peak = jnp.max(s, axis=-1, keepdims=True)
                e = jnp.exp(s - peak)
                total = jnp.sum(e, axis=-1, keepdims=True)
                lse = jnp.where(here == 2 * p + h, peak + jnp.log(total), lse)
                probs = (e * (1.0 / total)).astype(bf16)
                ctx = ctx + jnp.dot(probs, vs[h, 0:keys, :], preferred_element_type=f32)
            ctx_ref[rows, pair_at(g * REPEAT * HEAD_SIZE + p * PAIR)] = ctx.astype(bf16)
        lse_ref[0, start : start + size, :] = lse
    @pl.when(g == KEY_VALUE_HEADS - 1)
    def _():
        for cp in sends: cp.wait_recv()
        for cp in relays: cp.start()
        line.step(0, 2, lambda z: twin(z).start())
        pltpu.make_async_copy(wo_hbm, wo, loc.at[2]).wait()
        def project(j, carry):
            at = pl.ds(pl.multiple_of(j * 256, 256), 256)
            hidden[:, at] = tok[:, at].astype(f32) + lax.dot_general(ctx_ref[...], wo[at, :], contract_last, preferred_element_type=f32)
            return carry
        lax.fori_loop(0, width // 256, project, 0)
        def norm(i, carry):
            at = pl.ds(pl.multiple_of(i * 16, 16), 16)
            xn2[at, :] = scaled(hidden[at, :], gain2[...])
            return carry
        lax.fori_loop(0, slots // 16, norm, 0)
        for s in range(3, nz): line.step(0, s, lambda z: twin(z).start())
        for cp in relays: cp.wait()
        for z in range(nz): twin(z).wait()
        for cp in sends: cp.wait_send()
        mine[1].wait()
        line.finish(0)


def attend_all(nz, tokens, gain1, gain2, tables, w_qkv, w_out, gy, gd_own):
    slots, width = tokens.shape
    dma, vm = pltpu.SemaphoreType.DMA, pltpu.VMEM
    bf16, f32 = jnp.bfloat16, jnp.float32
    keys = -(-slots // 128) * 128
    heads = QUERY_HEADS * HEAD_SIZE
    shape = jax.ShapeDtypeStruct
    def fixed(*dims): return pl.BlockSpec(dims, lambda g: (0,) * len(dims))
    per_head = pl.BlockSpec((1, slots, PAIR), lambda g: (g, 0, 0))
    per_head_shape = (KEY_VALUE_HEADS, slots, PAIR)
    return pl.pallas_call(
        functools.partial(attend_kernel, nz),
        grid=(KEY_VALUE_HEADS,),
        out_shape=(shape((slots, heads), bf16), shape(per_head_shape, bf16), shape(per_head_shape, bf16), shape(per_head_shape, f32),
                   shape((slots, heads), bf16), shape((slots, width), bf16), shape((slots, width), f32), shape((slots, width), bf16),
                   shape((CHIPS,) + gy.shape, bf16), shape((CHIPS, CORES * nz) + gd_own.shape[1:], bf16)),
        in_specs=[fixed(slots, width), fixed(1, width), fixed(1, width), fixed(3, slots, PAIR), ANY, ANY, fixed(*gy.shape), fixed(*gd_own.shape)],
        out_specs=(pl.BlockSpec((slots, REPEAT * HEAD_SIZE), lambda g: (0, g)), per_head, per_head, per_head,
                   fixed(slots, heads), fixed(slots, width), fixed(slots, width), fixed(slots, width), ANY, ANY),
        scratch_shapes=[vm((2, keys, PAIR), bf16), vm((2, keys, PAIR), bf16), vm(w_qkv.shape, bf16), vm(w_out.shape, bf16),
                        vm((slots, w_qkv.shape[1]), f32), dma((w_qkv.shape[1] // 256,)), dma((3,)), dma((2,)), dma((2,)), dma((2,)), dma((2,)),
                        dma((1, 2, nz)), dma((1, 2, nz)), dma((nz,)), dma((nz,))],
        compiler_params=pltpu.CompilerParams(collective_id=4, has_side_effects=True, vmem_limit_bytes=56 << 20),
        cost_estimate=pl.CostEstimate(flops=4 * slots * width * heads, bytes_accessed=40 << 20, transcendentals=QUERY_HEADS * slots * slots),
        name="attend",
    )(tokens, gain1, gain2, tables, w_qkv, w_out, gy, gd_own)


def attend_back_kernel(q_ref, k_ref, v_ref, lse_ref, gc_ref, tab_ref, part, gq_ref, gk_ref, gv_ref, crossed,
                       ks, kt, vt, ds, pr, qs, gs, s_s, s_r):
    g = pl.program_id(0)
    c, k, n = place()
    copy = remote(part, crossed, s_s, s_r, chip_at(c, 3), k, n)
    @pl.when(g == 0)
    def _():
        hello([(None, chip_at(c, 3), k, n)])
        copy.start()
    f32, bf16 = jnp.float32, jnp.bfloat16
    slots = q_ref.shape[0]
    scale = HEAD_SIZE ** -0.5
    @pl.when(g == 0)
    def _():
        for ref in (ks, kt, vt, ds, pr): ref[...] = jnp.zeros_like(ref)
    lane = lax.broadcasted_iota(jnp.int32, (slots, PAIR), 1)
    tables = (tab_ref[0], tab_ref[1], tab_ref[2])
    key, val = k_ref[0].astype(f32), v_ref[0].astype(f32)
    for stack, x in ((ks, key * scale), (kt, key), (vt, val)):
        stack[0, 0:slots, :] = x.astype(bf16)
        stack[1, 0:slots, :] = pltpu.roll(x, HEAD_SIZE, 1).astype(bf16)
    for at, size, keys in row_blocks(slots):
        rows = slice(at, at + size)
        below = lax.broadcasted_iota(jnp.int32, (size, 128), 0) >= lax.broadcasted_iota(jnp.int32, (size, 128), 1)
        lse = lse_ref[0, rows, :]
        for p in range(PAIRS):
            span = slice(p * PAIR, (p + 1) * PAIR)
            deep = slice(p * slots + at, p * slots + at + size)
            q, gc = q_ref[rows, span], gc_ref[rows, span]
            qs[deep, :] = q
            gs[deep, :] = gc
            gq = jnp.zeros((size, PAIR), f32)
            for h in range(2):
                s = lax.dot_general(q, ks[h, 0:keys, :], contract_last, preferred_element_type=f32)
                e = jnp.exp(s - lse[:, 2 * p + h : 2 * p + h + 1])
                probs = causal(e, below, 0.0)
                pr[h, deep, 0:keys] = probs.astype(bf16)
                gp = lax.dot_general(gc, vt[h, 0:keys, :], contract_last, preferred_element_type=f32)
                inner = jnp.sum(gp * probs, axis=-1, keepdims=True)
                grad = (probs * (gp - inner) * scale).astype(bf16)
                ds[h, deep, 0:keys] = grad
                gq = gq + jnp.dot(grad, kt[h, 0:keys, :], preferred_element_type=f32)
            gq_ref[rows, span] = unrotate(gq, tuple(t[rows] for t in tables)).astype(bf16)
    for src, right, out, turn in ((ds, qs, gk_ref, True), (pr, gs, gv_ref, False)):
        lo, hi = (
            lax.dot_general(src[h], right[...], contract_first, preferred_element_type=f32)[0:slots] for h in range(2)
        )
        x = jnp.where(lane < HEAD_SIZE, lo + pltpu.roll(hi, HEAD_SIZE, 1), 0.0)
        if turn: x = unrotate(x, tables)
        @pl.when(g % 2 == 0)
        def _(): out[...] = x
        @pl.when(g % 2 == 1)
        def _(): out[...] = jnp.where(lane < HEAD_SIZE, out[...], pltpu.roll(x, HEAD_SIZE, 1))
    @pl.when(g == KEY_VALUE_HEADS - 1)
    def _(): copy.wait()


def attend_back_all(q, k, v, lse, grad_context, tables, part):
    slots = q.shape[0]
    wide = REPEAT * HEAD_SIZE
    bf16, f32, vm = jnp.bfloat16, jnp.float32, pltpu.VMEM
    keys = -(-slots // 128) * 128
    shape = jax.ShapeDtypeStruct
    per_head = pl.BlockSpec((1, slots, PAIR), lambda g: (g, 0, 0))
    wide_spec = pl.BlockSpec((slots, wide), lambda g: (0, g))
    two = pl.BlockSpec((slots, PAIR), lambda g: (0, g // 2))
    return pl.pallas_call(
        attend_back_kernel,
        grid=(KEY_VALUE_HEADS,),
        out_shape=(shape((slots, QUERY_HEADS * HEAD_SIZE), bf16), shape((slots, KEY_VALUE_HEADS * HEAD_SIZE), f32),
                   shape((slots, KEY_VALUE_HEADS * HEAD_SIZE), f32), shape(part.shape, part.dtype)),
        in_specs=[wide_spec, per_head, per_head, per_head, wide_spec, pl.BlockSpec((3, slots, PAIR), lambda g: (0, 0, 0)), ANY],
        out_specs=(wide_spec, two, two, ANY),
        scratch_shapes=[vm((2, keys, PAIR), bf16)] * 3 + [vm((2, PAIRS * slots, keys), bf16)] * 2 + [vm((PAIRS * slots, PAIR), bf16)] * 2
        + [pltpu.SemaphoreType.DMA] * 2,
        compiler_params=pltpu.CompilerParams(collective_id=2, has_side_effects=True, vmem_limit_bytes=40 << 20),
        name="attend_back",
    )(q, k, v, lse, grad_context, tables, part)


class Many:
    def __init__(self, copies): self.copies = copies
    def start(self):
        for cp in self.copies: cp.start()
    def wait(self):
        for cp in self.copies: cp.wait()


def columns_home(src, outs, c, k, n, send, recv, loc):
    cols = src.shape[-1] // len(outs)
    at = pl.ds(pl.multiple_of(c * cols, 128), cols)
    local, away = [], []
    for m, out in enumerate(outs):
        local.append(pltpu.make_async_copy(src.at[c, :, pl.ds(m * cols, cols)], out.at[:, at], loc))
        for r in (1, 2, 3):
            cc = chip_at(c, r)
            away.append(remote(src.at[cc, :, pl.ds(m * cols, cols)], out.at[:, at], send.at[m, r - 1], recv.at[m, r - 1], cc, k, n))
    return away + [Many(local)]


def gradient_kernel(nz, gal_hbm, ctx_hbm, xn_hbm, gq_hbm, wq_hbm, tok_hbm, gh_hbm, down, gain, gain_mlp,
                    out0, out1, out2, grad_tokens, down_out,
                    took0, took1, took2, away0, away1, away2, zbuf0, zbuf1, zbuf2, gal, ctx, xn, gq, wq, tok, gh, gx, xt, gain_row,
                    core_s, core_r, half_s, half_r, main_s, main_r, z_s, z_r, ff_s, ff_r, load, loc):
    f32, bf16 = jnp.float32, jnp.bfloat16
    items = 3
    outs, took, away, zbuf = (out0, out1, out2), (took0, took1, took2), (away0, away1, away2), (zbuf0, zbuf1, zbuf2)
    c, k, n = place()
    left, right = n > 0, n < nz - 1
    cx, cy, cd = (chip_at(c, r) for r in (1, 2, 3))
    loads = [pltpu.make_async_copy(a, b, load.at[i]) for i, (a, b) in enumerate(
        ((gal_hbm, gal), (ctx_hbm, ctx), (xn_hbm, xn), (gq_hbm, gq), (wq_hbm, wq), (tok_hbm, tok), (gh_hbm, gh)))]
    for cp in loads: cp.start()
    hello([(None, cc, k, n) for cc in (cx, cy, cd)] + [(None, c, 1 - k, n), (left, c, k, n - 1), (right, c, k, n + 1)])
    slots, width = gal.shape
    rows = outs[0].shape[0]
    part = nz * rows
    half = part // 2
    top, low = pl.ds(0, half), pl.ds(half, half)
    def arrive(a, at, size): return zbuf[a].at[pl.ds(at, size)]
    swap = [remote(away[a], took[a], core_s.at[a], core_r.at[a], c, 1 - k, n) for a in range(items)]
    cross = [[remote(took[a].at[cd, top], arrive(a, 2 * part, half), half_s.at[a, 0], half_r.at[a, 0], cx, k, n),
              remote(took[a].at[cd, low], arrive(a, 2 * part + half, half), half_s.at[a, 1], half_r.at[a, 1], cy, k, n)]
             for a in range(items)]
    main = [[remote(took[a].at[cx, top], arrive(a, 0, half), main_s.at[a, 0], main_r.at[a, 0], cx, k, n),
             remote(took[a].at[cy, low], arrive(a, part + half, half), main_s.at[a, 1], main_r.at[a, 1], cy, k, n),
             remote(took[a].at[cx, low], arrive(a, half, half), main_s.at[a, 2], main_r.at[a, 2], cx, k, n),
             remote(took[a].at[cy, top], arrive(a, part, half), main_s.at[a, 3], main_r.at[a, 3], cy, k, n)]
            for a in range(items)]

    def products(left_side, right_side, kk, put):
        for t in range(CHIPS):
            at = pl.ds(pl.multiple_of((t * CORES + kk) * part, 128), part)
            xt[t * part : (t + 1) * part, :] = left_side[:, at].T
        def step(j, carry):
            at = pl.ds(pl.multiple_of(j * 256, 256), 256)
            put(at, jnp.dot(xt[...], right_side[:, at], preferred_element_type=f32).reshape(CHIPS, part, 256))
            return carry
        lax.fori_loop(0, right_side.shape[1] // 256, step, 0)

    def theirs(a, left_side, right_side):
        def put(at, v): away[a][:, :, at] = v.astype(bf16)
        products(left_side, right_side, 1 - k, put)
        swap[a].start()

    def ours(a, left_side, right_side):
        swap[a].wait_recv()
        def put(at, v): took[a][:, :, at] = (took[a][:, :, at].astype(f32) + v).astype(bf16)
        products(left_side, right_side, k, put)
        for cp in cross[a]: cp.start()

    def input_gradient():
        loads[4].wait()
        def step(j, carry):
            at = pl.ds(pl.multiple_of(j * 256, 256), 256)
            gx[:, at] = lax.dot_general(gq[...], wq[at, :], contract_last, preferred_element_type=f32)
            return carry
        lax.fori_loop(0, width // 256, step, 0)

    def input_norm():
        for cp in loads[5:]: cp.wait()
        def step(j, total):
            at = pl.ds(pl.multiple_of(j * 16, 16), 16)
            x, g = tok[at, :].astype(f32), gx[at, :]
            scale = lax.rsqrt(jnp.mean(x * x, axis=-1, keepdims=True) + norm_eps)
            hat = x * scale
            g1 = g * gain[...]
            gh[at, :] = gh[at, :] + scale * (g1 - hat * jnp.mean(g1 * hat, axis=-1, keepdims=True))
            t = g * hat
            return total + t[0:8] + t[8:16]
        total = lax.fori_loop(0, slots // 16, step, jnp.zeros((8, width), f32))
        return jnp.sum(total, axis=0, keepdims=True)

    def gains_swap(of_attn):
        row = lax.broadcasted_iota(jnp.int32, (128, part), 0)
        def columns_of(t, kk):
            at = pl.ds(pl.multiple_of((t * CORES + kk) * part, 128), part)
            return jnp.where(row == 0, gain_row[0:1, at], jnp.where(row == 1, gain_mlp[0:1, at], 0.0)).T
        gain_row[0:1, :] = of_attn
        for t in range(CHIPS): away[2][t] = columns_of(t, 1 - k).astype(bf16)
        swap[2].start()
        swap[2].wait_recv()
        for t in range(CHIPS): took[2][t] = (took[2][t].astype(f32) + columns_of(t, k)).astype(bf16)
        for cp in cross[2]: cp.start()

    def relay(a):
        cross[a][0].wait_recv()
        add_into(took[a].at[cy, top], arrive(a, 2 * part, half))
        main[a][3].start()
        cross[a][1].wait_recv()
        add_into(took[a].at[cx, low], arrive(a, 2 * part + half, half))
        for i in (2, 0, 1): main[a][i].start()

    def mine(a):
        for cp in main[a]: cp.wait_recv()
        add_into(took[a].at[c], arrive(a, 0, part), arrive(a, part, part))

    def slot(a, way, j): return arrive(a, pl.multiple_of(2 * part + 2 * half + (way * nz + j) * rows, rows), rows)
    def piece(a, j): return took[a].at[c, pl.ds(pl.multiple_of(j * rows, rows), rows)]
    def hop(a, way, j):
        return remote(piece(a, j), slot(a, way, j), z_s.at[a, way, j], z_r.at[a, way, j], c, k, n + 1 if way == 0 else n - 1)

    def along(some):
        for t in range(nz):
            for way in range(2):
                hops = n if way == 0 else nz - 1 - n
                j = jnp.clip(n + nz - 1 - t if way == 0 else t - hops, 0, nz - 1)
                for a in some:
                    @pl.when((hops > 0) & (t >= hops))
                    def _():
                        hop(a, way, j).wait_recv()
                        add_into(piece(a, j), slot(a, way, j))
                    @pl.when((t >= hops) & (j != n))
                    def _(): hop(a, way, j).start()
        done = [pltpu.make_async_copy(piece(a, n), outs[a], loc.at[a]) for a in some]
        for cp in done: cp.start()
        return done

    for cp in loads[:2]: cp.wait()
    theirs(0, gal, ctx)
    for cp in loads[2:4]: cp.wait()
    theirs(1, xn, gq)
    ours(0, gal, ctx)
    ours(1, xn, gq)
    input_gradient()
    relay(0)
    gains_swap(input_norm())
    stores = [pltpu.make_async_copy(gh, grad_tokens, loc.at[items])]
    stores[0].start()
    for a in range(1, items): relay(a)
    mine(0)
    stores += along([0])
    for a in range(1, items): mine(a)
    copies = columns_home(down, (down_out,), c, k, n, ff_s, ff_r, loc.at[items + 1])
    for cp in copies: cp.start()
    stores += along(list(range(1, items)))
    for cp in stores + copies: cp.wait()
    for a in range(items):
        swap[a].wait_send()
        for cp in cross[a] + main[a]: cp.wait_send()
        for j in range(nz):
            for way in range(2):
                @pl.when(n < j if way == 0 else n > j)
                def _(): hop(a, way, j).wait_send()


def gradient_all(nz, gal, ctx, xn, gq, wq, tokens, grad_hidden, down, gain, gain_mlp, cid):
    dma, vm = pltpu.SemaphoreType.DMA, pltpu.VMEM
    bf16, f32 = jnp.bfloat16, jnp.float32
    slots, width = gal.shape
    m = 3
    part = width // (CHIPS * CORES)
    rows = part // nz
    widths = (ctx.shape[1], gq.shape[1], 128)
    shape = jax.ShapeDtypeStruct
    blocks = [vm((CHIPS, part, w), bf16) for w in widths]
    row = pl.BlockSpec((1, width), lambda: (0, 0))
    return pl.pallas_call(
        functools.partial(gradient_kernel, nz),
        out_shape=tuple(shape((rows, w), bf16) for w in widths) + (shape((slots, width), f32), shape((rows, CHIPS * down.shape[2]), bf16)),
        in_specs=[ANY] * 7 + [VMEM, row, row], out_specs=(ANY,) * (m + 2),
        scratch_shapes=blocks + blocks + [vm((3 * part + 2 * nz * rows, w), bf16) for w in widths]
        + [vm(gal.shape, bf16), vm(ctx.shape, bf16), vm(xn.shape, bf16), vm(gq.shape, bf16), vm(wq.shape, bf16), vm(tokens.shape, bf16),
           vm((slots, width), f32), vm((slots, width), f32), vm((CHIPS * part, slots), bf16), vm((8, width), f32)]
        + [dma((m,)), dma((m,)), dma((m, 2)), dma((m, 2)), dma((m, 4)), dma((m, 4)), dma((m, 2, nz)), dma((m, 2, nz)), dma((1, 3)), dma((1, 3)), dma((7,)), dma((m + 2,))],
        compiler_params=pltpu.CompilerParams(collective_id=cid, has_side_effects=True, vmem_limit_bytes=62 << 20),
        name="gradient_all",
    )(gal, ctx, xn, gq, wq, tokens, grad_hidden, down, gain, gain_mlp)


def spread_kernel(parts, src, *refs):
    outs, (s_s, s_r, loc) = refs[:parts], refs[parts:]
    c, k, n = place()
    hello([(None, chip_at(c, r), k, n) for r in (1, 2, 3)])
    cps = columns_home(src, outs, c, k, n, s_s, s_r, loc)
    for cp in cps: cp.start()
    for cp in cps: cp.wait()


def spread(src, parts, cid):
    dma = pltpu.SemaphoreType.DMA
    rows, cols = src.shape[1], src.shape[2] // parts
    return pl.pallas_call(
        functools.partial(spread_kernel, parts),
        out_shape=(jax.ShapeDtypeStruct((rows, CHIPS * cols), src.dtype),) * parts, in_specs=[VMEM], out_specs=(ANY,) * parts,
        scratch_shapes=[dma((parts, 3)), dma((parts, 3)), dma],
        compiler_params=pltpu.CompilerParams(collective_id=cid, has_side_effects=True),
        name="spread",
    )(src)


def fits(mesh):
    return mesh.shape["wide"] == CHIPS * CORES


def fast_device(
    nz,
    tokens,
    cotangent,
    lengths,
    positions,
    norm_attn,
    w_query,
    w_key,
    w_value,
    w_output,
    norm_mlp,
    w_gate,
    w_up,
    w_down,
):
    f32, bf16 = jnp.float32, jnp.bfloat16
    c, k, n = place()
    slots, width = tokens.shape
    rows = w_query.shape[0]
    query_width, key_width = w_query.shape[1], w_key.shape[1]
    cols = w_gate.shape[1] // CHIPS
    valid_rows = (jnp.arange(slots) < lengths[0]).astype(f32)[:, None]
    tables = lane_tables(positions)
    grad_y = cotangent.astype(f32) * valid_rows
    grad_y_low = grad_y.astype(bf16)
    gains = jnp.zeros((rows, 128), bf16).at[:, 0].set(norm_attn).at[:, 1].set(norm_mlp)
    w_qkv, w_out, gain_cols, ff_gate_up, ff_down = gather_all(
        nz, w_query, w_key, w_value, w_output, gains, w_gate, w_up, w_down
    )
    gain_attn = gain_cols[:, 0].astype(f32)
    gain_mlp = gain_cols[:, 1].astype(f32)

    query_rotated, key_rotated, value_reduced, log_totals, context, scaled_attn, hidden, scaled_mlp, gy_all, ff_down = attend_all(
        nz, tokens, gain_attn[None], gain_mlp[None], tables, w_qkv, w_out, grad_y_low, ff_down
    )
    ff_gate_up, ff_down = (w.reshape(CHIPS * CORES, nz, rows, w.shape[-1]) for w in (ff_gate_up, ff_down))
    normed_mlp = normalize(hidden)
    grad_x_parts, mlp_parts, mlp_cross, down_sums, ff_sums = mlp_all(nz, scaled_mlp, gy_all, ff_gate_up, ff_down)
    grad_xn2 = jnp.sum(grad_x_parts.astype(f32), axis=0)
    grad_gain_mlp = jnp.sum(grad_xn2 * normed_mlp, axis=0)
    grad_hidden = grad_y + norm_back(grad_xn2 * gain_mlp, normed_mlp, hidden)
    grad_attn_low = grad_hidden.astype(bf16)
    grad_context = jnp.dot(grad_attn_low, w_out, preferred_element_type=f32).astype(bf16)
    grad_query, grad_key, grad_value, mlp_crossed = attend_back_all(
        query_rotated, key_rotated, value_reduced, log_totals, grad_context, tables, mlp_cross
    )
    output = (valid_rows * (hidden + jnp.sum(mlp_parts.astype(f32), axis=0) + mlp_crossed.astype(f32))).astype(bf16)
    grad_qkv = jnp.concatenate([grad_query, grad_key.astype(bf16), grad_value.astype(bf16)], 1)
    ff_sums = lax.psum_scatter(ff_sums, "narrow", scatter_dimension=0, tiled=True)
    grad_w_output, grad_qkv_rows, gain_sums, grad_tokens, grad_w_down = gradient_all(
        nz, grad_attn_low, context, scaled_attn, grad_qkv, w_qkv, tokens, grad_hidden, down_sums, gain_attn[None], grad_gain_mlp[None], 3
    )
    grad_w_gate, grad_w_up = (g.astype(f32) for g in spread(ff_sums.reshape(CHIPS, rows, 2 * cols), 2, 5))
    grad_w_down = grad_w_down.astype(f32)
    grad_w_output = grad_w_output.astype(f32)
    grad_w_query = grad_qkv_rows[:, :query_width].astype(f32)
    grad_w_key = grad_qkv_rows[:, query_width : query_width + key_width].astype(f32)
    grad_w_value = grad_qkv_rows[:, query_width + key_width :].astype(f32)
    grad_norm_attn, grad_norm_mlp = gain_sums[:, 0].astype(f32), gain_sums[:, 1].astype(f32)
    return (
        output,
        grad_tokens,
        grad_norm_attn,
        grad_w_query,
        grad_w_key,
        grad_w_value,
        grad_w_output,
        grad_norm_mlp,
        grad_w_gate,
        grad_w_up,
        grad_w_down,
    )


def solution(mesh):
    in_specs = (
        P(("wide", "narrow"), None),
        P(("wide", "narrow"), None),
        P(("wide", "narrow")),
        P(("wide", "narrow")),
        P(("wide", "narrow")),
        P(("wide", "narrow"), None),
        P(("wide", "narrow"), None),
        P(("wide", "narrow"), None),
        P(("wide", "narrow"), None),
        P(("wide", "narrow")),
        P(("wide", "narrow"), None),
        P(("wide", "narrow"), None),
        P(("wide", "narrow"), None),
    )
    out_specs = (
        P(("wide", "narrow"), None),
        P(("wide", "narrow"), None),
        P(("wide", "narrow")),
        P(("wide", "narrow"), None),
        P(("wide", "narrow"), None),
        P(("wide", "narrow"), None),
        P(("wide", "narrow"), None),
        P(("wide", "narrow")),
        P(("wide", "narrow"), None),
        P(("wide", "narrow"), None),
        P(("wide", "narrow"), None),
    )
    body = functools.partial(fast_device, mesh.shape["narrow"]) if fits(mesh) else per_device
    return jax.shard_map(
        body, mesh=mesh, in_specs=in_specs, out_specs=out_specs, check_vma=False
    )
```

```python
import functools
import math

import jax
import jax.numpy as jnp
from jax import lax
from jax.experimental import pallas as pl
from jax.experimental.pallas import tpu as pltpu
from jax.sharding import PartitionSpec as P

QUERY_HEADS = 32
KEY_VALUE_HEADS = 4
HEAD_SIZE = 64


norm_eps = 1e-05
rope_base = 10000.0
masked_score = -1e30
contract_last = (((1,), (1,)), ((), ()))
contract_first = (((0,), (0,)), ((), ()))


def rope_tables(positions):
    half_dim = HEAD_SIZE // 2
    inv_freq = jnp.exp(
        -math.log(rope_base) * jnp.arange(half_dim, dtype=jnp.float32) * 2.0 / HEAD_SIZE
    )
    angles = positions.astype(jnp.float32)[..., None] * inv_freq
    cosine = jnp.cos(angles)
    sine_part = jnp.sin(angles)
    return (jnp.concatenate([cosine, cosine], -1), jnp.concatenate([sine_part, sine_part], -1))


def apply_rotary(values, cosine_table, sine_table):
    half_dim = values.shape[-1] // 2
    turned = jnp.concatenate([-values[..., half_dim:], values[..., :half_dim]], -1)
    return values * cosine_table[..., None, :] + turned * sine_table[..., None, :]


def invert_rotary(grad_rows, cosine_table, sine_table):
    half_dim = grad_rows.shape[-1] // 2
    with_cos = grad_rows * cosine_table[..., None, :]
    with_sin = grad_rows * sine_table[..., None, :]
    return with_cos + jnp.concatenate([with_sin[..., half_dim:], -with_sin[..., :half_dim]], -1)


def normalize(values):
    return values * lax.rsqrt(jnp.mean(values * values, axis=-1, keepdims=True) + norm_eps)


def norm_back(grad_hat, normed, values):
    row_scale = lax.rsqrt(jnp.mean(values * values, axis=-1, keepdims=True) + norm_eps)
    return row_scale * (grad_hat - normed * jnp.mean(grad_hat * normed, axis=-1, keepdims=True))


def attention_inputs(normed, norm_attn, w_query, w_key, w_value):
    gain_piece = lax.all_gather(norm_attn, ("wide", "narrow"), axis=0, tiled=True)
    query_rows = lax.all_gather(w_query, ("wide", "narrow"), axis=0, tiled=True)
    key_rows = lax.all_gather(w_key, ("wide", "narrow"), axis=0, tiled=True)
    value_rows = lax.all_gather(w_value, ("wide", "narrow"), axis=0, tiled=True)
    gain_float = gain_piece.astype(jnp.float32)
    columns = (normed * gain_float).astype(jnp.bfloat16)
    query_sum = jnp.dot(columns, query_rows, preferred_element_type=jnp.float32)
    key_sum = jnp.dot(columns, key_rows, preferred_element_type=jnp.float32)
    value_sum = jnp.dot(columns, value_rows, preferred_element_type=jnp.float32)
    return (gain_float, columns, query_sum, key_sum, value_sum)


def mlp_inputs(normed, norm_mlp, w_gate, w_up):
    gain_piece = lax.all_gather(norm_mlp, ("wide", "narrow"), axis=0, tiled=True)
    gate_rows = lax.all_gather(w_gate, ("wide", "narrow"), axis=0, tiled=True)
    up_rows = lax.all_gather(w_up, ("wide", "narrow"), axis=0, tiled=True)
    gain_float = gain_piece.astype(jnp.float32)
    columns = (normed * gain_float).astype(jnp.bfloat16)
    gate_sum = jnp.dot(columns, gate_rows, preferred_element_type=jnp.float32)
    up_sum = jnp.dot(columns, up_rows, preferred_element_type=jnp.float32)
    return (gain_float, columns, gate_sum, up_sum)


def head_slices(query_rotated, key_rotated, value_reduced, shared_key_head):
    row_total_count = query_rotated.shape[0]
    heads_per_group = QUERY_HEADS // KEY_VALUE_HEADS
    query_head = query_rotated[
        :,
        shared_key_head
        * heads_per_group
        * HEAD_SIZE : (shared_key_head + 1)
        * heads_per_group
        * HEAD_SIZE,
    ].reshape(row_total_count, heads_per_group, HEAD_SIZE)
    key_head = key_rotated[:, shared_key_head * HEAD_SIZE : (shared_key_head + 1) * HEAD_SIZE]
    value_head = value_reduced[:, shared_key_head * HEAD_SIZE : (shared_key_head + 1) * HEAD_SIZE]
    return (query_head, key_head, value_head)


def head_scores(query_head, key_head):
    row_total_count = query_head.shape[0]
    causal = jnp.arange(row_total_count)[:, None] >= jnp.arange(row_total_count)[None, :]
    raw_scores = jnp.einsum("qrd,kd->rqk", query_head, key_head, preferred_element_type=jnp.float32)
    return jnp.where(causal, raw_scores * HEAD_SIZE ** (-0.5), masked_score)


def attend(query_rotated, key_rotated, value_reduced):
    row_total_count = query_rotated.shape[0]
    heads_per_group = QUERY_HEADS // KEY_VALUE_HEADS
    contexts = []
    log_totals = []
    for shared_key_head in range(KEY_VALUE_HEADS):
        query_head, key_head, value_head = head_slices(
            query_rotated, key_rotated, value_reduced, shared_key_head
        )
        scores = head_scores(query_head, key_head)
        row_peak = jnp.max(scores, axis=-1, keepdims=True)
        exp_scores = jnp.exp(scores - row_peak)
        row_total = jnp.sum(exp_scores, axis=-1, keepdims=True)
        probs = exp_scores / row_total
        context_head = jnp.einsum(
            "rqk,kd->qrd",
            probs.astype(jnp.bfloat16),
            value_head,
            preferred_element_type=jnp.float32,
        )
        contexts.append(context_head.reshape(row_total_count, heads_per_group * HEAD_SIZE))
        log_totals.append(row_peak + jnp.log(row_total))
    return (jnp.concatenate(contexts, 1).astype(jnp.bfloat16), log_totals)


def attend_back(query_rotated, key_rotated, value_reduced, log_totals, grad_context):
    row_total_count = query_rotated.shape[0]
    heads_per_group = QUERY_HEADS // KEY_VALUE_HEADS
    score_scale = HEAD_SIZE ** (-0.5)
    query_grads = []
    key_grads = []
    value_grads = []
    for shared_key_head in range(KEY_VALUE_HEADS):
        query_head, key_head, value_head = head_slices(
            query_rotated, key_rotated, value_reduced, shared_key_head
        )
        scores = head_scores(query_head, key_head)
        probs = jnp.exp(scores - log_totals[shared_key_head])
        probs_low = probs.astype(jnp.bfloat16)
        grad_head = grad_context[
            :,
            shared_key_head
            * heads_per_group
            * HEAD_SIZE : (shared_key_head + 1)
            * heads_per_group
            * HEAD_SIZE,
        ].reshape(row_total_count, heads_per_group, HEAD_SIZE)
        grad_probs = jnp.einsum(
            "qrd,kd->rqk", grad_head, value_head, preferred_element_type=jnp.float32
        )
        value_grads.append(
            jnp.einsum("rqk,qrd->kd", probs_low, grad_head, preferred_element_type=jnp.float32)
        )
        inner_sum = jnp.sum(grad_probs * probs, axis=-1, keepdims=True)
        grad_scores = (probs * (grad_probs - inner_sum) * score_scale).astype(jnp.bfloat16)
        query_grad = jnp.einsum(
            "rqk,kd->qrd", grad_scores, key_head, preferred_element_type=jnp.float32
        )
        query_grads.append(query_grad.reshape(row_total_count, heads_per_group * HEAD_SIZE))
        key_grads.append(
            jnp.einsum("rqk,qrd->kd", grad_scores, query_head, preferred_element_type=jnp.float32)
        )
    return (
        jnp.concatenate(query_grads, 1),
        jnp.concatenate(key_grads, 1),
        jnp.concatenate(value_grads, 1),
    )


def make_term(width_sides, other_sides):
    down_side, mlp_side, attn_side, qkv_side = width_sides
    mixed_rows, gate_rows, up_rows, context_rows, query_rows, key_rows, value_rows = other_sides

    def grad_term(first_row, row_span):
        pieces = [
            lax.dot_general(
                down_side, mixed_rows, contract_first, preferred_element_type=jnp.float32
            ),
            lax.dot_general(
                mlp_side, gate_rows, contract_first, preferred_element_type=jnp.float32
            ),
            lax.dot_general(mlp_side, up_rows, contract_first, preferred_element_type=jnp.float32),
            lax.dot_general(
                attn_side, context_rows, contract_first, preferred_element_type=jnp.float32
            ),
            lax.dot_general(
                qkv_side, query_rows, contract_first, preferred_element_type=jnp.float32
            ),
            lax.dot_general(qkv_side, key_rows, contract_first, preferred_element_type=jnp.float32),
            lax.dot_general(
                qkv_side, value_rows, contract_first, preferred_element_type=jnp.float32
            ),
        ]
        return jnp.concatenate(pieces, 1)

    return grad_term


def per_device(
    tokens,
    cotangent,
    lengths,
    positions,
    norm_attn,
    w_query,
    w_key,
    w_value,
    w_output,
    norm_mlp,
    w_gate,
    w_up,
    w_down,
):
    row_total_count = tokens.shape[0]
    shard_rows = w_query.shape[0]
    query_width = w_query.shape[1]
    key_width = w_key.shape[1]
    hidden_width = w_gate.shape[1]
    inputs = tokens.astype(jnp.float32)
    valid_rows = (jnp.arange(row_total_count) < lengths[0]).astype(jnp.float32)[:, None]
    cosine_table, sine_table = rope_tables(positions)
    normed_attn = normalize(inputs)
    gain_attn_full, scaled_attn, query_pre, key_unrotated, value_pre = attention_inputs(
        normed_attn, norm_attn, w_query, w_key, w_value
    )
    query_rotated = (
        apply_rotary(
            query_pre.reshape(row_total_count, QUERY_HEADS, HEAD_SIZE), cosine_table, sine_table
        )
        .reshape(row_total_count, query_width)
        .astype(jnp.bfloat16)
    )
    key_rotated = (
        apply_rotary(
            key_unrotated.reshape(row_total_count, KEY_VALUE_HEADS, HEAD_SIZE),
            cosine_table,
            sine_table,
        )
        .reshape(row_total_count, key_width)
        .astype(jnp.bfloat16)
    )
    value_reduced = value_pre.astype(jnp.bfloat16)
    context, log_totals = attend(query_rotated, key_rotated, value_reduced)
    attn_out = lax.dot_general(
        context,
        lax.all_gather(w_output, ("wide", "narrow"), axis=0, tiled=True),
        contract_last,
        preferred_element_type=jnp.float32,
    )
    hidden = inputs + attn_out
    normed_mlp = normalize(hidden)
    gain_mlp_full, scaled_mlp, gate_proj, up_proj = mlp_inputs(normed_mlp, norm_mlp, w_gate, w_up)
    mixed_low = (gate_proj * jax.nn.sigmoid(gate_proj) * up_proj).astype(jnp.bfloat16)
    mlp_out = lax.dot_general(
        mixed_low,
        lax.all_gather(w_down, ("wide", "narrow"), axis=0, tiled=True),
        contract_last,
        preferred_element_type=jnp.float32,
    )
    output = (valid_rows * (hidden + mlp_out)).astype(jnp.bfloat16)
    grad_y = cotangent.astype(jnp.float32) * valid_rows
    grad_y_low = grad_y.astype(jnp.bfloat16)
    grad_cols = grad_y_low
    grad_mixed = jnp.dot(
        grad_cols,
        lax.all_gather(w_down, ("wide", "narrow"), axis=0, tiled=True),
        preferred_element_type=jnp.float32,
    )
    again_values = mlp_inputs(normed_mlp, norm_mlp, w_gate, w_up)
    gate_proj = again_values[2]
    up_proj = again_values[3]
    sigmoid_gate = jax.nn.sigmoid(gate_proj)
    grad_gate = (
        grad_mixed * up_proj * (sigmoid_gate * (1.0 + gate_proj * (1.0 - sigmoid_gate)))
    ).astype(jnp.bfloat16)
    grad_up = (grad_mixed * (gate_proj * sigmoid_gate)).astype(jnp.bfloat16)
    gate_rows = lax.all_gather(w_gate, ("wide", "narrow"), axis=0, tiled=True)
    up_rows = lax.all_gather(w_up, ("wide", "narrow"), axis=0, tiled=True)
    columns = lax.dot_general(
        grad_gate, gate_rows, contract_last, preferred_element_type=jnp.float32
    )
    columns = columns + lax.dot_general(
        grad_up, up_rows, contract_last, preferred_element_type=jnp.float32
    )
    grad_xn2 = columns
    grad_gain_mlp = jnp.sum(grad_xn2 * normed_mlp, axis=0)
    grad_hidden = grad_y + norm_back(grad_xn2 * gain_mlp_full, normed_mlp, hidden)
    grad_attn_low = grad_hidden.astype(jnp.bfloat16)
    grad_cols = grad_attn_low
    grad_context = jnp.dot(
        grad_cols,
        lax.all_gather(w_output, ("wide", "narrow"), axis=0, tiled=True),
        preferred_element_type=jnp.float32,
    )
    grad_context = grad_context.astype(jnp.bfloat16)
    grad_query_rot, gradient_key_rotated, grad_value_sum = attend_back(
        query_rotated, key_rotated, value_reduced, log_totals, grad_context
    )
    grad_query = (
        invert_rotary(
            grad_query_rot.reshape(row_total_count, QUERY_HEADS, HEAD_SIZE),
            cosine_table,
            sine_table,
        )
        .reshape(row_total_count, query_width)
        .astype(jnp.bfloat16)
    )
    grad_key = (
        invert_rotary(
            gradient_key_rotated.reshape(row_total_count, KEY_VALUE_HEADS, HEAD_SIZE),
            cosine_table,
            sine_table,
        )
        .reshape(row_total_count, key_width)
        .astype(jnp.bfloat16)
    )
    grad_value = grad_value_sum.astype(jnp.bfloat16)
    query_rows = lax.all_gather(w_query, ("wide", "narrow"), axis=0, tiled=True)
    key_rows = lax.all_gather(w_key, ("wide", "narrow"), axis=0, tiled=True)
    value_rows = lax.all_gather(w_value, ("wide", "narrow"), axis=0, tiled=True)
    columns = lax.dot_general(
        grad_query, query_rows, contract_last, preferred_element_type=jnp.float32
    )
    columns = columns + lax.dot_general(
        grad_key, key_rows, contract_last, preferred_element_type=jnp.float32
    )
    columns = columns + lax.dot_general(
        grad_value, value_rows, contract_last, preferred_element_type=jnp.float32
    )
    local_term = make_term(
        (grad_y_low, scaled_mlp, grad_attn_low, scaled_attn),
        (mixed_low, grad_gate, grad_up, context, grad_query, grad_key, grad_value),
    )
    all_sums = lax.psum_scatter(
        local_term(jnp.int32(0), lax.axis_size(("wide", "narrow")) * shard_rows),
        ("wide", "narrow"),
        scatter_dimension=0,
        tiled=True,
    )
    edges = [0]
    for width in (
        hidden_width,
        hidden_width,
        hidden_width,
        query_width,
        query_width,
        key_width,
        key_width,
    ):
        edges.append(edges[-1] + width)
    grad_w_down = all_sums[:, edges[0] : edges[1]]
    grad_w_gate = all_sums[:, edges[1] : edges[2]]
    grad_w_up = all_sums[:, edges[2] : edges[3]]
    grad_w_output = all_sums[:, edges[3] : edges[4]]
    grad_w_query = all_sums[:, edges[4] : edges[5]]
    grad_w_key = all_sums[:, edges[5] : edges[6]]
    grad_w_value = all_sums[:, edges[6] : edges[7]]
    grad_gain_attn = jnp.sum(columns * normed_attn, axis=0)
    grad_tokens = grad_hidden + norm_back(columns * gain_attn_full, normed_attn, inputs)
    grad_norm_attn, grad_norm_mlp = (
        lax.psum_scatter(grad_gain_attn, ("wide", "narrow"), scatter_dimension=0, tiled=True),
        lax.psum_scatter(grad_gain_mlp, ("wide", "narrow"), scatter_dimension=0, tiled=True),
    )
    return (
        output,
        grad_tokens,
        grad_norm_attn,
        grad_w_query,
        grad_w_key,
        grad_w_value,
        grad_w_output,
        grad_norm_mlp,
        grad_w_gate,
        grad_w_up,
        grad_w_down,
    )


MESH = pl.DeviceIdType.MESH
ANY = pl.BlockSpec(memory_space=pl.ANY)
VMEM = pl.BlockSpec(memory_space=pltpu.VMEM)

CHIPS, CORES = 4, 2

def place():
    w = lax.axis_index("wide"); n = lax.axis_index("narrow")
    return w // CORES, w % CORES, n

def chip_at(c, r):
    xb, yb, rx, ry = c % 2, c // 2, r % 2, r // 2
    return (yb + ry - 2 * yb * ry) * 2 + (xb + rx - 2 * xb * rx)


def remote(src, dst, send, recv, chip, core, z):
    return pltpu.make_async_remote_copy(src_ref=src, dst_ref=dst, send_sem=send, recv_sem=recv,
        device_id={"wide": chip * CORES + core, "narrow": z}, device_id_type=MESH)

def hello(partners):
    barrier = pltpu.get_barrier_semaphore()
    count = 0
    for cond, chip, core, z in partners:
        def sig(chip=chip, core=core, z=z):
            pl.semaphore_signal(barrier, inc=1, device_id={"wide": chip * CORES + core, "narrow": z}, device_id_type=MESH)
        if cond is None:
            sig(); count = count + 1
        else:
            pl.when(cond)(sig); count = count + jnp.where(cond, 1, 0)
    pl.semaphore_wait(barrier, count)

class Line:
    def __init__(self, nz, at, refs, send, recv, place_of):
        self.nz, self.at, self.refs, self.send, self.recv, self.place_of = nz, at, refs, send, recv, place_of

    def _copy(self, a, way, s, origin):
        c, k, n = self.at
        ref = self.place_of(self.refs[a], origin)
        return remote(ref, ref, self.send.at[a, way, s], self.recv.at[a, way, s], c, k, n + 1 if way == 0 else n - 1)

    def _origin(self, way, s):
        n = self.at[2]
        o = n - s if way == 0 else n + s
        return (n >= s) if way == 0 else (n + s <= self.nz - 1), jnp.clip(o, 0, self.nz - 1)

    def _sends(self, way, s):
        n = self.at[2]
        return self._origin(way, s)[0] & ((n < self.nz - 1) if way == 0 else (n > 0))

    def start(self, a, s, way):
        @pl.when(self._sends(way, s))
        def _(): self._copy(a, way, s, self._origin(way, s)[1]).start()

    def step(self, a, s, then=None):
        for way in range(2):
            came, origin = self._origin(way, s)
            @pl.when(came)
            def _(): self._copy(a, way, s - 1, origin).wait_recv()
            if s < self.nz - 1: self.start(a, s, way)
            if then is not None:
                @pl.when(came)
                def _(): then(origin)

    def finish(self, a):
        for s in range(self.nz - 1):
            for way in range(2):
                @pl.when(self._sends(way, s))
                def _(): self._copy(a, way, s, self._origin(way, s)[1]).wait_send()


def gather_kernel(nz, wq, wk, wv, wo, gains, wg, wu, wd, qkv, out, gain, gu, gd,
                  loc, sw_s, sw_r, z_s, z_r, f_s, f_r, p_s, p_r, h_s, h_r, d_s, d_r, e_s, e_r):
    c, k, n = at = place()
    rows, q = wq.shape
    kv = wk.shape[1]
    cols = gd.shape[-1]
    part = nz * rows
    half = part // 2
    kn = k * nz + n
    cx, cy, cd = (chip_at(c, r) for r in (1, 2, 3))
    hello([(None, cc, k, n) for cc in (cx, cy, cd)] + [(None, c, 1 - k, n), (n > 0, c, k, n - 1), (n < nz - 1, c, k, n + 1)])

    def mycols(w, cc): return w.at[:, pl.ds(pl.multiple_of(cc * cols, 128), cols)]
    def landing(i, cc): return gd.at[cc] if i == 2 else gu.at[cc, kn, :, pl.ds(i * cols, cols)]
    whole = (qkv, out, gain)
    def block(ref, z): return ref.at[pl.ds(pl.multiple_of(((c * CORES + k) * nz + z) * rows, rows), rows)]
    own = [pltpu.make_async_copy(wq, block(qkv, n).at[:, pl.ds(0, q)], loc.at[0]),
           pltpu.make_async_copy(wk, block(qkv, n).at[:, pl.ds(q, kv)], loc.at[1]),
           pltpu.make_async_copy(wv, block(qkv, n).at[:, pl.ds(q + kv, kv)], loc.at[2]),
           pltpu.make_async_copy(wo, block(out, n), loc.at[3]), pltpu.make_async_copy(gains, block(gain, n), loc.at[4])]
    ownff = [pltpu.make_async_copy(mycols(w, c), landing(i, c), loc.at[5 + i]) for i, w in enumerate((wg, wu, wd))]
    for cp in own + ownff: cp.start()
    swap = [[remote(mycols(w, cc), landing(i, c), sw_s.at[i, r], sw_r.at[i, r], cc, k, n) for r, cc in enumerate((cx, cy, cd))]
            for i, w in enumerate((wg, wu, wd))]
    for i in range(3):
        for cp in swap[i]: cp.start()
    for cp in own: cp.wait()

    line = Line(nz, at, whole, z_s, z_r, block)
    for a in range(3):
        for way in range(2): line.start(a, 0, way)

    def span(ref, cc, first, size):
        return ref.at[pl.ds(pl.multiple_of((cc * CORES + k) * part, part) + first, size)]
    plane = [[remote(span(ref, c, 0, part), span(ref, c, 0, part), p_s.at[a, r], p_r.at[a, r], cc, k, n) for r, cc in enumerate((cx, cy))]
             for a, ref in enumerate(whole)]
    across = [[remote(span(ref, cx, 0, half), span(ref, cx, 0, half), h_s.at[a, 0], h_r.at[a, 0], cy, k, n),
               remote(span(ref, cy, half, half), span(ref, cy, half, half), h_s.at[a, 1], h_r.at[a, 1], cx, k, n)]
              for a, ref in enumerate(whole)]
    cores = [[remote(span(ref, cc, 0, part), span(ref, cc, 0, part), d_s.at[a, r], d_r.at[a, r], c, 1 - k, n)
              for r, cc in enumerate((c, cx, cy, cd))] for a, ref in enumerate(whole)]

    def plane_start(a):
        for cp in plane[a] + cores[a][:1]: cp.start()
    def plane_next(a):
        for i in range(2):
            plane[a][i].wait_recv()
            across[a][i].start()
            cores[a][1 + i].start()
    def plane_last(a):
        for cp in across[a]: cp.wait_recv()
        cores[a][3].start()

    for s in range(1, nz):
        for a in range(3):
            line.step(a, s)
            if s == nz - 1: plane_start(a)

    ff = Line(nz, at, (gu,), f_s, f_r, lambda ref, z: ref.at[:, k * nz + z])
    def twin(z):
        ref = gu.at[:, k * nz + z]
        return remote(ref, ref, e_s.at[z], e_r.at[z], c, 1 - k, n)
    for i in range(2):
        ownff[i].wait()
        for cp in swap[i]: cp.wait_recv()
    for way in range(2): ff.start(0, 0, way)
    twin(n).start()
    plane_next(0)
    ff.step(0, 1, lambda z: twin(z).start())
    for a in (1, 2): plane_next(a)
    ff.step(0, 2, lambda z: twin(z).start())
    for a in range(3): plane_last(a)
    ownff[2].wait()
    for cp in swap[2]: cp.wait_recv()
    for s in range(3, nz): ff.step(0, s, lambda z: twin(z).start())
    for a in range(3):
        for cp in cores[a]: cp.wait_recv()
    for z in range(nz): twin(z).wait()
    for i in range(3):
        for cp in swap[i]: cp.wait_send()
    for a in range(3):
        line.finish(a)
        for cp in plane[a] + across[a] + cores[a]: cp.wait_send()
    ff.finish(0)


def gather_all(nz, wq, wk, wv, wo, gains, wg, wu, wd):
    rows = wq.shape[0]
    width = rows * CHIPS * CORES * nz
    cols = wg.shape[1] // CHIPS
    bf = jnp.bfloat16
    shape = jax.ShapeDtypeStruct
    dma = pltpu.SemaphoreType.DMA
    return pl.pallas_call(
        functools.partial(gather_kernel, nz),
        out_shape=(shape((width, wq.shape[1] + 2 * wk.shape[1]), bf), shape((width, wo.shape[1]), bf), shape((width, gains.shape[1]), bf),
                   shape((CHIPS, CORES * nz, rows, 2 * cols), bf), shape((CHIPS, rows, cols), bf)),
        in_specs=[VMEM] * 8, out_specs=(ANY,) * 5,
        scratch_shapes=[dma((8,)), dma((3, 3)), dma((3, 3)), dma((3, 2, nz)), dma((3, 2, nz)), dma((1, 2, nz)), dma((1, 2, nz)),
                        dma((3, 2)), dma((3, 2)), dma((3, 2)), dma((3, 2)), dma((3, 4)), dma((3, 4)), dma((nz,)), dma((nz,))],
        compiler_params=pltpu.CompilerParams(collective_id=0, has_side_effects=True),
        name="gather_all",
    )(wq, wk, wv, wo, gains, wg, wu, wd)


def add_into(dst, *srcs):
    rows = dst.shape[0]
    step = 16
    def body(i, carry):
        at = pl.ds(pl.multiple_of(i * step, step), step)
        total = dst[at, :].astype(jnp.float32)
        for s in srcs: total = total + s[at, :].astype(jnp.float32)
        dst[at, :] = total.astype(dst.dtype)
        return carry
    lax.fori_loop(0, rows // step, body, 0)


HALVES = ((0, 0), (0, 1), (1, 0), (2, 0), (1, 1), (2, 1), (3, 0), (3, 1))


def mlp_kernel(nz, x, gy, gu_hbm, gd_hbm, gx_parts, mlp_parts, mlp_cross, down_sums, sums,
               xs, gys, gu, gd, mix, ggu, gx, mo, xt, zin, load, ag_s, ag_r, rs_s, rs_r, mo_s, mo_r, out, core_s, core_r, ready, done, z_s, z_r):
    c, k, n = place()
    f32, bf16 = jnp.float32, jnp.bfloat16
    slots, width = x.shape
    half = slots // 2
    rows, cols = gd.shape[2:]
    tile = nz * rows
    hello([(None, chip_at(c, r), k, n) for r in (1, 2, 3)]
          + [(None, c, 1 - k, n), (n > 0, c, k, n - 1), (n < nz - 1, c, k, n + 1)])
    def half_of(ref, h): return ref.at[pl.ds(h * half, half)]
    index = {place_: i for i, place_ in enumerate(HALVES)}
    sends = {}
    for h in range(2):
        for r in (1, 2):
            i = index[r, h]
            sends[i] = remote(half_of(x, h), xs.at[i], ag_s.at[i], ag_r.at[i], chip_at(c, r), k, n)
            if h == 0: sends[i].start()
    loads = [pltpu.make_async_copy(half_of(x, h), xs.at[h], load.at[h]) for h in range(2)]
    loads += [pltpu.make_async_copy(half_of(gy.at[r], h), gys.at[i], load.at[2 + i]) for i, (r, h) in enumerate(HALVES)]
    for cp in loads: cp.start()
    def weights(col, w, j):
        return [pltpu.make_async_copy(a.at[:, :, :, pl.ds(first + col, w)], b.at[:, :, :, pl.ds(first + col, w)], load.at[10 + 3 * j + i])
                for i, (a, b, first) in enumerate(((gu_hbm, gu, 0), (gu_hbm, gu, cols), (gd_hbm, gd, 0)))]
    for j in range(-(-cols // 256)):
        for cp in weights(j * 256, min(256, cols - j * 256), j): cp.start()
    relays = {index[3, 0]: (index[1, 0], 2), index[3, 1]: (index[2, 1], 1)}
    relays = {i: remote(xs.at[j], xs.at[i], ag_s.at[i], ag_r.at[i], chip_at(c, r), k, n) for i, (j, r) in relays.items()}
    for cp in loads: cp.wait()

    def columns(ref, at, size):
        return ref[:, :, :, pl.ds(at, size)].reshape(width, size)

    def some_rows(ref, i): return ref[i].reshape(tile, ref.shape[3])

    def to_owner(src, dst, i, s_s, s_r):
        r, h = HALVES[i]
        return remote(src.at[i], half_of(dst.at[r], h), s_s.at[i], s_r.at[i], chip_at(c, r), k, n)

    def kept(src, dst, i, j):
        return pltpu.make_async_copy(src.at[i], half_of(dst, HALVES[i][1]), out.at[j])

    def block(r, carry):
        two = pl.ds(2 * r, 2)
        @pl.when(r == 1)
        def _():
            for i in (2, 3): sends[i].wait_recv()
            relays[index[3, 0]].start()
        @pl.when(r == 3)
        def _():
            for cp in relays.values(): cp.wait_recv()
        def both(ref): return ref[two].reshape(slots, ref.shape[2])
        def put(ref, at, v): ref[two, :, at] = v.astype(bf16).reshape(2, half, v.shape[1])
        def chunk(col, w, j):
            @pl.when(r == 0)
            def _():
                for cp in weights(col, w, j): cp.wait()
            tokens = both(xs)
            hg = jnp.dot(tokens, columns(gu, col, w), preferred_element_type=f32)
            hu = jnp.dot(tokens, columns(gu, cols + col, w), preferred_element_type=f32)
            gm = jnp.dot(both(gys), columns(gd, col, w), preferred_element_type=f32)
            for q in range(w // 128):
                gate, up, g = (t[:, 128 * q : 128 * q + 128] for t in (hg, hu, gm))
                sg = 1.0 / (1.0 + jnp.exp(-gate))
                act = gate * sg
                put(mix, pl.ds(col + 128 * q, 128), act * up)
                put(ggu, pl.ds(col + 128 * q, 128), g * up * (sg * (1.0 + gate * (1.0 - sg))))
                put(ggu, pl.ds(cols + col + 128 * q, 128), g * act)
        def pair(j, carry):
            chunk(pl.multiple_of(j * 256, 256), 256, j)
            return carry
        lax.fori_loop(0, cols // 256, pair, 0)
        if cols % 256: chunk(cols // 256 * 256, cols % 256, cols // 256)
        @pl.when(r == 0)
        def _():
            for i in (4, 5): sends[i].start()
        @pl.when(r == 1)
        def _():
            for i in (4, 5): sends[i].wait_recv()
            relays[index[3, 1]].start()
        def back(i, carry):
            at = pl.ds(pl.multiple_of(i * tile, 128), tile)
            put(gx, at, lax.dot_general(both(ggu), some_rows(gu, i), contract_last, preferred_element_type=f32))
            return carry
        lax.fori_loop(0, CHIPS * CORES, back, 0)
        for t in range(CHIPS):
            @pl.when(r == t)
            def _():
                for i in (2 * t, 2 * t + 1):
                    (to_owner(gx, gx_parts, i, rs_s, rs_r) if t else kept(gx, gx_parts.at[0], i, i)).start()
        def down(i, carry):
            at = pl.ds(pl.multiple_of(i * tile, 128), tile)
            put(mo, at, lax.dot_general(both(mix), some_rows(gd, i), contract_last, preferred_element_type=f32))
            return carry
        lax.fori_loop(0, CHIPS * CORES, down, 0)
        for t in range(CHIPS):
            @pl.when(r == t)
            def _():
                for i in (2 * t, 2 * t + 1):
                    (kept(mo, mlp_parts.at[0], i, 2 + i) if t == 0 else kept(mo, mlp_cross, i, i - 2) if t == 3
                     else to_owner(mo, mlp_parts, i, mo_s, mo_r)).start()
        return carry
    lax.fori_loop(0, CHIPS, block, 0)

    pl.semaphore_signal(ready, inc=1, device_id={"wide": c * CORES + 1 - k, "narrow": n}, device_id_type=MESH)
    pl.semaphore_wait(ready, 1)
    sent, came = pl.ds(0, CHIPS), pl.ds(CHIPS, CHIPS)
    pairs = ((gys, mix, gd), (xs, ggu, gu))

    def tiles(total): return [(t * 256, min(256, total - t * 256)) for t in range(-(-total // 256))]

    def to_core(i, col, w, sem):
        ref = pairs[i][2]
        return remote(ref.at[sent, :, :, pl.ds(col, w)], ref.at[came, :, :, pl.ds(col, w)], core_s.at[sem], core_r.at[sem], c, 1 - k, n)

    def to_sums(t): return pltpu.make_async_copy(gu.at[CHIPS + t], sums.at[:, t], done.at[t])

    def each(i, body):
        total, base = pairs[i][2].shape[-1], 0 if i == 0 else len(tiles(cols))
        def step(j, carry):
            body(pl.multiple_of(j * 256, 256), 256, base + j)
            return carry
        lax.fori_loop(0, total // 256, step, 0)
        if total % 256: body(total // 256 * 256, total % 256, base + total // 256)

    def terms(i, kk, use):
        src, right, ref = pairs[i]
        for t in range(CHIPS):
            at = pl.ds(pl.multiple_of((t * CORES + kk) * tile, 128), tile)
            for r in range(CHIPS):
                xt[t * tile : (t + 1) * tile, r * slots : (r + 1) * slots] = src[2 * r : 2 * r + 2, :, at].reshape(slots, tile).T
        def body(col, w, sem):
            b = right[:, :, pl.ds(col, w)].reshape(CHIPS * slots, w)
            use(i, col, w, sem, jnp.dot(xt[...], b, preferred_element_type=f32).reshape(CHIPS, nz, rows, w))
        each(i, body)

    def theirs(i, col, w, sem, v):
        pairs[i][2][sent, :, :, pl.ds(col, w)] = v.astype(bf16)
        to_core(i, col, w, sem).start()

    def ours(i, col, w, sem, v):
        to_core(i, col, w, sem).wait_recv()
        ref = pairs[i][2]
        here = (came, slice(None), slice(None), pl.ds(col, w))
        ref[here] = (ref[here].astype(f32) + v).astype(bf16)

    def hop(way, j):
        return remote(gd.at[came, j], zin.at[way, jnp.clip(j - n - 1 if way == 0 else n - 1 - j, 0, nz - 2)],
                      z_s.at[way, j], z_r.at[way, j], c, k, n + 1 if way == 0 else n - 1)

    def along(t):
        for way in range(2):
            hops = n if way == 0 else nz - 1 - n
            j = jnp.clip(n + nz - 1 - t if way == 0 else t - hops, 0, nz - 1)
            @pl.when((hops > 0) & (t >= hops))
            def _():
                hop(way, j).wait_recv()
                for i in range(CHIPS):
                    add_into(gd.at[CHIPS + i, j], zin.at[way, jnp.clip(j - n if way == 0 else n - j, 0, nz - 2), i])
            @pl.when((t >= hops) & (j != n))
            def _(): hop(way, j).start()

    terms(0, 1 - k, theirs)
    terms(0, k, ours)
    along(0)
    terms(1, 1 - k, theirs)
    along(1)
    terms(1, k, ours)
    for t in range(CHIPS): to_sums(t).start()
    for t in range(2, nz): along(t)
    own_down = pltpu.make_async_copy(gd.at[came, n], down_sums, done.at[CHIPS])
    own_down.start()

    for cp in (*sends.values(), *relays.values()): cp.wait_send()
    for i in range(2):
        kept(gx, gx_parts.at[0], i, i).wait()
        kept(mo, mlp_parts.at[0], i, 2 + i).wait()
        kept(mo, mlp_cross, 6 + i, 4 + i).wait()
    for i in range(2): each(i, lambda col, w, sem: to_core(i, col, w, sem).wait_send())
    for t in range(CHIPS): to_sums(t).wait()
    for j in range(nz):
        for way in range(2):
            @pl.when(n < j if way == 0 else n > j)
            def _(): hop(way, j).wait_send()
    own_down.wait()
    for i in range(2, 6): to_owner(mo, mlp_parts, i, mo_s, mo_r).wait()
    for i in range(2, 8): to_owner(gx, gx_parts, i, rs_s, rs_r).wait()


def mlp_all(nz, x, gy, gu, gd):
    slots, width = x.shape
    rows, cols = gd.shape[2:]
    bf, dma, vm = jnp.bfloat16, pltpu.SemaphoreType.DMA, pltpu.VMEM
    def blocks(w): return jax.ShapeDtypeStruct((CHIPS, slots, w), bf)
    def halves(w): return vm((2 * CHIPS, slots // 2, w), bf)
    tiles = -(-cols // 256)
    flops = 2 * 9 * CHIPS * slots * width * cols
    return pl.pallas_call(
        functools.partial(mlp_kernel, nz),
        out_shape=(blocks(width), jax.ShapeDtypeStruct((3, slots, width), bf), jax.ShapeDtypeStruct((slots, width), bf),
                   jax.ShapeDtypeStruct((CHIPS, rows, cols), bf), jax.ShapeDtypeStruct((nz, CHIPS, rows, 2 * cols), bf)),
        in_specs=[ANY] * 4, out_specs=(ANY,) * 5,
        scratch_shapes=[halves(width), halves(width), vm(gu.shape, bf), vm(gd.shape, bf), halves(cols), halves(2 * cols), halves(width),
                        halves(width), vm((CHIPS * nz * rows, CHIPS * slots), bf), vm((2, nz - 1, CHIPS, rows, cols), bf), dma((10 + 3 * tiles,)), dma((8,)), dma((8,)), dma((8,)), dma((8,)),
                        dma((8,)), dma((8,)), dma((6,)), dma((3 * tiles,)), dma((3 * tiles,)), pltpu.SemaphoreType.REGULAR, dma((CHIPS + 1,)), dma((2, nz)), dma((2, nz))],
        compiler_params=pltpu.CompilerParams(collective_id=1, has_side_effects=True, vmem_limit_bytes=62 << 20),
        cost_estimate=pl.CostEstimate(flops=flops, bytes_accessed=60 << 20, transcendentals=CHIPS * slots * cols),
        name="mlp_all",
    )(x, gy, gu, gd)


PAIR = 2 * HEAD_SIZE
REPEAT = QUERY_HEADS // KEY_VALUE_HEADS
PAIRS = REPEAT // 2


def lane_tables(positions):
    cosine, sine = rope_tables(positions)
    first = jnp.arange(HEAD_SIZE) < HEAD_SIZE // 2
    low, high = jnp.where(first, -sine, 0.0), jnp.where(first, 0.0, sine)
    return jnp.stack([jnp.concatenate([t, t], 1) for t in (cosine, low, high)])


def rotate(u, tables):
    half = HEAD_SIZE // 2
    return u * tables[0] + pltpu.roll(u, PAIR - half, 1) * tables[1] + pltpu.roll(u, half, 1) * tables[2]


def unrotate(g, tables):
    half = HEAD_SIZE // 2
    return g * tables[0] + pltpu.roll(g * tables[2], PAIR - half, 1) + pltpu.roll(g * tables[1], half, 1)


def row_blocks(slots):
    return [(at, min(128, slots - at), at + 128) for at in range(0, slots, 128)]


def causal(s, below, fill):
    clear = s.shape[1] - 128
    last = jnp.where(below, s[:, clear:], fill)
    return jnp.concatenate([s[:, :clear], last], 1) if clear else last


def scaled(x, gain):
    return (x * lax.rsqrt(jnp.mean(x * x, axis=-1, keepdims=True) + norm_eps) * gain).astype(jnp.bfloat16)


def attend_kernel(nz, tok, gain1, gain2, tab_ref, wq_hbm, wo_hbm, gy, gd_own,
                  qr_ref, k_out, v_out, lse_ref, ctx_ref, xn1, hidden, xn2, gys, gd, ks, vs, wq, wo, qkv,
                  load, loc, g_s, g_r, h_s, h_r, f_s, f_r, e_s, e_r):
    g = pl.program_id(0)
    f32, bf16 = jnp.float32, jnp.bfloat16
    slots, width = tok.shape
    c, k, n = at = place()
    mine = [pltpu.make_async_copy(gd_own, gd.at[:, k * nz + n], loc.at[0]), pltpu.make_async_copy(gy, gys.at[0], loc.at[1])]
    line = Line(nz, at, (gd,), f_s, f_r, lambda ref, z: ref.at[:, k * nz + z])
    half = slots // 2
    sends = [remote(gy, gys.at[r], g_s.at[r - 1], g_r.at[r - 1], chip_at(c, r), k, n) for r in (1, 2)]
    relays = [remote(gys.at[1, pl.ds(0, half)], gys.at[3, pl.ds(0, half)], h_s.at[0], h_r.at[0], chip_at(c, 2), k, n),
              remote(gys.at[2, pl.ds(half, half)], gys.at[3, pl.ds(half, half)], h_s.at[1], h_r.at[1], chip_at(c, 1), k, n)]
    def twin(z):
        ref = gd.at[:, k * nz + z]
        return remote(ref, ref, e_s.at[z], e_r.at[z], c, 1 - k, n)
    def load_q(j):
        at = pl.ds(j * 256 if isinstance(j, int) else pl.multiple_of(j * 256, 256), 256)
        return pltpu.make_async_copy(wq_hbm.at[:, at], wq.at[:, at], load.at[j])
    @pl.when(g == 0)
    def _():
        hello([(None, chip_at(c, r), k, n) for r in (1, 2)]
              + [(None, c, 1 - k, n), (n > 0, c, k, n - 1), (n < nz - 1, c, k, n + 1)])
        for cp in mine + sends: cp.start()
        for j in range(wq.shape[1] // 256): load_q(j).start()
        pltpu.make_async_copy(wo_hbm, wo, loc.at[2]).start()
        mine[0].wait()
        for way in range(2): line.start(0, 0, way)
        twin(n).start()
        def norm(i, carry):
            at = pl.ds(pl.multiple_of(i * 16, 16), 16)
            xn1[at, :] = scaled(tok[at, :].astype(f32), gain1[...])
            return carry
        lax.fori_loop(0, slots // 16, norm, 0)
        def project(j, carry):
            load_q(j).wait()
            at = pl.ds(pl.multiple_of(j * 256, 256), 256)
            qkv[:, at] = jnp.dot(xn1[...], wq[:, at], preferred_element_type=f32)
            return carry
        lax.fori_loop(0, wq.shape[1] // 256, project, 0)
    @pl.when(g == 1)
    def _(): line.step(0, 1, lambda z: twin(z).start())
    @pl.when(g == 0)
    def _():
        ks[...] = jnp.zeros_like(ks)
        vs[...] = jnp.zeros_like(vs)
    lane = lax.broadcasted_iota(jnp.int32, (slots, PAIR), 1)
    tables = (tab_ref[0], tab_ref[1], tab_ref[2])
    first = QUERY_HEADS * HEAD_SIZE
    def pair_at(at): return pl.ds(pl.multiple_of(at, PAIR), PAIR)
    key = rotate(qkv[:, pair_at(first + g // 2 * PAIR)], tables)
    val = qkv[:, pair_at(first + KEY_VALUE_HEADS * HEAD_SIZE + g // 2 * PAIR)]
    odd = g % 2 == 1
    for x, own, stack, scale in ((key, k_out, ks, HEAD_SIZE ** -0.5), (val, v_out, vs, 1.0)):
        x = jnp.where(lane < HEAD_SIZE, jnp.where(odd, pltpu.roll(x, HEAD_SIZE, 1), x), 0.0).astype(bf16)
        own[0] = x
        x = x.astype(f32) * scale
        stack[0, 0:slots, :] = x.astype(bf16)
        stack[1, 0:slots, :] = pltpu.roll(x, HEAD_SIZE, 1).astype(bf16)
    for start, size, keys in row_blocks(slots):
        below = lax.broadcasted_iota(jnp.int32, (size, 128), 0) >= lax.broadcasted_iota(jnp.int32, (size, 128), 1)
        lse = jnp.zeros((size, PAIR), f32)
        here = lane[0:size]
        for p in range(PAIRS):
            span = slice(p * PAIR, (p + 1) * PAIR)
            rows = slice(start, start + size)
            q = rotate(qkv[rows, pair_at(g * REPEAT * HEAD_SIZE + p * PAIR)], tuple(t[rows] for t in tables)).astype(bf16)
            qr_ref[rows, span] = q
            ctx = jnp.zeros((size, PAIR), f32)
            for h in range(2):
                s = lax.dot_general(q, ks[h, 0:keys, :], contract_last, preferred_element_type=f32)
                s = causal(s, below, masked_score)
                peak = jnp.max(s, axis=-1, keepdims=True)
                e = jnp.exp(s - peak)
                total = jnp.sum(e, axis=-1, keepdims=True)
                lse = jnp.where(here == 2 * p + h, peak + jnp.log(total), lse)
                probs = (e * (1.0 / total)).astype(bf16)
                ctx = ctx + jnp.dot(probs, vs[h, 0:keys, :], preferred_element_type=f32)
            ctx_ref[rows, pair_at(g * REPEAT * HEAD_SIZE + p * PAIR)] = ctx.astype(bf16)
        lse_ref[0, start : start + size, :] = lse
    @pl.when(g == KEY_VALUE_HEADS - 1)
    def _():
        for cp in sends: cp.wait_recv()
        for cp in relays: cp.start()
        line.step(0, 2, lambda z: twin(z).start())
        pltpu.make_async_copy(wo_hbm, wo, loc.at[2]).wait()
        def project(j, carry):
            at = pl.ds(pl.multiple_of(j * 256, 256), 256)
            hidden[:, at] = tok[:, at].astype(f32) + lax.dot_general(ctx_ref[...], wo[at, :], contract_last, preferred_element_type=f32)
            return carry
        lax.fori_loop(0, width // 256, project, 0)
        def norm(i, carry):
            at = pl.ds(pl.multiple_of(i * 16, 16), 16)
            xn2[at, :] = scaled(hidden[at, :], gain2[...])
            return carry
        lax.fori_loop(0, slots // 16, norm, 0)
        for s in range(3, nz): line.step(0, s, lambda z: twin(z).start())
        for cp in relays: cp.wait()
        for z in range(nz): twin(z).wait()
        for cp in sends: cp.wait_send()
        mine[1].wait()
        line.finish(0)


def attend_all(nz, tokens, gain1, gain2, tables, w_qkv, w_out, gy, gd_own):
    slots, width = tokens.shape
    dma, vm = pltpu.SemaphoreType.DMA, pltpu.VMEM
    bf16, f32 = jnp.bfloat16, jnp.float32
    keys = -(-slots // 128) * 128
    heads = QUERY_HEADS * HEAD_SIZE
    shape = jax.ShapeDtypeStruct
    def fixed(*dims): return pl.BlockSpec(dims, lambda g: (0,) * len(dims))
    per_head = pl.BlockSpec((1, slots, PAIR), lambda g: (g, 0, 0))
    per_head_shape = (KEY_VALUE_HEADS, slots, PAIR)
    return pl.pallas_call(
        functools.partial(attend_kernel, nz),
        grid=(KEY_VALUE_HEADS,),
        out_shape=(shape((slots, heads), bf16), shape(per_head_shape, bf16), shape(per_head_shape, bf16), shape(per_head_shape, f32),
                   shape((slots, heads), bf16), shape((slots, width), bf16), shape((slots, width), f32), shape((slots, width), bf16),
                   shape((CHIPS,) + gy.shape, bf16), shape((CHIPS, CORES * nz) + gd_own.shape[1:], bf16)),
        in_specs=[fixed(slots, width), fixed(1, width), fixed(1, width), fixed(3, slots, PAIR), ANY, ANY, fixed(*gy.shape), fixed(*gd_own.shape)],
        out_specs=(pl.BlockSpec((slots, REPEAT * HEAD_SIZE), lambda g: (0, g)), per_head, per_head, per_head,
                   fixed(slots, heads), fixed(slots, width), fixed(slots, width), fixed(slots, width), ANY, ANY),
        scratch_shapes=[vm((2, keys, PAIR), bf16), vm((2, keys, PAIR), bf16), vm(w_qkv.shape, bf16), vm(w_out.shape, bf16),
                        vm((slots, w_qkv.shape[1]), f32), dma((w_qkv.shape[1] // 256,)), dma((3,)), dma((2,)), dma((2,)), dma((2,)), dma((2,)),
                        dma((1, 2, nz)), dma((1, 2, nz)), dma((nz,)), dma((nz,))],
        compiler_params=pltpu.CompilerParams(collective_id=4, has_side_effects=True, vmem_limit_bytes=56 << 20),
        cost_estimate=pl.CostEstimate(flops=4 * slots * width * heads, bytes_accessed=40 << 20, transcendentals=QUERY_HEADS * slots * slots),
        name="attend",
    )(tokens, gain1, gain2, tables, w_qkv, w_out, gy, gd_own)


def attend_back_kernel(q_ref, k_ref, v_ref, lse_ref, gc_ref, tab_ref, part, gq_ref, gk_ref, gv_ref, crossed,
                       ks, kt, vt, ds, pr, qs, gs, s_s, s_r):
    g = pl.program_id(0)
    c, k, n = place()
    copy = remote(part, crossed, s_s, s_r, chip_at(c, 3), k, n)
    @pl.when(g == 0)
    def _():
        hello([(None, chip_at(c, 3), k, n)])
        copy.start()
    f32, bf16 = jnp.float32, jnp.bfloat16
    slots = q_ref.shape[0]
    scale = HEAD_SIZE ** -0.5
    @pl.when(g == 0)
    def _():
        for ref in (ks, kt, vt, ds, pr): ref[...] = jnp.zeros_like(ref)
    lane = lax.broadcasted_iota(jnp.int32, (slots, PAIR), 1)
    tables = (tab_ref[0], tab_ref[1], tab_ref[2])
    key, val = k_ref[0].astype(f32), v_ref[0].astype(f32)
    for stack, x in ((ks, key * scale), (kt, key), (vt, val)):
        stack[0, 0:slots, :] = x.astype(bf16)
        stack[1, 0:slots, :] = pltpu.roll(x, HEAD_SIZE, 1).astype(bf16)
    for at, size, keys in row_blocks(slots):
        rows = slice(at, at + size)
        below = lax.broadcasted_iota(jnp.int32, (size, 128), 0) >= lax.broadcasted_iota(jnp.int32, (size, 128), 1)
        lse = lse_ref[0, rows, :]
        for p in range(PAIRS):
            span = slice(p * PAIR, (p + 1) * PAIR)
            deep = slice(p * slots + at, p * slots + at + size)
            q, gc = q_ref[rows, span], gc_ref[rows, span]
            qs[deep, :] = q
            gs[deep, :] = gc
            gq = jnp.zeros((size, PAIR), f32)
            for h in range(2):
                s = lax.dot_general(q, ks[h, 0:keys, :], contract_last, preferred_element_type=f32)
                e = jnp.exp(s - lse[:, 2 * p + h : 2 * p + h + 1])
                probs = causal(e, below, 0.0)
                pr[h, deep, 0:keys] = probs.astype(bf16)
                gp = lax.dot_general(gc, vt[h, 0:keys, :], contract_last, preferred_element_type=f32)
                inner = jnp.sum(gp * probs, axis=-1, keepdims=True)
                grad = (probs * (gp - inner) * scale).astype(bf16)
                ds[h, deep, 0:keys] = grad
                gq = gq + jnp.dot(grad, kt[h, 0:keys, :], preferred_element_type=f32)
            gq_ref[rows, span] = unrotate(gq, tuple(t[rows] for t in tables)).astype(bf16)
    for src, right, out, turn in ((ds, qs, gk_ref, True), (pr, gs, gv_ref, False)):
        lo, hi = (
            lax.dot_general(src[h], right[...], contract_first, preferred_element_type=f32)[0:slots] for h in range(2)
        )
        x = jnp.where(lane < HEAD_SIZE, lo + pltpu.roll(hi, HEAD_SIZE, 1), 0.0)
        if turn: x = unrotate(x, tables)
        @pl.when(g % 2 == 0)
        def _(): out[...] = x
        @pl.when(g % 2 == 1)
        def _(): out[...] = jnp.where(lane < HEAD_SIZE, out[...], pltpu.roll(x, HEAD_SIZE, 1))
    @pl.when(g == KEY_VALUE_HEADS - 1)
    def _(): copy.wait()


def attend_back_all(q, k, v, lse, grad_context, tables, part):
    slots = q.shape[0]
    wide = REPEAT * HEAD_SIZE
    bf16, f32, vm = jnp.bfloat16, jnp.float32, pltpu.VMEM
    keys = -(-slots // 128) * 128
    shape = jax.ShapeDtypeStruct
    per_head = pl.BlockSpec((1, slots, PAIR), lambda g: (g, 0, 0))
    wide_spec = pl.BlockSpec((slots, wide), lambda g: (0, g))
    two = pl.BlockSpec((slots, PAIR), lambda g: (0, g // 2))
    return pl.pallas_call(
        attend_back_kernel,
        grid=(KEY_VALUE_HEADS,),
        out_shape=(shape((slots, QUERY_HEADS * HEAD_SIZE), bf16), shape((slots, KEY_VALUE_HEADS * HEAD_SIZE), f32),
                   shape((slots, KEY_VALUE_HEADS * HEAD_SIZE), f32), shape(part.shape, part.dtype)),
        in_specs=[wide_spec, per_head, per_head, per_head, wide_spec, pl.BlockSpec((3, slots, PAIR), lambda g: (0, 0, 0)), ANY],
        out_specs=(wide_spec, two, two, ANY),
        scratch_shapes=[vm((2, keys, PAIR), bf16)] * 3 + [vm((2, PAIRS * slots, keys), bf16)] * 2 + [vm((PAIRS * slots, PAIR), bf16)] * 2
        + [pltpu.SemaphoreType.DMA] * 2,
        compiler_params=pltpu.CompilerParams(collective_id=2, has_side_effects=True, vmem_limit_bytes=40 << 20),
        name="attend_back",
    )(q, k, v, lse, grad_context, tables, part)


class SumLine:
    def __init__(self, nz, at, piece, slot, send, recv):
        self.nz, self.at, self.piece, self.slot, self.send, self.recv = nz, at, piece, slot, send, recv

    def _hop(self, a, way, j):
        c, k, n = self.at
        i = jnp.clip(j - n - 1 if way == 0 else n - 1 - j, 0, self.nz - 2)
        return remote(self.piece(a, j), self.slot(a, way, i), self.send.at[a, way, j], self.recv.at[a, way, j],
                      c, k, n + 1 if way == 0 else n - 1)

    def step(self, some, t):
        nz, n = self.nz, self.at[2]
        for way in range(2):
            hops = n if way == 0 else nz - 1 - n
            j = jnp.clip(n + nz - 1 - t if way == 0 else t - hops, 0, nz - 1)
            for a in some:
                @pl.when((hops > 0) & (t >= hops))
                def _():
                    self._hop(a, way, j).wait_recv()
                    add_into(self.piece(a, j), self.slot(a, way, jnp.clip(j - n if way == 0 else n - j, 0, nz - 2)))
                @pl.when((t >= hops) & (j != n))
                def _(): self._hop(a, way, j).start()

    def finish(self, a):
        n = self.at[2]
        for j in range(self.nz):
            for way in range(2):
                @pl.when(n < j if way == 0 else n > j)
                def _(): self._hop(a, way, j).wait_send()


def gradient_kernel(nz, gal_hbm, ctx_hbm, xn_hbm, gq_hbm, wq_hbm, tok_hbm, gh_hbm, gain, gain_mlp, out0, out1, out2, grad_tokens,
                    took0, took1, took2, away0, away1, away2, zbuf0, zbuf1, zbuf2, gal, ctx, xn, gq, wq, tok, gh, gx, xt, gain_row,
                    core_s, core_r, half_s, half_r, main_s, main_r, z_s, z_r, load, loc):
    f32, bf16 = jnp.float32, jnp.bfloat16
    items = 3
    outs, took, away, zbuf = (out0, out1, out2), (took0, took1, took2), (away0, away1, away2), (zbuf0, zbuf1, zbuf2)
    c, k, n = place()
    left, right = n > 0, n < nz - 1
    cx, cy, cd = (chip_at(c, r) for r in (1, 2, 3))
    loads = [pltpu.make_async_copy(a, b, load.at[i]) for i, (a, b) in enumerate(
        ((gal_hbm, gal), (ctx_hbm, ctx), (xn_hbm, xn), (gq_hbm, gq), (wq_hbm, wq), (tok_hbm, tok), (gh_hbm, gh)))]
    for cp in loads: cp.start()
    hello([(None, cc, k, n) for cc in (cx, cy, cd)] + [(None, c, 1 - k, n), (left, c, k, n - 1), (right, c, k, n + 1)])
    slots, width = gal.shape
    rows = out0.shape[0]
    part = nz * rows
    half = part // 2
    top, low = pl.ds(0, half), pl.ds(half, half)
    def arrive(a, at, size): return zbuf[a].at[pl.ds(at, size)]
    swap = [remote(away[a], took[a], core_s.at[a], core_r.at[a], c, 1 - k, n) for a in range(items)]
    cross = [[remote(took[a].at[cd, top], arrive(a, 2 * part, half), half_s.at[a, 0], half_r.at[a, 0], cx, k, n),
              remote(took[a].at[cd, low], arrive(a, 2 * part + half, half), half_s.at[a, 1], half_r.at[a, 1], cy, k, n)]
             for a in range(items)]
    main = [[remote(took[a].at[cx, top], arrive(a, 0, half), main_s.at[a, 0], main_r.at[a, 0], cx, k, n),
             remote(took[a].at[cy, low], arrive(a, part + half, half), main_s.at[a, 1], main_r.at[a, 1], cy, k, n),
             remote(took[a].at[cx, low], arrive(a, half, half), main_s.at[a, 2], main_r.at[a, 2], cx, k, n),
             remote(took[a].at[cy, top], arrive(a, part, half), main_s.at[a, 3], main_r.at[a, 3], cy, k, n)]
            for a in range(items)]

    def products(left_side, right_side, kk, put):
        for t in range(CHIPS):
            at = pl.ds(pl.multiple_of((t * CORES + kk) * part, 128), part)
            xt[t * part : (t + 1) * part, :] = left_side[:, at].T
        def step(j, carry):
            at = pl.ds(pl.multiple_of(j * 256, 256), 256)
            put(at, jnp.dot(xt[...], right_side[:, at], preferred_element_type=f32).reshape(CHIPS, part, 256))
            return carry
        lax.fori_loop(0, right_side.shape[1] // 256, step, 0)

    def theirs(a, left_side, right_side):
        def put(at, v): away[a][:, :, at] = v.astype(bf16)
        products(left_side, right_side, 1 - k, put)
        swap[a].start()

    def ours(a, left_side, right_side):
        swap[a].wait_recv()
        def put(at, v): took[a][:, :, at] = (took[a][:, :, at].astype(f32) + v).astype(bf16)
        products(left_side, right_side, k, put)
        for cp in cross[a]: cp.start()

    def input_gradient():
        loads[4].wait()
        def step(j, carry):
            at = pl.ds(pl.multiple_of(j * 256, 256), 256)
            gx[:, at] = lax.dot_general(gq[...], wq[at, :], contract_last, preferred_element_type=f32)
            return carry
        lax.fori_loop(0, width // 256, step, 0)

    def input_norm():
        for cp in loads[5:]: cp.wait()
        def step(j, total):
            at = pl.ds(pl.multiple_of(j * 16, 16), 16)
            x, g = tok[at, :].astype(f32), gx[at, :]
            scale = lax.rsqrt(jnp.mean(x * x, axis=-1, keepdims=True) + norm_eps)
            hat = x * scale
            g1 = g * gain[...]
            gh[at, :] = gh[at, :] + scale * (g1 - hat * jnp.mean(g1 * hat, axis=-1, keepdims=True))
            t = g * hat
            return total + t[0:8] + t[8:16]
        total = lax.fori_loop(0, slots // 16, step, jnp.zeros((8, width), f32))
        return jnp.sum(total, axis=0, keepdims=True)

    def gains_swap(of_attn):
        row = lax.broadcasted_iota(jnp.int32, (128, part), 0)
        def columns_of(t, kk):
            at = pl.ds(pl.multiple_of((t * CORES + kk) * part, 128), part)
            return jnp.where(row == 0, gain_row[0:1, at], jnp.where(row == 1, gain_mlp[0:1, at], 0.0)).T
        gain_row[0:1, :] = of_attn
        for t in range(CHIPS): away[2][t] = columns_of(t, 1 - k).astype(bf16)
        swap[2].start()
        swap[2].wait_recv()
        for t in range(CHIPS): took[2][t] = (took[2][t].astype(f32) + columns_of(t, k)).astype(bf16)
        for cp in cross[2]: cp.start()

    def relay(a):
        cross[a][0].wait_recv()
        add_into(took[a].at[cy, top], arrive(a, 2 * part, half))
        main[a][3].start()
        cross[a][1].wait_recv()
        add_into(took[a].at[cx, low], arrive(a, 2 * part + half, half))
        for i in (2, 0, 1): main[a][i].start()

    def mine(a):
        for cp in main[a]: cp.wait_recv()
        add_into(took[a].at[c], arrive(a, 0, part), arrive(a, part, part))

    line = SumLine(nz, (c, k, n), lambda a, j: took[a].at[c, pl.ds(pl.multiple_of(j * rows, rows), rows)],
                   lambda a, way, i: arrive(a, pl.multiple_of(2 * part + 2 * half + (way * (nz - 1) + i) * rows, rows), rows), z_s, z_r)

    for cp in loads[:2]: cp.wait()
    theirs(0, gal, ctx)
    for cp in loads[2:4]: cp.wait()
    theirs(1, xn, gq)
    ours(0, gal, ctx)
    ours(1, xn, gq)
    input_gradient()
    relay(0)
    gains_swap(input_norm())
    stores = [pltpu.make_async_copy(gh, grad_tokens, loc.at[items])]
    stores[0].start()
    for a in range(1, items): relay(a)
    mine(0)
    for t in range(nz): line.step([0], t)
    stores.append(pltpu.make_async_copy(line.piece(0, n), outs[0], loc.at[0]))
    stores[-1].start()
    for a in range(1, items):
        mine(a)
        stores.append(pltpu.make_async_copy(took[a].at[c], outs[a], loc.at[a]))
        stores[-1].start()
    for cp in stores: cp.wait()
    for a in range(items):
        swap[a].wait_send()
        for cp in cross[a] + main[a]: cp.wait_send()
    line.finish(0)


def gradient_all(nz, gal, ctx, xn, gq, wq, tokens, grad_hidden, gain, gain_mlp, cid):
    dma, vm = pltpu.SemaphoreType.DMA, pltpu.VMEM
    bf16, f32 = jnp.bfloat16, jnp.float32
    slots, width = gal.shape
    m = 3
    part = width // (CHIPS * CORES)
    rows = part // nz
    widths = (ctx.shape[1], gq.shape[1], 128)
    shape = jax.ShapeDtypeStruct
    blocks = [vm((CHIPS, part, w), bf16) for w in widths]
    row = pl.BlockSpec((1, width), lambda: (0, 0))
    return pl.pallas_call(
        functools.partial(gradient_kernel, nz),
        out_shape=(shape((rows, widths[0]), bf16),) + tuple(shape((part, w), bf16) for w in widths[1:]) + (shape((slots, width), f32),),
        in_specs=[ANY] * 7 + [row, row], out_specs=(ANY,) * (m + 1),
        scratch_shapes=blocks + blocks + [vm((3 * part + 2 * nz * rows, w), bf16) for w in widths]
        + [vm(gal.shape, bf16), vm(ctx.shape, bf16), vm(xn.shape, bf16), vm(gq.shape, bf16), vm(wq.shape, bf16), vm(tokens.shape, bf16),
           vm((slots, width), f32), vm((slots, width), f32), vm((CHIPS * part, slots), bf16), vm((8, width), f32)]
        + [dma((m,)), dma((m,)), dma((m, 2)), dma((m, 2)), dma((m, 4)), dma((m, 4)), dma((m, 2, nz)), dma((m, 2, nz)), dma((7,)), dma((m + 1,))],
        compiler_params=pltpu.CompilerParams(collective_id=cid, has_side_effects=True, vmem_limit_bytes=62 << 20),
        name="gradient_all",
    )(gal, ctx, xn, gq, wq, tokens, grad_hidden, gain, gain_mlp)


def finish_kernel(nz, down, gu, part1, part2, out_q, out_k, out_v, out_gain, out_d, out_g, out_u,
                  acc1, acc2, in1, in2, ff, wide1, wide2, wide_ff, z_s, z_r, ff_s, ff_r, load, loc):
    f32 = jnp.float32
    c, k, n = place()
    rows, cols = down.shape[1:]
    loads = [pltpu.make_async_copy(a, b, load.at[i]) for i, (a, b) in enumerate(((part1, acc1), (part2, acc2)))]
    for cp in loads: cp.start()
    hello([(None, chip_at(c, r), k, n) for r in (1, 2, 3)] + [(n > 0, c, k, n - 1), (n < nz - 1, c, k, n + 1)])
    acc, came = (acc1, acc2), (in1, in2)
    line = SumLine(nz, (c, k, n), lambda a, j: acc[a].at[pl.ds(pl.multiple_of(j * rows, rows), rows)],
                   lambda a, way, i: came[a].at[way, i], z_s, z_r)
    def term(m, cc): return down.at[cc] if m == 0 else gu.at[cc, :, pl.ds((m - 1) * cols, cols)]
    home = [[remote(term(m, chip_at(c, r)), ff.at[m, r - 1], ff_s.at[m, r - 1], ff_r.at[m, r - 1], chip_at(c, r), k, n)
             for r in (1, 2, 3)] for m in range(3)]
    for cps in home:
        for cp in cps: cp.start()
    for cp in loads: cp.wait()
    line.step([0, 1], 0)
    stores = []
    def store(src, dst, i):
        stores.append(pltpu.make_async_copy(src, dst, loc.at[i]))
        stores[-1].start()
    outs = (out_d, out_g, out_u)
    def put(m, r, value):
        wide_ff[m, r] = value.astype(f32)
        at = pl.ds(pl.multiple_of(chip_at(c, r) * cols, 128), cols)
        store(wide_ff.at[m, r], outs[m].at[:, at], 4 + m * CHIPS + r)
    for m in range(3): put(m, 0, term(m, c)[...])
    for t in range(1, nz): line.step([0, 1], t)
    for m in range(3):
        for r in (1, 2, 3):
            home[m][r - 1].wait_recv()
            put(m, r, ff[m, r - 1])
    wide1[...] = line.piece(0, n)[...].astype(f32)
    wide2[...] = line.piece(1, n)[...].astype(f32)
    first = 0
    for i, out in enumerate((out_q, out_k, out_v)):
        store(wide1.at[:, pl.ds(first, out.shape[1])], out, i)
        first += out.shape[1]
    store(wide2, out_gain, 3)
    for cp in stores: cp.wait()
    for cps in home:
        for cp in cps: cp.wait_send()
    for a in range(2): line.finish(a)


def finish_all(nz, down, gu, part1, part2, key_width, cid):
    dma, vm = pltpu.SemaphoreType.DMA, pltpu.VMEM
    bf16, f32 = jnp.bfloat16, jnp.float32
    rows, cols = down.shape[1:]
    w1, w2 = part1.shape[1], part2.shape[1]
    def out(w): return jax.ShapeDtypeStruct((rows, w), f32)
    return pl.pallas_call(
        functools.partial(finish_kernel, nz),
        out_shape=(out(w1 - 2 * key_width), out(key_width), out(key_width), out(w2)) + (out(CHIPS * cols),) * 3,
        in_specs=[VMEM, VMEM, ANY, ANY], out_specs=(ANY,) * 7,
        scratch_shapes=[vm(part1.shape, bf16), vm(part2.shape, bf16), vm((2, nz - 1, rows, w1), bf16), vm((2, nz - 1, rows, w2), bf16),
                        vm((3, CHIPS - 1, rows, cols), bf16), vm((rows, w1), f32), vm((rows, w2), f32), vm((3, CHIPS, rows, cols), f32),
                        dma((2, 2, nz)), dma((2, 2, nz)), dma((3, 3)), dma((3, 3)), dma((2,)), dma((4 + 3 * CHIPS,))],
        compiler_params=pltpu.CompilerParams(collective_id=cid, has_side_effects=True, vmem_limit_bytes=40 << 20),
        name="finish_all",
    )(down, gu, part1, part2)


def fits(mesh):
    return mesh.shape["wide"] == CHIPS * CORES


def fast_device(
    nz,
    tokens,
    cotangent,
    lengths,
    positions,
    norm_attn,
    w_query,
    w_key,
    w_value,
    w_output,
    norm_mlp,
    w_gate,
    w_up,
    w_down,
):
    f32, bf16 = jnp.float32, jnp.bfloat16
    c, k, n = place()
    slots, width = tokens.shape
    rows = w_query.shape[0]
    query_width, key_width = w_query.shape[1], w_key.shape[1]
    cols = w_gate.shape[1] // CHIPS
    valid_rows = (jnp.arange(slots) < lengths[0]).astype(f32)[:, None]
    tables = lane_tables(positions)
    grad_y = cotangent.astype(f32) * valid_rows
    grad_y_low = grad_y.astype(bf16)
    gains = jnp.zeros((rows, 128), bf16).at[:, 0].set(norm_attn).at[:, 1].set(norm_mlp)
    w_qkv, w_out, gain_cols, ff_gate_up, ff_down = gather_all(
        nz, w_query, w_key, w_value, w_output, gains, w_gate, w_up, w_down
    )
    gain_attn = gain_cols[:, 0].astype(f32)
    gain_mlp = gain_cols[:, 1].astype(f32)

    query_rotated, key_rotated, value_reduced, log_totals, context, scaled_attn, hidden, scaled_mlp, gy_all, ff_down = attend_all(
        nz, tokens, gain_attn[None], gain_mlp[None], tables, w_qkv, w_out, grad_y_low, ff_down
    )
    ff_gate_up, ff_down = (w.reshape(CHIPS * CORES, nz, rows, w.shape[-1]) for w in (ff_gate_up, ff_down))
    normed_mlp = normalize(hidden)
    grad_x_parts, mlp_parts, mlp_cross, down_sums, ff_sums = mlp_all(nz, scaled_mlp, gy_all, ff_gate_up, ff_down)
    grad_xn2 = jnp.sum(grad_x_parts.astype(f32), axis=0)
    grad_gain_mlp = jnp.sum(grad_xn2 * normed_mlp, axis=0)
    grad_hidden = grad_y + norm_back(grad_xn2 * gain_mlp, normed_mlp, hidden)
    grad_attn_low = grad_hidden.astype(bf16)
    grad_context = jnp.dot(grad_attn_low, w_out, preferred_element_type=f32).astype(bf16)
    grad_query, grad_key, grad_value, mlp_crossed = attend_back_all(
        query_rotated, key_rotated, value_reduced, log_totals, grad_context, tables, mlp_cross
    )
    output = (valid_rows * (hidden + jnp.sum(mlp_parts.astype(f32), axis=0) + mlp_crossed.astype(f32))).astype(bf16)
    grad_qkv = jnp.concatenate([grad_query, grad_key.astype(bf16), grad_value.astype(bf16)], 1)
    ff_sums = lax.psum_scatter(ff_sums, "narrow", scatter_dimension=0, tiled=True)
    grad_w_output, qkv_part, gain_part, grad_tokens = gradient_all(
        nz, grad_attn_low, context, scaled_attn, grad_qkv, w_qkv, tokens, grad_hidden, gain_attn[None], grad_gain_mlp[None], 3
    )
    grad_w_output = grad_w_output.astype(f32)
    grad_w_query, grad_w_key, grad_w_value, gain_sums, grad_w_down, grad_w_gate, grad_w_up = finish_all(
        nz, down_sums, ff_sums.reshape(CHIPS, rows, 2 * cols), qkv_part, gain_part, key_width, 5
    )
    grad_norm_attn, grad_norm_mlp = gain_sums[:, 0], gain_sums[:, 1]
    return (
        output,
        grad_tokens,
        grad_norm_attn,
        grad_w_query,
        grad_w_key,
        grad_w_value,
        grad_w_output,
        grad_norm_mlp,
        grad_w_gate,
        grad_w_up,
        grad_w_down,
    )


def solution(mesh):
    in_specs = (
        P(("wide", "narrow"), None),
        P(("wide", "narrow"), None),
        P(("wide", "narrow")),
        P(("wide", "narrow")),
        P(("wide", "narrow")),
        P(("wide", "narrow"), None),
        P(("wide", "narrow"), None),
        P(("wide", "narrow"), None),
        P(("wide", "narrow"), None),
        P(("wide", "narrow")),
        P(("wide", "narrow"), None),
        P(("wide", "narrow"), None),
        P(("wide", "narrow"), None),
    )
    out_specs = (
        P(("wide", "narrow"), None),
        P(("wide", "narrow"), None),
        P(("wide", "narrow")),
        P(("wide", "narrow"), None),
        P(("wide", "narrow"), None),
        P(("wide", "narrow"), None),
        P(("wide", "narrow"), None),
        P(("wide", "narrow")),
        P(("wide", "narrow"), None),
        P(("wide", "narrow"), None),
        P(("wide", "narrow"), None),
    )
    body = functools.partial(fast_device, mesh.shape["narrow"]) if fits(mesh) else per_device
    return jax.shard_map(
        body, mesh=mesh, in_specs=in_specs, out_specs=out_specs, check_vma=False
    )
```

```python
import functools
import math

import jax
import jax.numpy as jnp
from jax import lax
from jax.experimental import pallas as pl
from jax.experimental.pallas import tpu as pltpu
from jax.sharding import PartitionSpec as P

QUERY_HEADS = 32
KEY_VALUE_HEADS = 4
HEAD_SIZE = 64


norm_eps = 1e-05
rope_base = 10000.0
masked_score = -1e30
contract_last = (((1,), (1,)), ((), ()))
contract_first = (((0,), (0,)), ((), ()))


def rope_tables(positions):
    half_dim = HEAD_SIZE // 2
    inv_freq = jnp.exp(
        -math.log(rope_base) * jnp.arange(half_dim, dtype=jnp.float32) * 2.0 / HEAD_SIZE
    )
    angles = positions.astype(jnp.float32)[..., None] * inv_freq
    cosine = jnp.cos(angles)
    sine_part = jnp.sin(angles)
    return (jnp.concatenate([cosine, cosine], -1), jnp.concatenate([sine_part, sine_part], -1))


def apply_rotary(values, cosine_table, sine_table):
    half_dim = values.shape[-1] // 2
    turned = jnp.concatenate([-values[..., half_dim:], values[..., :half_dim]], -1)
    return values * cosine_table[..., None, :] + turned * sine_table[..., None, :]


def invert_rotary(grad_rows, cosine_table, sine_table):
    half_dim = grad_rows.shape[-1] // 2
    with_cos = grad_rows * cosine_table[..., None, :]
    with_sin = grad_rows * sine_table[..., None, :]
    return with_cos + jnp.concatenate([with_sin[..., half_dim:], -with_sin[..., :half_dim]], -1)


def normalize(values):
    return values * lax.rsqrt(jnp.mean(values * values, axis=-1, keepdims=True) + norm_eps)


def norm_back(grad_hat, normed, values):
    row_scale = lax.rsqrt(jnp.mean(values * values, axis=-1, keepdims=True) + norm_eps)
    return row_scale * (grad_hat - normed * jnp.mean(grad_hat * normed, axis=-1, keepdims=True))


def attention_inputs(normed, norm_attn, w_query, w_key, w_value):
    gain_piece = lax.all_gather(norm_attn, ("wide", "narrow"), axis=0, tiled=True)
    query_rows = lax.all_gather(w_query, ("wide", "narrow"), axis=0, tiled=True)
    key_rows = lax.all_gather(w_key, ("wide", "narrow"), axis=0, tiled=True)
    value_rows = lax.all_gather(w_value, ("wide", "narrow"), axis=0, tiled=True)
    gain_float = gain_piece.astype(jnp.float32)
    columns = (normed * gain_float).astype(jnp.bfloat16)
    query_sum = jnp.dot(columns, query_rows, preferred_element_type=jnp.float32)
    key_sum = jnp.dot(columns, key_rows, preferred_element_type=jnp.float32)
    value_sum = jnp.dot(columns, value_rows, preferred_element_type=jnp.float32)
    return (gain_float, columns, query_sum, key_sum, value_sum)


def mlp_inputs(normed, norm_mlp, w_gate, w_up):
    gain_piece = lax.all_gather(norm_mlp, ("wide", "narrow"), axis=0, tiled=True)
    gate_rows = lax.all_gather(w_gate, ("wide", "narrow"), axis=0, tiled=True)
    up_rows = lax.all_gather(w_up, ("wide", "narrow"), axis=0, tiled=True)
    gain_float = gain_piece.astype(jnp.float32)
    columns = (normed * gain_float).astype(jnp.bfloat16)
    gate_sum = jnp.dot(columns, gate_rows, preferred_element_type=jnp.float32)
    up_sum = jnp.dot(columns, up_rows, preferred_element_type=jnp.float32)
    return (gain_float, columns, gate_sum, up_sum)


def head_slices(query_rotated, key_rotated, value_reduced, shared_key_head):
    row_total_count = query_rotated.shape[0]
    heads_per_group = QUERY_HEADS // KEY_VALUE_HEADS
    query_head = query_rotated[
        :,
        shared_key_head
        * heads_per_group
        * HEAD_SIZE : (shared_key_head + 1)
        * heads_per_group
        * HEAD_SIZE,
    ].reshape(row_total_count, heads_per_group, HEAD_SIZE)
    key_head = key_rotated[:, shared_key_head * HEAD_SIZE : (shared_key_head + 1) * HEAD_SIZE]
    value_head = value_reduced[:, shared_key_head * HEAD_SIZE : (shared_key_head + 1) * HEAD_SIZE]
    return (query_head, key_head, value_head)


def head_scores(query_head, key_head):
    row_total_count = query_head.shape[0]
    causal = jnp.arange(row_total_count)[:, None] >= jnp.arange(row_total_count)[None, :]
    raw_scores = jnp.einsum("qrd,kd->rqk", query_head, key_head, preferred_element_type=jnp.float32)
    return jnp.where(causal, raw_scores * HEAD_SIZE ** (-0.5), masked_score)


def attend(query_rotated, key_rotated, value_reduced):
    row_total_count = query_rotated.shape[0]
    heads_per_group = QUERY_HEADS // KEY_VALUE_HEADS
    contexts = []
    log_totals = []
    for shared_key_head in range(KEY_VALUE_HEADS):
        query_head, key_head, value_head = head_slices(
            query_rotated, key_rotated, value_reduced, shared_key_head
        )
        scores = head_scores(query_head, key_head)
        row_peak = jnp.max(scores, axis=-1, keepdims=True)
        exp_scores = jnp.exp(scores - row_peak)
        row_total = jnp.sum(exp_scores, axis=-1, keepdims=True)
        probs = exp_scores / row_total
        context_head = jnp.einsum(
            "rqk,kd->qrd",
            probs.astype(jnp.bfloat16),
            value_head,
            preferred_element_type=jnp.float32,
        )
        contexts.append(context_head.reshape(row_total_count, heads_per_group * HEAD_SIZE))
        log_totals.append(row_peak + jnp.log(row_total))
    return (jnp.concatenate(contexts, 1).astype(jnp.bfloat16), log_totals)


def attend_back(query_rotated, key_rotated, value_reduced, log_totals, grad_context):
    row_total_count = query_rotated.shape[0]
    heads_per_group = QUERY_HEADS // KEY_VALUE_HEADS
    score_scale = HEAD_SIZE ** (-0.5)
    query_grads = []
    key_grads = []
    value_grads = []
    for shared_key_head in range(KEY_VALUE_HEADS):
        query_head, key_head, value_head = head_slices(
            query_rotated, key_rotated, value_reduced, shared_key_head
        )
        scores = head_scores(query_head, key_head)
        probs = jnp.exp(scores - log_totals[shared_key_head])
        probs_low = probs.astype(jnp.bfloat16)
        grad_head = grad_context[
            :,
            shared_key_head
            * heads_per_group
            * HEAD_SIZE : (shared_key_head + 1)
            * heads_per_group
            * HEAD_SIZE,
        ].reshape(row_total_count, heads_per_group, HEAD_SIZE)
        grad_probs = jnp.einsum(
            "qrd,kd->rqk", grad_head, value_head, preferred_element_type=jnp.float32
        )
        value_grads.append(
            jnp.einsum("rqk,qrd->kd", probs_low, grad_head, preferred_element_type=jnp.float32)
        )
        inner_sum = jnp.sum(grad_probs * probs, axis=-1, keepdims=True)
        grad_scores = (probs * (grad_probs - inner_sum) * score_scale).astype(jnp.bfloat16)
        query_grad = jnp.einsum(
            "rqk,kd->qrd", grad_scores, key_head, preferred_element_type=jnp.float32
        )
        query_grads.append(query_grad.reshape(row_total_count, heads_per_group * HEAD_SIZE))
        key_grads.append(
            jnp.einsum("rqk,qrd->kd", grad_scores, query_head, preferred_element_type=jnp.float32)
        )
    return (
        jnp.concatenate(query_grads, 1),
        jnp.concatenate(key_grads, 1),
        jnp.concatenate(value_grads, 1),
    )


def make_term(width_sides, other_sides):
    down_side, mlp_side, attn_side, qkv_side = width_sides
    mixed_rows, gate_rows, up_rows, context_rows, query_rows, key_rows, value_rows = other_sides

    def grad_term(first_row, row_span):
        pieces = [
            lax.dot_general(
                down_side, mixed_rows, contract_first, preferred_element_type=jnp.float32
            ),
            lax.dot_general(
                mlp_side, gate_rows, contract_first, preferred_element_type=jnp.float32
            ),
            lax.dot_general(mlp_side, up_rows, contract_first, preferred_element_type=jnp.float32),
            lax.dot_general(
                attn_side, context_rows, contract_first, preferred_element_type=jnp.float32
            ),
            lax.dot_general(
                qkv_side, query_rows, contract_first, preferred_element_type=jnp.float32
            ),
            lax.dot_general(qkv_side, key_rows, contract_first, preferred_element_type=jnp.float32),
            lax.dot_general(
                qkv_side, value_rows, contract_first, preferred_element_type=jnp.float32
            ),
        ]
        return jnp.concatenate(pieces, 1)

    return grad_term


def per_device(
    tokens,
    cotangent,
    lengths,
    positions,
    norm_attn,
    w_query,
    w_key,
    w_value,
    w_output,
    norm_mlp,
    w_gate,
    w_up,
    w_down,
):
    row_total_count = tokens.shape[0]
    shard_rows = w_query.shape[0]
    query_width = w_query.shape[1]
    key_width = w_key.shape[1]
    hidden_width = w_gate.shape[1]
    inputs = tokens.astype(jnp.float32)
    valid_rows = (jnp.arange(row_total_count) < lengths[0]).astype(jnp.float32)[:, None]
    cosine_table, sine_table = rope_tables(positions)
    normed_attn = normalize(inputs)
    gain_attn_full, scaled_attn, query_pre, key_unrotated, value_pre = attention_inputs(
        normed_attn, norm_attn, w_query, w_key, w_value
    )
    query_rotated = (
        apply_rotary(
            query_pre.reshape(row_total_count, QUERY_HEADS, HEAD_SIZE), cosine_table, sine_table
        )
        .reshape(row_total_count, query_width)
        .astype(jnp.bfloat16)
    )
    key_rotated = (
        apply_rotary(
            key_unrotated.reshape(row_total_count, KEY_VALUE_HEADS, HEAD_SIZE),
            cosine_table,
            sine_table,
        )
        .reshape(row_total_count, key_width)
        .astype(jnp.bfloat16)
    )
    value_reduced = value_pre.astype(jnp.bfloat16)
    context, log_totals = attend(query_rotated, key_rotated, value_reduced)
    attn_out = lax.dot_general(
        context,
        lax.all_gather(w_output, ("wide", "narrow"), axis=0, tiled=True),
        contract_last,
        preferred_element_type=jnp.float32,
    )
    hidden = inputs + attn_out
    normed_mlp = normalize(hidden)
    gain_mlp_full, scaled_mlp, gate_proj, up_proj = mlp_inputs(normed_mlp, norm_mlp, w_gate, w_up)
    mixed_low = (gate_proj * jax.nn.sigmoid(gate_proj) * up_proj).astype(jnp.bfloat16)
    mlp_out = lax.dot_general(
        mixed_low,
        lax.all_gather(w_down, ("wide", "narrow"), axis=0, tiled=True),
        contract_last,
        preferred_element_type=jnp.float32,
    )
    output = (valid_rows * (hidden + mlp_out)).astype(jnp.bfloat16)
    grad_y = cotangent.astype(jnp.float32) * valid_rows
    grad_y_low = grad_y.astype(jnp.bfloat16)
    grad_cols = grad_y_low
    grad_mixed = jnp.dot(
        grad_cols,
        lax.all_gather(w_down, ("wide", "narrow"), axis=0, tiled=True),
        preferred_element_type=jnp.float32,
    )
    again_values = mlp_inputs(normed_mlp, norm_mlp, w_gate, w_up)
    gate_proj = again_values[2]
    up_proj = again_values[3]
    sigmoid_gate = jax.nn.sigmoid(gate_proj)
    grad_gate = (
        grad_mixed * up_proj * (sigmoid_gate * (1.0 + gate_proj * (1.0 - sigmoid_gate)))
    ).astype(jnp.bfloat16)
    grad_up = (grad_mixed * (gate_proj * sigmoid_gate)).astype(jnp.bfloat16)
    gate_rows = lax.all_gather(w_gate, ("wide", "narrow"), axis=0, tiled=True)
    up_rows = lax.all_gather(w_up, ("wide", "narrow"), axis=0, tiled=True)
    columns = lax.dot_general(
        grad_gate, gate_rows, contract_last, preferred_element_type=jnp.float32
    )
    columns = columns + lax.dot_general(
        grad_up, up_rows, contract_last, preferred_element_type=jnp.float32
    )
    grad_xn2 = columns
    grad_gain_mlp = jnp.sum(grad_xn2 * normed_mlp, axis=0)
    grad_hidden = grad_y + norm_back(grad_xn2 * gain_mlp_full, normed_mlp, hidden)
    grad_attn_low = grad_hidden.astype(jnp.bfloat16)
    grad_cols = grad_attn_low
    grad_context = jnp.dot(
        grad_cols,
        lax.all_gather(w_output, ("wide", "narrow"), axis=0, tiled=True),
        preferred_element_type=jnp.float32,
    )
    grad_context = grad_context.astype(jnp.bfloat16)
    grad_query_rot, gradient_key_rotated, grad_value_sum = attend_back(
        query_rotated, key_rotated, value_reduced, log_totals, grad_context
    )
    grad_query = (
        invert_rotary(
            grad_query_rot.reshape(row_total_count, QUERY_HEADS, HEAD_SIZE),
            cosine_table,
            sine_table,
        )
        .reshape(row_total_count, query_width)
        .astype(jnp.bfloat16)
    )
    grad_key = (
        invert_rotary(
            gradient_key_rotated.reshape(row_total_count, KEY_VALUE_HEADS, HEAD_SIZE),
            cosine_table,
            sine_table,
        )
        .reshape(row_total_count, key_width)
        .astype(jnp.bfloat16)
    )
    grad_value = grad_value_sum.astype(jnp.bfloat16)
    query_rows = lax.all_gather(w_query, ("wide", "narrow"), axis=0, tiled=True)
    key_rows = lax.all_gather(w_key, ("wide", "narrow"), axis=0, tiled=True)
    value_rows = lax.all_gather(w_value, ("wide", "narrow"), axis=0, tiled=True)
    columns = lax.dot_general(
        grad_query, query_rows, contract_last, preferred_element_type=jnp.float32
    )
    columns = columns + lax.dot_general(
        grad_key, key_rows, contract_last, preferred_element_type=jnp.float32
    )
    columns = columns + lax.dot_general(
        grad_value, value_rows, contract_last, preferred_element_type=jnp.float32
    )
    local_term = make_term(
        (grad_y_low, scaled_mlp, grad_attn_low, scaled_attn),
        (mixed_low, grad_gate, grad_up, context, grad_query, grad_key, grad_value),
    )
    all_sums = lax.psum_scatter(
        local_term(jnp.int32(0), lax.axis_size(("wide", "narrow")) * shard_rows),
        ("wide", "narrow"),
        scatter_dimension=0,
        tiled=True,
    )
    edges = [0]
    for width in (
        hidden_width,
        hidden_width,
        hidden_width,
        query_width,
        query_width,
        key_width,
        key_width,
    ):
        edges.append(edges[-1] + width)
    grad_w_down = all_sums[:, edges[0] : edges[1]]
    grad_w_gate = all_sums[:, edges[1] : edges[2]]
    grad_w_up = all_sums[:, edges[2] : edges[3]]
    grad_w_output = all_sums[:, edges[3] : edges[4]]
    grad_w_query = all_sums[:, edges[4] : edges[5]]
    grad_w_key = all_sums[:, edges[5] : edges[6]]
    grad_w_value = all_sums[:, edges[6] : edges[7]]
    grad_gain_attn = jnp.sum(columns * normed_attn, axis=0)
    grad_tokens = grad_hidden + norm_back(columns * gain_attn_full, normed_attn, inputs)
    grad_norm_attn, grad_norm_mlp = (
        lax.psum_scatter(grad_gain_attn, ("wide", "narrow"), scatter_dimension=0, tiled=True),
        lax.psum_scatter(grad_gain_mlp, ("wide", "narrow"), scatter_dimension=0, tiled=True),
    )
    return (
        output,
        grad_tokens,
        grad_norm_attn,
        grad_w_query,
        grad_w_key,
        grad_w_value,
        grad_w_output,
        grad_norm_mlp,
        grad_w_gate,
        grad_w_up,
        grad_w_down,
    )


MESH = pl.DeviceIdType.MESH
ANY = pl.BlockSpec(memory_space=pl.ANY)
VMEM = pl.BlockSpec(memory_space=pltpu.VMEM)

CHIPS, CORES = 4, 2

def place():
    w = lax.axis_index("wide"); n = lax.axis_index("narrow")
    return w // CORES, w % CORES, n

def chip_at(c, r):
    xb, yb, rx, ry = c % 2, c // 2, r % 2, r // 2
    return (yb + ry - 2 * yb * ry) * 2 + (xb + rx - 2 * xb * rx)


def remote(src, dst, send, recv, chip, core, z):
    return pltpu.make_async_remote_copy(src_ref=src, dst_ref=dst, send_sem=send, recv_sem=recv,
        device_id={"wide": chip * CORES + core, "narrow": z}, device_id_type=MESH)

def hello(partners):
    barrier = pltpu.get_barrier_semaphore()
    count = 0
    for cond, chip, core, z in partners:
        def sig(chip=chip, core=core, z=z):
            pl.semaphore_signal(barrier, inc=1, device_id={"wide": chip * CORES + core, "narrow": z}, device_id_type=MESH)
        if cond is None:
            sig(); count = count + 1
        else:
            pl.when(cond)(sig); count = count + jnp.where(cond, 1, 0)
    pl.semaphore_wait(barrier, count)

class Line:
    def __init__(self, nz, at, refs, send, recv, place_of):
        self.nz, self.at, self.refs, self.send, self.recv, self.place_of = nz, at, refs, send, recv, place_of

    def _copy(self, a, way, s, origin):
        c, k, n = self.at
        ref = self.place_of(self.refs[a], origin)
        return remote(ref, ref, self.send.at[a, way, s], self.recv.at[a, way, s], c, k, n + 1 if way == 0 else n - 1)

    def _origin(self, way, s):
        n = self.at[2]
        o = n - s if way == 0 else n + s
        return (n >= s) if way == 0 else (n + s <= self.nz - 1), jnp.clip(o, 0, self.nz - 1)

    def _sends(self, way, s):
        n = self.at[2]
        return self._origin(way, s)[0] & ((n < self.nz - 1) if way == 0 else (n > 0))

    def start(self, a, s, way):
        @pl.when(self._sends(way, s))
        def _(): self._copy(a, way, s, self._origin(way, s)[1]).start()

    def step(self, a, s, then=None):
        for way in range(2):
            came, origin = self._origin(way, s)
            @pl.when(came)
            def _(): self._copy(a, way, s - 1, origin).wait_recv()
            if s < self.nz - 1: self.start(a, s, way)
            if then is not None:
                @pl.when(came)
                def _(): then(origin)

    def finish(self, a):
        for s in range(self.nz - 1):
            for way in range(2):
                @pl.when(self._sends(way, s))
                def _(): self._copy(a, way, s, self._origin(way, s)[1]).wait_send()


def gather_kernel(nz, wq, wk, wv, wo, gains, wg, wu, wd, qkv, out, gain, gu, gd,
                  loc, sw_s, sw_r, z_s, z_r, f_s, f_r, p_s, p_r, h_s, h_r, d_s, d_r, e_s, e_r):
    c, k, n = at = place()
    rows, q = wq.shape
    kv = wk.shape[1]
    cols = gd.shape[-1]
    part = nz * rows
    half = part // 2
    kn = k * nz + n
    cx, cy, cd = (chip_at(c, r) for r in (1, 2, 3))
    hello([(None, cc, k, n) for cc in (cx, cy, cd)] + [(None, c, 1 - k, n), (n > 0, c, k, n - 1), (n < nz - 1, c, k, n + 1)])

    def mycols(w, cc): return w.at[:, pl.ds(pl.multiple_of(cc * cols, 128), cols)]
    def landing(i, cc): return gd.at[cc] if i == 2 else gu.at[cc, kn, :, pl.ds(i * cols, cols)]
    whole = (qkv, out, gain)
    def block(ref, z): return ref.at[pl.ds(pl.multiple_of(((c * CORES + k) * nz + z) * rows, rows), rows)]
    own = [pltpu.make_async_copy(wq, block(qkv, n).at[:, pl.ds(0, q)], loc.at[0]),
           pltpu.make_async_copy(wk, block(qkv, n).at[:, pl.ds(q, kv)], loc.at[1]),
           pltpu.make_async_copy(wv, block(qkv, n).at[:, pl.ds(q + kv, kv)], loc.at[2]),
           pltpu.make_async_copy(wo, block(out, n), loc.at[3]), pltpu.make_async_copy(gains, block(gain, n), loc.at[4])]
    ownff = [pltpu.make_async_copy(mycols(w, c), landing(i, c), loc.at[5 + i]) for i, w in enumerate((wg, wu, wd))]
    for cp in own + ownff: cp.start()
    swap = [[remote(mycols(w, cc), landing(i, c), sw_s.at[i, r], sw_r.at[i, r], cc, k, n) for r, cc in enumerate((cx, cy, cd))]
            for i, w in enumerate((wg, wu, wd))]
    for i in range(3):
        for cp in swap[i]: cp.start()
    for cp in own: cp.wait()

    line = Line(nz, at, whole, z_s, z_r, block)
    for a in range(3):
        for way in range(2): line.start(a, 0, way)

    def span(ref, cc, first, size):
        return ref.at[pl.ds(pl.multiple_of((cc * CORES + k) * part, part) + first, size)]
    plane = [[remote(span(ref, c, 0, part), span(ref, c, 0, part), p_s.at[a, r], p_r.at[a, r], cc, k, n) for r, cc in enumerate((cx, cy))]
             for a, ref in enumerate(whole)]
    across = [[remote(span(ref, cx, 0, half), span(ref, cx, 0, half), h_s.at[a, 0], h_r.at[a, 0], cy, k, n),
               remote(span(ref, cy, half, half), span(ref, cy, half, half), h_s.at[a, 1], h_r.at[a, 1], cx, k, n)]
              for a, ref in enumerate(whole)]
    cores = [[remote(span(ref, cc, 0, part), span(ref, cc, 0, part), d_s.at[a, r], d_r.at[a, r], c, 1 - k, n)
              for r, cc in enumerate((c, cx, cy, cd))] for a, ref in enumerate(whole)]

    def plane_start(a):
        for cp in plane[a] + cores[a][:1]: cp.start()
    def plane_next(a):
        for i in range(2):
            plane[a][i].wait_recv()
            across[a][i].start()
            cores[a][1 + i].start()
    def plane_last(a):
        for cp in across[a]: cp.wait_recv()
        cores[a][3].start()

    for s in range(1, nz):
        for a in range(3):
            line.step(a, s)
            if s == nz - 1: plane_start(a)

    ff = Line(nz, at, (gu,), f_s, f_r, lambda ref, z: ref.at[:, k * nz + z])
    def twin(z):
        ref = gu.at[:, k * nz + z]
        return remote(ref, ref, e_s.at[z], e_r.at[z], c, 1 - k, n)
    for i in range(2):
        ownff[i].wait()
        for cp in swap[i]: cp.wait_recv()
    for way in range(2): ff.start(0, 0, way)
    twin(n).start()
    plane_next(0)
    ff.step(0, 1, lambda z: twin(z).start())
    for a in (1, 2): plane_next(a)
    ff.step(0, 2, lambda z: twin(z).start())
    for a in range(3): plane_last(a)
    ownff[2].wait()
    for cp in swap[2]: cp.wait_recv()
    for s in range(3, nz): ff.step(0, s, lambda z: twin(z).start())
    for a in range(3):
        for cp in cores[a]: cp.wait_recv()
    for z in range(nz): twin(z).wait()
    for i in range(3):
        for cp in swap[i]: cp.wait_send()
    for a in range(3):
        line.finish(a)
        for cp in plane[a] + across[a] + cores[a]: cp.wait_send()
    ff.finish(0)


def gather_all(nz, wq, wk, wv, wo, gains, wg, wu, wd):
    rows = wq.shape[0]
    width = rows * CHIPS * CORES * nz
    cols = wg.shape[1] // CHIPS
    bf = jnp.bfloat16
    shape = jax.ShapeDtypeStruct
    dma = pltpu.SemaphoreType.DMA
    return pl.pallas_call(
        functools.partial(gather_kernel, nz),
        out_shape=(shape((width, wq.shape[1] + 2 * wk.shape[1]), bf), shape((width, wo.shape[1]), bf), shape((width, gains.shape[1]), bf),
                   shape((CHIPS, CORES * nz, rows, 2 * cols), bf), shape((CHIPS, rows, cols), bf)),
        in_specs=[VMEM] * 8, out_specs=(ANY,) * 5,
        scratch_shapes=[dma((8,)), dma((3, 3)), dma((3, 3)), dma((3, 2, nz)), dma((3, 2, nz)), dma((1, 2, nz)), dma((1, 2, nz)),
                        dma((3, 2)), dma((3, 2)), dma((3, 2)), dma((3, 2)), dma((3, 4)), dma((3, 4)), dma((nz,)), dma((nz,))],
        compiler_params=pltpu.CompilerParams(collective_id=0, has_side_effects=True),
        name="gather_all",
    )(wq, wk, wv, wo, gains, wg, wu, wd)


def add_into(dst, *srcs):
    rows = dst.shape[0]
    step = 16
    def body(i, carry):
        at = pl.ds(pl.multiple_of(i * step, step), step)
        total = dst[at, :].astype(jnp.float32)
        for s in srcs: total = total + s[at, :].astype(jnp.float32)
        dst[at, :] = total.astype(dst.dtype)
        return carry
    lax.fori_loop(0, rows // step, body, 0)


HALVES = ((0, 0), (0, 1), (1, 0), (2, 0), (1, 1), (2, 1), (3, 0), (3, 1))


def mlp_kernel(nz, x, gy, gu_hbm, gd_hbm, gx_parts, mlp_parts, mlp_cross, down_sums, sums,
               xs, gys, gu, gd, mix, ggu, gx, mo, xt, zin, load, ag_s, ag_r, rs_s, rs_r, mo_s, mo_r, out, core_s, core_r, ready, done, z_s, z_r):
    c, k, n = place()
    f32, bf16 = jnp.float32, jnp.bfloat16
    slots, width = x.shape
    half = slots // 2
    rows, cols = gd.shape[2:]
    tile = nz * rows
    hello([(None, chip_at(c, r), k, n) for r in (1, 2, 3)]
          + [(None, c, 1 - k, n), (n > 0, c, k, n - 1), (n < nz - 1, c, k, n + 1)])
    def half_of(ref, h): return ref.at[pl.ds(h * half, half)]
    index = {place_: i for i, place_ in enumerate(HALVES)}
    sends = {}
    for h in range(2):
        for r in (1, 2):
            i = index[r, h]
            sends[i] = remote(half_of(x, h), xs.at[i], ag_s.at[i], ag_r.at[i], chip_at(c, r), k, n)
            if h == 0: sends[i].start()
    loads = [pltpu.make_async_copy(half_of(x, h), xs.at[h], load.at[h]) for h in range(2)]
    loads += [pltpu.make_async_copy(half_of(gy.at[r], h), gys.at[i], load.at[2 + i]) for i, (r, h) in enumerate(HALVES)]
    for cp in loads: cp.start()
    def weights(col, w, j):
        return [pltpu.make_async_copy(a.at[:, :, :, pl.ds(first + col, w)], b.at[:, :, :, pl.ds(first + col, w)], load.at[10 + 3 * j + i])
                for i, (a, b, first) in enumerate(((gu_hbm, gu, 0), (gu_hbm, gu, cols), (gd_hbm, gd, 0)))]
    for j in range(-(-cols // 256)):
        for cp in weights(j * 256, min(256, cols - j * 256), j): cp.start()
    relays = {index[3, 0]: (index[1, 0], 2), index[3, 1]: (index[2, 1], 1)}
    relays = {i: remote(xs.at[j], xs.at[i], ag_s.at[i], ag_r.at[i], chip_at(c, r), k, n) for i, (j, r) in relays.items()}
    for cp in loads: cp.wait()

    def columns(ref, at, size):
        return ref[:, :, :, pl.ds(at, size)].reshape(width, size)

    def some_rows(ref, i): return ref[i].reshape(tile, ref.shape[3])

    def to_owner(src, dst, i, s_s, s_r):
        r, h = HALVES[i]
        return remote(src.at[i], half_of(dst.at[r], h), s_s.at[i], s_r.at[i], chip_at(c, r), k, n)

    def kept(src, dst, i, j):
        return pltpu.make_async_copy(src.at[i], half_of(dst, HALVES[i][1]), out.at[j])

    def block(r, carry):
        two = pl.ds(2 * r, 2)
        @pl.when(r == 1)
        def _():
            for i in (2, 3): sends[i].wait_recv()
            relays[index[3, 0]].start()
        @pl.when(r == 3)
        def _():
            for cp in relays.values(): cp.wait_recv()
        def both(ref): return ref[two].reshape(slots, ref.shape[2])
        def put(ref, at, v): ref[two, :, at] = v.astype(bf16).reshape(2, half, v.shape[1])
        def chunk(col, w, j):
            @pl.when(r == 0)
            def _():
                for cp in weights(col, w, j): cp.wait()
            tokens = both(xs)
            hg = jnp.dot(tokens, columns(gu, col, w), preferred_element_type=f32)
            hu = jnp.dot(tokens, columns(gu, cols + col, w), preferred_element_type=f32)
            gm = jnp.dot(both(gys), columns(gd, col, w), preferred_element_type=f32)
            for q in range(w // 128):
                gate, up, g = (t[:, 128 * q : 128 * q + 128] for t in (hg, hu, gm))
                sg = 1.0 / (1.0 + jnp.exp(-gate))
                act = gate * sg
                put(mix, pl.ds(col + 128 * q, 128), act * up)
                put(ggu, pl.ds(col + 128 * q, 128), g * up * (sg * (1.0 + gate * (1.0 - sg))))
                put(ggu, pl.ds(cols + col + 128 * q, 128), g * act)
        def pair(j, carry):
            chunk(pl.multiple_of(j * 256, 256), 256, j)
            return carry
        lax.fori_loop(0, cols // 256, pair, 0)
        if cols % 256: chunk(cols // 256 * 256, cols % 256, cols // 256)
        @pl.when(r == 0)
        def _():
            for i in (4, 5): sends[i].start()
        @pl.when(r == 1)
        def _():
            for i in (4, 5): sends[i].wait_recv()
            relays[index[3, 1]].start()
        def back(i, carry):
            at = pl.ds(pl.multiple_of(i * tile, 128), tile)
            put(gx, at, lax.dot_general(both(ggu), some_rows(gu, i), contract_last, preferred_element_type=f32))
            return carry
        lax.fori_loop(0, CHIPS * CORES, back, 0)
        for t in range(CHIPS):
            @pl.when(r == t)
            def _():
                for i in (2 * t, 2 * t + 1):
                    (to_owner(gx, gx_parts, i, rs_s, rs_r) if t else kept(gx, gx_parts.at[0], i, i)).start()
        def down(i, carry):
            at = pl.ds(pl.multiple_of(i * tile, 128), tile)
            put(mo, at, lax.dot_general(both(mix), some_rows(gd, i), contract_last, preferred_element_type=f32))
            return carry
        lax.fori_loop(0, CHIPS * CORES, down, 0)
        for t in range(CHIPS):
            @pl.when(r == t)
            def _():
                for i in (2 * t, 2 * t + 1):
                    (kept(mo, mlp_parts.at[0], i, 2 + i) if t == 0 else kept(mo, mlp_cross, i, i - 2) if t == 3
                     else to_owner(mo, mlp_parts, i, mo_s, mo_r)).start()
        return carry
    lax.fori_loop(0, CHIPS, block, 0)

    pl.semaphore_signal(ready, inc=1, device_id={"wide": c * CORES + 1 - k, "narrow": n}, device_id_type=MESH)
    pl.semaphore_wait(ready, 1)
    sent, came = pl.ds(0, CHIPS), pl.ds(CHIPS, CHIPS)
    pairs = ((gys, mix, gd), (xs, ggu, gu))

    def tiles(total): return [(t * 256, min(256, total - t * 256)) for t in range(-(-total // 256))]

    def to_core(i, col, w, sem):
        ref = pairs[i][2]
        return remote(ref.at[sent, :, :, pl.ds(col, w)], ref.at[came, :, :, pl.ds(col, w)], core_s.at[sem], core_r.at[sem], c, 1 - k, n)

    def to_sums(t): return pltpu.make_async_copy(gu.at[CHIPS + t], sums.at[:, t], done.at[t])

    def each(i, body):
        total, base = pairs[i][2].shape[-1], 0 if i == 0 else len(tiles(cols))
        def step(j, carry):
            body(pl.multiple_of(j * 256, 256), 256, base + j)
            return carry
        lax.fori_loop(0, total // 256, step, 0)
        if total % 256: body(total // 256 * 256, total % 256, base + total // 256)

    def terms(i, kk, use):
        src, right, ref = pairs[i]
        for t in range(CHIPS):
            at = pl.ds(pl.multiple_of((t * CORES + kk) * tile, 128), tile)
            for r in range(CHIPS):
                xt[t * tile : (t + 1) * tile, r * slots : (r + 1) * slots] = src[2 * r : 2 * r + 2, :, at].reshape(slots, tile).T
        def body(col, w, sem):
            b = right[:, :, pl.ds(col, w)].reshape(CHIPS * slots, w)
            use(i, col, w, sem, jnp.dot(xt[...], b, preferred_element_type=f32).reshape(CHIPS, nz, rows, w))
        each(i, body)

    def theirs(i, col, w, sem, v):
        pairs[i][2][sent, :, :, pl.ds(col, w)] = v.astype(bf16)
        to_core(i, col, w, sem).start()

    def ours(i, col, w, sem, v):
        to_core(i, col, w, sem).wait_recv()
        ref = pairs[i][2]
        here = (came, slice(None), slice(None), pl.ds(col, w))
        ref[here] = (ref[here].astype(f32) + v).astype(bf16)

    def hop(way, j):
        return remote(gd.at[came, j], zin.at[way, jnp.clip(j - n - 1 if way == 0 else n - 1 - j, 0, nz - 2)],
                      z_s.at[way, j], z_r.at[way, j], c, k, n + 1 if way == 0 else n - 1)

    def along(t):
        for way in range(2):
            hops = n if way == 0 else nz - 1 - n
            j = jnp.clip(n + nz - 1 - t if way == 0 else t - hops, 0, nz - 1)
            @pl.when((hops > 0) & (t >= hops))
            def _():
                hop(way, j).wait_recv()
                for i in range(CHIPS):
                    add_into(gd.at[CHIPS + i, j], zin.at[way, jnp.clip(j - n if way == 0 else n - j, 0, nz - 2), i])
            @pl.when((t >= hops) & (j != n))
            def _(): hop(way, j).start()

    terms(0, 1 - k, theirs)
    terms(0, k, ours)
    along(0)
    terms(1, 1 - k, theirs)
    along(1)
    terms(1, k, ours)
    for t in range(CHIPS): to_sums(t).start()
    for t in range(2, nz): along(t)
    own_down = pltpu.make_async_copy(gd.at[came, n], down_sums, done.at[CHIPS])
    own_down.start()

    for cp in (*sends.values(), *relays.values()): cp.wait_send()
    for i in range(2):
        kept(gx, gx_parts.at[0], i, i).wait()
        kept(mo, mlp_parts.at[0], i, 2 + i).wait()
        kept(mo, mlp_cross, 6 + i, 4 + i).wait()
    for i in range(2): each(i, lambda col, w, sem: to_core(i, col, w, sem).wait_send())
    for t in range(CHIPS): to_sums(t).wait()
    for j in range(nz):
        for way in range(2):
            @pl.when(n < j if way == 0 else n > j)
            def _(): hop(way, j).wait_send()
    own_down.wait()
    for i in range(2, 6): to_owner(mo, mlp_parts, i, mo_s, mo_r).wait()
    for i in range(2, 8): to_owner(gx, gx_parts, i, rs_s, rs_r).wait()


def mlp_all(nz, x, gy, gu, gd):
    slots, width = x.shape
    rows, cols = gd.shape[2:]
    bf, dma, vm = jnp.bfloat16, pltpu.SemaphoreType.DMA, pltpu.VMEM
    def blocks(w): return jax.ShapeDtypeStruct((CHIPS, slots, w), bf)
    def halves(w): return vm((2 * CHIPS, slots // 2, w), bf)
    tiles = -(-cols // 256)
    flops = 2 * 9 * CHIPS * slots * width * cols
    return pl.pallas_call(
        functools.partial(mlp_kernel, nz),
        out_shape=(blocks(width), jax.ShapeDtypeStruct((3, slots, width), bf), jax.ShapeDtypeStruct((slots, width), bf),
                   jax.ShapeDtypeStruct((CHIPS, rows, cols), bf), jax.ShapeDtypeStruct((nz, CHIPS, rows, 2 * cols), bf)),
        in_specs=[ANY] * 4, out_specs=(ANY,) * 5,
        scratch_shapes=[halves(width), halves(width), vm(gu.shape, bf), vm(gd.shape, bf), halves(cols), halves(2 * cols), halves(width),
                        halves(width), vm((CHIPS * nz * rows, CHIPS * slots), bf), vm((2, nz - 1, CHIPS, rows, cols), bf), dma((10 + 3 * tiles,)), dma((8,)), dma((8,)), dma((8,)), dma((8,)),
                        dma((8,)), dma((8,)), dma((6,)), dma((3 * tiles,)), dma((3 * tiles,)), pltpu.SemaphoreType.REGULAR, dma((CHIPS + 1,)), dma((2, nz)), dma((2, nz))],
        compiler_params=pltpu.CompilerParams(collective_id=1, has_side_effects=True, vmem_limit_bytes=62 << 20),
        cost_estimate=pl.CostEstimate(flops=flops, bytes_accessed=60 << 20, transcendentals=CHIPS * slots * cols),
        name="mlp_all",
    )(x, gy, gu, gd)


PAIR = 2 * HEAD_SIZE
REPEAT = QUERY_HEADS // KEY_VALUE_HEADS
PAIRS = REPEAT // 2


def lane_tables(positions):
    cosine, sine = rope_tables(positions)
    first = jnp.arange(HEAD_SIZE) < HEAD_SIZE // 2
    low, high = jnp.where(first, -sine, 0.0), jnp.where(first, 0.0, sine)
    return jnp.stack([jnp.concatenate([t, t], 1) for t in (cosine, low, high)])


def rotate(u, tables):
    half = HEAD_SIZE // 2
    return u * tables[0] + pltpu.roll(u, PAIR - half, 1) * tables[1] + pltpu.roll(u, half, 1) * tables[2]


def unrotate(g, tables):
    half = HEAD_SIZE // 2
    return g * tables[0] + pltpu.roll(g * tables[2], PAIR - half, 1) + pltpu.roll(g * tables[1], half, 1)


def row_blocks(slots):
    return [(at, min(128, slots - at), at + 128) for at in range(0, slots, 128)]


def causal(s, below, fill):
    clear = s.shape[1] - 128
    last = jnp.where(below, s[:, clear:], fill)
    return jnp.concatenate([s[:, :clear], last], 1) if clear else last


def scaled(x, gain):
    return (x * lax.rsqrt(jnp.mean(x * x, axis=-1, keepdims=True) + norm_eps) * gain).astype(jnp.bfloat16)


def attend_kernel(nz, tok, gain1, gain2, tab_ref, wq_hbm, wo_hbm, gy, gd_own,
                  qr_ref, k_out, v_out, lse_ref, ctx_ref, xn1, hidden, xn2, gys, gd, ks, vs, wq, wo, qkv,
                  load, loc, g_s, g_r, h_s, h_r, f_s, f_r, e_s, e_r):
    g = pl.program_id(0)
    f32, bf16 = jnp.float32, jnp.bfloat16
    slots, width = tok.shape
    c, k, n = at = place()
    mine = [pltpu.make_async_copy(gd_own, gd.at[:, k * nz + n], loc.at[0]), pltpu.make_async_copy(gy, gys.at[0], loc.at[1])]
    line = Line(nz, at, (gd,), f_s, f_r, lambda ref, z: ref.at[:, k * nz + z])
    half = slots // 2
    sends = [remote(gy, gys.at[r], g_s.at[r - 1], g_r.at[r - 1], chip_at(c, r), k, n) for r in (1, 2)]
    relays = [remote(gys.at[1, pl.ds(0, half)], gys.at[3, pl.ds(0, half)], h_s.at[0], h_r.at[0], chip_at(c, 2), k, n),
              remote(gys.at[2, pl.ds(half, half)], gys.at[3, pl.ds(half, half)], h_s.at[1], h_r.at[1], chip_at(c, 1), k, n)]
    def twin(z):
        ref = gd.at[:, k * nz + z]
        return remote(ref, ref, e_s.at[z], e_r.at[z], c, 1 - k, n)
    def load_q(j):
        at = pl.ds(j * 256 if isinstance(j, int) else pl.multiple_of(j * 256, 256), 256)
        return pltpu.make_async_copy(wq_hbm.at[:, at], wq.at[:, at], load.at[j])
    @pl.when(g == 0)
    def _():
        hello([(None, chip_at(c, r), k, n) for r in (1, 2)]
              + [(None, c, 1 - k, n), (n > 0, c, k, n - 1), (n < nz - 1, c, k, n + 1)])
        for cp in mine + sends: cp.start()
        for j in range(wq.shape[1] // 256): load_q(j).start()
        pltpu.make_async_copy(wo_hbm, wo, loc.at[2]).start()
        mine[0].wait()
        for way in range(2): line.start(0, 0, way)
        twin(n).start()
        def norm(i, carry):
            at = pl.ds(pl.multiple_of(i * 16, 16), 16)
            xn1[at, :] = scaled(tok[at, :].astype(f32), gain1[...])
            return carry
        lax.fori_loop(0, slots // 16, norm, 0)
        def project(j, carry):
            load_q(j).wait()
            at = pl.ds(pl.multiple_of(j * 256, 256), 256)
            qkv[:, at] = jnp.dot(xn1[...], wq[:, at], preferred_element_type=f32)
            return carry
        lax.fori_loop(0, wq.shape[1] // 256, project, 0)
    @pl.when(g == 1)
    def _(): line.step(0, 1, lambda z: twin(z).start())
    @pl.when(g == 0)
    def _():
        ks[...] = jnp.zeros_like(ks)
        vs[...] = jnp.zeros_like(vs)
    lane = lax.broadcasted_iota(jnp.int32, (slots, PAIR), 1)
    tables = (tab_ref[0], tab_ref[1], tab_ref[2])
    first = QUERY_HEADS * HEAD_SIZE
    def pair_at(at): return pl.ds(pl.multiple_of(at, PAIR), PAIR)
    key = rotate(qkv[:, pair_at(first + g // 2 * PAIR)], tables)
    val = qkv[:, pair_at(first + KEY_VALUE_HEADS * HEAD_SIZE + g // 2 * PAIR)]
    odd = g % 2 == 1
    for x, own, stack, scale in ((key, k_out, ks, HEAD_SIZE ** -0.5), (val, v_out, vs, 1.0)):
        x = jnp.where(lane < HEAD_SIZE, jnp.where(odd, pltpu.roll(x, HEAD_SIZE, 1), x), 0.0).astype(bf16)
        own[0] = x
        x = x.astype(f32) * scale
        stack[0, 0:slots, :] = x.astype(bf16)
        stack[1, 0:slots, :] = pltpu.roll(x, HEAD_SIZE, 1).astype(bf16)
    for start, size, keys in row_blocks(slots):
        below = lax.broadcasted_iota(jnp.int32, (size, 128), 0) >= lax.broadcasted_iota(jnp.int32, (size, 128), 1)
        lse = jnp.zeros((size, PAIR), f32)
        here = lane[0:size]
        for p in range(PAIRS):
            span = slice(p * PAIR, (p + 1) * PAIR)
            rows = slice(start, start + size)
            q = rotate(qkv[rows, pair_at(g * REPEAT * HEAD_SIZE + p * PAIR)], tuple(t[rows] for t in tables)).astype(bf16)
            qr_ref[rows, span] = q
            ctx = jnp.zeros((size, PAIR), f32)
            for h in range(2):
                s = lax.dot_general(q, ks[h, 0:keys, :], contract_last, preferred_element_type=f32)
                s = causal(s, below, masked_score)
                peak = jnp.max(s, axis=-1, keepdims=True)
                e = jnp.exp(s - peak)
                total = jnp.sum(e, axis=-1, keepdims=True)
                lse = jnp.where(here == 2 * p + h, peak + jnp.log(total), lse)
                probs = (e * (1.0 / total)).astype(bf16)
                ctx = ctx + jnp.dot(probs, vs[h, 0:keys, :], preferred_element_type=f32)
            ctx_ref[rows, pair_at(g * REPEAT * HEAD_SIZE + p * PAIR)] = ctx.astype(bf16)
        lse_ref[0, start : start + size, :] = lse
    @pl.when(g == KEY_VALUE_HEADS - 1)
    def _():
        for cp in sends: cp.wait_recv()
        for cp in relays: cp.start()
        line.step(0, 2, lambda z: twin(z).start())
        pltpu.make_async_copy(wo_hbm, wo, loc.at[2]).wait()
        def project(j, carry):
            at = pl.ds(pl.multiple_of(j * 256, 256), 256)
            hidden[:, at] = tok[:, at].astype(f32) + lax.dot_general(ctx_ref[...], wo[at, :], contract_last, preferred_element_type=f32)
            return carry
        lax.fori_loop(0, width // 256, project, 0)
        def norm(i, carry):
            at = pl.ds(pl.multiple_of(i * 16, 16), 16)
            xn2[at, :] = scaled(hidden[at, :], gain2[...])
            return carry
        lax.fori_loop(0, slots // 16, norm, 0)
        for s in range(3, nz): line.step(0, s, lambda z: twin(z).start())
        for cp in relays: cp.wait()
        for z in range(nz): twin(z).wait()
        for cp in sends: cp.wait_send()
        mine[1].wait()
        line.finish(0)


def attend_all(nz, tokens, gain1, gain2, tables, w_qkv, w_out, gy, gd_own):
    slots, width = tokens.shape
    dma, vm = pltpu.SemaphoreType.DMA, pltpu.VMEM
    bf16, f32 = jnp.bfloat16, jnp.float32
    keys = -(-slots // 128) * 128
    heads = QUERY_HEADS * HEAD_SIZE
    shape = jax.ShapeDtypeStruct
    def fixed(*dims): return pl.BlockSpec(dims, lambda g: (0,) * len(dims))
    per_head = pl.BlockSpec((1, slots, PAIR), lambda g: (g, 0, 0))
    per_head_shape = (KEY_VALUE_HEADS, slots, PAIR)
    return pl.pallas_call(
        functools.partial(attend_kernel, nz),
        grid=(KEY_VALUE_HEADS,),
        out_shape=(shape((slots, heads), bf16), shape(per_head_shape, bf16), shape(per_head_shape, bf16), shape(per_head_shape, f32),
                   shape((slots, heads), bf16), shape((slots, width), bf16), shape((slots, width), f32), shape((slots, width), bf16),
                   shape((CHIPS,) + gy.shape, bf16), shape((CHIPS, CORES * nz) + gd_own.shape[1:], bf16)),
        in_specs=[fixed(slots, width), fixed(1, width), fixed(1, width), fixed(3, slots, PAIR), ANY, ANY, fixed(*gy.shape), fixed(*gd_own.shape)],
        out_specs=(pl.BlockSpec((slots, REPEAT * HEAD_SIZE), lambda g: (0, g)), per_head, per_head, per_head,
                   fixed(slots, heads), fixed(slots, width), fixed(slots, width), fixed(slots, width), ANY, ANY),
        scratch_shapes=[vm((2, keys, PAIR), bf16), vm((2, keys, PAIR), bf16), vm(w_qkv.shape, bf16), vm(w_out.shape, bf16),
                        vm((slots, w_qkv.shape[1]), f32), dma((w_qkv.shape[1] // 256,)), dma((3,)), dma((2,)), dma((2,)), dma((2,)), dma((2,)),
                        dma((1, 2, nz)), dma((1, 2, nz)), dma((nz,)), dma((nz,))],
        compiler_params=pltpu.CompilerParams(collective_id=4, has_side_effects=True, vmem_limit_bytes=56 << 20),
        cost_estimate=pl.CostEstimate(flops=4 * slots * width * heads, bytes_accessed=40 << 20, transcendentals=QUERY_HEADS * slots * slots),
        name="attend",
    )(tokens, gain1, gain2, tables, w_qkv, w_out, gy, gd_own)


def products(left_side, right_side, kk, xt, put):
    part = xt.shape[0] // CHIPS
    for t in range(CHIPS):
        at = pl.ds(pl.multiple_of((t * CORES + kk) * part, 128), part)
        xt[t * part : (t + 1) * part, :] = left_side[:, at].T
    def step(j, carry):
        at = pl.ds(pl.multiple_of(j * 256, 256), 256)
        put(at, jnp.dot(xt[...], right_side[:, at], preferred_element_type=jnp.float32).reshape(CHIPS, part, 256))
        return carry
    lax.fori_loop(0, right_side.shape[1] // 256, step, 0)


def to_their_core(left_side, right_side, k, xt, away, swap):
    def put(at, v): away[:, :, at] = v.astype(jnp.bfloat16)
    products(left_side, right_side, 1 - k, xt, put)
    swap.start()


def with_their_core(left_side, right_side, k, xt, took, swap):
    swap.wait_recv()
    def put(at, v): took[:, :, at] = (took[:, :, at].astype(jnp.float32) + v).astype(jnp.bfloat16)
    products(left_side, right_side, k, xt, put)


def attend_back_kernel(q_ref, k_ref, v_ref, lse_ref, gc_ref, tab_ref, part, gal, ctx, gq_ref, gk_ref, gv_ref, crossed, core_sums,
                       ks, kt, vt, ds, pr, qs, gs, away, took, xt, s_s, s_r, core_s, core_r, done):
    g = pl.program_id(0)
    c, k, n = place()
    copy = remote(part, crossed, s_s, s_r, chip_at(c, 3), k, n)
    swap = remote(away, took, core_s, core_r, c, 1 - k, n)
    store = pltpu.make_async_copy(took, core_sums, done)
    @pl.when(g == 0)
    def _():
        hello([(None, chip_at(c, 3), k, n), (None, c, 1 - k, n)])
        copy.start()
        to_their_core(gal, ctx, k, xt, away, swap)
    @pl.when(g == KEY_VALUE_HEADS - 1)
    def _():
        with_their_core(gal, ctx, k, xt, took, swap)
        store.start()
    f32, bf16 = jnp.float32, jnp.bfloat16
    slots = q_ref.shape[0]
    scale = HEAD_SIZE ** -0.5
    @pl.when(g == 0)
    def _():
        for ref in (ks, kt, vt, ds, pr): ref[...] = jnp.zeros_like(ref)
    lane = lax.broadcasted_iota(jnp.int32, (slots, PAIR), 1)
    tables = (tab_ref[0], tab_ref[1], tab_ref[2])
    key, val = k_ref[0].astype(f32), v_ref[0].astype(f32)
    for stack, x in ((ks, key * scale), (kt, key), (vt, val)):
        stack[0, 0:slots, :] = x.astype(bf16)
        stack[1, 0:slots, :] = pltpu.roll(x, HEAD_SIZE, 1).astype(bf16)
    for at, size, keys in row_blocks(slots):
        rows = slice(at, at + size)
        below = lax.broadcasted_iota(jnp.int32, (size, 128), 0) >= lax.broadcasted_iota(jnp.int32, (size, 128), 1)
        lse = lse_ref[0, rows, :]
        for p in range(PAIRS):
            span = slice(p * PAIR, (p + 1) * PAIR)
            deep = slice(p * slots + at, p * slots + at + size)
            q, gc = q_ref[rows, span], gc_ref[rows, span]
            qs[deep, :] = q
            gs[deep, :] = gc
            gq = jnp.zeros((size, PAIR), f32)
            for h in range(2):
                s = lax.dot_general(q, ks[h, 0:keys, :], contract_last, preferred_element_type=f32)
                e = jnp.exp(s - lse[:, 2 * p + h : 2 * p + h + 1])
                probs = causal(e, below, 0.0)
                pr[h, deep, 0:keys] = probs.astype(bf16)
                gp = lax.dot_general(gc, vt[h, 0:keys, :], contract_last, preferred_element_type=f32)
                inner = jnp.sum(gp * probs, axis=-1, keepdims=True)
                grad = (probs * (gp - inner) * scale).astype(bf16)
                ds[h, deep, 0:keys] = grad
                gq = gq + jnp.dot(grad, kt[h, 0:keys, :], preferred_element_type=f32)
            gq_ref[rows, span] = unrotate(gq, tuple(t[rows] for t in tables)).astype(bf16)
    for src, right, out, turn in ((ds, qs, gk_ref, True), (pr, gs, gv_ref, False)):
        lo, hi = (
            lax.dot_general(src[h], right[...], contract_first, preferred_element_type=f32)[0:slots] for h in range(2)
        )
        x = jnp.where(lane < HEAD_SIZE, lo + pltpu.roll(hi, HEAD_SIZE, 1), 0.0)
        if turn: x = unrotate(x, tables)
        @pl.when(g % 2 == 0)
        def _(): out[...] = x
        @pl.when(g % 2 == 1)
        def _(): out[...] = jnp.where(lane < HEAD_SIZE, out[...], pltpu.roll(x, HEAD_SIZE, 1))
    @pl.when(g == KEY_VALUE_HEADS - 1)
    def _():
        copy.wait()
        swap.wait_send()
        store.wait()


def attend_back_all(q, k, v, lse, grad_context, tables, part, gal, ctx):
    slots, width = gal.shape
    block = (CHIPS, width // (CHIPS * CORES), ctx.shape[1])
    wide = REPEAT * HEAD_SIZE
    bf16, f32, vm = jnp.bfloat16, jnp.float32, pltpu.VMEM
    keys = -(-slots // 128) * 128
    shape = jax.ShapeDtypeStruct
    per_head = pl.BlockSpec((1, slots, PAIR), lambda g: (g, 0, 0))
    wide_spec = pl.BlockSpec((slots, wide), lambda g: (0, g))
    two = pl.BlockSpec((slots, PAIR), lambda g: (0, g // 2))
    return pl.pallas_call(
        attend_back_kernel,
        grid=(KEY_VALUE_HEADS,),
        out_shape=(shape((slots, QUERY_HEADS * HEAD_SIZE), bf16), shape((slots, KEY_VALUE_HEADS * HEAD_SIZE), f32),
                   shape((slots, KEY_VALUE_HEADS * HEAD_SIZE), f32), shape(part.shape, part.dtype), shape(block, bf16)),
        in_specs=[wide_spec, per_head, per_head, per_head, wide_spec, pl.BlockSpec((3, slots, PAIR), lambda g: (0, 0, 0)), ANY,
                  pl.BlockSpec(gal.shape, lambda g: (0, 0)), pl.BlockSpec(ctx.shape, lambda g: (0, 0))],
        out_specs=(wide_spec, two, two, ANY, ANY),
        scratch_shapes=[vm((2, keys, PAIR), bf16)] * 3 + [vm((2, PAIRS * slots, keys), bf16)] * 2 + [vm((PAIRS * slots, PAIR), bf16)] * 2
        + [vm(block, bf16), vm(block, bf16), vm((CHIPS * block[1], slots), bf16)] + [pltpu.SemaphoreType.DMA] * 5,
        compiler_params=pltpu.CompilerParams(collective_id=2, has_side_effects=True, vmem_limit_bytes=48 << 20),
        name="attend_back",
    )(q, k, v, lse, grad_context, tables, part, gal, ctx)


class SumLine:
    def __init__(self, nz, at, piece, slot, send, recv):
        self.nz, self.at, self.piece, self.slot, self.send, self.recv = nz, at, piece, slot, send, recv

    def _hop(self, a, way, j):
        c, k, n = self.at
        i = jnp.clip(j - n - 1 if way == 0 else n - 1 - j, 0, self.nz - 2)
        return remote(self.piece(a, j), self.slot(a, way, i), self.send.at[a, way, j], self.recv.at[a, way, j],
                      c, k, n + 1 if way == 0 else n - 1)

    def step(self, some, t):
        nz, n = self.nz, self.at[2]
        for way in range(2):
            hops = n if way == 0 else nz - 1 - n
            j = jnp.clip(n + nz - 1 - t if way == 0 else t - hops, 0, nz - 1)
            for a in some:
                @pl.when((hops > 0) & (t >= hops))
                def _():
                    self._hop(a, way, j).wait_recv()
                    add_into(self.piece(a, j), self.slot(a, way, jnp.clip(j - n if way == 0 else n - j, 0, nz - 2)))
                @pl.when((t >= hops) & (j != n))
                def _(): self._hop(a, way, j).start()

    def finish(self, a):
        n = self.at[2]
        for j in range(self.nz):
            for way in range(2):
                @pl.when(n < j if way == 0 else n > j)
                def _(): self._hop(a, way, j).wait_send()


def gradient_kernel(nz, sums_hbm, xn_hbm, gq_hbm, wq_hbm, tok_hbm, gh_hbm, gain, gain_mlp, out0, out1, out2, grad_tokens,
                    took0, took1, took2, away1, away2, zbuf0, zbuf1, zbuf2, xn, gq, wq, tok, gh, gx, xt, gain_row,
                    core_s, core_r, half_s, half_r, main_s, main_r, z_s, z_r, load, loc):
    f32, bf16 = jnp.float32, jnp.bfloat16
    items = 3
    outs, took, away, zbuf = (out0, out1, out2), (took0, took1, took2), (None, away1, away2), (zbuf0, zbuf1, zbuf2)
    c, k, n = place()
    left, right = n > 0, n < nz - 1
    cx, cy, cd = (chip_at(c, r) for r in (1, 2, 3))
    loads = [pltpu.make_async_copy(a, b, load.at[i]) for i, (a, b) in enumerate(
        ((sums_hbm, took0), (xn_hbm, xn), (gq_hbm, gq), (wq_hbm, wq), (tok_hbm, tok), (gh_hbm, gh)))]
    for cp in loads: cp.start()
    hello([(None, cc, k, n) for cc in (cx, cy, cd)] + [(None, c, 1 - k, n), (left, c, k, n - 1), (right, c, k, n + 1)])
    slots, width = xn.shape
    rows = out0.shape[0]
    part = nz * rows
    half = part // 2
    top, low = pl.ds(0, half), pl.ds(half, half)
    def arrive(a, at, size): return zbuf[a].at[pl.ds(at, size)]
    swap = [a and remote(away[a], took[a], core_s.at[a - 1], core_r.at[a - 1], c, 1 - k, n) for a in range(items)]
    cross = [[remote(took[a].at[cd, top], arrive(a, 2 * part, half), half_s.at[a, 0], half_r.at[a, 0], cx, k, n),
              remote(took[a].at[cd, low], arrive(a, 2 * part + half, half), half_s.at[a, 1], half_r.at[a, 1], cy, k, n)]
             for a in range(items)]
    main = [[remote(took[a].at[cx, top], arrive(a, 0, half), main_s.at[a, 0], main_r.at[a, 0], cx, k, n),
             remote(took[a].at[cy, low], arrive(a, part + half, half), main_s.at[a, 1], main_r.at[a, 1], cy, k, n),
             remote(took[a].at[cx, low], arrive(a, half, half), main_s.at[a, 2], main_r.at[a, 2], cx, k, n),
             remote(took[a].at[cy, top], arrive(a, part, half), main_s.at[a, 3], main_r.at[a, 3], cy, k, n)]
            for a in range(items)]

    def input_gradient():
        loads[3].wait()
        def step(j, carry):
            at = pl.ds(pl.multiple_of(j * 256, 256), 256)
            gx[:, at] = lax.dot_general(gq[...], wq[at, :], contract_last, preferred_element_type=f32)
            return carry
        lax.fori_loop(0, width // 256, step, 0)

    def input_norm():
        for cp in loads[4:]: cp.wait()
        def step(j, total):
            at = pl.ds(pl.multiple_of(j * 16, 16), 16)
            x, g = tok[at, :].astype(f32), gx[at, :]
            scale = lax.rsqrt(jnp.mean(x * x, axis=-1, keepdims=True) + norm_eps)
            hat = x * scale
            g1 = g * gain[...]
            gh[at, :] = gh[at, :] + scale * (g1 - hat * jnp.mean(g1 * hat, axis=-1, keepdims=True))
            t = g * hat
            return total + t[0:8] + t[8:16]
        total = lax.fori_loop(0, slots // 16, step, jnp.zeros((8, width), f32))
        return jnp.sum(total, axis=0, keepdims=True)

    def gains_swap(of_attn):
        row = lax.broadcasted_iota(jnp.int32, (128, part), 0)
        def columns_of(t, kk):
            at = pl.ds(pl.multiple_of((t * CORES + kk) * part, 128), part)
            return jnp.where(row == 0, gain_row[0:1, at], jnp.where(row == 1, gain_mlp[0:1, at], 0.0)).T
        gain_row[0:1, :] = of_attn
        for t in range(CHIPS): away[2][t] = columns_of(t, 1 - k).astype(bf16)
        swap[2].start()
        swap[2].wait_recv()
        for t in range(CHIPS): took[2][t] = (took[2][t].astype(f32) + columns_of(t, k)).astype(bf16)
        for cp in cross[2]: cp.start()

    def relay(a):
        cross[a][0].wait_recv()
        add_into(took[a].at[cy, top], arrive(a, 2 * part, half))
        main[a][3].start()
        cross[a][1].wait_recv()
        add_into(took[a].at[cx, low], arrive(a, 2 * part + half, half))
        for i in (2, 0, 1): main[a][i].start()

    def mine(a):
        for cp in main[a]: cp.wait_recv()
        add_into(took[a].at[c], arrive(a, 0, part), arrive(a, part, part))

    line = SumLine(nz, (c, k, n), lambda a, j: took[a].at[c, pl.ds(pl.multiple_of(j * rows, rows), rows)],
                   lambda a, way, i: arrive(a, pl.multiple_of(2 * part + 2 * half + (way * (nz - 1) + i) * rows, rows), rows), z_s, z_r)

    loads[0].wait()
    for cp in cross[0]: cp.start()
    for cp in loads[1:3]: cp.wait()
    to_their_core(xn, gq, k, xt, away[1], swap[1])
    relay(0)
    with_their_core(xn, gq, k, xt, took[1], swap[1])
    for cp in cross[1]: cp.start()
    input_gradient()
    gains_swap(input_norm())
    stores = [pltpu.make_async_copy(gh, grad_tokens, loc.at[items])]
    stores[0].start()
    for a in range(1, items): relay(a)
    mine(0)
    for t in range(nz): line.step([0], t)
    stores.append(pltpu.make_async_copy(line.piece(0, n), outs[0], loc.at[0]))
    stores[-1].start()
    for a in range(1, items):
        mine(a)
        stores.append(pltpu.make_async_copy(took[a].at[c], outs[a], loc.at[a]))
        stores[-1].start()
    for cp in stores: cp.wait()
    for a in range(items):
        if a: swap[a].wait_send()
        for cp in cross[a] + main[a]: cp.wait_send()
    line.finish(0)


def gradient_all(nz, sums, xn, gq, wq, tokens, grad_hidden, gain, gain_mlp, cid):
    dma, vm = pltpu.SemaphoreType.DMA, pltpu.VMEM
    bf16, f32 = jnp.bfloat16, jnp.float32
    slots, width = xn.shape
    m = 3
    part = width // (CHIPS * CORES)
    rows = part // nz
    widths = (sums.shape[2], gq.shape[1], 128)
    shape = jax.ShapeDtypeStruct
    blocks = [vm((CHIPS, part, w), bf16) for w in widths]
    row = pl.BlockSpec((1, width), lambda: (0, 0))
    return pl.pallas_call(
        functools.partial(gradient_kernel, nz),
        out_shape=(shape((rows, widths[0]), bf16),) + tuple(shape((part, w), bf16) for w in widths[1:]) + (shape((slots, width), f32),),
        in_specs=[ANY] * 6 + [row, row], out_specs=(ANY,) * (m + 1),
        scratch_shapes=blocks + blocks[1:] + [vm((3 * part + 2 * nz * rows, w), bf16) for w in widths]
        + [vm(xn.shape, bf16), vm(gq.shape, bf16), vm(wq.shape, bf16), vm(tokens.shape, bf16),
           vm((slots, width), f32), vm((slots, width), f32), vm((CHIPS * part, slots), bf16), vm((8, width), f32)]
        + [dma((m - 1,)), dma((m - 1,)), dma((m, 2)), dma((m, 2)), dma((m, 4)), dma((m, 4)), dma((1, 2, nz)), dma((1, 2, nz)), dma((6,)), dma((m + 1,))],
        compiler_params=pltpu.CompilerParams(collective_id=cid, has_side_effects=True, vmem_limit_bytes=62 << 20),
        name="gradient_all",
    )(sums, xn, gq, wq, tokens, grad_hidden, gain, gain_mlp)


def finish_kernel(nz, down, gu, part1, part2, sum_o, parts_hbm, crossed_hbm, hidden_hbm, valid,
                  out_q, out_k, out_v, out_gain, out_d, out_g, out_u, out_o, output,
                  acc1, acc2, in1, in2, ff, wide1, wide2, wide_ff, wide_o, parts, crossed, hidden, result,
                  z_s, z_r, ff_s, ff_r, load, loc):
    f32 = jnp.float32
    c, k, n = place()
    rows, cols = down.shape[1:]
    loads = [pltpu.make_async_copy(a, b, load.at[i]) for i, (a, b) in enumerate(
        ((part1, acc1), (part2, acc2), (parts_hbm, parts), (crossed_hbm, crossed), (hidden_hbm, hidden)))]
    for cp in loads: cp.start()
    hello([(None, chip_at(c, r), k, n) for r in (1, 2, 3)] + [(n > 0, c, k, n - 1), (n < nz - 1, c, k, n + 1)])
    acc, came = (acc1, acc2), (in1, in2)
    line = SumLine(nz, (c, k, n), lambda a, j: acc[a].at[pl.ds(pl.multiple_of(j * rows, rows), rows)],
                   lambda a, way, i: came[a].at[way, i], z_s, z_r)
    def term(m, cc): return down.at[cc] if m == 0 else gu.at[cc, :, pl.ds((m - 1) * cols, cols)]
    home = [[remote(term(m, chip_at(c, r)), ff.at[m, r - 1], ff_s.at[m, r - 1], ff_r.at[m, r - 1], chip_at(c, r), k, n)
             for r in (1, 2, 3)] for m in range(3)]
    for cps in home:
        for cp in cps: cp.start()
    for cp in loads[:2]: cp.wait()
    line.step([0, 1], 0)
    stores = []
    def store(src, dst, i):
        stores.append(pltpu.make_async_copy(src, dst, loc.at[i]))
        stores[-1].start()
    outs = (out_d, out_g, out_u)
    def put(m, r, value):
        wide_ff[m, r] = value.astype(f32)
        at = pl.ds(pl.multiple_of(chip_at(c, r) * cols, 128), cols)
        store(wide_ff.at[m, r], outs[m].at[:, at], 4 + m * CHIPS + r)
    for m in range(3): put(m, 0, term(m, c)[...])
    wide_o[...] = sum_o[...].astype(f32)
    store(wide_o, out_o, 4 + 3 * CHIPS)
    line.step([0, 1], 1)
    for cp in loads[2:]: cp.wait()
    def add(i, carry):
        at = pl.ds(pl.multiple_of(i * 16, 16), 16)
        total = hidden[at, :] + (parts[0, at, :].astype(f32) + parts[1, at, :].astype(f32) + parts[2, at, :].astype(f32)
                                 + crossed[at, :].astype(f32))
        result[at, :] = (valid[at, :] * total).astype(result.dtype)
        return carry
    lax.fori_loop(0, result.shape[0] // 16, add, 0)
    store(result, output, 5 + 3 * CHIPS)
    for t in range(2, nz): line.step([0, 1], t)
    for m in range(3):
        for r in (1, 2, 3):
            home[m][r - 1].wait_recv()
            put(m, r, ff[m, r - 1])
    wide1[...] = line.piece(0, n)[...].astype(f32)
    wide2[...] = line.piece(1, n)[...].astype(f32)
    first = 0
    for i, out in enumerate((out_q, out_k, out_v)):
        store(wide1.at[:, pl.ds(first, out.shape[1])], out, i)
        first += out.shape[1]
    store(wide2, out_gain, 3)
    for cp in stores: cp.wait()
    for cps in home:
        for cp in cps: cp.wait_send()
    for a in range(2): line.finish(a)


def finish_all(nz, down, gu, part1, part2, sum_o, parts, crossed, hidden, valid, key_width, cid):
    dma, vm = pltpu.SemaphoreType.DMA, pltpu.VMEM
    bf16, f32 = jnp.bfloat16, jnp.float32
    rows, cols = down.shape[1:]
    w1, w2 = part1.shape[1], part2.shape[1]
    def out(w): return jax.ShapeDtypeStruct((rows, w), f32)
    return pl.pallas_call(
        functools.partial(finish_kernel, nz),
        out_shape=(out(w1 - 2 * key_width), out(key_width), out(key_width), out(w2)) + (out(CHIPS * cols),) * 3
        + (out(sum_o.shape[1]), jax.ShapeDtypeStruct(hidden.shape, bf16)),
        in_specs=[VMEM, VMEM, ANY, ANY, VMEM, ANY, ANY, ANY, VMEM], out_specs=(ANY,) * 9,
        scratch_shapes=[vm(part1.shape, bf16), vm(part2.shape, bf16), vm((2, nz - 1, rows, w1), bf16), vm((2, nz - 1, rows, w2), bf16),
                        vm((3, CHIPS - 1, rows, cols), bf16), vm((rows, w1), f32), vm((rows, w2), f32), vm((3, CHIPS, rows, cols), f32),
                        vm(sum_o.shape, f32), vm(parts.shape, bf16), vm(crossed.shape, bf16), vm(hidden.shape, f32), vm(hidden.shape, bf16),
                        dma((2, 2, nz)), dma((2, 2, nz)), dma((3, 3)), dma((3, 3)), dma((5,)), dma((6 + 3 * CHIPS,))],
        compiler_params=pltpu.CompilerParams(collective_id=cid, has_side_effects=True, vmem_limit_bytes=40 << 20),
        name="finish_all",
    )(down, gu, part1, part2, sum_o, parts, crossed, hidden, valid)


def fits(mesh):
    return mesh.shape["wide"] == CHIPS * CORES


def fast_device(
    nz,
    tokens,
    cotangent,
    lengths,
    positions,
    norm_attn,
    w_query,
    w_key,
    w_value,
    w_output,
    norm_mlp,
    w_gate,
    w_up,
    w_down,
):
    f32, bf16 = jnp.float32, jnp.bfloat16
    c, k, n = place()
    slots, width = tokens.shape
    rows = w_query.shape[0]
    query_width, key_width = w_query.shape[1], w_key.shape[1]
    cols = w_gate.shape[1] // CHIPS
    valid_rows = (jnp.arange(slots) < lengths[0]).astype(f32)[:, None]
    tables = lane_tables(positions)
    grad_y = cotangent.astype(f32) * valid_rows
    grad_y_low = grad_y.astype(bf16)
    gains = jnp.zeros((rows, 128), bf16).at[:, 0].set(norm_attn).at[:, 1].set(norm_mlp)
    w_qkv, w_out, gain_cols, ff_gate_up, ff_down = gather_all(
        nz, w_query, w_key, w_value, w_output, gains, w_gate, w_up, w_down
    )
    gain_attn = gain_cols[:, 0].astype(f32)
    gain_mlp = gain_cols[:, 1].astype(f32)

    query_rotated, key_rotated, value_reduced, log_totals, context, scaled_attn, hidden, scaled_mlp, gy_all, ff_down = attend_all(
        nz, tokens, gain_attn[None], gain_mlp[None], tables, w_qkv, w_out, grad_y_low, ff_down
    )
    ff_gate_up, ff_down = (w.reshape(CHIPS * CORES, nz, rows, w.shape[-1]) for w in (ff_gate_up, ff_down))
    normed_mlp = normalize(hidden)
    grad_x_parts, mlp_parts, mlp_cross, down_sums, ff_sums = mlp_all(nz, scaled_mlp, gy_all, ff_gate_up, ff_down)
    grad_xn2 = jnp.sum(grad_x_parts.astype(f32), axis=0)
    grad_gain_mlp = jnp.sum(grad_xn2 * normed_mlp, axis=0)
    grad_hidden = grad_y + norm_back(grad_xn2 * gain_mlp, normed_mlp, hidden)
    grad_attn_low = grad_hidden.astype(bf16)
    grad_context = jnp.dot(grad_attn_low, w_out, preferred_element_type=f32).astype(bf16)
    grad_query, grad_key, grad_value, mlp_crossed, out_sums = attend_back_all(
        query_rotated, key_rotated, value_reduced, log_totals, grad_context, tables, mlp_cross, grad_attn_low, context
    )
    grad_qkv = jnp.concatenate([grad_query, grad_key.astype(bf16), grad_value.astype(bf16)], 1)
    ff_sums = lax.psum_scatter(ff_sums, "narrow", scatter_dimension=0, tiled=True)
    out_part, qkv_part, gain_part, grad_tokens = gradient_all(
        nz, out_sums, scaled_attn, grad_qkv, w_qkv, tokens, grad_hidden, gain_attn[None], grad_gain_mlp[None], 3
    )
    grad_w_query, grad_w_key, grad_w_value, gain_sums, grad_w_down, grad_w_gate, grad_w_up, grad_w_output, output = finish_all(
        nz,
        down_sums,
        ff_sums.reshape(CHIPS, rows, 2 * cols),
        qkv_part,
        gain_part,
        out_part,
        mlp_parts,
        mlp_crossed,
        hidden,
        valid_rows,
        key_width,
        5,
    )
    grad_norm_attn, grad_norm_mlp = gain_sums[:, 0], gain_sums[:, 1]
    return (
        output,
        grad_tokens,
        grad_norm_attn,
        grad_w_query,
        grad_w_key,
        grad_w_value,
        grad_w_output,
        grad_norm_mlp,
        grad_w_gate,
        grad_w_up,
        grad_w_down,
    )


def solution(mesh):
    in_specs = (
        P(("wide", "narrow"), None),
        P(("wide", "narrow"), None),
        P(("wide", "narrow")),
        P(("wide", "narrow")),
        P(("wide", "narrow")),
        P(("wide", "narrow"), None),
        P(("wide", "narrow"), None),
        P(("wide", "narrow"), None),
        P(("wide", "narrow"), None),
        P(("wide", "narrow")),
        P(("wide", "narrow"), None),
        P(("wide", "narrow"), None),
        P(("wide", "narrow"), None),
    )
    out_specs = (
        P(("wide", "narrow"), None),
        P(("wide", "narrow"), None),
        P(("wide", "narrow")),
        P(("wide", "narrow"), None),
        P(("wide", "narrow"), None),
        P(("wide", "narrow"), None),
        P(("wide", "narrow"), None),
        P(("wide", "narrow")),
        P(("wide", "narrow"), None),
        P(("wide", "narrow"), None),
        P(("wide", "narrow"), None),
    )
    body = functools.partial(fast_device, mesh.shape["narrow"]) if fits(mesh) else per_device
    return jax.shard_map(
        body, mesh=mesh, in_specs=in_specs, out_specs=out_specs, check_vma=False
    )
```

```python
import functools
import math

import jax
import jax.numpy as jnp
from jax import lax
from jax.experimental import pallas as pl
from jax.experimental.pallas import tpu as pltpu
from jax.sharding import PartitionSpec as P

QUERY_HEADS = 32
KEY_VALUE_HEADS = 4
HEAD_SIZE = 64


norm_eps = 1e-05
rope_base = 10000.0
masked_score = -1e30
contract_last = (((1,), (1,)), ((), ()))
contract_first = (((0,), (0,)), ((), ()))


def rope_tables(positions):
    half_dim = HEAD_SIZE // 2
    inv_freq = jnp.exp(
        -math.log(rope_base) * jnp.arange(half_dim, dtype=jnp.float32) * 2.0 / HEAD_SIZE
    )
    angles = positions.astype(jnp.float32)[..., None] * inv_freq
    cosine = jnp.cos(angles)
    sine_part = jnp.sin(angles)
    return (jnp.concatenate([cosine, cosine], -1), jnp.concatenate([sine_part, sine_part], -1))


def apply_rotary(values, cosine_table, sine_table):
    half_dim = values.shape[-1] // 2
    turned = jnp.concatenate([-values[..., half_dim:], values[..., :half_dim]], -1)
    return values * cosine_table[..., None, :] + turned * sine_table[..., None, :]


def invert_rotary(grad_rows, cosine_table, sine_table):
    half_dim = grad_rows.shape[-1] // 2
    with_cos = grad_rows * cosine_table[..., None, :]
    with_sin = grad_rows * sine_table[..., None, :]
    return with_cos + jnp.concatenate([with_sin[..., half_dim:], -with_sin[..., :half_dim]], -1)


def normalize(values):
    return values * lax.rsqrt(jnp.mean(values * values, axis=-1, keepdims=True) + norm_eps)


def norm_back(grad_hat, normed, values):
    row_scale = lax.rsqrt(jnp.mean(values * values, axis=-1, keepdims=True) + norm_eps)
    return row_scale * (grad_hat - normed * jnp.mean(grad_hat * normed, axis=-1, keepdims=True))


def attention_inputs(normed, norm_attn, w_query, w_key, w_value):
    gain_piece = lax.all_gather(norm_attn, ("wide", "narrow"), axis=0, tiled=True)
    query_rows = lax.all_gather(w_query, ("wide", "narrow"), axis=0, tiled=True)
    key_rows = lax.all_gather(w_key, ("wide", "narrow"), axis=0, tiled=True)
    value_rows = lax.all_gather(w_value, ("wide", "narrow"), axis=0, tiled=True)
    gain_float = gain_piece.astype(jnp.float32)
    columns = (normed * gain_float).astype(jnp.bfloat16)
    query_sum = jnp.dot(columns, query_rows, preferred_element_type=jnp.float32)
    key_sum = jnp.dot(columns, key_rows, preferred_element_type=jnp.float32)
    value_sum = jnp.dot(columns, value_rows, preferred_element_type=jnp.float32)
    return (gain_float, columns, query_sum, key_sum, value_sum)


def mlp_inputs(normed, norm_mlp, w_gate, w_up):
    gain_piece = lax.all_gather(norm_mlp, ("wide", "narrow"), axis=0, tiled=True)
    gate_rows = lax.all_gather(w_gate, ("wide", "narrow"), axis=0, tiled=True)
    up_rows = lax.all_gather(w_up, ("wide", "narrow"), axis=0, tiled=True)
    gain_float = gain_piece.astype(jnp.float32)
    columns = (normed * gain_float).astype(jnp.bfloat16)
    gate_sum = jnp.dot(columns, gate_rows, preferred_element_type=jnp.float32)
    up_sum = jnp.dot(columns, up_rows, preferred_element_type=jnp.float32)
    return (gain_float, columns, gate_sum, up_sum)


def head_slices(query_rotated, key_rotated, value_reduced, shared_key_head):
    row_total_count = query_rotated.shape[0]
    heads_per_group = QUERY_HEADS // KEY_VALUE_HEADS
    query_head = query_rotated[
        :,
        shared_key_head
        * heads_per_group
        * HEAD_SIZE : (shared_key_head + 1)
        * heads_per_group
        * HEAD_SIZE,
    ].reshape(row_total_count, heads_per_group, HEAD_SIZE)
    key_head = key_rotated[:, shared_key_head * HEAD_SIZE : (shared_key_head + 1) * HEAD_SIZE]
    value_head = value_reduced[:, shared_key_head * HEAD_SIZE : (shared_key_head + 1) * HEAD_SIZE]
    return (query_head, key_head, value_head)


def head_scores(query_head, key_head):
    row_total_count = query_head.shape[0]
    causal = jnp.arange(row_total_count)[:, None] >= jnp.arange(row_total_count)[None, :]
    raw_scores = jnp.einsum("qrd,kd->rqk", query_head, key_head, preferred_element_type=jnp.float32)
    return jnp.where(causal, raw_scores * HEAD_SIZE ** (-0.5), masked_score)


def attend(query_rotated, key_rotated, value_reduced):
    row_total_count = query_rotated.shape[0]
    heads_per_group = QUERY_HEADS // KEY_VALUE_HEADS
    contexts = []
    log_totals = []
    for shared_key_head in range(KEY_VALUE_HEADS):
        query_head, key_head, value_head = head_slices(
            query_rotated, key_rotated, value_reduced, shared_key_head
        )
        scores = head_scores(query_head, key_head)
        row_peak = jnp.max(scores, axis=-1, keepdims=True)
        exp_scores = jnp.exp(scores - row_peak)
        row_total = jnp.sum(exp_scores, axis=-1, keepdims=True)
        probs = exp_scores / row_total
        context_head = jnp.einsum(
            "rqk,kd->qrd",
            probs.astype(jnp.bfloat16),
            value_head,
            preferred_element_type=jnp.float32,
        )
        contexts.append(context_head.reshape(row_total_count, heads_per_group * HEAD_SIZE))
        log_totals.append(row_peak + jnp.log(row_total))
    return (jnp.concatenate(contexts, 1).astype(jnp.bfloat16), log_totals)


def attend_back(query_rotated, key_rotated, value_reduced, log_totals, grad_context):
    row_total_count = query_rotated.shape[0]
    heads_per_group = QUERY_HEADS // KEY_VALUE_HEADS
    score_scale = HEAD_SIZE ** (-0.5)
    query_grads = []
    key_grads = []
    value_grads = []
    for shared_key_head in range(KEY_VALUE_HEADS):
        query_head, key_head, value_head = head_slices(
            query_rotated, key_rotated, value_reduced, shared_key_head
        )
        scores = head_scores(query_head, key_head)
        probs = jnp.exp(scores - log_totals[shared_key_head])
        probs_low = probs.astype(jnp.bfloat16)
        grad_head = grad_context[
            :,
            shared_key_head
            * heads_per_group
            * HEAD_SIZE : (shared_key_head + 1)
            * heads_per_group
            * HEAD_SIZE,
        ].reshape(row_total_count, heads_per_group, HEAD_SIZE)
        grad_probs = jnp.einsum(
            "qrd,kd->rqk", grad_head, value_head, preferred_element_type=jnp.float32
        )
        value_grads.append(
            jnp.einsum("rqk,qrd->kd", probs_low, grad_head, preferred_element_type=jnp.float32)
        )
        inner_sum = jnp.sum(grad_probs * probs, axis=-1, keepdims=True)
        grad_scores = (probs * (grad_probs - inner_sum) * score_scale).astype(jnp.bfloat16)
        query_grad = jnp.einsum(
            "rqk,kd->qrd", grad_scores, key_head, preferred_element_type=jnp.float32
        )
        query_grads.append(query_grad.reshape(row_total_count, heads_per_group * HEAD_SIZE))
        key_grads.append(
            jnp.einsum("rqk,qrd->kd", grad_scores, query_head, preferred_element_type=jnp.float32)
        )
    return (
        jnp.concatenate(query_grads, 1),
        jnp.concatenate(key_grads, 1),
        jnp.concatenate(value_grads, 1),
    )


def make_term(width_sides, other_sides):
    down_side, mlp_side, attn_side, qkv_side = width_sides
    mixed_rows, gate_rows, up_rows, context_rows, query_rows, key_rows, value_rows = other_sides

    def grad_term(first_row, row_span):
        pieces = [
            lax.dot_general(
                down_side, mixed_rows, contract_first, preferred_element_type=jnp.float32
            ),
            lax.dot_general(
                mlp_side, gate_rows, contract_first, preferred_element_type=jnp.float32
            ),
            lax.dot_general(mlp_side, up_rows, contract_first, preferred_element_type=jnp.float32),
            lax.dot_general(
                attn_side, context_rows, contract_first, preferred_element_type=jnp.float32
            ),
            lax.dot_general(
                qkv_side, query_rows, contract_first, preferred_element_type=jnp.float32
            ),
            lax.dot_general(qkv_side, key_rows, contract_first, preferred_element_type=jnp.float32),
            lax.dot_general(
                qkv_side, value_rows, contract_first, preferred_element_type=jnp.float32
            ),
        ]
        return jnp.concatenate(pieces, 1)

    return grad_term


def per_device(
    tokens,
    cotangent,
    lengths,
    positions,
    norm_attn,
    w_query,
    w_key,
    w_value,
    w_output,
    norm_mlp,
    w_gate,
    w_up,
    w_down,
):
    row_total_count = tokens.shape[0]
    shard_rows = w_query.shape[0]
    query_width = w_query.shape[1]
    key_width = w_key.shape[1]
    hidden_width = w_gate.shape[1]
    inputs = tokens.astype(jnp.float32)
    valid_rows = (jnp.arange(row_total_count) < lengths[0]).astype(jnp.float32)[:, None]
    cosine_table, sine_table = rope_tables(positions)
    normed_attn = normalize(inputs)
    gain_attn_full, scaled_attn, query_pre, key_unrotated, value_pre = attention_inputs(
        normed_attn, norm_attn, w_query, w_key, w_value
    )
    query_rotated = (
        apply_rotary(
            query_pre.reshape(row_total_count, QUERY_HEADS, HEAD_SIZE), cosine_table, sine_table
        )
        .reshape(row_total_count, query_width)
        .astype(jnp.bfloat16)
    )
    key_rotated = (
        apply_rotary(
            key_unrotated.reshape(row_total_count, KEY_VALUE_HEADS, HEAD_SIZE),
            cosine_table,
            sine_table,
        )
        .reshape(row_total_count, key_width)
        .astype(jnp.bfloat16)
    )
    value_reduced = value_pre.astype(jnp.bfloat16)
    context, log_totals = attend(query_rotated, key_rotated, value_reduced)
    attn_out = lax.dot_general(
        context,
        lax.all_gather(w_output, ("wide", "narrow"), axis=0, tiled=True),
        contract_last,
        preferred_element_type=jnp.float32,
    )
    hidden = inputs + attn_out
    normed_mlp = normalize(hidden)
    gain_mlp_full, scaled_mlp, gate_proj, up_proj = mlp_inputs(normed_mlp, norm_mlp, w_gate, w_up)
    mixed_low = (gate_proj * jax.nn.sigmoid(gate_proj) * up_proj).astype(jnp.bfloat16)
    mlp_out = lax.dot_general(
        mixed_low,
        lax.all_gather(w_down, ("wide", "narrow"), axis=0, tiled=True),
        contract_last,
        preferred_element_type=jnp.float32,
    )
    output = (valid_rows * (hidden + mlp_out)).astype(jnp.bfloat16)
    grad_y = cotangent.astype(jnp.float32) * valid_rows
    grad_y_low = grad_y.astype(jnp.bfloat16)
    grad_cols = grad_y_low
    grad_mixed = jnp.dot(
        grad_cols,
        lax.all_gather(w_down, ("wide", "narrow"), axis=0, tiled=True),
        preferred_element_type=jnp.float32,
    )
    again_values = mlp_inputs(normed_mlp, norm_mlp, w_gate, w_up)
    gate_proj = again_values[2]
    up_proj = again_values[3]
    sigmoid_gate = jax.nn.sigmoid(gate_proj)
    grad_gate = (
        grad_mixed * up_proj * (sigmoid_gate * (1.0 + gate_proj * (1.0 - sigmoid_gate)))
    ).astype(jnp.bfloat16)
    grad_up = (grad_mixed * (gate_proj * sigmoid_gate)).astype(jnp.bfloat16)
    gate_rows = lax.all_gather(w_gate, ("wide", "narrow"), axis=0, tiled=True)
    up_rows = lax.all_gather(w_up, ("wide", "narrow"), axis=0, tiled=True)
    columns = lax.dot_general(
        grad_gate, gate_rows, contract_last, preferred_element_type=jnp.float32
    )
    columns = columns + lax.dot_general(
        grad_up, up_rows, contract_last, preferred_element_type=jnp.float32
    )
    grad_xn2 = columns
    grad_gain_mlp = jnp.sum(grad_xn2 * normed_mlp, axis=0)
    grad_hidden = grad_y + norm_back(grad_xn2 * gain_mlp_full, normed_mlp, hidden)
    grad_attn_low = grad_hidden.astype(jnp.bfloat16)
    grad_cols = grad_attn_low
    grad_context = jnp.dot(
        grad_cols,
        lax.all_gather(w_output, ("wide", "narrow"), axis=0, tiled=True),
        preferred_element_type=jnp.float32,
    )
    grad_context = grad_context.astype(jnp.bfloat16)
    grad_query_rot, gradient_key_rotated, grad_value_sum = attend_back(
        query_rotated, key_rotated, value_reduced, log_totals, grad_context
    )
    grad_query = (
        invert_rotary(
            grad_query_rot.reshape(row_total_count, QUERY_HEADS, HEAD_SIZE),
            cosine_table,
            sine_table,
        )
        .reshape(row_total_count, query_width)
        .astype(jnp.bfloat16)
    )
    grad_key = (
        invert_rotary(
            gradient_key_rotated.reshape(row_total_count, KEY_VALUE_HEADS, HEAD_SIZE),
            cosine_table,
            sine_table,
        )
        .reshape(row_total_count, key_width)
        .astype(jnp.bfloat16)
    )
    grad_value = grad_value_sum.astype(jnp.bfloat16)
    query_rows = lax.all_gather(w_query, ("wide", "narrow"), axis=0, tiled=True)
    key_rows = lax.all_gather(w_key, ("wide", "narrow"), axis=0, tiled=True)
    value_rows = lax.all_gather(w_value, ("wide", "narrow"), axis=0, tiled=True)
    columns = lax.dot_general(
        grad_query, query_rows, contract_last, preferred_element_type=jnp.float32
    )
    columns = columns + lax.dot_general(
        grad_key, key_rows, contract_last, preferred_element_type=jnp.float32
    )
    columns = columns + lax.dot_general(
        grad_value, value_rows, contract_last, preferred_element_type=jnp.float32
    )
    local_term = make_term(
        (grad_y_low, scaled_mlp, grad_attn_low, scaled_attn),
        (mixed_low, grad_gate, grad_up, context, grad_query, grad_key, grad_value),
    )
    all_sums = lax.psum_scatter(
        local_term(jnp.int32(0), lax.axis_size(("wide", "narrow")) * shard_rows),
        ("wide", "narrow"),
        scatter_dimension=0,
        tiled=True,
    )
    edges = [0]
    for width in (
        hidden_width,
        hidden_width,
        hidden_width,
        query_width,
        query_width,
        key_width,
        key_width,
    ):
        edges.append(edges[-1] + width)
    grad_w_down = all_sums[:, edges[0] : edges[1]]
    grad_w_gate = all_sums[:, edges[1] : edges[2]]
    grad_w_up = all_sums[:, edges[2] : edges[3]]
    grad_w_output = all_sums[:, edges[3] : edges[4]]
    grad_w_query = all_sums[:, edges[4] : edges[5]]
    grad_w_key = all_sums[:, edges[5] : edges[6]]
    grad_w_value = all_sums[:, edges[6] : edges[7]]
    grad_gain_attn = jnp.sum(columns * normed_attn, axis=0)
    grad_tokens = grad_hidden + norm_back(columns * gain_attn_full, normed_attn, inputs)
    grad_norm_attn, grad_norm_mlp = (
        lax.psum_scatter(grad_gain_attn, ("wide", "narrow"), scatter_dimension=0, tiled=True),
        lax.psum_scatter(grad_gain_mlp, ("wide", "narrow"), scatter_dimension=0, tiled=True),
    )
    return (
        output,
        grad_tokens,
        grad_norm_attn,
        grad_w_query,
        grad_w_key,
        grad_w_value,
        grad_w_output,
        grad_norm_mlp,
        grad_w_gate,
        grad_w_up,
        grad_w_down,
    )


MESH = pl.DeviceIdType.MESH
ANY = pl.BlockSpec(memory_space=pl.ANY)
VMEM = pl.BlockSpec(memory_space=pltpu.VMEM)

CHIPS, CORES = 4, 2

def place():
    w = lax.axis_index("wide"); n = lax.axis_index("narrow")
    return w // CORES, w % CORES, n

def chip_at(c, r):
    xb, yb, rx, ry = c % 2, c // 2, r % 2, r // 2
    return (yb + ry - 2 * yb * ry) * 2 + (xb + rx - 2 * xb * rx)


def remote(src, dst, send, recv, chip, core, z):
    return pltpu.make_async_remote_copy(src_ref=src, dst_ref=dst, send_sem=send, recv_sem=recv,
        device_id={"wide": chip * CORES + core, "narrow": z}, device_id_type=MESH)

def hello(partners):
    barrier = pltpu.get_barrier_semaphore()
    count = 0
    for cond, chip, core, z in partners:
        def sig(chip=chip, core=core, z=z):
            pl.semaphore_signal(barrier, inc=1, device_id={"wide": chip * CORES + core, "narrow": z}, device_id_type=MESH)
        if cond is None:
            sig(); count = count + 1
        else:
            pl.when(cond)(sig); count = count + jnp.where(cond, 1, 0)
    pl.semaphore_wait(barrier, count)

class Line:
    def __init__(self, nz, at, refs, send, recv, place_of):
        self.nz, self.at, self.refs, self.send, self.recv, self.place_of = nz, at, refs, send, recv, place_of

    def _copy(self, a, way, s, origin):
        c, k, n = self.at
        ref = self.place_of(self.refs[a], origin)
        return remote(ref, ref, self.send.at[a, way, s], self.recv.at[a, way, s], c, k, n + 1 if way == 0 else n - 1)

    def _origin(self, way, s):
        n = self.at[2]
        o = n - s if way == 0 else n + s
        return (n >= s) if way == 0 else (n + s <= self.nz - 1), jnp.clip(o, 0, self.nz - 1)

    def _sends(self, way, s):
        n = self.at[2]
        return self._origin(way, s)[0] & ((n < self.nz - 1) if way == 0 else (n > 0))

    def start(self, a, s, way):
        @pl.when(self._sends(way, s))
        def _(): self._copy(a, way, s, self._origin(way, s)[1]).start()

    def step(self, a, s, then=None):
        for way in range(2):
            came, origin = self._origin(way, s)
            @pl.when(came)
            def _(): self._copy(a, way, s - 1, origin).wait_recv()
            if s < self.nz - 1: self.start(a, s, way)
            if then is not None:
                @pl.when(came)
                def _(): then(origin)

    def finish(self, a):
        for s in range(self.nz - 1):
            for way in range(2):
                @pl.when(self._sends(way, s))
                def _(): self._copy(a, way, s, self._origin(way, s)[1]).wait_send()


def gather_kernel(nz, wq, wk, wv, wo, gains, wg, wu, wd, qkv, out, gain, gu, gd,
                  loc, sw_s, sw_r, z_s, z_r, f_s, f_r, p_s, p_r, h_s, h_r, d_s, d_r, e_s, e_r):
    c, k, n = at = place()
    rows, q = wq.shape
    kv = wk.shape[1]
    cols = gd.shape[-1]
    part = nz * rows
    half = part // 2
    kn = k * nz + n
    cx, cy, cd = (chip_at(c, r) for r in (1, 2, 3))
    hello([(None, cc, k, n) for cc in (cx, cy, cd)] + [(None, c, 1 - k, n), (n > 0, c, k, n - 1), (n < nz - 1, c, k, n + 1)])

    def mycols(w, cc): return w.at[:, pl.ds(pl.multiple_of(cc * cols, 128), cols)]
    def landing(i, cc): return gd.at[cc] if i == 2 else gu.at[cc, kn, :, pl.ds(i * cols, cols)]
    whole = (qkv, out, gain)
    def block(ref, z): return ref.at[pl.ds(pl.multiple_of(((c * CORES + k) * nz + z) * rows, rows), rows)]
    own = [pltpu.make_async_copy(wq, block(qkv, n).at[:, pl.ds(0, q)], loc.at[0]),
           pltpu.make_async_copy(wk, block(qkv, n).at[:, pl.ds(q, kv)], loc.at[1]),
           pltpu.make_async_copy(wv, block(qkv, n).at[:, pl.ds(q + kv, kv)], loc.at[2]),
           pltpu.make_async_copy(wo, block(out, n), loc.at[3]), pltpu.make_async_copy(gains, block(gain, n), loc.at[4])]
    ownff = [pltpu.make_async_copy(mycols(w, c), landing(i, c), loc.at[5 + i]) for i, w in enumerate((wg, wu, wd))]
    for cp in own + ownff: cp.start()
    swap = [[remote(mycols(w, cc), landing(i, c), sw_s.at[i, r], sw_r.at[i, r], cc, k, n) for r, cc in enumerate((cx, cy, cd))]
            for i, w in enumerate((wg, wu, wd))]
    for i in range(3):
        for cp in swap[i]: cp.start()
    for cp in own: cp.wait()

    line = Line(nz, at, whole, z_s, z_r, block)
    for a in range(3):
        for way in range(2): line.start(a, 0, way)

    def span(ref, cc, first, size):
        return ref.at[pl.ds(pl.multiple_of((cc * CORES + k) * part, part) + first, size)]
    plane = [[remote(span(ref, c, 0, part), span(ref, c, 0, part), p_s.at[a, r], p_r.at[a, r], cc, k, n) for r, cc in enumerate((cx, cy))]
             for a, ref in enumerate(whole)]
    across = [[remote(span(ref, cx, 0, half), span(ref, cx, 0, half), h_s.at[a, 0], h_r.at[a, 0], cy, k, n),
               remote(span(ref, cy, half, half), span(ref, cy, half, half), h_s.at[a, 1], h_r.at[a, 1], cx, k, n)]
              for a, ref in enumerate(whole)]
    cores = [[remote(span(ref, cc, 0, part), span(ref, cc, 0, part), d_s.at[a, r], d_r.at[a, r], c, 1 - k, n)
              for r, cc in enumerate((c, cx, cy, cd))] for a, ref in enumerate(whole)]

    def plane_start(a):
        for cp in plane[a] + cores[a][:1]: cp.start()
    def plane_next(a):
        for i in range(2):
            plane[a][i].wait_recv()
            across[a][i].start()
            cores[a][1 + i].start()
    def plane_last(a):
        for cp in across[a]: cp.wait_recv()
        cores[a][3].start()

    for s in range(1, nz):
        for a in range(3):
            line.step(a, s)
            if s == nz - 1: plane_start(a)

    ff = Line(nz, at, (gu,), f_s, f_r, lambda ref, z: ref.at[:, k * nz + z])
    def twin(z):
        ref = gu.at[:, k * nz + z]
        return remote(ref, ref, e_s.at[z], e_r.at[z], c, 1 - k, n)
    for i in range(2):
        ownff[i].wait()
        for cp in swap[i]: cp.wait_recv()
    for way in range(2): ff.start(0, 0, way)
    twin(n).start()
    plane_next(0)
    ff.step(0, 1, lambda z: twin(z).start())
    for a in (1, 2): plane_next(a)
    ff.step(0, 2, lambda z: twin(z).start())
    for a in range(3): plane_last(a)
    ownff[2].wait()
    for cp in swap[2]: cp.wait_recv()
    for s in range(3, nz): ff.step(0, s, lambda z: twin(z).start())
    for a in range(3):
        for cp in cores[a]: cp.wait_recv()
    for z in range(nz): twin(z).wait()
    for i in range(3):
        for cp in swap[i]: cp.wait_send()
    for a in range(3):
        line.finish(a)
        for cp in plane[a] + across[a] + cores[a]: cp.wait_send()
    ff.finish(0)


def gather_all(nz, wq, wk, wv, wo, gains, wg, wu, wd):
    rows = wq.shape[0]
    width = rows * CHIPS * CORES * nz
    cols = wg.shape[1] // CHIPS
    bf = jnp.bfloat16
    shape = jax.ShapeDtypeStruct
    dma = pltpu.SemaphoreType.DMA
    return pl.pallas_call(
        functools.partial(gather_kernel, nz),
        out_shape=(shape((width, wq.shape[1] + 2 * wk.shape[1]), bf), shape((width, wo.shape[1]), bf), shape((width, gains.shape[1]), bf),
                   shape((CHIPS, CORES * nz, rows, 2 * cols), bf), shape((CHIPS, rows, cols), bf)),
        in_specs=[VMEM] * 8, out_specs=(ANY,) * 5,
        scratch_shapes=[dma((8,)), dma((3, 3)), dma((3, 3)), dma((3, 2, nz)), dma((3, 2, nz)), dma((1, 2, nz)), dma((1, 2, nz)),
                        dma((3, 2)), dma((3, 2)), dma((3, 2)), dma((3, 2)), dma((3, 4)), dma((3, 4)), dma((nz,)), dma((nz,))],
        compiler_params=pltpu.CompilerParams(collective_id=0, has_side_effects=True),
        name="gather_all",
    )(wq, wk, wv, wo, gains, wg, wu, wd)


def add_into(dst, *srcs):
    rows = dst.shape[0]
    step = 16
    def body(i, carry):
        at = pl.ds(pl.multiple_of(i * step, step), step)
        total = dst[at, :].astype(jnp.float32)
        for s in srcs: total = total + s[at, :].astype(jnp.float32)
        dst[at, :] = total.astype(dst.dtype)
        return carry
    lax.fori_loop(0, rows // step, body, 0)


HALVES = ((0, 0), (0, 1), (1, 0), (2, 0), (1, 1), (2, 1), (3, 0), (3, 1))


def mlp_kernel(nz, x, gy, gu_hbm, gd_hbm, gx_parts, mlp_parts, mlp_cross, down_sums, sums,
               xs, gys, gu, gd, mix, ggu, gx, mo, xt, zin, load, ag_s, ag_r, rs_s, rs_r, mo_s, mo_r, out, core_s, core_r, ready, done, z_s, z_r):
    c, k, n = place()
    f32, bf16 = jnp.float32, jnp.bfloat16
    slots, width = x.shape
    half = slots // 2
    rows, cols = gd.shape[2:]
    tile = nz * rows
    hello([(None, chip_at(c, r), k, n) for r in (1, 2, 3)]
          + [(None, c, 1 - k, n), (n > 0, c, k, n - 1), (n < nz - 1, c, k, n + 1)])
    def half_of(ref, h): return ref.at[pl.ds(h * half, half)]
    index = {place_: i for i, place_ in enumerate(HALVES)}
    sends = {}
    for h in range(2):
        for r in (1, 2):
            i = index[r, h]
            sends[i] = remote(half_of(x, h), xs.at[i], ag_s.at[i], ag_r.at[i], chip_at(c, r), k, n)
            if h == 0: sends[i].start()
    loads = [pltpu.make_async_copy(half_of(x, h), xs.at[h], load.at[h]) for h in range(2)]
    loads += [pltpu.make_async_copy(half_of(gy.at[r], h), gys.at[i], load.at[2 + i]) for i, (r, h) in enumerate(HALVES)]
    for cp in loads: cp.start()
    def weights(col, w, j):
        return [pltpu.make_async_copy(a.at[:, :, :, pl.ds(first + col, w)], b.at[:, :, :, pl.ds(first + col, w)], load.at[10 + 3 * j + i])
                for i, (a, b, first) in enumerate(((gu_hbm, gu, 0), (gu_hbm, gu, cols), (gd_hbm, gd, 0)))]
    for j in range(-(-cols // 256)):
        for cp in weights(j * 256, min(256, cols - j * 256), j): cp.start()
    relays = {index[3, 0]: (index[1, 0], 2), index[3, 1]: (index[2, 1], 1)}
    relays = {i: remote(xs.at[j], xs.at[i], ag_s.at[i], ag_r.at[i], chip_at(c, r), k, n) for i, (j, r) in relays.items()}
    for cp in loads: cp.wait()

    def columns(ref, at, size):
        return ref[:, :, :, pl.ds(at, size)].reshape(width, size)

    def some_rows(ref, i): return ref[i].reshape(tile, ref.shape[3])

    def to_owner(src, dst, i, s_s, s_r):
        r, h = HALVES[i]
        return remote(src.at[i], half_of(dst.at[r], h), s_s.at[i], s_r.at[i], chip_at(c, r), k, n)

    def kept(src, dst, i, j):
        return pltpu.make_async_copy(src.at[i], half_of(dst, HALVES[i][1]), out.at[j])

    def block(r, carry):
        two = pl.ds(2 * r, 2)
        @pl.when(r == 1)
        def _():
            for i in (2, 3): sends[i].wait_recv()
            relays[index[3, 0]].start()
        @pl.when(r == 3)
        def _():
            for cp in relays.values(): cp.wait_recv()
        def both(ref): return ref[two].reshape(slots, ref.shape[2])
        def put(ref, at, v): ref[two, :, at] = v.astype(bf16).reshape(2, half, v.shape[1])
        def chunk(col, w, j):
            @pl.when(r == 0)
            def _():
                for cp in weights(col, w, j): cp.wait()
            tokens = both(xs)
            hg = jnp.dot(tokens, columns(gu, col, w), preferred_element_type=f32)
            hu = jnp.dot(tokens, columns(gu, cols + col, w), preferred_element_type=f32)
            gm = jnp.dot(both(gys), columns(gd, col, w), preferred_element_type=f32)
            for q in range(w // 128):
                gate, up, g = (t[:, 128 * q : 128 * q + 128] for t in (hg, hu, gm))
                sg = 1.0 / (1.0 + jnp.exp(-gate))
                act = gate * sg
                put(mix, pl.ds(col + 128 * q, 128), act * up)
                put(ggu, pl.ds(col + 128 * q, 128), g * up * (sg * (1.0 + gate * (1.0 - sg))))
                put(ggu, pl.ds(cols + col + 128 * q, 128), g * act)
        def pair(j, carry):
            chunk(pl.multiple_of(j * 256, 256), 256, j)
            return carry
        lax.fori_loop(0, cols // 256, pair, 0)
        if cols % 256: chunk(cols // 256 * 256, cols % 256, cols // 256)
        @pl.when(r == 0)
        def _():
            for i in (4, 5): sends[i].start()
        @pl.when(r == 1)
        def _():
            for i in (4, 5): sends[i].wait_recv()
            relays[index[3, 1]].start()
        def back(i, carry):
            at = pl.ds(pl.multiple_of(i * tile, 128), tile)
            put(gx, at, lax.dot_general(both(ggu), some_rows(gu, i), contract_last, preferred_element_type=f32))
            return carry
        lax.fori_loop(0, CHIPS * CORES, back, 0)
        for t in range(CHIPS):
            @pl.when(r == t)
            def _():
                for i in (2 * t, 2 * t + 1):
                    (to_owner(gx, gx_parts, i, rs_s, rs_r) if t else kept(gx, gx_parts.at[0], i, i)).start()
        def down(i, carry):
            at = pl.ds(pl.multiple_of(i * tile, 128), tile)
            put(mo, at, lax.dot_general(both(mix), some_rows(gd, i), contract_last, preferred_element_type=f32))
            return carry
        lax.fori_loop(0, CHIPS * CORES, down, 0)
        for t in range(CHIPS):
            @pl.when(r == t)
            def _():
                for i in (2 * t, 2 * t + 1):
                    (kept(mo, mlp_parts.at[0], i, 2 + i) if t == 0 else kept(mo, mlp_cross, i, i - 2) if t == 3
                     else to_owner(mo, mlp_parts, i, mo_s, mo_r)).start()
        return carry
    lax.fori_loop(0, CHIPS, block, 0)

    pl.semaphore_signal(ready, inc=1, device_id={"wide": c * CORES + 1 - k, "narrow": n}, device_id_type=MESH)
    pl.semaphore_wait(ready, 1)
    sent, came = pl.ds(0, CHIPS), pl.ds(CHIPS, CHIPS)
    pairs = ((gys, mix, gd), (xs, ggu, gu))

    def tiles(total): return [(t * 256, min(256, total - t * 256)) for t in range(-(-total // 256))]

    def to_core(i, col, w, sem):
        ref = pairs[i][2]
        return remote(ref.at[sent, :, :, pl.ds(col, w)], ref.at[came, :, :, pl.ds(col, w)], core_s.at[sem], core_r.at[sem], c, 1 - k, n)

    def to_sums(t): return pltpu.make_async_copy(gu.at[CHIPS + t], sums.at[:, t], done.at[t])

    def each(i, body):
        total, base = pairs[i][2].shape[-1], 0 if i == 0 else len(tiles(cols))
        def step(j, carry):
            body(pl.multiple_of(j * 256, 256), 256, base + j)
            return carry
        lax.fori_loop(0, total // 256, step, 0)
        if total % 256: body(total // 256 * 256, total % 256, base + total // 256)

    def terms(i, kk, use):
        src, right, ref = pairs[i]
        for t in range(CHIPS):
            at = pl.ds(pl.multiple_of((t * CORES + kk) * tile, 128), tile)
            for r in range(CHIPS):
                xt[t * tile : (t + 1) * tile, r * slots : (r + 1) * slots] = src[2 * r : 2 * r + 2, :, at].reshape(slots, tile).T
        def body(col, w, sem):
            b = right[:, :, pl.ds(col, w)].reshape(CHIPS * slots, w)
            use(i, col, w, sem, jnp.dot(xt[...], b, preferred_element_type=f32).reshape(CHIPS, nz, rows, w))
        each(i, body)

    def theirs(i, col, w, sem, v):
        pairs[i][2][sent, :, :, pl.ds(col, w)] = v.astype(bf16)
        to_core(i, col, w, sem).start()

    def ours(i, col, w, sem, v):
        to_core(i, col, w, sem).wait_recv()
        ref = pairs[i][2]
        here = (came, slice(None), slice(None), pl.ds(col, w))
        ref[here] = (ref[here].astype(f32) + v).astype(bf16)

    def hop(way, j):
        return remote(gd.at[came, j], zin.at[way, jnp.clip(j - n - 1 if way == 0 else n - 1 - j, 0, nz - 2)],
                      z_s.at[way, j], z_r.at[way, j], c, k, n + 1 if way == 0 else n - 1)

    def along(t):
        for way in range(2):
            hops = n if way == 0 else nz - 1 - n
            j = jnp.clip(n + nz - 1 - t if way == 0 else t - hops, 0, nz - 1)
            @pl.when((hops > 0) & (t >= hops))
            def _():
                hop(way, j).wait_recv()
                for i in range(CHIPS):
                    add_into(gd.at[CHIPS + i, j], zin.at[way, jnp.clip(j - n if way == 0 else n - j, 0, nz - 2), i])
            @pl.when((t >= hops) & (j != n))
            def _(): hop(way, j).start()

    terms(0, 1 - k, theirs)
    terms(0, k, ours)
    along(0)
    terms(1, 1 - k, theirs)
    along(1)
    terms(1, k, ours)
    for t in range(CHIPS): to_sums(t).start()
    for t in range(2, nz): along(t)
    own_down = pltpu.make_async_copy(gd.at[came, n], down_sums, done.at[CHIPS])
    own_down.start()

    for cp in (*sends.values(), *relays.values()): cp.wait_send()
    for i in range(2):
        kept(gx, gx_parts.at[0], i, i).wait()
        kept(mo, mlp_parts.at[0], i, 2 + i).wait()
        kept(mo, mlp_cross, 6 + i, 4 + i).wait()
    for i in range(2): each(i, lambda col, w, sem: to_core(i, col, w, sem).wait_send())
    for t in range(CHIPS): to_sums(t).wait()
    for j in range(nz):
        for way in range(2):
            @pl.when(n < j if way == 0 else n > j)
            def _(): hop(way, j).wait_send()
    own_down.wait()
    for i in range(2, 6): to_owner(mo, mlp_parts, i, mo_s, mo_r).wait()
    for i in range(2, 8): to_owner(gx, gx_parts, i, rs_s, rs_r).wait()


def mlp_all(nz, x, gy, gu, gd):
    slots, width = x.shape
    rows, cols = gd.shape[2:]
    bf, dma, vm = jnp.bfloat16, pltpu.SemaphoreType.DMA, pltpu.VMEM
    def blocks(w): return jax.ShapeDtypeStruct((CHIPS, slots, w), bf)
    def halves(w): return vm((2 * CHIPS, slots // 2, w), bf)
    tiles = -(-cols // 256)
    flops = 2 * 9 * CHIPS * slots * width * cols
    return pl.pallas_call(
        functools.partial(mlp_kernel, nz),
        out_shape=(blocks(width), jax.ShapeDtypeStruct((3, slots, width), bf), jax.ShapeDtypeStruct((slots, width), bf),
                   jax.ShapeDtypeStruct((CHIPS, rows, cols), bf), jax.ShapeDtypeStruct((nz, CHIPS, rows, 2 * cols), bf)),
        in_specs=[ANY] * 4, out_specs=(ANY,) * 5,
        scratch_shapes=[halves(width), halves(width), vm(gu.shape, bf), vm(gd.shape, bf), halves(cols), halves(2 * cols), halves(width),
                        halves(width), vm((CHIPS * nz * rows, CHIPS * slots), bf), vm((2, nz - 1, CHIPS, rows, cols), bf), dma((10 + 3 * tiles,)), dma((8,)), dma((8,)), dma((8,)), dma((8,)),
                        dma((8,)), dma((8,)), dma((6,)), dma((3 * tiles,)), dma((3 * tiles,)), pltpu.SemaphoreType.REGULAR, dma((CHIPS + 1,)), dma((2, nz)), dma((2, nz))],
        compiler_params=pltpu.CompilerParams(collective_id=1, has_side_effects=True, vmem_limit_bytes=62 << 20),
        cost_estimate=pl.CostEstimate(flops=flops, bytes_accessed=60 << 20, transcendentals=CHIPS * slots * cols),
        name="mlp_all",
    )(x, gy, gu, gd)


PAIR = 2 * HEAD_SIZE
REPEAT = QUERY_HEADS // KEY_VALUE_HEADS
PAIRS = REPEAT // 2


def lane_tables(positions):
    cosine, sine = rope_tables(positions)
    first = jnp.arange(HEAD_SIZE) < HEAD_SIZE // 2
    low, high = jnp.where(first, -sine, 0.0), jnp.where(first, 0.0, sine)
    return jnp.stack([jnp.concatenate([t, t], 1) for t in (cosine, low, high)])


def rotate(u, tables):
    half = HEAD_SIZE // 2
    return u * tables[0] + pltpu.roll(u, PAIR - half, 1) * tables[1] + pltpu.roll(u, half, 1) * tables[2]


def unrotate(g, tables):
    half = HEAD_SIZE // 2
    return g * tables[0] + pltpu.roll(g * tables[2], PAIR - half, 1) + pltpu.roll(g * tables[1], half, 1)


def row_blocks(slots):
    return [(at, min(128, slots - at), at + 128) for at in range(0, slots, 128)]


def causal(s, below, fill):
    clear = s.shape[1] - 128
    last = jnp.where(below, s[:, clear:], fill)
    return jnp.concatenate([s[:, :clear], last], 1) if clear else last


def scaled(x, gain):
    return (x * lax.rsqrt(jnp.mean(x * x, axis=-1, keepdims=True) + norm_eps) * gain).astype(jnp.bfloat16)


def attend_kernel(nz, tok, gain1, gain2, tab_ref, wq_hbm, wo_hbm, gy, gd_own,
                  qr_ref, k_out, v_out, lse_ref, ctx_ref, xn1, hidden, xn2, gys, gd, ks, vs, wq, wo, qkv,
                  load, loc, g_s, g_r, h_s, h_r, f_s, f_r, e_s, e_r):
    g = pl.program_id(0)
    f32, bf16 = jnp.float32, jnp.bfloat16
    slots, width = tok.shape
    c, k, n = at = place()
    mine = [pltpu.make_async_copy(gd_own, gd.at[:, k * nz + n], loc.at[0]), pltpu.make_async_copy(gy, gys.at[0], loc.at[1])]
    line = Line(nz, at, (gd,), f_s, f_r, lambda ref, z: ref.at[:, k * nz + z])
    half = slots // 2
    sends = [remote(gy, gys.at[r], g_s.at[r - 1], g_r.at[r - 1], chip_at(c, r), k, n) for r in (1, 2)]
    relays = [remote(gys.at[1, pl.ds(0, half)], gys.at[3, pl.ds(0, half)], h_s.at[0], h_r.at[0], chip_at(c, 2), k, n),
              remote(gys.at[2, pl.ds(half, half)], gys.at[3, pl.ds(half, half)], h_s.at[1], h_r.at[1], chip_at(c, 1), k, n)]
    def twin(z):
        ref = gd.at[:, k * nz + z]
        return remote(ref, ref, e_s.at[z], e_r.at[z], c, 1 - k, n)
    def load_q(j):
        at = pl.ds(j * 256 if isinstance(j, int) else pl.multiple_of(j * 256, 256), 256)
        return pltpu.make_async_copy(wq_hbm.at[:, at], wq.at[:, at], load.at[j])
    @pl.when(g == 0)
    def _():
        hello([(None, chip_at(c, r), k, n) for r in (1, 2)]
              + [(None, c, 1 - k, n), (n > 0, c, k, n - 1), (n < nz - 1, c, k, n + 1)])
        for cp in mine + sends: cp.start()
        for j in range(wq.shape[1] // 256): load_q(j).start()
        pltpu.make_async_copy(wo_hbm, wo, loc.at[2]).start()
        mine[0].wait()
        for way in range(2): line.start(0, 0, way)
        twin(n).start()
        def norm(i, carry):
            at = pl.ds(pl.multiple_of(i * 16, 16), 16)
            xn1[at, :] = scaled(tok[at, :].astype(f32), gain1[...])
            return carry
        lax.fori_loop(0, slots // 16, norm, 0)
        def project(j, carry):
            load_q(j).wait()
            at = pl.ds(pl.multiple_of(j * 256, 256), 256)
            qkv[:, at] = jnp.dot(xn1[...], wq[:, at], preferred_element_type=f32)
            return carry
        lax.fori_loop(0, wq.shape[1] // 256, project, 0)
    @pl.when(g == 1)
    def _(): line.step(0, 1, lambda z: twin(z).start())
    @pl.when(g == 0)
    def _():
        ks[...] = jnp.zeros_like(ks)
        vs[...] = jnp.zeros_like(vs)
    lane = lax.broadcasted_iota(jnp.int32, (slots, PAIR), 1)
    tables = (tab_ref[0], tab_ref[1], tab_ref[2])
    first = QUERY_HEADS * HEAD_SIZE
    def pair_at(at): return pl.ds(pl.multiple_of(at, PAIR), PAIR)
    key = rotate(qkv[:, pair_at(first + g // 2 * PAIR)], tables)
    val = qkv[:, pair_at(first + KEY_VALUE_HEADS * HEAD_SIZE + g // 2 * PAIR)]
    odd = g % 2 == 1
    for x, own, stack, scale in ((key, k_out, ks, HEAD_SIZE ** -0.5), (val, v_out, vs, 1.0)):
        x = jnp.where(lane < HEAD_SIZE, jnp.where(odd, pltpu.roll(x, HEAD_SIZE, 1), x), 0.0).astype(bf16)
        own[0] = x
        x = x.astype(f32) * scale
        stack[0, 0:slots, :] = x.astype(bf16)
        stack[1, 0:slots, :] = pltpu.roll(x, HEAD_SIZE, 1).astype(bf16)
    for start, size, keys in row_blocks(slots):
        below = lax.broadcasted_iota(jnp.int32, (size, 128), 0) >= lax.broadcasted_iota(jnp.int32, (size, 128), 1)
        lse = jnp.zeros((size, PAIR), f32)
        here = lane[0:size]
        for p in range(PAIRS):
            span = slice(p * PAIR, (p + 1) * PAIR)
            rows = slice(start, start + size)
            q = rotate(qkv[rows, pair_at(g * REPEAT * HEAD_SIZE + p * PAIR)], tuple(t[rows] for t in tables)).astype(bf16)
            qr_ref[rows, span] = q
            ctx = jnp.zeros((size, PAIR), f32)
            for h in range(2):
                s = lax.dot_general(q, ks[h, 0:keys, :], contract_last, preferred_element_type=f32)
                s = causal(s, below, masked_score)
                peak = jnp.max(s, axis=-1, keepdims=True)
                e = jnp.exp(s - peak)
                total = jnp.sum(e, axis=-1, keepdims=True)
                lse = jnp.where(here == 2 * p + h, peak + jnp.log(total), lse)
                probs = (e * (1.0 / total)).astype(bf16)
                ctx = ctx + jnp.dot(probs, vs[h, 0:keys, :], preferred_element_type=f32)
            ctx_ref[rows, pair_at(g * REPEAT * HEAD_SIZE + p * PAIR)] = ctx.astype(bf16)
        lse_ref[0, start : start + size, :] = lse
    @pl.when(g == KEY_VALUE_HEADS - 1)
    def _():
        for cp in sends: cp.wait_recv()
        for cp in relays: cp.start()
        line.step(0, 2, lambda z: twin(z).start())
        pltpu.make_async_copy(wo_hbm, wo, loc.at[2]).wait()
        def project(j, carry):
            at = pl.ds(pl.multiple_of(j * 256, 256), 256)
            hidden[:, at] = tok[:, at].astype(f32) + lax.dot_general(ctx_ref[...], wo[at, :], contract_last, preferred_element_type=f32)
            return carry
        lax.fori_loop(0, width // 256, project, 0)
        def norm(i, carry):
            at = pl.ds(pl.multiple_of(i * 16, 16), 16)
            xn2[at, :] = scaled(hidden[at, :], gain2[...])
            return carry
        lax.fori_loop(0, slots // 16, norm, 0)
        for s in range(3, nz): line.step(0, s, lambda z: twin(z).start())
        for cp in relays: cp.wait()
        for z in range(nz): twin(z).wait()
        for cp in sends: cp.wait_send()
        mine[1].wait()
        line.finish(0)


def attend_all(nz, tokens, gain1, gain2, tables, w_qkv, w_out, gy, gd_own):
    slots, width = tokens.shape
    dma, vm = pltpu.SemaphoreType.DMA, pltpu.VMEM
    bf16, f32 = jnp.bfloat16, jnp.float32
    keys = -(-slots // 128) * 128
    heads = QUERY_HEADS * HEAD_SIZE
    shape = jax.ShapeDtypeStruct
    def fixed(*dims): return pl.BlockSpec(dims, lambda g: (0,) * len(dims))
    per_head = pl.BlockSpec((1, slots, PAIR), lambda g: (g, 0, 0))
    per_head_shape = (KEY_VALUE_HEADS, slots, PAIR)
    return pl.pallas_call(
        functools.partial(attend_kernel, nz),
        grid=(KEY_VALUE_HEADS,),
        out_shape=(shape((slots, heads), bf16), shape(per_head_shape, bf16), shape(per_head_shape, bf16), shape(per_head_shape, f32),
                   shape((slots, heads), bf16), shape((slots, width), bf16), shape((slots, width), f32), shape((slots, width), bf16),
                   shape((CHIPS,) + gy.shape, bf16), shape((CHIPS, CORES * nz) + gd_own.shape[1:], bf16)),
        in_specs=[fixed(slots, width), fixed(1, width), fixed(1, width), fixed(3, slots, PAIR), ANY, ANY, fixed(*gy.shape), fixed(*gd_own.shape)],
        out_specs=(pl.BlockSpec((slots, REPEAT * HEAD_SIZE), lambda g: (0, g)), per_head, per_head, per_head,
                   fixed(slots, heads), fixed(slots, width), fixed(slots, width), fixed(slots, width), ANY, ANY),
        scratch_shapes=[vm((2, keys, PAIR), bf16), vm((2, keys, PAIR), bf16), vm(w_qkv.shape, bf16), vm(w_out.shape, bf16),
                        vm((slots, w_qkv.shape[1]), f32), dma((w_qkv.shape[1] // 256,)), dma((3,)), dma((2,)), dma((2,)), dma((2,)), dma((2,)),
                        dma((1, 2, nz)), dma((1, 2, nz)), dma((nz,)), dma((nz,))],
        compiler_params=pltpu.CompilerParams(collective_id=4, has_side_effects=True, vmem_limit_bytes=56 << 20),
        cost_estimate=pl.CostEstimate(flops=4 * slots * width * heads, bytes_accessed=40 << 20, transcendentals=QUERY_HEADS * slots * slots),
        name="attend",
    )(tokens, gain1, gain2, tables, w_qkv, w_out, gy, gd_own)


def products(left_side, right_side, kk, xt, put):
    part = xt.shape[0] // CHIPS
    for t in range(CHIPS):
        at = pl.ds(pl.multiple_of((t * CORES + kk) * part, 128), part)
        xt[t * part : (t + 1) * part, :] = left_side[:, at].T
    def step(j, carry):
        at = pl.ds(pl.multiple_of(j * 256, 256), 256)
        put(at, jnp.dot(xt[...], right_side[:, at], preferred_element_type=jnp.float32).reshape(CHIPS, part, 256))
        return carry
    lax.fori_loop(0, right_side.shape[1] // 256, step, 0)


def to_their_core(left_side, right_side, k, xt, away, swap):
    def put(at, v): away[:, :, at] = v.astype(jnp.bfloat16)
    products(left_side, right_side, 1 - k, xt, put)
    swap.start()


def with_their_core(left_side, right_side, k, xt, took, swap):
    swap.wait_recv()
    def put(at, v): took[:, :, at] = (took[:, :, at].astype(jnp.float32) + v).astype(jnp.bfloat16)
    products(left_side, right_side, k, xt, put)


def attend_back_kernel(q_ref, k_ref, v_ref, lse_ref, gc_ref, tab_ref, part, gal, ctx, gq_ref, gk_ref, gv_ref, crossed, core_sums,
                       ks, kt, vt, ds, pr, qs, gs, away, took, xt, s_s, s_r, core_s, core_r, done):
    g = pl.program_id(0)
    c, k, n = place()
    copy = remote(part, crossed, s_s, s_r, chip_at(c, 3), k, n)
    swap = remote(away, took, core_s, core_r, c, 1 - k, n)
    store = pltpu.make_async_copy(took, core_sums, done)
    @pl.when(g == 0)
    def _():
        hello([(None, chip_at(c, 3), k, n), (None, c, 1 - k, n)])
        copy.start()
        to_their_core(gal, ctx, k, xt, away, swap)
    @pl.when(g == KEY_VALUE_HEADS - 1)
    def _():
        with_their_core(gal, ctx, k, xt, took, swap)
        store.start()
    f32, bf16 = jnp.float32, jnp.bfloat16
    slots = q_ref.shape[0]
    scale = HEAD_SIZE ** -0.5
    @pl.when(g == 0)
    def _():
        for ref in (ks, kt, vt, ds, pr): ref[...] = jnp.zeros_like(ref)
    lane = lax.broadcasted_iota(jnp.int32, (slots, PAIR), 1)
    tables = (tab_ref[0], tab_ref[1], tab_ref[2])
    key, val = k_ref[0].astype(f32), v_ref[0].astype(f32)
    for stack, x in ((ks, key * scale), (kt, key), (vt, val)):
        stack[0, 0:slots, :] = x.astype(bf16)
        stack[1, 0:slots, :] = pltpu.roll(x, HEAD_SIZE, 1).astype(bf16)
    for at, size, keys in row_blocks(slots):
        rows = slice(at, at + size)
        below = lax.broadcasted_iota(jnp.int32, (size, 128), 0) >= lax.broadcasted_iota(jnp.int32, (size, 128), 1)
        lse = lse_ref[0, rows, :]
        for p in range(PAIRS):
            span = slice(p * PAIR, (p + 1) * PAIR)
            deep = slice(p * slots + at, p * slots + at + size)
            q, gc = q_ref[rows, span], gc_ref[rows, span]
            qs[deep, :] = q
            gs[deep, :] = gc
            gq = jnp.zeros((size, PAIR), f32)
            for h in range(2):
                s = lax.dot_general(q, ks[h, 0:keys, :], contract_last, preferred_element_type=f32)
                e = jnp.exp(s - lse[:, 2 * p + h : 2 * p + h + 1])
                probs = causal(e, below, 0.0)
                pr[h, deep, 0:keys] = probs.astype(bf16)
                gp = lax.dot_general(gc, vt[h, 0:keys, :], contract_last, preferred_element_type=f32)
                inner = jnp.sum(gp * probs, axis=-1, keepdims=True)
                grad = (probs * (gp - inner) * scale).astype(bf16)
                ds[h, deep, 0:keys] = grad
                gq = gq + jnp.dot(grad, kt[h, 0:keys, :], preferred_element_type=f32)
            gq_ref[rows, span] = unrotate(gq, tuple(t[rows] for t in tables)).astype(bf16)
    for src, right, out, turn in ((ds, qs, gk_ref, True), (pr, gs, gv_ref, False)):
        lo, hi = (
            lax.dot_general(src[h], right[...], contract_first, preferred_element_type=f32)[0:slots] for h in range(2)
        )
        x = jnp.where(lane < HEAD_SIZE, lo + pltpu.roll(hi, HEAD_SIZE, 1), 0.0)
        if turn: x = unrotate(x, tables)
        @pl.when(g % 2 == 0)
        def _(): out[...] = x
        @pl.when(g % 2 == 1)
        def _(): out[...] = jnp.where(lane < HEAD_SIZE, out[...], pltpu.roll(x, HEAD_SIZE, 1))
    @pl.when(g == KEY_VALUE_HEADS - 1)
    def _():
        copy.wait()
        swap.wait_send()
        store.wait()


def attend_back_all(q, k, v, lse, grad_context, tables, part, gal, ctx):
    slots, width = gal.shape
    block = (CHIPS, width // (CHIPS * CORES), ctx.shape[1])
    wide = REPEAT * HEAD_SIZE
    bf16, f32, vm = jnp.bfloat16, jnp.float32, pltpu.VMEM
    keys = -(-slots // 128) * 128
    shape = jax.ShapeDtypeStruct
    per_head = pl.BlockSpec((1, slots, PAIR), lambda g: (g, 0, 0))
    wide_spec = pl.BlockSpec((slots, wide), lambda g: (0, g))
    two = pl.BlockSpec((slots, PAIR), lambda g: (0, g // 2))
    return pl.pallas_call(
        attend_back_kernel,
        grid=(KEY_VALUE_HEADS,),
        out_shape=(shape((slots, QUERY_HEADS * HEAD_SIZE), bf16), shape((slots, KEY_VALUE_HEADS * HEAD_SIZE), f32),
                   shape((slots, KEY_VALUE_HEADS * HEAD_SIZE), f32), shape(part.shape, part.dtype), shape(block, bf16)),
        in_specs=[wide_spec, per_head, per_head, per_head, wide_spec, pl.BlockSpec((3, slots, PAIR), lambda g: (0, 0, 0)), ANY,
                  pl.BlockSpec(gal.shape, lambda g: (0, 0)), pl.BlockSpec(ctx.shape, lambda g: (0, 0))],
        out_specs=(wide_spec, two, two, ANY, ANY),
        scratch_shapes=[vm((2, keys, PAIR), bf16)] * 3 + [vm((2, PAIRS * slots, keys), bf16)] * 2 + [vm((PAIRS * slots, PAIR), bf16)] * 2
        + [vm(block, bf16), vm(block, bf16), vm((CHIPS * block[1], slots), bf16)] + [pltpu.SemaphoreType.DMA] * 5,
        compiler_params=pltpu.CompilerParams(collective_id=2, has_side_effects=True, vmem_limit_bytes=48 << 20),
        name="attend_back",
    )(q, k, v, lse, grad_context, tables, part, gal, ctx)


class SumLine:
    def __init__(self, nz, at, piece, slot, send, recv):
        self.nz, self.at, self.piece, self.slot, self.send, self.recv = nz, at, piece, slot, send, recv

    def _hop(self, a, way, j):
        c, k, n = self.at
        i = jnp.clip(j - n - 1 if way == 0 else n - 1 - j, 0, self.nz - 2)
        return remote(self.piece(a, j), self.slot(a, way, i), self.send.at[a, way, j], self.recv.at[a, way, j],
                      c, k, n + 1 if way == 0 else n - 1)

    def step(self, some, t):
        nz, n = self.nz, self.at[2]
        for way in range(2):
            hops = n if way == 0 else nz - 1 - n
            j = jnp.clip(n + nz - 1 - t if way == 0 else t - hops, 0, nz - 1)
            for a in some:
                @pl.when((hops > 0) & (t >= hops))
                def _():
                    self._hop(a, way, j).wait_recv()
                    add_into(self.piece(a, j), self.slot(a, way, jnp.clip(j - n if way == 0 else n - j, 0, nz - 2)))
                @pl.when((t >= hops) & (j != n))
                def _(): self._hop(a, way, j).start()

    def finish(self, a):
        n = self.at[2]
        for j in range(self.nz):
            for way in range(2):
                @pl.when(n < j if way == 0 else n > j)
                def _(): self._hop(a, way, j).wait_send()


def gradient_kernel(nz, sums_hbm, xn_hbm, gq_hbm, wq_hbm, tok_hbm, gh_hbm, gain, gain_mlp, out0, out1, out2, grad_tokens,
                    took0, took1, took2, away1, away2, zbuf0, zbuf1, zbuf2, xn, gq, wq, tok, gh, gx, xt, gain_row,
                    core_s, core_r, half_s, half_r, main_s, main_r, z_s, z_r, load, loc):
    f32, bf16 = jnp.float32, jnp.bfloat16
    items = 3
    outs, took, away, zbuf = (out0, out1, out2), (took0, took1, took2), (None, away1, away2), (zbuf0, zbuf1, zbuf2)
    c, k, n = place()
    left, right = n > 0, n < nz - 1
    cx, cy, cd = (chip_at(c, r) for r in (1, 2, 3))
    loads = [pltpu.make_async_copy(a, b, load.at[i]) for i, (a, b) in enumerate(
        ((sums_hbm, took0), (xn_hbm, xn), (gq_hbm, gq), (wq_hbm, wq), (tok_hbm, tok), (gh_hbm, gh)))]
    for cp in loads: cp.start()
    hello([(None, cc, k, n) for cc in (cx, cy, cd)] + [(None, c, 1 - k, n), (left, c, k, n - 1), (right, c, k, n + 1)])
    slots, width = xn.shape
    rows = out0.shape[0]
    part = nz * rows
    half = part // 2
    top, low = pl.ds(0, half), pl.ds(half, half)
    def arrive(a, at, size): return zbuf[a].at[pl.ds(at, size)]
    swap = [a and remote(away[a], took[a], core_s.at[a - 1], core_r.at[a - 1], c, 1 - k, n) for a in range(items)]
    cross = [[remote(took[a].at[cd, top], arrive(a, 2 * part, half), half_s.at[a, 0], half_r.at[a, 0], cx, k, n),
              remote(took[a].at[cd, low], arrive(a, 2 * part + half, half), half_s.at[a, 1], half_r.at[a, 1], cy, k, n)]
             for a in range(items)]
    main = [[remote(took[a].at[cx, top], arrive(a, 0, half), main_s.at[a, 0], main_r.at[a, 0], cx, k, n),
             remote(took[a].at[cy, low], arrive(a, part + half, half), main_s.at[a, 1], main_r.at[a, 1], cy, k, n),
             remote(took[a].at[cx, low], arrive(a, half, half), main_s.at[a, 2], main_r.at[a, 2], cx, k, n),
             remote(took[a].at[cy, top], arrive(a, part, half), main_s.at[a, 3], main_r.at[a, 3], cy, k, n)]
            for a in range(items)]

    def input_gradient():
        loads[3].wait()
        def step(j, carry):
            at = pl.ds(pl.multiple_of(j * 256, 256), 256)
            gx[:, at] = lax.dot_general(gq[...], wq[at, :], contract_last, preferred_element_type=f32)
            return carry
        lax.fori_loop(0, width // 256, step, 0)

    def input_norm():
        for cp in loads[4:]: cp.wait()
        def step(j, total):
            at = pl.ds(pl.multiple_of(j * 16, 16), 16)
            x, g = tok[at, :].astype(f32), gx[at, :]
            scale = lax.rsqrt(jnp.mean(x * x, axis=-1, keepdims=True) + norm_eps)
            hat = x * scale
            g1 = g * gain[...]
            gh[at, :] = gh[at, :] + scale * (g1 - hat * jnp.mean(g1 * hat, axis=-1, keepdims=True))
            t = g * hat
            return total + t[0:8] + t[8:16]
        total = lax.fori_loop(0, slots // 16, step, jnp.zeros((8, width), f32))
        return jnp.sum(total, axis=0, keepdims=True)

    def gains_swap(of_attn):
        row = lax.broadcasted_iota(jnp.int32, (128, part), 0)
        def columns_of(t, kk):
            at = pl.ds(pl.multiple_of((t * CORES + kk) * part, 128), part)
            return jnp.where(row == 0, gain_row[0:1, at], jnp.where(row == 1, gain_mlp[0:1, at], 0.0)).T
        gain_row[0:1, :] = of_attn
        for t in range(CHIPS): away[2][t] = columns_of(t, 1 - k).astype(bf16)
        swap[2].start()
        swap[2].wait_recv()
        for t in range(CHIPS): took[2][t] = (took[2][t].astype(f32) + columns_of(t, k)).astype(bf16)
        for cp in cross[2]: cp.start()

    def relay(a):
        cross[a][0].wait_recv()
        add_into(took[a].at[cy, top], arrive(a, 2 * part, half))
        main[a][3].start()
        cross[a][1].wait_recv()
        add_into(took[a].at[cx, low], arrive(a, 2 * part + half, half))
        for i in (2, 0, 1): main[a][i].start()

    def mine(a):
        for cp in main[a]: cp.wait_recv()
        add_into(took[a].at[c], arrive(a, 0, part), arrive(a, part, part))

    line = SumLine(nz, (c, k, n), lambda a, j: took[a].at[c, pl.ds(pl.multiple_of(j * rows, rows), rows)],
                   lambda a, way, i: arrive(a, pl.multiple_of(2 * part + 2 * half + (way * (nz - 1) + i) * rows, rows), rows), z_s, z_r)

    loads[0].wait()
    for cp in cross[0]: cp.start()
    for cp in loads[1:3]: cp.wait()
    to_their_core(xn, gq, k, xt, away[1], swap[1])
    relay(0)
    with_their_core(xn, gq, k, xt, took[1], swap[1])
    for cp in cross[1]: cp.start()
    input_gradient()
    gains_swap(input_norm())
    stores = [pltpu.make_async_copy(gh, grad_tokens, loc.at[items])]
    stores[0].start()
    for a in range(1, items): relay(a)
    mine(0)
    for t in range(nz): line.step([0], t)
    stores.append(pltpu.make_async_copy(line.piece(0, n), outs[0], loc.at[0]))
    stores[-1].start()
    for a in range(1, items):
        mine(a)
        stores.append(pltpu.make_async_copy(took[a].at[c], outs[a], loc.at[a]))
        stores[-1].start()
    for cp in stores: cp.wait()
    for a in range(items):
        if a: swap[a].wait_send()
        for cp in cross[a] + main[a]: cp.wait_send()
    line.finish(0)


def gradient_all(nz, sums, xn, gq, wq, tokens, grad_hidden, gain, gain_mlp, cid):
    dma, vm = pltpu.SemaphoreType.DMA, pltpu.VMEM
    bf16, f32 = jnp.bfloat16, jnp.float32
    slots, width = xn.shape
    m = 3
    part = width // (CHIPS * CORES)
    rows = part // nz
    widths = (sums.shape[2], gq.shape[1], 128)
    shape = jax.ShapeDtypeStruct
    blocks = [vm((CHIPS, part, w), bf16) for w in widths]
    row = pl.BlockSpec((1, width), lambda: (0, 0))
    return pl.pallas_call(
        functools.partial(gradient_kernel, nz),
        out_shape=(shape((rows, widths[0]), bf16),) + tuple(shape((part, w), bf16) for w in widths[1:]) + (shape((slots, width), f32),),
        in_specs=[ANY] * 6 + [row, row], out_specs=(ANY,) * (m + 1),
        scratch_shapes=blocks + blocks[1:] + [vm((3 * part + 2 * nz * rows, w), bf16) for w in widths]
        + [vm(xn.shape, bf16), vm(gq.shape, bf16), vm(wq.shape, bf16), vm(tokens.shape, bf16),
           vm((slots, width), f32), vm((slots, width), f32), vm((CHIPS * part, slots), bf16), vm((8, width), f32)]
        + [dma((m - 1,)), dma((m - 1,)), dma((m, 2)), dma((m, 2)), dma((m, 4)), dma((m, 4)), dma((1, 2, nz)), dma((1, 2, nz)), dma((6,)), dma((m + 1,))],
        compiler_params=pltpu.CompilerParams(collective_id=cid, has_side_effects=True, vmem_limit_bytes=62 << 20),
        name="gradient_all",
    )(sums, xn, gq, wq, tokens, grad_hidden, gain, gain_mlp)


def finish_kernel(nz, down, gu, part1, part2, sum_o, parts_hbm, crossed_hbm, hidden_hbm, valid,
                  out_q, out_k, out_v, out_gain, out_d, out_g, out_u, out_o, output,
                  acc1, acc2, in1, in2, ff, wide1, wide2, wide_ff, wide_o, parts, crossed, hidden, result,
                  z_s, z_r, ff_s, ff_r, load, loc):
    f32 = jnp.float32
    c, k, n = place()
    rows, cols = down.shape[1:]
    loads = [pltpu.make_async_copy(a, b, load.at[i]) for i, (a, b) in enumerate(
        ((part1, acc1), (part2, acc2), (parts_hbm, parts), (crossed_hbm, crossed), (hidden_hbm, hidden)))]
    for cp in loads: cp.start()
    hello([(None, chip_at(c, r), k, n) for r in (1, 2, 3)] + [(n > 0, c, k, n - 1), (n < nz - 1, c, k, n + 1)])
    acc, came = (acc1, acc2), (in1, in2)
    line = SumLine(nz, (c, k, n), lambda a, j: acc[a].at[pl.ds(pl.multiple_of(j * rows, rows), rows)],
                   lambda a, way, i: came[a].at[way, i], z_s, z_r)
    def term(m, cc): return down.at[cc] if m == 0 else gu.at[cc, :, pl.ds((m - 1) * cols, cols)]
    home = [[remote(term(m, chip_at(c, r)), ff.at[m, r - 1], ff_s.at[m, r - 1], ff_r.at[m, r - 1], chip_at(c, r), k, n)
             for r in (1, 2, 3)] for m in range(3)]
    for cps in home:
        for cp in cps: cp.start()
    for cp in loads[:2]: cp.wait()
    line.step([0, 1], 0)
    stores = []
    def store(src, dst, i):
        stores.append(pltpu.make_async_copy(src, dst, loc.at[i]))
        stores[-1].start()
    outs = (out_d, out_g, out_u)
    def put(m, r, value):
        wide_ff[m, r] = value.astype(f32)
        at = pl.ds(pl.multiple_of(chip_at(c, r) * cols, 128), cols)
        store(wide_ff.at[m, r], outs[m].at[:, at], 4 + m * CHIPS + r)
    for m in range(3): put(m, 0, term(m, c)[...])
    wide_o[...] = sum_o[...].astype(f32)
    store(wide_o, out_o, 4 + 3 * CHIPS)
    line.step([0, 1], 1)
    for cp in loads[2:]: cp.wait()
    def add(i, carry):
        at = pl.ds(pl.multiple_of(i * 16, 16), 16)
        total = hidden[at, :] + (parts[0, at, :].astype(f32) + parts[1, at, :].astype(f32) + parts[2, at, :].astype(f32)
                                 + crossed[at, :].astype(f32))
        result[at, :] = (valid[at, :] * total).astype(result.dtype)
        return carry
    lax.fori_loop(0, result.shape[0] // 16, add, 0)
    store(result, output, 5 + 3 * CHIPS)
    for t in range(2, nz): line.step([0, 1], t)
    for m in range(3):
        for r in (1, 2, 3):
            home[m][r - 1].wait_recv()
            put(m, r, ff[m, r - 1])
    wide1[...] = line.piece(0, n)[...].astype(f32)
    wide2[...] = line.piece(1, n)[...].astype(f32)
    first = 0
    for i, out in enumerate((out_q, out_k, out_v)):
        store(wide1.at[:, pl.ds(first, out.shape[1])], out, i)
        first += out.shape[1]
    store(wide2, out_gain, 3)
    for cp in stores: cp.wait()
    for cps in home:
        for cp in cps: cp.wait_send()
    for a in range(2): line.finish(a)


def finish_all(nz, down, gu, part1, part2, sum_o, parts, crossed, hidden, valid, key_width, cid):
    dma, vm = pltpu.SemaphoreType.DMA, pltpu.VMEM
    bf16, f32 = jnp.bfloat16, jnp.float32
    rows, cols = down.shape[1:]
    w1, w2 = part1.shape[1], part2.shape[1]
    def out(w): return jax.ShapeDtypeStruct((rows, w), f32)
    return pl.pallas_call(
        functools.partial(finish_kernel, nz),
        out_shape=(out(w1 - 2 * key_width), out(key_width), out(key_width), out(w2)) + (out(CHIPS * cols),) * 3
        + (out(sum_o.shape[1]), jax.ShapeDtypeStruct(hidden.shape, bf16)),
        in_specs=[VMEM, VMEM, ANY, ANY, VMEM, ANY, ANY, ANY, VMEM], out_specs=(ANY,) * 9,
        scratch_shapes=[vm(part1.shape, bf16), vm(part2.shape, bf16), vm((2, nz - 1, rows, w1), bf16), vm((2, nz - 1, rows, w2), bf16),
                        vm((3, CHIPS - 1, rows, cols), bf16), vm((rows, w1), f32), vm((rows, w2), f32), vm((3, CHIPS, rows, cols), f32),
                        vm(sum_o.shape, f32), vm(parts.shape, bf16), vm(crossed.shape, bf16), vm(hidden.shape, f32), vm(hidden.shape, bf16),
                        dma((2, 2, nz)), dma((2, 2, nz)), dma((3, 3)), dma((3, 3)), dma((5,)), dma((6 + 3 * CHIPS,))],
        compiler_params=pltpu.CompilerParams(collective_id=cid, has_side_effects=True, vmem_limit_bytes=40 << 20),
        name="finish_all",
    )(down, gu, part1, part2, sum_o, parts, crossed, hidden, valid)


def fits(mesh):
    return mesh.shape["wide"] == CHIPS * CORES


def fast_device(
    nz,
    tokens,
    cotangent,
    lengths,
    positions,
    norm_attn,
    w_query,
    w_key,
    w_value,
    w_output,
    norm_mlp,
    w_gate,
    w_up,
    w_down,
):
    f32, bf16 = jnp.float32, jnp.bfloat16
    c, k, n = place()
    slots, width = tokens.shape
    rows = w_query.shape[0]
    query_width, key_width = w_query.shape[1], w_key.shape[1]
    cols = w_gate.shape[1] // CHIPS
    valid_rows = (jnp.arange(slots) < lengths[0]).astype(f32)[:, None]
    tables = lane_tables(positions)
    grad_y = cotangent.astype(f32) * valid_rows
    grad_y_low = grad_y.astype(bf16)
    lanes = jnp.arange(128)[None]
    gains = jnp.where(lanes == 0, norm_attn[:, None], jnp.where(lanes == 1, norm_mlp[:, None], jnp.zeros((), bf16)))
    w_qkv, w_out, gain_cols, ff_gate_up, ff_down = gather_all(
        nz, w_query, w_key, w_value, w_output, gains, w_gate, w_up, w_down
    )
    gain_rows = lax.dot_general(jnp.eye(8, 128, dtype=bf16), gain_cols, contract_last, preferred_element_type=f32)
    gain_attn, gain_mlp = gain_rows[0], gain_rows[1]

    query_rotated, key_rotated, value_reduced, log_totals, context, scaled_attn, hidden, scaled_mlp, gy_all, ff_down = attend_all(
        nz, tokens, gain_attn[None], gain_mlp[None], tables, w_qkv, w_out, grad_y_low, ff_down
    )
    ff_gate_up, ff_down = (w.reshape(CHIPS * CORES, nz, rows, w.shape[-1]) for w in (ff_gate_up, ff_down))
    normed_mlp = normalize(hidden)
    grad_x_parts, mlp_parts, mlp_cross, down_sums, ff_sums = mlp_all(nz, scaled_mlp, gy_all, ff_gate_up, ff_down)
    grad_xn2 = jnp.sum(grad_x_parts.astype(f32), axis=0)
    grad_gain_mlp = jnp.sum(grad_xn2 * normed_mlp, axis=0)
    grad_hidden = grad_y + norm_back(grad_xn2 * gain_mlp, normed_mlp, hidden)
    grad_attn_low = grad_hidden.astype(bf16)
    grad_context = jnp.dot(grad_attn_low, w_out, preferred_element_type=f32).astype(bf16)
    grad_query, grad_key, grad_value, mlp_crossed, out_sums = attend_back_all(
        query_rotated, key_rotated, value_reduced, log_totals, grad_context, tables, mlp_cross, grad_attn_low, context
    )
    grad_qkv = jnp.concatenate([grad_query, grad_key.astype(bf16), grad_value.astype(bf16)], 1)
    ff_sums = lax.psum_scatter(ff_sums, "narrow", scatter_dimension=0, tiled=True)
    out_part, qkv_part, gain_part, grad_tokens = gradient_all(
        nz, out_sums, scaled_attn, grad_qkv, w_qkv, tokens, grad_hidden, gain_attn[None], grad_gain_mlp[None], 3
    )
    grad_w_query, grad_w_key, grad_w_value, gain_sums, grad_w_down, grad_w_gate, grad_w_up, grad_w_output, output = finish_all(
        nz,
        down_sums,
        ff_sums.reshape(CHIPS, rows, 2 * cols),
        qkv_part,
        gain_part,
        out_part,
        mlp_parts,
        mlp_crossed,
        hidden,
        valid_rows,
        key_width,
        5,
    )
    grad_norm_attn, grad_norm_mlp = gain_sums[:, 0], gain_sums[:, 1]
    return (
        output,
        grad_tokens,
        grad_norm_attn,
        grad_w_query,
        grad_w_key,
        grad_w_value,
        grad_w_output,
        grad_norm_mlp,
        grad_w_gate,
        grad_w_up,
        grad_w_down,
    )


def solution(mesh):
    in_specs = (
        P(("wide", "narrow"), None),
        P(("wide", "narrow"), None),
        P(("wide", "narrow")),
        P(("wide", "narrow")),
        P(("wide", "narrow")),
        P(("wide", "narrow"), None),
        P(("wide", "narrow"), None),
        P(("wide", "narrow"), None),
        P(("wide", "narrow"), None),
        P(("wide", "narrow")),
        P(("wide", "narrow"), None),
        P(("wide", "narrow"), None),
        P(("wide", "narrow"), None),
    )
    out_specs = (
        P(("wide", "narrow"), None),
        P(("wide", "narrow"), None),
        P(("wide", "narrow")),
        P(("wide", "narrow"), None),
        P(("wide", "narrow"), None),
        P(("wide", "narrow"), None),
        P(("wide", "narrow"), None),
        P(("wide", "narrow")),
        P(("wide", "narrow"), None),
        P(("wide", "narrow"), None),
        P(("wide", "narrow"), None),
    )
    body = functools.partial(fast_device, mesh.shape["narrow"]) if fits(mesh) else per_device
    return jax.shard_map(
        body, mesh=mesh, in_specs=in_specs, out_specs=out_specs, check_vma=False
    )
```

```python
import functools
import math

import jax
import jax.numpy as jnp
from jax import lax
from jax.experimental import pallas as pl
from jax.experimental.pallas import tpu as pltpu
from jax.sharding import PartitionSpec as P

QUERY_HEADS = 32
KEY_VALUE_HEADS = 4
HEAD_SIZE = 64


norm_eps = 1e-05
rope_base = 10000.0
masked_score = -1e30
contract_last = (((1,), (1,)), ((), ()))
contract_first = (((0,), (0,)), ((), ()))


def rope_tables(positions):
    half_dim = HEAD_SIZE // 2
    inv_freq = jnp.exp(
        -math.log(rope_base) * jnp.arange(half_dim, dtype=jnp.float32) * 2.0 / HEAD_SIZE
    )
    angles = positions.astype(jnp.float32)[..., None] * inv_freq
    cosine = jnp.cos(angles)
    sine_part = jnp.sin(angles)
    return (jnp.concatenate([cosine, cosine], -1), jnp.concatenate([sine_part, sine_part], -1))


def apply_rotary(values, cosine_table, sine_table):
    half_dim = values.shape[-1] // 2
    turned = jnp.concatenate([-values[..., half_dim:], values[..., :half_dim]], -1)
    return values * cosine_table[..., None, :] + turned * sine_table[..., None, :]


def invert_rotary(grad_rows, cosine_table, sine_table):
    half_dim = grad_rows.shape[-1] // 2
    with_cos = grad_rows * cosine_table[..., None, :]
    with_sin = grad_rows * sine_table[..., None, :]
    return with_cos + jnp.concatenate([with_sin[..., half_dim:], -with_sin[..., :half_dim]], -1)


def normalize(values):
    return values * lax.rsqrt(jnp.mean(values * values, axis=-1, keepdims=True) + norm_eps)


def norm_back(grad_hat, normed, values):
    row_scale = lax.rsqrt(jnp.mean(values * values, axis=-1, keepdims=True) + norm_eps)
    return row_scale * (grad_hat - normed * jnp.mean(grad_hat * normed, axis=-1, keepdims=True))


def attention_inputs(normed, norm_attn, w_query, w_key, w_value):
    gain_piece = lax.all_gather(norm_attn, ("wide", "narrow"), axis=0, tiled=True)
    query_rows = lax.all_gather(w_query, ("wide", "narrow"), axis=0, tiled=True)
    key_rows = lax.all_gather(w_key, ("wide", "narrow"), axis=0, tiled=True)
    value_rows = lax.all_gather(w_value, ("wide", "narrow"), axis=0, tiled=True)
    gain_float = gain_piece.astype(jnp.float32)
    columns = (normed * gain_float).astype(jnp.bfloat16)
    query_sum = jnp.dot(columns, query_rows, preferred_element_type=jnp.float32)
    key_sum = jnp.dot(columns, key_rows, preferred_element_type=jnp.float32)
    value_sum = jnp.dot(columns, value_rows, preferred_element_type=jnp.float32)
    return (gain_float, columns, query_sum, key_sum, value_sum)


def mlp_inputs(normed, norm_mlp, w_gate, w_up):
    gain_piece = lax.all_gather(norm_mlp, ("wide", "narrow"), axis=0, tiled=True)
    gate_rows = lax.all_gather(w_gate, ("wide", "narrow"), axis=0, tiled=True)
    up_rows = lax.all_gather(w_up, ("wide", "narrow"), axis=0, tiled=True)
    gain_float = gain_piece.astype(jnp.float32)
    columns = (normed * gain_float).astype(jnp.bfloat16)
    gate_sum = jnp.dot(columns, gate_rows, preferred_element_type=jnp.float32)
    up_sum = jnp.dot(columns, up_rows, preferred_element_type=jnp.float32)
    return (gain_float, columns, gate_sum, up_sum)


def head_slices(query_rotated, key_rotated, value_reduced, shared_key_head):
    row_total_count = query_rotated.shape[0]
    heads_per_group = QUERY_HEADS // KEY_VALUE_HEADS
    query_head = query_rotated[
        :,
        shared_key_head
        * heads_per_group
        * HEAD_SIZE : (shared_key_head + 1)
        * heads_per_group
        * HEAD_SIZE,
    ].reshape(row_total_count, heads_per_group, HEAD_SIZE)
    key_head = key_rotated[:, shared_key_head * HEAD_SIZE : (shared_key_head + 1) * HEAD_SIZE]
    value_head = value_reduced[:, shared_key_head * HEAD_SIZE : (shared_key_head + 1) * HEAD_SIZE]
    return (query_head, key_head, value_head)


def head_scores(query_head, key_head):
    row_total_count = query_head.shape[0]
    causal = jnp.arange(row_total_count)[:, None] >= jnp.arange(row_total_count)[None, :]
    raw_scores = jnp.einsum("qrd,kd->rqk", query_head, key_head, preferred_element_type=jnp.float32)
    return jnp.where(causal, raw_scores * HEAD_SIZE ** (-0.5), masked_score)


def attend(query_rotated, key_rotated, value_reduced):
    row_total_count = query_rotated.shape[0]
    heads_per_group = QUERY_HEADS // KEY_VALUE_HEADS
    contexts = []
    log_totals = []
    for shared_key_head in range(KEY_VALUE_HEADS):
        query_head, key_head, value_head = head_slices(
            query_rotated, key_rotated, value_reduced, shared_key_head
        )
        scores = head_scores(query_head, key_head)
        row_peak = jnp.max(scores, axis=-1, keepdims=True)
        exp_scores = jnp.exp(scores - row_peak)
        row_total = jnp.sum(exp_scores, axis=-1, keepdims=True)
        probs = exp_scores / row_total
        context_head = jnp.einsum(
            "rqk,kd->qrd",
            probs.astype(jnp.bfloat16),
            value_head,
            preferred_element_type=jnp.float32,
        )
        contexts.append(context_head.reshape(row_total_count, heads_per_group * HEAD_SIZE))
        log_totals.append(row_peak + jnp.log(row_total))
    return (jnp.concatenate(contexts, 1).astype(jnp.bfloat16), log_totals)


def attend_back(query_rotated, key_rotated, value_reduced, log_totals, grad_context):
    row_total_count = query_rotated.shape[0]
    heads_per_group = QUERY_HEADS // KEY_VALUE_HEADS
    score_scale = HEAD_SIZE ** (-0.5)
    query_grads = []
    key_grads = []
    value_grads = []
    for shared_key_head in range(KEY_VALUE_HEADS):
        query_head, key_head, value_head = head_slices(
            query_rotated, key_rotated, value_reduced, shared_key_head
        )
        scores = head_scores(query_head, key_head)
        probs = jnp.exp(scores - log_totals[shared_key_head])
        probs_low = probs.astype(jnp.bfloat16)
        grad_head = grad_context[
            :,
            shared_key_head
            * heads_per_group
            * HEAD_SIZE : (shared_key_head + 1)
            * heads_per_group
            * HEAD_SIZE,
        ].reshape(row_total_count, heads_per_group, HEAD_SIZE)
        grad_probs = jnp.einsum(
            "qrd,kd->rqk", grad_head, value_head, preferred_element_type=jnp.float32
        )
        value_grads.append(
            jnp.einsum("rqk,qrd->kd", probs_low, grad_head, preferred_element_type=jnp.float32)
        )
        inner_sum = jnp.sum(grad_probs * probs, axis=-1, keepdims=True)
        grad_scores = (probs * (grad_probs - inner_sum) * score_scale).astype(jnp.bfloat16)
        query_grad = jnp.einsum(
            "rqk,kd->qrd", grad_scores, key_head, preferred_element_type=jnp.float32
        )
        query_grads.append(query_grad.reshape(row_total_count, heads_per_group * HEAD_SIZE))
        key_grads.append(
            jnp.einsum("rqk,qrd->kd", grad_scores, query_head, preferred_element_type=jnp.float32)
        )
    return (
        jnp.concatenate(query_grads, 1),
        jnp.concatenate(key_grads, 1),
        jnp.concatenate(value_grads, 1),
    )


def make_term(width_sides, other_sides):
    down_side, mlp_side, attn_side, qkv_side = width_sides
    mixed_rows, gate_rows, up_rows, context_rows, query_rows, key_rows, value_rows = other_sides

    def grad_term(first_row, row_span):
        pieces = [
            lax.dot_general(
                down_side, mixed_rows, contract_first, preferred_element_type=jnp.float32
            ),
            lax.dot_general(
                mlp_side, gate_rows, contract_first, preferred_element_type=jnp.float32
            ),
            lax.dot_general(mlp_side, up_rows, contract_first, preferred_element_type=jnp.float32),
            lax.dot_general(
                attn_side, context_rows, contract_first, preferred_element_type=jnp.float32
            ),
            lax.dot_general(
                qkv_side, query_rows, contract_first, preferred_element_type=jnp.float32
            ),
            lax.dot_general(qkv_side, key_rows, contract_first, preferred_element_type=jnp.float32),
            lax.dot_general(
                qkv_side, value_rows, contract_first, preferred_element_type=jnp.float32
            ),
        ]
        return jnp.concatenate(pieces, 1)

    return grad_term


def per_device(
    tokens,
    cotangent,
    lengths,
    positions,
    norm_attn,
    w_query,
    w_key,
    w_value,
    w_output,
    norm_mlp,
    w_gate,
    w_up,
    w_down,
):
    row_total_count = tokens.shape[0]
    shard_rows = w_query.shape[0]
    query_width = w_query.shape[1]
    key_width = w_key.shape[1]
    hidden_width = w_gate.shape[1]
    inputs = tokens.astype(jnp.float32)
    valid_rows = (jnp.arange(row_total_count) < lengths[0]).astype(jnp.float32)[:, None]
    cosine_table, sine_table = rope_tables(positions)
    normed_attn = normalize(inputs)
    gain_attn_full, scaled_attn, query_pre, key_unrotated, value_pre = attention_inputs(
        normed_attn, norm_attn, w_query, w_key, w_value
    )
    query_rotated = (
        apply_rotary(
            query_pre.reshape(row_total_count, QUERY_HEADS, HEAD_SIZE), cosine_table, sine_table
        )
        .reshape(row_total_count, query_width)
        .astype(jnp.bfloat16)
    )
    key_rotated = (
        apply_rotary(
            key_unrotated.reshape(row_total_count, KEY_VALUE_HEADS, HEAD_SIZE),
            cosine_table,
            sine_table,
        )
        .reshape(row_total_count, key_width)
        .astype(jnp.bfloat16)
    )
    value_reduced = value_pre.astype(jnp.bfloat16)
    context, log_totals = attend(query_rotated, key_rotated, value_reduced)
    attn_out = lax.dot_general(
        context,
        lax.all_gather(w_output, ("wide", "narrow"), axis=0, tiled=True),
        contract_last,
        preferred_element_type=jnp.float32,
    )
    hidden = inputs + attn_out
    normed_mlp = normalize(hidden)
    gain_mlp_full, scaled_mlp, gate_proj, up_proj = mlp_inputs(normed_mlp, norm_mlp, w_gate, w_up)
    mixed_low = (gate_proj * jax.nn.sigmoid(gate_proj) * up_proj).astype(jnp.bfloat16)
    mlp_out = lax.dot_general(
        mixed_low,
        lax.all_gather(w_down, ("wide", "narrow"), axis=0, tiled=True),
        contract_last,
        preferred_element_type=jnp.float32,
    )
    output = (valid_rows * (hidden + mlp_out)).astype(jnp.bfloat16)
    grad_y = cotangent.astype(jnp.float32) * valid_rows
    grad_y_low = grad_y.astype(jnp.bfloat16)
    grad_cols = grad_y_low
    grad_mixed = jnp.dot(
        grad_cols,
        lax.all_gather(w_down, ("wide", "narrow"), axis=0, tiled=True),
        preferred_element_type=jnp.float32,
    )
    again_values = mlp_inputs(normed_mlp, norm_mlp, w_gate, w_up)
    gate_proj = again_values[2]
    up_proj = again_values[3]
    sigmoid_gate = jax.nn.sigmoid(gate_proj)
    grad_gate = (
        grad_mixed * up_proj * (sigmoid_gate * (1.0 + gate_proj * (1.0 - sigmoid_gate)))
    ).astype(jnp.bfloat16)
    grad_up = (grad_mixed * (gate_proj * sigmoid_gate)).astype(jnp.bfloat16)
    gate_rows = lax.all_gather(w_gate, ("wide", "narrow"), axis=0, tiled=True)
    up_rows = lax.all_gather(w_up, ("wide", "narrow"), axis=0, tiled=True)
    columns = lax.dot_general(
        grad_gate, gate_rows, contract_last, preferred_element_type=jnp.float32
    )
    columns = columns + lax.dot_general(
        grad_up, up_rows, contract_last, preferred_element_type=jnp.float32
    )
    grad_xn2 = columns
    grad_gain_mlp = jnp.sum(grad_xn2 * normed_mlp, axis=0)
    grad_hidden = grad_y + norm_back(grad_xn2 * gain_mlp_full, normed_mlp, hidden)
    grad_attn_low = grad_hidden.astype(jnp.bfloat16)
    grad_cols = grad_attn_low
    grad_context = jnp.dot(
        grad_cols,
        lax.all_gather(w_output, ("wide", "narrow"), axis=0, tiled=True),
        preferred_element_type=jnp.float32,
    )
    grad_context = grad_context.astype(jnp.bfloat16)
    grad_query_rot, gradient_key_rotated, grad_value_sum = attend_back(
        query_rotated, key_rotated, value_reduced, log_totals, grad_context
    )
    grad_query = (
        invert_rotary(
            grad_query_rot.reshape(row_total_count, QUERY_HEADS, HEAD_SIZE),
            cosine_table,
            sine_table,
        )
        .reshape(row_total_count, query_width)
        .astype(jnp.bfloat16)
    )
    grad_key = (
        invert_rotary(
            gradient_key_rotated.reshape(row_total_count, KEY_VALUE_HEADS, HEAD_SIZE),
            cosine_table,
            sine_table,
        )
        .reshape(row_total_count, key_width)
        .astype(jnp.bfloat16)
    )
    grad_value = grad_value_sum.astype(jnp.bfloat16)
    query_rows = lax.all_gather(w_query, ("wide", "narrow"), axis=0, tiled=True)
    key_rows = lax.all_gather(w_key, ("wide", "narrow"), axis=0, tiled=True)
    value_rows = lax.all_gather(w_value, ("wide", "narrow"), axis=0, tiled=True)
    columns = lax.dot_general(
        grad_query, query_rows, contract_last, preferred_element_type=jnp.float32
    )
    columns = columns + lax.dot_general(
        grad_key, key_rows, contract_last, preferred_element_type=jnp.float32
    )
    columns = columns + lax.dot_general(
        grad_value, value_rows, contract_last, preferred_element_type=jnp.float32
    )
    local_term = make_term(
        (grad_y_low, scaled_mlp, grad_attn_low, scaled_attn),
        (mixed_low, grad_gate, grad_up, context, grad_query, grad_key, grad_value),
    )
    all_sums = lax.psum_scatter(
        local_term(jnp.int32(0), lax.axis_size(("wide", "narrow")) * shard_rows),
        ("wide", "narrow"),
        scatter_dimension=0,
        tiled=True,
    )
    edges = [0]
    for width in (
        hidden_width,
        hidden_width,
        hidden_width,
        query_width,
        query_width,
        key_width,
        key_width,
    ):
        edges.append(edges[-1] + width)
    grad_w_down = all_sums[:, edges[0] : edges[1]]
    grad_w_gate = all_sums[:, edges[1] : edges[2]]
    grad_w_up = all_sums[:, edges[2] : edges[3]]
    grad_w_output = all_sums[:, edges[3] : edges[4]]
    grad_w_query = all_sums[:, edges[4] : edges[5]]
    grad_w_key = all_sums[:, edges[5] : edges[6]]
    grad_w_value = all_sums[:, edges[6] : edges[7]]
    grad_gain_attn = jnp.sum(columns * normed_attn, axis=0)
    grad_tokens = grad_hidden + norm_back(columns * gain_attn_full, normed_attn, inputs)
    grad_norm_attn, grad_norm_mlp = (
        lax.psum_scatter(grad_gain_attn, ("wide", "narrow"), scatter_dimension=0, tiled=True),
        lax.psum_scatter(grad_gain_mlp, ("wide", "narrow"), scatter_dimension=0, tiled=True),
    )
    return (
        output,
        grad_tokens,
        grad_norm_attn,
        grad_w_query,
        grad_w_key,
        grad_w_value,
        grad_w_output,
        grad_norm_mlp,
        grad_w_gate,
        grad_w_up,
        grad_w_down,
    )


MESH = pl.DeviceIdType.MESH
ANY = pl.BlockSpec(memory_space=pl.ANY)
VMEM = pl.BlockSpec(memory_space=pltpu.VMEM)

CHIPS, CORES = 4, 2

def place():
    w = lax.axis_index("wide"); n = lax.axis_index("narrow")
    return w // CORES, w % CORES, n

def chip_at(c, r):
    xb, yb, rx, ry = c % 2, c // 2, r % 2, r // 2
    return (yb + ry - 2 * yb * ry) * 2 + (xb + rx - 2 * xb * rx)


def remote(src, dst, send, recv, chip, core, z):
    return pltpu.make_async_remote_copy(src_ref=src, dst_ref=dst, send_sem=send, recv_sem=recv,
        device_id={"wide": chip * CORES + core, "narrow": z}, device_id_type=MESH)

def hello(partners):
    barrier = pltpu.get_barrier_semaphore()
    count = 0
    for cond, chip, core, z in partners:
        def sig(chip=chip, core=core, z=z):
            pl.semaphore_signal(barrier, inc=1, device_id={"wide": chip * CORES + core, "narrow": z}, device_id_type=MESH)
        if cond is None:
            sig(); count = count + 1
        else:
            pl.when(cond)(sig); count = count + jnp.where(cond, 1, 0)
    pl.semaphore_wait(barrier, count)

class Line:
    def __init__(self, nz, at, refs, send, recv, place_of):
        self.nz, self.at, self.refs, self.send, self.recv, self.place_of = nz, at, refs, send, recv, place_of

    def _copy(self, a, way, s, origin):
        c, k, n = self.at
        ref = self.place_of(self.refs[a], origin)
        return remote(ref, ref, self.send.at[a, way, s], self.recv.at[a, way, s], c, k, n + 1 if way == 0 else n - 1)

    def _origin(self, way, s):
        n = self.at[2]
        o = n - s if way == 0 else n + s
        return (n >= s) if way == 0 else (n + s <= self.nz - 1), jnp.clip(o, 0, self.nz - 1)

    def _sends(self, way, s):
        n = self.at[2]
        return self._origin(way, s)[0] & ((n < self.nz - 1) if way == 0 else (n > 0))

    def start(self, a, s, way):
        @pl.when(self._sends(way, s))
        def _(): self._copy(a, way, s, self._origin(way, s)[1]).start()

    def step(self, a, s, then=None):
        for way in range(2):
            came, origin = self._origin(way, s)
            @pl.when(came)
            def _(): self._copy(a, way, s - 1, origin).wait_recv()
            if s < self.nz - 1: self.start(a, s, way)
            if then is not None:
                @pl.when(came)
                def _(): then(origin)

    def finish(self, a):
        for s in range(self.nz - 1):
            for way in range(2):
                @pl.when(self._sends(way, s))
                def _(): self._copy(a, way, s, self._origin(way, s)[1]).wait_send()


def gather_kernel(nz, wq, wk, wv, wo, gains, wg, wu, wd, qkv, out, gain, gu, gd,
                  loc, sw_s, sw_r, z_s, z_r, f_s, f_r, p_s, p_r, h_s, h_r, d_s, d_r, e_s, e_r):
    c, k, n = at = place()
    rows, q = wq.shape
    kv = wk.shape[1]
    cols = gd.shape[-1]
    part = nz * rows
    half = part // 2
    kn = k * nz + n
    cx, cy, cd = (chip_at(c, r) for r in (1, 2, 3))
    hello([(None, cc, k, n) for cc in (cx, cy, cd)] + [(None, c, 1 - k, n), (n > 0, c, k, n - 1), (n < nz - 1, c, k, n + 1)])

    def mycols(w, cc): return w.at[:, pl.ds(pl.multiple_of(cc * cols, 128), cols)]
    def landing(i, cc): return gd.at[cc] if i == 2 else gu.at[cc, kn, :, pl.ds(i * cols, cols)]
    whole = (qkv, out, gain)
    def block(ref, z): return ref.at[pl.ds(pl.multiple_of(((c * CORES + k) * nz + z) * rows, rows), rows)]
    own = [pltpu.make_async_copy(wq, block(qkv, n).at[:, pl.ds(0, q)], loc.at[0]),
           pltpu.make_async_copy(wk, block(qkv, n).at[:, pl.ds(q, kv)], loc.at[1]),
           pltpu.make_async_copy(wv, block(qkv, n).at[:, pl.ds(q + kv, kv)], loc.at[2]),
           pltpu.make_async_copy(wo, block(out, n), loc.at[3]), pltpu.make_async_copy(gains, block(gain, n), loc.at[4])]
    ownff = [pltpu.make_async_copy(mycols(w, c), landing(i, c), loc.at[5 + i]) for i, w in enumerate((wg, wu, wd))]
    for cp in own + ownff: cp.start()
    swap = [[remote(mycols(w, cc), landing(i, c), sw_s.at[i, r], sw_r.at[i, r], cc, k, n) for r, cc in enumerate((cx, cy, cd))]
            for i, w in enumerate((wg, wu, wd))]
    for i in range(3):
        for cp in swap[i]: cp.start()
    for cp in own: cp.wait()

    line = Line(nz, at, whole, z_s, z_r, block)
    for a in range(3):
        for way in range(2): line.start(a, 0, way)

    def span(ref, cc, first, size):
        return ref.at[pl.ds(pl.multiple_of((cc * CORES + k) * part, part) + first, size)]
    plane = [[remote(span(ref, c, 0, part), span(ref, c, 0, part), p_s.at[a, r], p_r.at[a, r], cc, k, n) for r, cc in enumerate((cx, cy))]
             for a, ref in enumerate(whole)]
    across = [[remote(span(ref, cx, 0, half), span(ref, cx, 0, half), h_s.at[a, 0], h_r.at[a, 0], cy, k, n),
               remote(span(ref, cy, half, half), span(ref, cy, half, half), h_s.at[a, 1], h_r.at[a, 1], cx, k, n)]
              for a, ref in enumerate(whole)]
    cores = [[remote(span(ref, cc, 0, part), span(ref, cc, 0, part), d_s.at[a, r], d_r.at[a, r], c, 1 - k, n)
              for r, cc in enumerate((c, cx, cy, cd))] for a, ref in enumerate(whole)]

    def plane_start(a):
        for cp in plane[a] + cores[a][:1]: cp.start()
    def plane_next(a):
        for i in range(2):
            plane[a][i].wait_recv()
            across[a][i].start()
            cores[a][1 + i].start()
    def plane_last(a):
        for cp in across[a]: cp.wait_recv()
        cores[a][3].start()

    for s in range(1, nz):
        for a in range(3):
            line.step(a, s)
            if s == nz - 1: plane_start(a)

    ff = Line(nz, at, (gu,), f_s, f_r, lambda ref, z: ref.at[:, k * nz + z])
    def twin(z):
        ref = gu.at[:, k * nz + z]
        return remote(ref, ref, e_s.at[z], e_r.at[z], c, 1 - k, n)
    for i in range(2):
        ownff[i].wait()
        for cp in swap[i]: cp.wait_recv()
    for way in range(2): ff.start(0, 0, way)
    twin(n).start()
    plane_next(0)
    ff.step(0, 1, lambda z: twin(z).start())
    for a in (1, 2): plane_next(a)
    ff.step(0, 2, lambda z: twin(z).start())
    for a in range(3): plane_last(a)
    ownff[2].wait()
    for cp in swap[2]: cp.wait_recv()
    for s in range(3, nz): ff.step(0, s, lambda z: twin(z).start())
    for a in range(3):
        for cp in cores[a]: cp.wait_recv()
    for z in range(nz): twin(z).wait()
    for i in range(3):
        for cp in swap[i]: cp.wait_send()
    for a in range(3):
        line.finish(a)
        for cp in plane[a] + across[a] + cores[a]: cp.wait_send()
    ff.finish(0)


def gather_all(nz, wq, wk, wv, wo, gains, wg, wu, wd):
    rows = wq.shape[0]
    width = rows * CHIPS * CORES * nz
    cols = wg.shape[1] // CHIPS
    bf = jnp.bfloat16
    shape = jax.ShapeDtypeStruct
    dma = pltpu.SemaphoreType.DMA
    return pl.pallas_call(
        functools.partial(gather_kernel, nz),
        out_shape=(shape((width, wq.shape[1] + 2 * wk.shape[1]), bf), shape((width, wo.shape[1]), bf), shape((width, gains.shape[1]), bf),
                   shape((CHIPS, CORES * nz, rows, 2 * cols), bf), shape((CHIPS, rows, cols), bf)),
        in_specs=[VMEM] * 8, out_specs=(ANY,) * 5,
        scratch_shapes=[dma((8,)), dma((3, 3)), dma((3, 3)), dma((3, 2, nz)), dma((3, 2, nz)), dma((1, 2, nz)), dma((1, 2, nz)),
                        dma((3, 2)), dma((3, 2)), dma((3, 2)), dma((3, 2)), dma((3, 4)), dma((3, 4)), dma((nz,)), dma((nz,))],
        compiler_params=pltpu.CompilerParams(collective_id=0, has_side_effects=True),
        name="gather_all",
    )(wq, wk, wv, wo, gains, wg, wu, wd)


def add_into(dst, *srcs):
    rows = dst.shape[0]
    step = 16
    def body(i, carry):
        at = pl.ds(pl.multiple_of(i * step, step), step)
        total = dst[at, :].astype(jnp.float32)
        for s in srcs: total = total + s[at, :].astype(jnp.float32)
        dst[at, :] = total.astype(dst.dtype)
        return carry
    lax.fori_loop(0, rows // step, body, 0)


HALVES = ((0, 0), (0, 1), (1, 0), (2, 0), (1, 1), (2, 1), (3, 0), (3, 1))


def mlp_kernel(nz, x, gy, gu_hbm, gd_hbm, gx_parts, mlp_parts, mlp_cross, down_sums, sums,
               xs, gys, gu, gd, mix, ggu, gx, mo, xt, zin, load, ag_s, ag_r, rs_s, rs_r, mo_s, mo_r, out, core_s, core_r, ready, done, z_s, z_r):
    c, k, n = place()
    f32, bf16 = jnp.float32, jnp.bfloat16
    slots, width = x.shape
    half = slots // 2
    rows, cols = gd.shape[2:]
    tile = nz * rows
    hello([(None, chip_at(c, r), k, n) for r in (1, 2, 3)]
          + [(None, c, 1 - k, n), (n > 0, c, k, n - 1), (n < nz - 1, c, k, n + 1)])
    def half_of(ref, h): return ref.at[pl.ds(h * half, half)]
    index = {place_: i for i, place_ in enumerate(HALVES)}
    sends = {}
    for h in range(2):
        for r in (1, 2):
            i = index[r, h]
            sends[i] = remote(half_of(x, h), xs.at[i], ag_s.at[i], ag_r.at[i], chip_at(c, r), k, n)
            if h == 0: sends[i].start()
    loads = [pltpu.make_async_copy(half_of(x, h), xs.at[h], load.at[h]) for h in range(2)]
    loads += [pltpu.make_async_copy(half_of(gy.at[r], h), gys.at[i], load.at[2 + i]) for i, (r, h) in enumerate(HALVES)]
    for cp in loads: cp.start()
    def weights(col, w, j):
        return [pltpu.make_async_copy(a.at[:, :, :, pl.ds(first + col, w)], b.at[:, :, :, pl.ds(first + col, w)], load.at[10 + 3 * j + i])
                for i, (a, b, first) in enumerate(((gu_hbm, gu, 0), (gu_hbm, gu, cols), (gd_hbm, gd, 0)))]
    for j in range(-(-cols // 256)):
        for cp in weights(j * 256, min(256, cols - j * 256), j): cp.start()
    relays = {index[3, 0]: (index[1, 0], 2), index[3, 1]: (index[2, 1], 1)}
    relays = {i: remote(xs.at[j], xs.at[i], ag_s.at[i], ag_r.at[i], chip_at(c, r), k, n) for i, (j, r) in relays.items()}
    for cp in loads: cp.wait()

    def columns(ref, at, size):
        return ref[:, :, :, pl.ds(at, size)].reshape(width, size)

    def some_rows(ref, i): return ref[i].reshape(tile, ref.shape[3])

    def to_owner(src, dst, i, s_s, s_r):
        r, h = HALVES[i]
        return remote(src.at[i], half_of(dst.at[r], h), s_s.at[i], s_r.at[i], chip_at(c, r), k, n)

    def kept(src, dst, i, j):
        return pltpu.make_async_copy(src.at[i], half_of(dst, HALVES[i][1]), out.at[j])

    def block(r, carry):
        two = pl.ds(2 * r, 2)
        @pl.when(r == 1)
        def _():
            for i in (2, 3): sends[i].wait_recv()
            relays[index[3, 0]].start()
        @pl.when(r == 3)
        def _():
            for cp in relays.values(): cp.wait_recv()
        def both(ref): return ref[two].reshape(slots, ref.shape[2])
        def put(ref, at, v): ref[two, :, at] = v.astype(bf16).reshape(2, half, v.shape[1])
        def chunk(col, w, j):
            @pl.when(r == 0)
            def _():
                for cp in weights(col, w, j): cp.wait()
            tokens = both(xs)
            hg = jnp.dot(tokens, columns(gu, col, w), preferred_element_type=f32)
            hu = jnp.dot(tokens, columns(gu, cols + col, w), preferred_element_type=f32)
            gm = jnp.dot(both(gys), columns(gd, col, w), preferred_element_type=f32)
            for q in range(w // 128):
                gate, up, g = (t[:, 128 * q : 128 * q + 128] for t in (hg, hu, gm))
                sg = 1.0 / (1.0 + jnp.exp(-gate))
                act = gate * sg
                put(mix, pl.ds(col + 128 * q, 128), act * up)
                put(ggu, pl.ds(col + 128 * q, 128), g * up * (sg * (1.0 + gate * (1.0 - sg))))
                put(ggu, pl.ds(cols + col + 128 * q, 128), g * act)
        def pair(j, carry):
            chunk(pl.multiple_of(j * 256, 256), 256, j)
            return carry
        lax.fori_loop(0, cols // 256, pair, 0)
        if cols % 256: chunk(cols // 256 * 256, cols % 256, cols // 256)
        @pl.when(r == 0)
        def _():
            for i in (4, 5): sends[i].start()
        @pl.when(r == 1)
        def _():
            for i in (4, 5): sends[i].wait_recv()
            relays[index[3, 1]].start()
        def back(i, carry):
            at = pl.ds(pl.multiple_of(i * tile, 128), tile)
            put(gx, at, lax.dot_general(both(ggu), some_rows(gu, i), contract_last, preferred_element_type=f32))
            return carry
        lax.fori_loop(0, CHIPS * CORES, back, 0)
        for t in range(CHIPS):
            @pl.when(r == t)
            def _():
                for i in (2 * t, 2 * t + 1):
                    (to_owner(gx, gx_parts, i, rs_s, rs_r) if t else kept(gx, gx_parts.at[0], i, i)).start()
                if t > 1:
                    for i in (2 * t - 2, 2 * t - 1): to_owner(mo, mlp_parts, i, mo_s, mo_r).start()
        def down(i, carry):
            at = pl.ds(pl.multiple_of(i * tile, 128), tile)
            put(mo, at, lax.dot_general(both(mix), some_rows(gd, i), contract_last, preferred_element_type=f32))
            return carry
        lax.fori_loop(0, CHIPS * CORES, down, 0)
        for t in (0, 3):
            @pl.when(r == t)
            def _():
                for i in (2 * t, 2 * t + 1):
                    (kept(mo, mlp_parts.at[0], i, 2 + i) if t == 0 else kept(mo, mlp_cross, i, i - 2)).start()
        return carry
    lax.fori_loop(0, CHIPS, block, 0)

    pl.semaphore_signal(ready, inc=1, device_id={"wide": c * CORES + 1 - k, "narrow": n}, device_id_type=MESH)
    pl.semaphore_wait(ready, 1)
    sent, came = pl.ds(0, CHIPS), pl.ds(CHIPS, CHIPS)
    pairs = ((gys, mix, gd), (xs, ggu, gu))

    def tiles(total): return [(t * 256, min(256, total - t * 256)) for t in range(-(-total // 256))]

    def to_core(i, col, w, sem):
        ref = pairs[i][2]
        return remote(ref.at[sent, :, :, pl.ds(col, w)], ref.at[came, :, :, pl.ds(col, w)], core_s.at[sem], core_r.at[sem], c, 1 - k, n)

    def to_sums(t): return pltpu.make_async_copy(gu.at[CHIPS + t], sums.at[:, t], done.at[t])

    def each(i, body):
        total, base = pairs[i][2].shape[-1], 0 if i == 0 else len(tiles(cols))
        def step(j, carry):
            body(pl.multiple_of(j * 256, 256), 256, base + j)
            return carry
        lax.fori_loop(0, total // 256, step, 0)
        if total % 256: body(total // 256 * 256, total % 256, base + total // 256)

    def terms(i, kk, use):
        src, right, ref = pairs[i]
        for t in range(CHIPS):
            at = pl.ds(pl.multiple_of((t * CORES + kk) * tile, 128), tile)
            for r in range(CHIPS):
                xt[t * tile : (t + 1) * tile, r * slots : (r + 1) * slots] = src[2 * r : 2 * r + 2, :, at].reshape(slots, tile).T
        def body(col, w, sem):
            b = right[:, :, pl.ds(col, w)].reshape(CHIPS * slots, w)
            use(i, col, w, sem, jnp.dot(xt[...], b, preferred_element_type=f32).reshape(CHIPS, nz, rows, w))
        each(i, body)

    def theirs(i, col, w, sem, v):
        pairs[i][2][sent, :, :, pl.ds(col, w)] = v.astype(bf16)
        to_core(i, col, w, sem).start()

    def ours(i, col, w, sem, v):
        to_core(i, col, w, sem).wait_recv()
        ref = pairs[i][2]
        here = (came, slice(None), slice(None), pl.ds(col, w))
        ref[here] = (ref[here].astype(f32) + v).astype(bf16)

    def hop(way, j):
        return remote(gd.at[came, j], zin.at[way, jnp.clip(j - n - 1 if way == 0 else n - 1 - j, 0, nz - 2)],
                      z_s.at[way, j], z_r.at[way, j], c, k, n + 1 if way == 0 else n - 1)

    def along(t):
        for way in range(2):
            hops = n if way == 0 else nz - 1 - n
            j = jnp.clip(n + nz - 1 - t if way == 0 else t - hops, 0, nz - 1)
            @pl.when((hops > 0) & (t >= hops))
            def _():
                hop(way, j).wait_recv()
                for i in range(CHIPS):
                    add_into(gd.at[CHIPS + i, j], zin.at[way, jnp.clip(j - n if way == 0 else n - j, 0, nz - 2), i])
            @pl.when((t >= hops) & (j != n))
            def _(): hop(way, j).start()

    terms(0, 1 - k, theirs)
    terms(0, k, ours)
    along(0)
    terms(1, 1 - k, theirs)
    along(1)
    terms(1, k, ours)
    for t in range(CHIPS): to_sums(t).start()
    for t in range(2, nz): along(t)
    own_down = pltpu.make_async_copy(gd.at[came, n], down_sums, done.at[CHIPS])
    own_down.start()

    for cp in (*sends.values(), *relays.values()): cp.wait_send()
    for i in range(2):
        kept(gx, gx_parts.at[0], i, i).wait()
        kept(mo, mlp_parts.at[0], i, 2 + i).wait()
        kept(mo, mlp_cross, 6 + i, 4 + i).wait()
    for i in range(2): each(i, lambda col, w, sem: to_core(i, col, w, sem).wait_send())
    for t in range(CHIPS): to_sums(t).wait()
    for j in range(nz):
        for way in range(2):
            @pl.when(n < j if way == 0 else n > j)
            def _(): hop(way, j).wait_send()
    own_down.wait()
    for i in range(2, 6): to_owner(mo, mlp_parts, i, mo_s, mo_r).wait()
    for i in range(2, 8): to_owner(gx, gx_parts, i, rs_s, rs_r).wait()


def mlp_all(nz, x, gy, gu, gd):
    slots, width = x.shape
    rows, cols = gd.shape[2:]
    bf, dma, vm = jnp.bfloat16, pltpu.SemaphoreType.DMA, pltpu.VMEM
    def blocks(w): return jax.ShapeDtypeStruct((CHIPS, slots, w), bf)
    def halves(w): return vm((2 * CHIPS, slots // 2, w), bf)
    tiles = -(-cols // 256)
    flops = 2 * 9 * CHIPS * slots * width * cols
    return pl.pallas_call(
        functools.partial(mlp_kernel, nz),
        out_shape=(blocks(width), jax.ShapeDtypeStruct((3, slots, width), bf), jax.ShapeDtypeStruct((slots, width), bf),
                   jax.ShapeDtypeStruct((CHIPS, rows, cols), bf), jax.ShapeDtypeStruct((nz, CHIPS, rows, 2 * cols), bf)),
        in_specs=[ANY] * 4, out_specs=(ANY,) * 5,
        scratch_shapes=[halves(width), halves(width), vm(gu.shape, bf), vm(gd.shape, bf), halves(cols), halves(2 * cols), halves(width),
                        halves(width), vm((CHIPS * nz * rows, CHIPS * slots), bf), vm((2, nz - 1, CHIPS, rows, cols), bf), dma((10 + 3 * tiles,)), dma((8,)), dma((8,)), dma((8,)), dma((8,)),
                        dma((8,)), dma((8,)), dma((6,)), dma((3 * tiles,)), dma((3 * tiles,)), pltpu.SemaphoreType.REGULAR, dma((CHIPS + 1,)), dma((2, nz)), dma((2, nz))],
        compiler_params=pltpu.CompilerParams(collective_id=1, has_side_effects=True, vmem_limit_bytes=62 << 20),
        cost_estimate=pl.CostEstimate(flops=flops, bytes_accessed=60 << 20, transcendentals=CHIPS * slots * cols),
        name="mlp_all",
    )(x, gy, gu, gd)


PAIR = 2 * HEAD_SIZE
REPEAT = QUERY_HEADS // KEY_VALUE_HEADS
PAIRS = REPEAT // 2


def lane_tables(positions):
    cosine, sine = rope_tables(positions)
    first = jnp.arange(HEAD_SIZE) < HEAD_SIZE // 2
    low, high = jnp.where(first, -sine, 0.0), jnp.where(first, 0.0, sine)
    return jnp.stack([jnp.concatenate([t, t], 1) for t in (cosine, low, high)])


def rotate(u, tables):
    half = HEAD_SIZE // 2
    return u * tables[0] + pltpu.roll(u, PAIR - half, 1) * tables[1] + pltpu.roll(u, half, 1) * tables[2]


def unrotate(g, tables):
    half = HEAD_SIZE // 2
    return g * tables[0] + pltpu.roll(g * tables[2], PAIR - half, 1) + pltpu.roll(g * tables[1], half, 1)


def row_blocks(slots):
    return [(at, min(128, slots - at), at + 128) for at in range(0, slots, 128)]


def causal(s, below, fill):
    clear = s.shape[1] - 128
    last = jnp.where(below, s[:, clear:], fill)
    return jnp.concatenate([s[:, :clear], last], 1) if clear else last


def scaled(x, gain):
    return (x * lax.rsqrt(jnp.mean(x * x, axis=-1, keepdims=True) + norm_eps) * gain).astype(jnp.bfloat16)


def attend_kernel(nz, tok, gain1, gain2, tab_ref, wq_hbm, wo_hbm, gy, gd_own,
                  qr_ref, k_out, v_out, lse_ref, ctx_ref, xn1, hidden, xn2, gys, gd, ks, vs, wq, wo, qkv,
                  load, loc, g_s, g_r, h_s, h_r, f_s, f_r, e_s, e_r):
    g = pl.program_id(0)
    f32, bf16 = jnp.float32, jnp.bfloat16
    slots, width = tok.shape
    c, k, n = at = place()
    mine = [pltpu.make_async_copy(gd_own, gd.at[:, k * nz + n], loc.at[0]), pltpu.make_async_copy(gy, gys.at[0], loc.at[1])]
    line = Line(nz, at, (gd,), f_s, f_r, lambda ref, z: ref.at[:, k * nz + z])
    half = slots // 2
    sends = [remote(gy, gys.at[r], g_s.at[r - 1], g_r.at[r - 1], chip_at(c, r), k, n) for r in (1, 2)]
    relays = [remote(gys.at[1, pl.ds(0, half)], gys.at[3, pl.ds(0, half)], h_s.at[0], h_r.at[0], chip_at(c, 2), k, n),
              remote(gys.at[2, pl.ds(half, half)], gys.at[3, pl.ds(half, half)], h_s.at[1], h_r.at[1], chip_at(c, 1), k, n)]
    def twin(z):
        ref = gd.at[:, k * nz + z]
        return remote(ref, ref, e_s.at[z], e_r.at[z], c, 1 - k, n)
    def load_q(j):
        at = pl.ds(j * 256 if isinstance(j, int) else pl.multiple_of(j * 256, 256), 256)
        return pltpu.make_async_copy(wq_hbm.at[:, at], wq.at[:, at], load.at[j])
    @pl.when(g == 0)
    def _():
        hello([(None, chip_at(c, r), k, n) for r in (1, 2)]
              + [(None, c, 1 - k, n), (n > 0, c, k, n - 1), (n < nz - 1, c, k, n + 1)])
        for cp in mine + sends: cp.start()
        for j in range(wq.shape[1] // 256): load_q(j).start()
        pltpu.make_async_copy(wo_hbm, wo, loc.at[2]).start()
        mine[0].wait()
        for way in range(2): line.start(0, 0, way)
        twin(n).start()
        def norm(i, carry):
            at = pl.ds(pl.multiple_of(i * 16, 16), 16)
            xn1[at, :] = scaled(tok[at, :].astype(f32), gain1[...])
            return carry
        lax.fori_loop(0, slots // 16, norm, 0)
        def project(j, carry):
            load_q(j).wait()
            at = pl.ds(pl.multiple_of(j * 256, 256), 256)
            qkv[:, at] = jnp.dot(xn1[...], wq[:, at], preferred_element_type=f32)
            return carry
        lax.fori_loop(0, wq.shape[1] // 256, project, 0)
    @pl.when(g == 1)
    def _(): line.step(0, 1, lambda z: twin(z).start())
    @pl.when(g == 0)
    def _():
        ks[...] = jnp.zeros_like(ks)
        vs[...] = jnp.zeros_like(vs)
    lane = lax.broadcasted_iota(jnp.int32, (slots, PAIR), 1)
    tables = (tab_ref[0], tab_ref[1], tab_ref[2])
    first = QUERY_HEADS * HEAD_SIZE
    def pair_at(at): return pl.ds(pl.multiple_of(at, PAIR), PAIR)
    key = rotate(qkv[:, pair_at(first + g // 2 * PAIR)], tables)
    val = qkv[:, pair_at(first + KEY_VALUE_HEADS * HEAD_SIZE + g // 2 * PAIR)]
    odd = g % 2 == 1
    for x, own, stack, scale in ((key, k_out, ks, HEAD_SIZE ** -0.5), (val, v_out, vs, 1.0)):
        x = jnp.where(lane < HEAD_SIZE, jnp.where(odd, pltpu.roll(x, HEAD_SIZE, 1), x), 0.0).astype(bf16)
        own[0] = x
        x = x.astype(f32) * scale
        stack[0, 0:slots, :] = x.astype(bf16)
        stack[1, 0:slots, :] = pltpu.roll(x, HEAD_SIZE, 1).astype(bf16)
    for start, size, keys in row_blocks(slots):
        below = lax.broadcasted_iota(jnp.int32, (size, 128), 0) >= lax.broadcasted_iota(jnp.int32, (size, 128), 1)
        lse = jnp.zeros((size, PAIR), f32)
        here = lane[0:size]
        for p in range(PAIRS):
            span = slice(p * PAIR, (p + 1) * PAIR)
            rows = slice(start, start + size)
            q = rotate(qkv[rows, pair_at(g * REPEAT * HEAD_SIZE + p * PAIR)], tuple(t[rows] for t in tables)).astype(bf16)
            qr_ref[rows, span] = q
            ctx = jnp.zeros((size, PAIR), f32)
            for h in range(2):
                s = lax.dot_general(q, ks[h, 0:keys, :], contract_last, preferred_element_type=f32)
                s = causal(s, below, masked_score)
                peak = jnp.max(s, axis=-1, keepdims=True)
                e = jnp.exp(s - peak)
                total = jnp.sum(e, axis=-1, keepdims=True)
                lse = jnp.where(here == 2 * p + h, peak + jnp.log(total), lse)
                probs = (e * (1.0 / total)).astype(bf16)
                ctx = ctx + jnp.dot(probs, vs[h, 0:keys, :], preferred_element_type=f32)
            ctx_ref[rows, pair_at(g * REPEAT * HEAD_SIZE + p * PAIR)] = ctx.astype(bf16)
        lse_ref[0, start : start + size, :] = lse
    @pl.when(g == KEY_VALUE_HEADS - 1)
    def _():
        for cp in sends: cp.wait_recv()
        for cp in relays: cp.start()
        line.step(0, 2, lambda z: twin(z).start())
        pltpu.make_async_copy(wo_hbm, wo, loc.at[2]).wait()
        def project(j, carry):
            at = pl.ds(pl.multiple_of(j * 256, 256), 256)
            hidden[:, at] = tok[:, at].astype(f32) + lax.dot_general(ctx_ref[...], wo[at, :], contract_last, preferred_element_type=f32)
            return carry
        lax.fori_loop(0, width // 256, project, 0)
        def norm(i, carry):
            at = pl.ds(pl.multiple_of(i * 16, 16), 16)
            xn2[at, :] = scaled(hidden[at, :], gain2[...])
            return carry
        lax.fori_loop(0, slots // 16, norm, 0)
        for s in range(3, nz): line.step(0, s, lambda z: twin(z).start())
        for cp in relays: cp.wait()
        for z in range(nz): twin(z).wait()
        for cp in sends: cp.wait_send()
        mine[1].wait()
        line.finish(0)


def attend_all(nz, tokens, gain1, gain2, tables, w_qkv, w_out, gy, gd_own):
    slots, width = tokens.shape
    dma, vm = pltpu.SemaphoreType.DMA, pltpu.VMEM
    bf16, f32 = jnp.bfloat16, jnp.float32
    keys = -(-slots // 128) * 128
    heads = QUERY_HEADS * HEAD_SIZE
    shape = jax.ShapeDtypeStruct
    def fixed(*dims): return pl.BlockSpec(dims, lambda g: (0,) * len(dims))
    per_head = pl.BlockSpec((1, slots, PAIR), lambda g: (g, 0, 0))
    per_head_shape = (KEY_VALUE_HEADS, slots, PAIR)
    return pl.pallas_call(
        functools.partial(attend_kernel, nz),
        grid=(KEY_VALUE_HEADS,),
        out_shape=(shape((slots, heads), bf16), shape(per_head_shape, bf16), shape(per_head_shape, bf16), shape(per_head_shape, f32),
                   shape((slots, heads), bf16), shape((slots, width), bf16), shape((slots, width), f32), shape((slots, width), bf16),
                   shape((CHIPS,) + gy.shape, bf16), shape((CHIPS, CORES * nz) + gd_own.shape[1:], bf16)),
        in_specs=[fixed(slots, width), fixed(1, width), fixed(1, width), fixed(3, slots, PAIR), ANY, ANY, fixed(*gy.shape), fixed(*gd_own.shape)],
        out_specs=(pl.BlockSpec((slots, REPEAT * HEAD_SIZE), lambda g: (0, g)), per_head, per_head, per_head,
                   fixed(slots, heads), fixed(slots, width), fixed(slots, width), fixed(slots, width), ANY, ANY),
        scratch_shapes=[vm((2, keys, PAIR), bf16), vm((2, keys, PAIR), bf16), vm(w_qkv.shape, bf16), vm(w_out.shape, bf16),
                        vm((slots, w_qkv.shape[1]), f32), dma((w_qkv.shape[1] // 256,)), dma((3,)), dma((2,)), dma((2,)), dma((2,)), dma((2,)),
                        dma((1, 2, nz)), dma((1, 2, nz)), dma((nz,)), dma((nz,))],
        compiler_params=pltpu.CompilerParams(collective_id=4, has_side_effects=True, vmem_limit_bytes=56 << 20),
        cost_estimate=pl.CostEstimate(flops=4 * slots * width * heads, bytes_accessed=40 << 20, transcendentals=QUERY_HEADS * slots * slots),
        name="attend",
    )(tokens, gain1, gain2, tables, w_qkv, w_out, gy, gd_own)


def products(left_side, right_side, kk, xt, put):
    part = xt.shape[0] // CHIPS
    for t in range(CHIPS):
        at = pl.ds(pl.multiple_of((t * CORES + kk) * part, 128), part)
        xt[t * part : (t + 1) * part, :] = left_side[:, at].T
    def step(j, carry):
        at = pl.ds(pl.multiple_of(j * 256, 256), 256)
        put(at, jnp.dot(xt[...], right_side[:, at], preferred_element_type=jnp.float32).reshape(CHIPS, part, 256))
        return carry
    lax.fori_loop(0, right_side.shape[1] // 256, step, 0)


def to_their_core(left_side, right_side, k, xt, away, swap):
    def put(at, v): away[:, :, at] = v.astype(jnp.bfloat16)
    products(left_side, right_side, 1 - k, xt, put)
    swap.start()


def with_their_core(left_side, right_side, k, xt, took, swap):
    swap.wait_recv()
    def put(at, v): took[:, :, at] = (took[:, :, at].astype(jnp.float32) + v).astype(jnp.bfloat16)
    products(left_side, right_side, k, xt, put)


def attend_back_kernel(q_ref, k_ref, v_ref, lse_ref, gc_ref, tab_ref, part, gal, ctx, gq_ref, gk_ref, gv_ref, crossed, core_sums,
                       ks, kt, vt, ds, pr, qs, gs, away, took, xt, s_s, s_r, core_s, core_r, done):
    g = pl.program_id(0)
    c, k, n = place()
    copy = remote(part, crossed, s_s, s_r, chip_at(c, 3), k, n)
    swap = remote(away, took, core_s, core_r, c, 1 - k, n)
    store = pltpu.make_async_copy(took, core_sums, done)
    @pl.when(g == 0)
    def _():
        hello([(None, chip_at(c, 3), k, n), (None, c, 1 - k, n)])
        copy.start()
        to_their_core(gal, ctx, k, xt, away, swap)
    @pl.when(g == KEY_VALUE_HEADS - 1)
    def _():
        with_their_core(gal, ctx, k, xt, took, swap)
        store.start()
    f32, bf16 = jnp.float32, jnp.bfloat16
    slots = q_ref.shape[0]
    scale = HEAD_SIZE ** -0.5
    @pl.when(g == 0)
    def _():
        for ref in (ks, kt, vt, ds, pr): ref[...] = jnp.zeros_like(ref)
    lane = lax.broadcasted_iota(jnp.int32, (slots, PAIR), 1)
    tables = (tab_ref[0], tab_ref[1], tab_ref[2])
    key, val = k_ref[0].astype(f32), v_ref[0].astype(f32)
    for stack, x in ((ks, key * scale), (kt, key), (vt, val)):
        stack[0, 0:slots, :] = x.astype(bf16)
        stack[1, 0:slots, :] = pltpu.roll(x, HEAD_SIZE, 1).astype(bf16)
    for at, size, keys in row_blocks(slots):
        rows = slice(at, at + size)
        below = lax.broadcasted_iota(jnp.int32, (size, 128), 0) >= lax.broadcasted_iota(jnp.int32, (size, 128), 1)
        lse = lse_ref[0, rows, :]
        for p in range(PAIRS):
            span = slice(p * PAIR, (p + 1) * PAIR)
            deep = slice(p * slots + at, p * slots + at + size)
            q, gc = q_ref[rows, span], gc_ref[rows, span]
            qs[deep, :] = q
            gs[deep, :] = gc
            gq = jnp.zeros((size, PAIR), f32)
            for h in range(2):
                s = lax.dot_general(q, ks[h, 0:keys, :], contract_last, preferred_element_type=f32)
                e = jnp.exp(s - lse[:, 2 * p + h : 2 * p + h + 1])
                probs = causal(e, below, 0.0)
                pr[h, deep, 0:keys] = probs.astype(bf16)
                gp = lax.dot_general(gc, vt[h, 0:keys, :], contract_last, preferred_element_type=f32)
                inner = jnp.sum(gp * probs, axis=-1, keepdims=True)
                grad = (probs * (gp - inner) * scale).astype(bf16)
                ds[h, deep, 0:keys] = grad
                gq = gq + jnp.dot(grad, kt[h, 0:keys, :], preferred_element_type=f32)
            gq_ref[rows, span] = unrotate(gq, tuple(t[rows] for t in tables)).astype(bf16)
    for src, right, out, turn in ((ds, qs, gk_ref, True), (pr, gs, gv_ref, False)):
        lo, hi = (
            lax.dot_general(src[h], right[...], contract_first, preferred_element_type=f32)[0:slots] for h in range(2)
        )
        x = jnp.where(lane < HEAD_SIZE, lo + pltpu.roll(hi, HEAD_SIZE, 1), 0.0)
        if turn: x = unrotate(x, tables)
        @pl.when(g % 2 == 0)
        def _(): out[...] = x
        @pl.when(g % 2 == 1)
        def _(): out[...] = jnp.where(lane < HEAD_SIZE, out[...], pltpu.roll(x, HEAD_SIZE, 1))
    @pl.when(g == KEY_VALUE_HEADS - 1)
    def _():
        copy.wait()
        swap.wait_send()
        store.wait()


def attend_back_all(q, k, v, lse, grad_context, tables, part, gal, ctx):
    slots, width = gal.shape
    block = (CHIPS, width // (CHIPS * CORES), ctx.shape[1])
    wide = REPEAT * HEAD_SIZE
    bf16, f32, vm = jnp.bfloat16, jnp.float32, pltpu.VMEM
    keys = -(-slots // 128) * 128
    shape = jax.ShapeDtypeStruct
    per_head = pl.BlockSpec((1, slots, PAIR), lambda g: (g, 0, 0))
    wide_spec = pl.BlockSpec((slots, wide), lambda g: (0, g))
    two = pl.BlockSpec((slots, PAIR), lambda g: (0, g // 2))
    return pl.pallas_call(
        attend_back_kernel,
        grid=(KEY_VALUE_HEADS,),
        out_shape=(shape((slots, QUERY_HEADS * HEAD_SIZE), bf16), shape((slots, KEY_VALUE_HEADS * HEAD_SIZE), f32),
                   shape((slots, KEY_VALUE_HEADS * HEAD_SIZE), f32), shape(part.shape, part.dtype), shape(block, bf16)),
        in_specs=[wide_spec, per_head, per_head, per_head, wide_spec, pl.BlockSpec((3, slots, PAIR), lambda g: (0, 0, 0)), ANY,
                  pl.BlockSpec(gal.shape, lambda g: (0, 0)), pl.BlockSpec(ctx.shape, lambda g: (0, 0))],
        out_specs=(wide_spec, two, two, ANY, ANY),
        scratch_shapes=[vm((2, keys, PAIR), bf16)] * 3 + [vm((2, PAIRS * slots, keys), bf16)] * 2 + [vm((PAIRS * slots, PAIR), bf16)] * 2
        + [vm(block, bf16), vm(block, bf16), vm((CHIPS * block[1], slots), bf16)] + [pltpu.SemaphoreType.DMA] * 5,
        compiler_params=pltpu.CompilerParams(collective_id=2, has_side_effects=True, vmem_limit_bytes=48 << 20),
        name="attend_back",
    )(q, k, v, lse, grad_context, tables, part, gal, ctx)


class SumLine:
    def __init__(self, nz, at, piece, slot, send, recv):
        self.nz, self.at, self.piece, self.slot, self.send, self.recv = nz, at, piece, slot, send, recv

    def _hop(self, a, way, j):
        c, k, n = self.at
        i = jnp.clip(j - n - 1 if way == 0 else n - 1 - j, 0, self.nz - 2)
        return remote(self.piece(a, j), self.slot(a, way, i), self.send.at[a, way, j], self.recv.at[a, way, j],
                      c, k, n + 1 if way == 0 else n - 1)

    def step(self, some, t):
        nz, n = self.nz, self.at[2]
        for way in range(2):
            hops = n if way == 0 else nz - 1 - n
            j = jnp.clip(n + nz - 1 - t if way == 0 else t - hops, 0, nz - 1)
            for a in some:
                @pl.when((hops > 0) & (t >= hops))
                def _():
                    self._hop(a, way, j).wait_recv()
                    add_into(self.piece(a, j), self.slot(a, way, jnp.clip(j - n if way == 0 else n - j, 0, nz - 2)))
                @pl.when((t >= hops) & (j != n))
                def _(): self._hop(a, way, j).start()

    def finish(self, a):
        n = self.at[2]
        for j in range(self.nz):
            for way in range(2):
                @pl.when(n < j if way == 0 else n > j)
                def _(): self._hop(a, way, j).wait_send()


def gradient_kernel(nz, sums_hbm, xn_hbm, gq_hbm, wq_hbm, tok_hbm, gh_hbm, gain, gain_mlp, out0, out1, out2, grad_tokens,
                    took0, took1, took2, away1, away2, zbuf0, zbuf1, zbuf2, xn, gq, wq, tok, gh, gx, xt, gain_row,
                    core_s, core_r, half_s, half_r, main_s, main_r, z_s, z_r, load, loc):
    f32, bf16 = jnp.float32, jnp.bfloat16
    items = 3
    outs, took, away, zbuf = (out0, out1, out2), (took0, took1, took2), (None, away1, away2), (zbuf0, zbuf1, zbuf2)
    c, k, n = place()
    left, right = n > 0, n < nz - 1
    cx, cy, cd = (chip_at(c, r) for r in (1, 2, 3))
    loads = [pltpu.make_async_copy(a, b, load.at[i]) for i, (a, b) in enumerate(
        ((sums_hbm, took0), (xn_hbm, xn), (gq_hbm, gq), (wq_hbm, wq), (tok_hbm, tok), (gh_hbm, gh)))]
    for cp in loads: cp.start()
    hello([(None, cc, k, n) for cc in (cx, cy, cd)] + [(None, c, 1 - k, n), (left, c, k, n - 1), (right, c, k, n + 1)])
    slots, width = xn.shape
    rows = out0.shape[0]
    part = nz * rows
    half = part // 2
    top, low = pl.ds(0, half), pl.ds(half, half)
    def arrive(a, at, size): return zbuf[a].at[pl.ds(at, size)]
    swap = [a and remote(away[a], took[a], core_s.at[a - 1], core_r.at[a - 1], c, 1 - k, n) for a in range(items)]
    cross = [[remote(took[a].at[cd, top], arrive(a, 2 * part, half), half_s.at[a, 0], half_r.at[a, 0], cx, k, n),
              remote(took[a].at[cd, low], arrive(a, 2 * part + half, half), half_s.at[a, 1], half_r.at[a, 1], cy, k, n)]
             for a in range(items)]
    main = [[remote(took[a].at[cx, top], arrive(a, 0, half), main_s.at[a, 0], main_r.at[a, 0], cx, k, n),
             remote(took[a].at[cy, low], arrive(a, part + half, half), main_s.at[a, 1], main_r.at[a, 1], cy, k, n),
             remote(took[a].at[cx, low], arrive(a, half, half), main_s.at[a, 2], main_r.at[a, 2], cx, k, n),
             remote(took[a].at[cy, top], arrive(a, part, half), main_s.at[a, 3], main_r.at[a, 3], cy, k, n)]
            for a in range(items)]

    def input_gradient():
        loads[3].wait()
        def step(j, carry):
            at = pl.ds(pl.multiple_of(j * 256, 256), 256)
            gx[:, at] = lax.dot_general(gq[...], wq[at, :], contract_last, preferred_element_type=f32)
            return carry
        lax.fori_loop(0, width // 256, step, 0)

    def input_norm():
        for cp in loads[4:]: cp.wait()
        def step(j, total):
            at = pl.ds(pl.multiple_of(j * 16, 16), 16)
            x, g = tok[at, :].astype(f32), gx[at, :]
            scale = lax.rsqrt(jnp.mean(x * x, axis=-1, keepdims=True) + norm_eps)
            hat = x * scale
            g1 = g * gain[...]
            gh[at, :] = gh[at, :] + scale * (g1 - hat * jnp.mean(g1 * hat, axis=-1, keepdims=True))
            t = g * hat
            return total + t[0:8] + t[8:16]
        total = lax.fori_loop(0, slots // 16, step, jnp.zeros((8, width), f32))
        return jnp.sum(total, axis=0, keepdims=True)

    def gains_swap(of_attn):
        row = lax.broadcasted_iota(jnp.int32, (128, part), 0)
        def columns_of(t, kk):
            at = pl.ds(pl.multiple_of((t * CORES + kk) * part, 128), part)
            return jnp.where(row == 0, gain_row[0:1, at], jnp.where(row == 1, gain_mlp[0:1, at], 0.0)).T
        gain_row[0:1, :] = of_attn
        for t in range(CHIPS): away[2][t] = columns_of(t, 1 - k).astype(bf16)
        swap[2].start()
        swap[2].wait_recv()
        for t in range(CHIPS): took[2][t] = (took[2][t].astype(f32) + columns_of(t, k)).astype(bf16)
        for cp in cross[2]: cp.start()

    def relay(a):
        cross[a][0].wait_recv()
        add_into(took[a].at[cy, top], arrive(a, 2 * part, half))
        main[a][3].start()
        cross[a][1].wait_recv()
        add_into(took[a].at[cx, low], arrive(a, 2 * part + half, half))
        for i in (2, 0, 1): main[a][i].start()

    def mine(a):
        for cp in main[a]: cp.wait_recv()
        add_into(took[a].at[c], arrive(a, 0, part), arrive(a, part, part))

    line = SumLine(nz, (c, k, n), lambda a, j: took[a].at[c, pl.ds(pl.multiple_of(j * rows, rows), rows)],
                   lambda a, way, i: arrive(a, pl.multiple_of(2 * part + 2 * half + (way * (nz - 1) + i) * rows, rows), rows), z_s, z_r)

    loads[0].wait()
    for cp in cross[0]: cp.start()
    for cp in loads[1:3]: cp.wait()
    to_their_core(xn, gq, k, xt, away[1], swap[1])
    relay(0)
    with_their_core(xn, gq, k, xt, took[1], swap[1])
    for cp in cross[1]: cp.start()
    input_gradient()
    gains_swap(input_norm())
    stores = [pltpu.make_async_copy(gh, grad_tokens, loc.at[items])]
    stores[0].start()
    for a in range(1, items): relay(a)
    mine(0)
    for t in range(nz): line.step([0], t)
    stores.append(pltpu.make_async_copy(line.piece(0, n), outs[0], loc.at[0]))
    stores[-1].start()
    for a in range(1, items):
        mine(a)
        stores.append(pltpu.make_async_copy(took[a].at[c], outs[a], loc.at[a]))
        stores[-1].start()
    for cp in stores: cp.wait()
    for a in range(items):
        if a: swap[a].wait_send()
        for cp in cross[a] + main[a]: cp.wait_send()
    line.finish(0)


def gradient_all(nz, sums, xn, gq, wq, tokens, grad_hidden, gain, gain_mlp, cid):
    dma, vm = pltpu.SemaphoreType.DMA, pltpu.VMEM
    bf16, f32 = jnp.bfloat16, jnp.float32
    slots, width = xn.shape
    m = 3
    part = width // (CHIPS * CORES)
    rows = part // nz
    widths = (sums.shape[2], gq.shape[1], 128)
    shape = jax.ShapeDtypeStruct
    blocks = [vm((CHIPS, part, w), bf16) for w in widths]
    row = pl.BlockSpec((1, width), lambda: (0, 0))
    return pl.pallas_call(
        functools.partial(gradient_kernel, nz),
        out_shape=(shape((rows, widths[0]), bf16),) + tuple(shape((part, w), bf16) for w in widths[1:]) + (shape((slots, width), f32),),
        in_specs=[ANY] * 6 + [row, row], out_specs=(ANY,) * (m + 1),
        scratch_shapes=blocks + blocks[1:] + [vm((3 * part + 2 * nz * rows, w), bf16) for w in widths]
        + [vm(xn.shape, bf16), vm(gq.shape, bf16), vm(wq.shape, bf16), vm(tokens.shape, bf16),
           vm((slots, width), f32), vm((slots, width), f32), vm((CHIPS * part, slots), bf16), vm((8, width), f32)]
        + [dma((m - 1,)), dma((m - 1,)), dma((m, 2)), dma((m, 2)), dma((m, 4)), dma((m, 4)), dma((1, 2, nz)), dma((1, 2, nz)), dma((6,)), dma((m + 1,))],
        compiler_params=pltpu.CompilerParams(collective_id=cid, has_side_effects=True, vmem_limit_bytes=62 << 20),
        name="gradient_all",
    )(sums, xn, gq, wq, tokens, grad_hidden, gain, gain_mlp)


def finish_kernel(nz, down, gu, part1, part2, sum_o, parts_hbm, crossed_hbm, hidden_hbm, valid,
                  out_q, out_k, out_v, out_gain, out_d, out_g, out_u, out_o, output,
                  acc1, acc2, in1, in2, ff, wide1, wide2, wide_ff, wide_o, parts, crossed, hidden, result,
                  z_s, z_r, ff_s, ff_r, load, loc):
    f32 = jnp.float32
    c, k, n = place()
    rows, cols = down.shape[1:]
    loads = [pltpu.make_async_copy(a, b, load.at[i]) for i, (a, b) in enumerate(
        ((part1, acc1), (part2, acc2), (parts_hbm, parts), (crossed_hbm, crossed), (hidden_hbm, hidden)))]
    for cp in loads: cp.start()
    hello([(None, chip_at(c, r), k, n) for r in (1, 2, 3)] + [(n > 0, c, k, n - 1), (n < nz - 1, c, k, n + 1)])
    acc, came = (acc1, acc2), (in1, in2)
    line = SumLine(nz, (c, k, n), lambda a, j: acc[a].at[pl.ds(pl.multiple_of(j * rows, rows), rows)],
                   lambda a, way, i: came[a].at[way, i], z_s, z_r)
    def term(m, cc): return down.at[cc] if m == 0 else gu.at[cc, :, pl.ds((m - 1) * cols, cols)]
    home = [[remote(term(m, chip_at(c, r)), ff.at[m, r - 1], ff_s.at[m, r - 1], ff_r.at[m, r - 1], chip_at(c, r), k, n)
             for r in (1, 2, 3)] for m in range(3)]
    for cps in home:
        for cp in cps: cp.start()
    for cp in loads[:2]: cp.wait()
    line.step([0, 1], 0)
    stores = []
    def store(src, dst, i):
        stores.append(pltpu.make_async_copy(src, dst, loc.at[i]))
        stores[-1].start()
    outs = (out_d, out_g, out_u)
    def put(m, r, value):
        wide_ff[m, r] = value.astype(f32)
        at = pl.ds(pl.multiple_of(chip_at(c, r) * cols, 128), cols)
        store(wide_ff.at[m, r], outs[m].at[:, at], 4 + m * CHIPS + r)
    for m in range(3): put(m, 0, term(m, c)[...])
    wide_o[...] = sum_o[...].astype(f32)
    store(wide_o, out_o, 4 + 3 * CHIPS)
    line.step([0, 1], 1)
    for cp in loads[2:]: cp.wait()
    def add(i, carry):
        at = pl.ds(pl.multiple_of(i * 16, 16), 16)
        total = hidden[at, :] + (parts[0, at, :].astype(f32) + parts[1, at, :].astype(f32) + parts[2, at, :].astype(f32)
                                 + crossed[at, :].astype(f32))
        result[at, :] = (valid[at, :] * total).astype(result.dtype)
        return carry
    lax.fori_loop(0, result.shape[0] // 16, add, 0)
    store(result, output, 5 + 3 * CHIPS)
    for t in range(2, nz): line.step([0, 1], t)
    for m in range(3):
        for r in (1, 2, 3):
            home[m][r - 1].wait_recv()
            put(m, r, ff[m, r - 1])
    wide1[...] = line.piece(0, n)[...].astype(f32)
    wide2[...] = line.piece(1, n)[...].astype(f32)
    first = 0
    for i, out in enumerate((out_q, out_k, out_v)):
        store(wide1.at[:, pl.ds(first, out.shape[1])], out, i)
        first += out.shape[1]
    store(wide2, out_gain, 3)
    for cp in stores: cp.wait()
    for cps in home:
        for cp in cps: cp.wait_send()
    for a in range(2): line.finish(a)


def finish_all(nz, down, gu, part1, part2, sum_o, parts, crossed, hidden, valid, key_width, cid):
    dma, vm = pltpu.SemaphoreType.DMA, pltpu.VMEM
    bf16, f32 = jnp.bfloat16, jnp.float32
    rows, cols = down.shape[1:]
    w1, w2 = part1.shape[1], part2.shape[1]
    def out(w): return jax.ShapeDtypeStruct((rows, w), f32)
    return pl.pallas_call(
        functools.partial(finish_kernel, nz),
        out_shape=(out(w1 - 2 * key_width), out(key_width), out(key_width), out(w2)) + (out(CHIPS * cols),) * 3
        + (out(sum_o.shape[1]), jax.ShapeDtypeStruct(hidden.shape, bf16)),
        in_specs=[VMEM, VMEM, ANY, ANY, VMEM, ANY, ANY, ANY, VMEM], out_specs=(ANY,) * 9,
        scratch_shapes=[vm(part1.shape, bf16), vm(part2.shape, bf16), vm((2, nz - 1, rows, w1), bf16), vm((2, nz - 1, rows, w2), bf16),
                        vm((3, CHIPS - 1, rows, cols), bf16), vm((rows, w1), f32), vm((rows, w2), f32), vm((3, CHIPS, rows, cols), f32),
                        vm(sum_o.shape, f32), vm(parts.shape, bf16), vm(crossed.shape, bf16), vm(hidden.shape, f32), vm(hidden.shape, bf16),
                        dma((2, 2, nz)), dma((2, 2, nz)), dma((3, 3)), dma((3, 3)), dma((5,)), dma((6 + 3 * CHIPS,))],
        compiler_params=pltpu.CompilerParams(collective_id=cid, has_side_effects=True, vmem_limit_bytes=40 << 20),
        name="finish_all",
    )(down, gu, part1, part2, sum_o, parts, crossed, hidden, valid)


def fits(mesh):
    return mesh.shape["wide"] == CHIPS * CORES


def fast_device(
    nz,
    tokens,
    cotangent,
    lengths,
    positions,
    norm_attn,
    w_query,
    w_key,
    w_value,
    w_output,
    norm_mlp,
    w_gate,
    w_up,
    w_down,
):
    f32, bf16 = jnp.float32, jnp.bfloat16
    c, k, n = place()
    slots, width = tokens.shape
    rows = w_query.shape[0]
    query_width, key_width = w_query.shape[1], w_key.shape[1]
    cols = w_gate.shape[1] // CHIPS
    valid_rows = (jnp.arange(slots) < lengths[0]).astype(f32)[:, None]
    tables = lane_tables(positions)
    grad_y = cotangent.astype(f32) * valid_rows
    grad_y_low = grad_y.astype(bf16)
    lanes = jnp.arange(128)[None]
    gains = jnp.where(lanes == 0, norm_attn[:, None], jnp.where(lanes == 1, norm_mlp[:, None], jnp.zeros((), bf16)))
    w_qkv, w_out, gain_cols, ff_gate_up, ff_down = gather_all(
        nz, w_query, w_key, w_value, w_output, gains, w_gate, w_up, w_down
    )
    gain_rows = lax.dot_general(jnp.eye(8, 128, dtype=bf16), gain_cols, contract_last, preferred_element_type=f32)
    gain_attn, gain_mlp = gain_rows[0], gain_rows[1]

    query_rotated, key_rotated, value_reduced, log_totals, context, scaled_attn, hidden, scaled_mlp, gy_all, ff_down = attend_all(
        nz, tokens, gain_attn[None], gain_mlp[None], tables, w_qkv, w_out, grad_y_low, ff_down
    )
    ff_gate_up, ff_down = (w.reshape(CHIPS * CORES, nz, rows, w.shape[-1]) for w in (ff_gate_up, ff_down))
    normed_mlp = normalize(hidden)
    grad_x_parts, mlp_parts, mlp_cross, down_sums, ff_sums = mlp_all(nz, scaled_mlp, gy_all, ff_gate_up, ff_down)
    grad_xn2 = jnp.sum(grad_x_parts.astype(f32), axis=0)
    grad_gain_mlp = jnp.sum(grad_xn2 * normed_mlp, axis=0)
    grad_hidden = grad_y + norm_back(grad_xn2 * gain_mlp, normed_mlp, hidden)
    grad_attn_low = grad_hidden.astype(bf16)
    grad_context = jnp.dot(grad_attn_low, w_out, preferred_element_type=f32).astype(bf16)
    grad_query, grad_key, grad_value, mlp_crossed, out_sums = attend_back_all(
        query_rotated, key_rotated, value_reduced, log_totals, grad_context, tables, mlp_cross, grad_attn_low, context
    )
    grad_qkv = jnp.concatenate([grad_query, grad_key.astype(bf16), grad_value.astype(bf16)], 1)
    ff_sums = lax.psum_scatter(ff_sums, "narrow", scatter_dimension=0, tiled=True)
    out_part, qkv_part, gain_part, grad_tokens = gradient_all(
        nz, out_sums, scaled_attn, grad_qkv, w_qkv, tokens, grad_hidden, gain_attn[None], grad_gain_mlp[None], 3
    )
    grad_w_query, grad_w_key, grad_w_value, gain_sums, grad_w_down, grad_w_gate, grad_w_up, grad_w_output, output = finish_all(
        nz,
        down_sums,
        ff_sums.reshape(CHIPS, rows, 2 * cols),
        qkv_part,
        gain_part,
        out_part,
        mlp_parts,
        mlp_crossed,
        hidden,
        valid_rows,
        key_width,
        5,
    )
    grad_norm_attn, grad_norm_mlp = gain_sums[:, 0], gain_sums[:, 1]
    return (
        output,
        grad_tokens,
        grad_norm_attn,
        grad_w_query,
        grad_w_key,
        grad_w_value,
        grad_w_output,
        grad_norm_mlp,
        grad_w_gate,
        grad_w_up,
        grad_w_down,
    )


def solution(mesh):
    in_specs = (
        P(("wide", "narrow"), None),
        P(("wide", "narrow"), None),
        P(("wide", "narrow")),
        P(("wide", "narrow")),
        P(("wide", "narrow")),
        P(("wide", "narrow"), None),
        P(("wide", "narrow"), None),
        P(("wide", "narrow"), None),
        P(("wide", "narrow"), None),
        P(("wide", "narrow")),
        P(("wide", "narrow"), None),
        P(("wide", "narrow"), None),
        P(("wide", "narrow"), None),
    )
    out_specs = (
        P(("wide", "narrow"), None),
        P(("wide", "narrow"), None),
        P(("wide", "narrow")),
        P(("wide", "narrow"), None),
        P(("wide", "narrow"), None),
        P(("wide", "narrow"), None),
        P(("wide", "narrow"), None),
        P(("wide", "narrow")),
        P(("wide", "narrow"), None),
        P(("wide", "narrow"), None),
        P(("wide", "narrow"), None),
    )
    body = functools.partial(fast_device, mesh.shape["narrow"]) if fits(mesh) else per_device
    return jax.shard_map(
        body, mesh=mesh, in_specs=in_specs, out_specs=out_specs, check_vma=False
    )
```
